32 devices in a mesh: dp: 4 (over y, core), seq: 2 (over x), tensor: 4 (over z).
Axes of the slice: x: 2, y: 2, z: 4, core: 2. Of those that a mesh axis runs over, the one named last changes fastest.
Arguments:
- tokens: bfloat16 [1024, 40, 1024], P(('seq', 'tensor'), 'dp'), may hold values from -6 to 6
- norm1_gain: float32 [1024], replicated, may hold values from 0.5 to 1.5
- norm1_bias: float32 [1024], replicated, may hold values from -0.12 to 0.12
- w_query: bfloat16 [1024, 1024], P(None, 'tensor'), may hold values from -0.1875 to 0.1875
- w_key: bfloat16 [1024, 1024], P(None, 'tensor'), may hold values from -0.1875 to 0.1875
- w_value: bfloat16 [1024, 1024], P(None, 'tensor'), may hold values from -0.1875 to 0.1875
- w_out: bfloat16 [1024, 1024], P('tensor'), may hold values from -3 to 3
- norm2_gain: float32 [1024], replicated, may hold values from 0.5 to 1.5
- norm2_bias: float32 [1024], replicated, may hold values from -1.8 to 1.8
- w_gate: bfloat16 [1024, 4096], P(None, 'tensor'), may hold values from -0.1875 to 0.1875
- w_up: bfloat16 [1024, 4096], P(None, 'tensor'), may hold values from -0.1875 to 0.1875
- w_down: bfloat16 [4096, 1024], P('tensor'), may hold values from -0.09375 to 0.09375
- out_grad: bfloat16 [40, 160, 1024], P('dp'), may hold values from -6 to 6
- masked_rows: int32 [40, 160], P('dp'), may hold values from 0 to 1024, as said below
- window_counts: int32 [4], P('dp'), may hold values from 1 to 10, as said below
Outputs:
- output: bfloat16 [1024, 40, 1024], P(('seq', 'tensor'), 'dp')
- grad_tokens: float32 [1024, 40, 1024], P(('seq', 'tensor'), 'dp')
- grad_norm1_gain: float32 [1024], P(('dp', 'seq', 'tensor'))
- grad_norm1_bias: float32 [1024], P(('dp', 'seq', 'tensor'))
- grad_w_query: float32 [1024, 1024], P(('dp', 'seq'), 'tensor')
- grad_w_key: float32 [1024, 1024], P(('dp', 'seq'), 'tensor')
- grad_w_value: float32 [1024, 1024], P(('dp', 'seq'), 'tensor')
- grad_w_out: float32 [1024, 1024], P('tensor', ('dp', 'seq'))
- grad_norm2_gain: float32 [1024], P(('dp', 'seq', 'tensor'))
- grad_norm2_bias: float32 [1024], P(('dp', 'seq', 'tensor'))
- grad_w_gate: float32 [1024, 4096], P(('dp', 'seq'), 'tensor')
- grad_w_up: float32 [1024, 4096], P(('dp', 'seq'), 'tensor')
- grad_w_down: float32 [4096, 1024], P('tensor', ('dp', 'seq'))
The draws below stay inside these ranges and needn't reach their ends.
Inputs may be any that keep to these rules, and one draw needn't show every extreme that they name: Group d's live windows are its first window_counts[d] slots; some group has all 10 slots live. `masked_rows`: each row lists distinct positions of its window first, then padding entries equal to 1024; a row holds at least 120 positions, and some row holds 160.
All inputs are finite; a program needn't handle non-finite values.
Results may differ from the reference program's by a relative error of at most 0.02.
Values may be sent and summed in bfloat16 or wider, within the bound.
A program may use at most 512 MiB of HBM per device.

```python
import math
import jax
import jax.numpy as jnp
from jax import lax

D = 1024
HEADS = 16
HEAD_DIM = 64
FF = 4096
L = 1024
W_CAP = 10
MPAD = 160
LOSS_SCALE = 1024
WINDOWS = 40
N_DP = 4


def draw_window_counts(key, part):
    shards = jnp.arange(N_DP)
    counts = jax.random.randint(jax.random.fold_in(key, 5), (N_DP,), max(1, W_CAP // 4), W_CAP + 1)
    full_group = jax.random.randint(jax.random.fold_in(key, 3), (), 0, N_DP)
    return jnp.where(shards == full_group, W_CAP, counts).astype(jnp.int32)


def draw_masked_rows(key, part):
    key_list = jax.random.split(jax.random.fold_in(key, 7), WINDOWS)
    chosen = jax.vmap(lambda key_one: jax.random.permutation(key_one, L)[:MPAD])(key_list)
    counts = jax.random.randint(jax.random.fold_in(key, 11), (WINDOWS,), 3 * MPAD // 4, MPAD + 1)
    counts = jnp.where(jnp.arange(WINDOWS) == 0, MPAD, counts)
    slot_ids = jnp.arange(MPAD)
    return jnp.where(slot_ids[None, :] < counts[:, None], chosen, L).astype(jnp.int32)


def block_scale(own_key, dims, cuts, least, high):
    def one(axis_at, parts):
        steps = jax.random.uniform(jax.random.fold_in(jax.random.fold_in(own_key, 6), axis_at), (parts,), jnp.float32, least / len(cuts), high / len(cuts))
        return jnp.repeat(jnp.exp(steps), dims[axis_at] // parts).reshape((-1,) + (1,) * (len(dims) - axis_at - 1))

    factor_of = one(*cuts[0])
    for cut in cuts[1:]:
        factor_of = factor_of * one(*cut)
    return factor_of


def scatter_about(stream_key, extent, scale, most, cuts=(), kind=jnp.bfloat16):
    factor_of = block_scale(stream_key, extent, cuts, -0.22, 0.18) if cuts else 1.0
    drawn = jax.random.normal(stream_key, extent, jnp.float32) * scale * factor_of
    return jnp.minimum(jnp.maximum(drawn, -most), most).astype(kind)


def setup_inputs(seed: int = 0) -> dict:
    splits = jax.random.split(jax.random.key(seed), 16)
    return {
        "tokens": scatter_about(splits[0], (L, WINDOWS, D), 1.0, 6.0, ((0, 8), (1, 4))),
        "norm1_gain": jnp.clip(1.0 + 0.1 * jax.random.normal(splits[1], (D,), jnp.float32), 0.5, 1.5),
        "norm1_bias": scatter_about(splits[2], (D,), 0.02, 0.12, (), jnp.float32),
        "w_query": scatter_about(splits[3], (D, D), D ** -0.5, 0.1875, ((1, 4),)),
        "w_key": scatter_about(splits[4], (D, D), D ** -0.5, 0.1875, ((1, 4),)),
        "w_value": scatter_about(splits[5], (D, D), D ** -0.5, 0.1875, ((1, 4),)),
        "w_out": scatter_about(splits[6], (D, D), (max(1, D // 256)) ** -0.5, 3.0, ((0, 4),)),
        "norm2_gain": jnp.clip(1.0 + 0.1 * jax.random.normal(splits[7], (D,), jnp.float32), 0.5, 1.5),
        "norm2_bias": scatter_about(splits[8], (D,), 0.3, 1.8, (), jnp.float32),
        "w_gate": scatter_about(splits[9], (D, FF), D ** -0.5, 0.1875, ((1, 4),)),
        "w_up": scatter_about(splits[10], (D, FF), D ** -0.5, 0.1875, ((1, 4),)),
        "w_down": scatter_about(splits[11], (FF, D), FF ** -0.5, 0.09375, ((0, 4),)),
        "out_grad": scatter_about(splits[12], (WINDOWS, MPAD, D), 1.0, 6.0, ((0, 4),)),
        "masked_rows": draw_masked_rows(jax.random.fold_in(splits[15], 71), 0),
        "window_counts": draw_window_counts(jax.random.fold_in(splits[15], 71), 0),
    }


epsilon = 1e-05

@jax.custom_vjp
def low(v):
    return lax.optimization_barrier(v.astype(jnp.bfloat16)).astype(jnp.float32)

@jax.custom_vjp
def low_back(v):
    return v

def low_keep(v):
    return (low(v), None)

def low_pass(kept, grad):
    return (grad,)

def back_keep(v):
    return (v, None)

def back_low(kept, grad):
    return (low(grad),)
low.defvjp(low_keep, low_pass)
low_back.defvjp(back_keep, back_low)

def matmul_hi(left, right):
    return jnp.dot(left, right, precision=lax.Precision.HIGHEST)

def layer_norm(inputs, gain_vec, bias_vec):
    row_mean = lax.optimization_barrier(jnp.mean(inputs, axis=-1, keepdims=True))
    centred = inputs - row_mean
    inv_std = lax.rsqrt(lax.optimization_barrier(jnp.mean(centred * centred, axis=-1, keepdims=True)) + epsilon)
    return centred * inv_std * gain_vec + bias_vec

def rotate_heads(values, cosine, sine):
    half_dim = values.shape[-1] // 2
    first_half = values[..., :half_dim]
    second_half = values[..., half_dim:]
    cos_b = cosine[:, None, :]
    sin_b = sine[:, None, :]
    return jnp.concatenate([first_half * cos_b - second_half * sin_b, second_half * cos_b + first_half * sin_b], axis=-1)

def reference(tokens, norm1_gain, norm1_bias, w_query, w_key, w_value, w_out, norm2_gain, norm2_bias, w_gate, w_up, w_down, out_grad, masked_rows, window_counts):
    params = tuple((entry.astype(jnp.float32) for entry in (norm1_gain, norm1_bias, w_query, w_key, w_value, w_out, norm2_gain, norm2_bias, w_gate, w_up, w_down)))
    half_dim = HEAD_DIM // 2
    inv_freq = 10000.0 ** (-jnp.arange(half_dim, dtype=jnp.float32) * 2.0 / HEAD_DIM)
    angles = jnp.arange(L, dtype=jnp.float32)[:, None] * inv_freq[None, :]
    cosine = jnp.cos(angles)
    sine = jnp.sin(angles)
    score_scale = 1.0 / math.sqrt(HEAD_DIM)
    head_shape = (L, HEADS, HEAD_DIM)

    def block(rows, gain_one, bias_one, query_w, key_w, value_w, out_w, gain_two, bias_two, gate_w, up_w, down_w):
        first_low = low(layer_norm(rows, gain_one, bias_one))
        query_lin = low_back(matmul_hi(first_low, query_w))
        key_lin = low_back(matmul_hi(first_low, key_w))
        value_lin = low(low_back(matmul_hi(first_low, value_w)))
        queries = low(rotate_heads(query_lin.reshape(head_shape), cosine, sine))
        keys_rot = low(rotate_heads(key_lin.reshape(head_shape), cosine, sine))
        value_heads = value_lin.reshape(head_shape)
        scores = low_back(jnp.einsum('qhd,khd->hqk', queries, keys_rot, precision=lax.Precision.HIGHEST) * score_scale)
        attn_prob = jax.nn.softmax(scores, axis=-1)
        attended = low(low_back(jnp.einsum('hqk,khd->qhd', low(attn_prob), value_heads, precision=lax.Precision.HIGHEST))).reshape(L, D)
        residual2 = rows + low_back(matmul_hi(attended, out_w))
        second_low = low(layer_norm(residual2, gain_two, bias_two))
        gate_proj = low_back(matmul_hi(second_low, gate_w))
        up_proj = low_back(matmul_hi(second_low, up_w))
        hidden = low(jax.nn.silu(gate_proj) * up_proj)
        return residual2 + low_back(matmul_hi(hidden, down_w))
    slot_ids = jnp.arange(WINDOWS)
    live_slot = slot_ids % W_CAP < window_counts[slot_ids // W_CAP]
    valid_slot = (masked_rows < L) & live_slot[:, None]
    mask_total = jnp.sum(valid_slot.astype(jnp.int32))
    loss_weight = LOSS_SCALE / mask_total.astype(jnp.float32)

    def window_step(totals, inputs):
        rows, grad_rows, index_rows, valid_rows = inputs
        kept = jnp.where(valid_rows[:, None], grad_rows, 0.0)
        cotangent = jnp.zeros((L + 1, D), jnp.float32).at[index_rows].set(kept)[:L] * loss_weight
        result, pullback = jax.vjp(block, rows, *params)
        grads = pullback(cotangent)
        updated = tuple((running + fresh for running, fresh in zip(totals, grads[1:])))
        return (updated, (result, grads[0]))
    init = tuple((jnp.zeros_like(entry) for entry in params))
    inputs_all = (jnp.swapaxes(tokens.astype(jnp.float32), 0, 1), out_grad.astype(jnp.float32), masked_rows, valid_slot)
    totals, (results, grad_rows_all) = lax.scan(window_step, init, inputs_all)
    output = jnp.swapaxes(results, 0, 1).astype(jnp.bfloat16)
    grad_tokens = jnp.swapaxes(grad_rows_all, 0, 1)
    return (output, grad_tokens, totals[0], totals[1], totals[2], totals[3], totals[4], totals[5], totals[6], totals[7], totals[8], totals[9], totals[10])
```

```python
import math

import functools

import jax
import jax.numpy as jnp
from jax import lax
from jax.experimental import pallas as pl
from jax.experimental.pallas import tpu as pltpu
from jax.sharding import PartitionSpec as P

HEAD_DIM = 64
L = 1024
LOSS_SCALE = 1024


epsilon = 1e-05


def layer_stats(inputs):
    row_mean = jnp.mean(inputs, axis=-1, keepdims=True)
    centred = inputs - row_mean
    inv_std = lax.rsqrt(jnp.mean(centred * centred, axis=-1, keepdims=True) + epsilon)
    return (centred * inv_std, inv_std)


def norm_back(grad_norm, normed, inv_std, gain_vec):
    scaled = grad_norm * gain_vec
    return inv_std * (
        scaled
        - jnp.mean(scaled, axis=-1, keepdims=True)
        - normed * jnp.mean(scaled * normed, axis=-1, keepdims=True)
    )


def rotary_tables(positions):
    half_dim = HEAD_DIM // 2
    inv_freq = 10000.0 ** (-jnp.arange(half_dim, dtype=jnp.float32) * 2.0 / HEAD_DIM)
    angles = positions.astype(jnp.float32)[:, None] * inv_freq[None, :]
    return (jnp.cos(angles), jnp.sin(angles))


def rotate(values, cosine, sine):
    half_dim = values.shape[-1] // 2
    first_half = values[..., :half_dim]
    second_half = values[..., half_dim:]
    cos_b = cosine[:, None, None, :]
    sin_b = sine[:, None, None, :]
    return jnp.concatenate(
        [first_half * cos_b - second_half * sin_b, second_half * cos_b + first_half * sin_b],
        axis=-1,
    )


def unrotate(grads, cosine, sine):
    half_dim = grads.shape[-1] // 2
    first_half = grads[..., :half_dim]
    second_half = grads[..., half_dim:]
    cos_b = cosine[:, None, None, :]
    sin_b = sine[:, None, None, :]
    return jnp.concatenate(
        [first_half * cos_b + second_half * sin_b, second_half * cos_b - first_half * sin_b],
        axis=-1,
    )


def block_shards(
    tokens,
    norm1_gain,
    norm1_bias,
    w_query,
    w_key,
    w_value,
    w_out,
    norm2_gain,
    norm2_bias,
    w_gate,
    w_up,
    w_down,
    out_grad,
    masked_rows,
    window_counts,
):
    rows_local, windows, model_width = tokens.shape
    span_rows = rows_local * lax.axis_size("tensor")
    seq_index = lax.axis_index("seq")
    tensor_index = lax.axis_index("tensor")
    head_width = w_query.shape[1]
    heads_local = head_width // HEAD_DIM
    score_scale = 1.0 / math.sqrt(HEAD_DIM)
    head_shape = (span_rows, windows, heads_local, HEAD_DIM)
    residual = tokens.astype(jnp.float32)
    normed1, inv_std1 = layer_stats(residual)
    first_low = (normed1 * norm1_gain + norm1_bias).astype(jnp.bfloat16)
    first_full = lax.all_gather(first_low, "tensor", axis=0, tiled=True)
    w_joined = jnp.concatenate([w_query, w_key, w_value], axis=1)
    projected = jnp.einsum("rwd,de->rwe", first_full, w_joined, preferred_element_type=jnp.float32)
    positions = seq_index * span_rows + jnp.arange(span_rows)
    cosine, sine = rotary_tables(positions)
    queries = rotate(projected[..., :head_width].reshape(head_shape), cosine, sine).astype(
        jnp.bfloat16
    )
    keys_rot = (
        rotate(projected[..., head_width : 2 * head_width].reshape(head_shape), cosine, sine)
        .astype(jnp.bfloat16)
        .reshape(span_rows, windows, head_width)
    )
    values_own = projected[..., 2 * head_width :].astype(jnp.bfloat16)
    keys_all, values_all = (
        lax.all_gather(keys_rot, "seq", axis=0, tiled=True),
        lax.all_gather(values_own, "seq", axis=0, tiled=True),
    )
    key_heads = keys_all.reshape(-1, windows, heads_local, HEAD_DIM)
    value_heads = values_all.reshape(-1, windows, heads_local, HEAD_DIM)
    scores = (
        jnp.einsum("qwhd,kwhd->whqk", queries, key_heads, preferred_element_type=jnp.float32)
        * score_scale
    )
    row_max = jnp.max(scores, axis=-1, keepdims=True)
    row_sum = jnp.sum(jnp.exp(scores - row_max), axis=-1, keepdims=True)
    log_norm = row_max + jnp.log(row_sum)
    attn_prob = jnp.exp(scores - log_norm)
    prob_low = attn_prob.astype(jnp.bfloat16)
    attended = (
        jnp.einsum("whqk,kwhd->qwhd", prob_low, value_heads, preferred_element_type=jnp.float32)
        .reshape(span_rows, windows, head_width)
        .astype(jnp.bfloat16)
    )
    block_part = attended
    attn_branch = lax.psum_scatter(
        jnp.einsum("rwe,ed->rwd", block_part, w_out, preferred_element_type=jnp.float32).astype(
            jnp.bfloat16
        ),
        "tensor",
        scatter_dimension=0,
        tiled=True,
    ).astype(jnp.float32)
    residual2 = residual + attn_branch
    normed2, inv_std2 = layer_stats(residual2)
    second_low = (normed2 * norm2_gain + norm2_bias).astype(jnp.bfloat16)
    second_full = lax.all_gather(second_low, "tensor", axis=0, tiled=True)
    gate_proj = jnp.einsum("rwd,df->rwf", second_full, w_gate, preferred_element_type=jnp.float32)
    up_proj = jnp.einsum("rwd,df->rwf", second_full, w_up, preferred_element_type=jnp.float32)
    hidden = (jax.nn.silu(gate_proj) * up_proj).astype(jnp.bfloat16)
    block_part = hidden
    ffn_branch = lax.psum_scatter(
        jnp.einsum("rwf,fd->rwd", block_part, w_down, preferred_element_type=jnp.float32).astype(
            jnp.bfloat16
        ),
        "tensor",
        scatter_dimension=0,
        tiled=True,
    ).astype(jnp.float32)
    output = (residual2 + ffn_branch).astype(jnp.bfloat16)
    live_slot = jnp.arange(windows) < window_counts[0]
    valid_slot = (masked_rows < L) & live_slot[:, None]
    local_masked = jnp.sum(jnp.where(valid_slot, 1, 0)).astype(jnp.int32)
    total_masked = lax.psum(local_masked, "dp")
    loss_weight = LOSS_SCALE / total_masked.astype(jnp.float32)
    own_positions = seq_index * span_rows + tensor_index * rows_local + jnp.arange(rows_local)
    matches = (masked_rows[:, None, :] == own_positions[None, :, None]) & live_slot[:, None, None]
    picked = jnp.einsum(
        "wrm,wmd->rwd", matches.astype(jnp.bfloat16), out_grad, preferred_element_type=jnp.float32
    )
    grad_out = picked * loss_weight
    grad_down_in = lax.all_gather(grad_out.astype(jnp.bfloat16), "tensor", axis=0, tiled=True)
    grad_w_down = jnp.einsum(
        "rwf,rwd->fd", hidden, grad_down_in, preferred_element_type=jnp.float32
    )
    grad_hidden = jnp.einsum(
        "rwd,fd->rwf", grad_down_in, w_down, preferred_element_type=jnp.float32
    )
    sigmoid_gate = jax.nn.sigmoid(gate_proj)
    silu_gate = gate_proj * sigmoid_gate
    grad_gate = (
        grad_hidden * up_proj * sigmoid_gate * (1.0 + gate_proj * (1.0 - sigmoid_gate))
    ).astype(jnp.bfloat16)
    grad_up = (grad_hidden * silu_gate).astype(jnp.bfloat16)
    grad_w_gate = jnp.einsum(
        "rwd,rwf->df", second_full, grad_gate, preferred_element_type=jnp.float32
    )
    grad_w_up = jnp.einsum("rwd,rwf->df", second_full, grad_up, preferred_element_type=jnp.float32)
    grad_second = lax.psum_scatter(
        (
            jnp.einsum("rwf,df->rwd", grad_gate, w_gate, preferred_element_type=jnp.float32)
            + jnp.einsum("rwf,df->rwd", grad_up, w_up, preferred_element_type=jnp.float32)
        ).astype(jnp.bfloat16),
        "tensor",
        scatter_dimension=0,
        tiled=True,
    ).astype(jnp.float32)
    grad_norm2_gain = jnp.sum(grad_second * normed2, axis=(0, 1))
    grad_norm2_bias = jnp.sum(grad_second, axis=(0, 1))
    grad_residual2 = grad_out + norm_back(grad_second, normed2, inv_std2, norm2_gain)
    grad_attn_in = lax.all_gather(grad_residual2.astype(jnp.bfloat16), "tensor", axis=0, tiled=True)
    grad_w_out = jnp.einsum(
        "rwe,rwd->ed", attended, grad_attn_in, preferred_element_type=jnp.float32
    )
    grad_attended = jnp.einsum(
        "rwd,ed->rwe", grad_attn_in, w_out, preferred_element_type=jnp.float32
    ).astype(jnp.bfloat16)
    grad_att_heads = grad_attended.reshape(head_shape)
    scores_again = (
        jnp.einsum("qwhd,kwhd->whqk", queries, key_heads, preferred_element_type=jnp.float32)
        * score_scale
    )
    probs_again = jnp.exp(scores_again - log_norm)
    grad_probs = jnp.einsum(
        "qwhd,kwhd->whqk", grad_att_heads, value_heads, preferred_element_type=jnp.float32
    )
    row_delta = jnp.sum(probs_again * grad_probs, axis=-1, keepdims=True)
    grad_scores = (probs_again * (grad_probs - row_delta)).astype(jnp.bfloat16)
    grad_queries = (
        jnp.einsum("whqk,kwhd->qwhd", grad_scores, key_heads, preferred_element_type=jnp.float32)
        * score_scale
    )
    grad_key_all = (
        jnp.einsum("whqk,qwhd->kwhd", grad_scores, queries, preferred_element_type=jnp.float32)
        * score_scale
    ).reshape(-1, windows, head_width)
    grad_value_all = jnp.einsum(
        "whqk,qwhd->kwhd",
        probs_again.astype(jnp.bfloat16),
        grad_att_heads,
        preferred_element_type=jnp.float32,
    ).reshape(-1, windows, head_width)
    grad_keys, grad_values = (
        lax.psum_scatter(
            grad_key_all.astype(jnp.bfloat16), "seq", scatter_dimension=0, tiled=True
        ).astype(jnp.float32),
        lax.psum_scatter(
            grad_value_all.astype(jnp.bfloat16), "seq", scatter_dimension=0, tiled=True
        ).astype(jnp.float32),
    )
    grad_query_lin = (
        unrotate(grad_queries, cosine, sine)
        .reshape(span_rows, windows, head_width)
        .astype(jnp.bfloat16)
    )
    grad_key_lin = (
        unrotate(grad_keys.reshape(head_shape), cosine, sine)
        .reshape(span_rows, windows, head_width)
        .astype(jnp.bfloat16)
    )
    grad_value_lin = grad_values.astype(jnp.bfloat16)
    grad_joined = jnp.concatenate([grad_query_lin, grad_key_lin, grad_value_lin], axis=-1)
    grad_w_joined = jnp.einsum(
        "rwd,rwe->de", first_full, grad_joined, preferred_element_type=jnp.float32
    )
    grad_w_query = grad_w_joined[:, :head_width]
    grad_w_key = grad_w_joined[:, head_width : 2 * head_width]
    grad_w_value = grad_w_joined[:, 2 * head_width :]
    block_part = grad_joined
    grad_first = lax.psum_scatter(
        jnp.einsum("rwe,de->rwd", block_part, w_joined, preferred_element_type=jnp.float32).astype(
            jnp.bfloat16
        ),
        "tensor",
        scatter_dimension=0,
        tiled=True,
    ).astype(jnp.float32)
    grad_norm1_gain = jnp.sum(grad_first * normed1, axis=(0, 1))
    grad_norm1_bias = jnp.sum(grad_first, axis=(0, 1))
    grad_tokens = grad_residual2 + norm_back(grad_first, normed1, inv_std1, norm1_gain)
    summed = (
        lax.psum_scatter(
            grad_w_query.astype(jnp.bfloat16), ("dp", "seq"), scatter_dimension=0, tiled=True
        ).astype(jnp.float32),
        lax.psum_scatter(
            grad_w_key.astype(jnp.bfloat16), ("dp", "seq"), scatter_dimension=0, tiled=True
        ).astype(jnp.float32),
        lax.psum_scatter(
            grad_w_value.astype(jnp.bfloat16), ("dp", "seq"), scatter_dimension=0, tiled=True
        ).astype(jnp.float32),
        lax.psum_scatter(
            grad_w_out.astype(jnp.bfloat16), ("dp", "seq"), scatter_dimension=1, tiled=True
        ).astype(jnp.float32),
        lax.psum_scatter(
            grad_w_gate.astype(jnp.bfloat16), ("dp", "seq"), scatter_dimension=0, tiled=True
        ).astype(jnp.float32),
        lax.psum_scatter(
            grad_w_up.astype(jnp.bfloat16), ("dp", "seq"), scatter_dimension=0, tiled=True
        ).astype(jnp.float32),
        lax.psum_scatter(
            grad_w_down.astype(jnp.bfloat16), ("dp", "seq"), scatter_dimension=1, tiled=True
        ).astype(jnp.float32),
    )
    norm_sums = (
        lax.psum_scatter(grad_norm1_gain, ("dp", "seq", "tensor"), scatter_dimension=0, tiled=True),
        lax.psum_scatter(grad_norm1_bias, ("dp", "seq", "tensor"), scatter_dimension=0, tiled=True),
        lax.psum_scatter(grad_norm2_gain, ("dp", "seq", "tensor"), scatter_dimension=0, tiled=True),
        lax.psum_scatter(grad_norm2_bias, ("dp", "seq", "tensor"), scatter_dimension=0, tiled=True),
    )
    return (
        output,
        grad_tokens,
        norm_sums[0],
        norm_sums[1],
        summed[0],
        summed[1],
        summed[2],
        summed[3],
        norm_sums[2],
        norm_sums[3],
        summed[4],
        summed[5],
        summed[6],
    )


BF = jnp.bfloat16
F32 = jnp.float32
LANES = 128


def dot_t(a, b):
    return lax.dot_general(a, b, (((1,), (1,)), ((), ())), preferred_element_type=F32)


def dot_n(a, b):
    return lax.dot_general(a, b, (((1,), (0,)), ((), ())), preferred_element_type=F32)


def t_dot(a, b):
    return lax.dot_general(a, b, (((0,), (0,)), ((), ())), preferred_element_type=F32)


def swap_halves(x):
    half = HEAD_DIM // 2
    lane = lax.broadcasted_iota(jnp.int32, x.shape, 1)
    down = pltpu.roll(x, half, 1)
    up = pltpu.roll(x, LANES - half, 1)
    return jnp.where(lane % HEAD_DIM < half, up, down)


def head_mask(h):
    lane = lax.broadcasted_iota(jnp.int32, (1, LANES), 1)
    return jnp.where(lane // HEAD_DIM == h, 1.0, 0.0).astype(BF)


def qkv_kernel(x_ref, w_ref, cos_ref, sin_ref, out_ref):
    acc = dot_n(x_ref[...], w_ref[...])
    cos, sin = cos_ref[...], sin_ref[...]
    chunks = acc.shape[1] // LANES
    third = chunks // 3
    for c in range(chunks):
        part = acc[:, c * LANES : (c + 1) * LANES]
        if c < 2 * third:
            part = part * cos + swap_halves(part) * sin
        if c < third:
            part = part * (1.0 / math.sqrt(HEAD_DIM))
        out_ref[:, c * LANES : (c + 1) * LANES] = part.astype(BF)


def qkv_project(x, w, cos, sin, block):
    rows, width = x.shape
    tile = 256
    return pl.pallas_call(
        qkv_kernel,
        grid=(w.shape[1] // block, rows // tile),
        in_specs=[
            pl.BlockSpec((tile, width), lambda t, r: (r, 0)),
            pl.BlockSpec((width, block), lambda t, r: (0, t)),
            pl.BlockSpec((tile, LANES), lambda t, r: (r, 0)),
            pl.BlockSpec((tile, LANES), lambda t, r: (r, 0)),
        ],
        out_specs=pl.BlockSpec((tile, block), lambda t, r: (r, t)),
        out_shape=jax.ShapeDtypeStruct((rows, w.shape[1]), BF),
        cost_estimate=pl.CostEstimate(
            flops=2 * rows * width * w.shape[1], bytes_accessed=2 * rows * (width + w.shape[1]), transcendentals=0
        ),
        name="qkv_project",
    )(x, w, cos, sin)


def attend_kernel(q_ref, k_ref, v_ref, o_ref):
    q, k, v = q_ref[...], k_ref[...], v_ref[...]
    outs = []
    for h in range(LANES // HEAD_DIM):
        s = dot_t(q * head_mask(h), k)
        p = jnp.exp(s - jnp.max(s, axis=1, keepdims=True))
        norm = jnp.sum(p, axis=1, keepdims=True)
        outs.append(dot_n(p.astype(BF), v) / norm)
    lane = lax.broadcasted_iota(jnp.int32, outs[0].shape, 1)
    o_ref[...] = jnp.where(lane < HEAD_DIM, outs[0], outs[1]).astype(BF)


def attend(qkv, block):
    rows = qkv.shape[0]
    per = block // 3 // LANES
    pairs = qkv.shape[1] // block * per
    tile = 512
    spec = lambda which: lambda p, r: (0, p // per * 3 * per + which * per + p % per)
    return pl.pallas_call(
        attend_kernel,
        grid=(pairs, rows // tile),
        in_specs=[
            pl.BlockSpec((tile, LANES), lambda p, r: (r, p // per * 3 * per + p % per)),
            pl.BlockSpec((rows, LANES), spec(1)),
            pl.BlockSpec((rows, LANES), spec(2)),
        ],
        out_specs=pl.BlockSpec((tile, LANES), lambda p, r: (r, p)),
        out_shape=jax.ShapeDtypeStruct((rows, pairs * LANES), BF),
        cost_estimate=pl.CostEstimate(
            flops=16 * pairs * rows * rows * LANES, bytes_accessed=8 * rows * pairs * LANES, transcendentals=2 * pairs * rows * rows
        ),
        name="attend",
    )(qkv, qkv, qkv)


def attend_back_kernel(q_ref, g_ref, k_ref, v_ref, cos_ref, sin_ref, qcos_ref, qsin_ref, dq_ref, dk_ref, dv_ref):
    q, g, k, v = q_ref[...], g_ref[...], k_ref[...], v_ref[...]
    dq = []
    all_p, all_ds, all_q, all_g = [], [], [], []
    for h in range(LANES // HEAD_DIM):
        mask = head_mask(h)
        qh, gh = q * mask, g * mask
        s = dot_t(qh, k)
        p = jnp.exp(s - jnp.max(s, axis=1, keepdims=True))
        p = p / jnp.sum(p, axis=1, keepdims=True)
        dp = dot_t(gh, v)
        ds = (p * (dp - jnp.sum(p * dp, axis=1, keepdims=True))).astype(BF)
        dq.append(dot_n(ds, k))
        all_p.append(p.astype(BF))
        all_ds.append(ds)
        all_q.append(qh)
        all_g.append(gh)
    lane = lax.broadcasted_iota(jnp.int32, dq[0].shape, 1)
    dq = jnp.where(lane < HEAD_DIM, dq[0], dq[1]) * (1.0 / math.sqrt(HEAD_DIM))
    dq_ref[...] = (dq * qcos_ref[...] - swap_halves(dq) * qsin_ref[...]).astype(BF)
    dk = t_dot(jnp.concatenate(all_ds, axis=0), jnp.concatenate(all_q, axis=0))
    dk_ref[...] = (dk * cos_ref[...] - swap_halves(dk) * sin_ref[...]).astype(BF)
    dv_ref[...] = t_dot(jnp.concatenate(all_p, axis=0), jnp.concatenate(all_g, axis=0)).astype(BF)


def attend_back(q_rows, grad_rows, qkv, block, cos, sin, row_cos, row_sin):
    rows, masked = qkv.shape[0], q_rows.shape[0]
    per = block // 3 // LANES
    pairs = qkv.shape[1] // block * per
    spec = lambda which: lambda p: (0, p // per * 3 * per + which * per + p % per)
    pick = pl.BlockSpec((masked, LANES), lambda p: (0, p))
    full = pl.BlockSpec((rows, LANES), lambda p: (0, p))
    same = pl.BlockSpec((rows, LANES), lambda p: (0, 0))
    row_same = pl.BlockSpec((masked, LANES), lambda p: (0, 0))
    return pl.pallas_call(
        attend_back_kernel,
        grid=(pairs,),
        in_specs=[
            pick,
            pick,
            pl.BlockSpec((rows, LANES), spec(1)),
            pl.BlockSpec((rows, LANES), spec(2)),
            same,
            same,
            row_same,
            row_same,
        ],
        out_specs=[pick, full, full],
        out_shape=[
            jax.ShapeDtypeStruct((masked, pairs * LANES), BF),
            jax.ShapeDtypeStruct((rows, pairs * LANES), BF),
            jax.ShapeDtypeStruct((rows, pairs * LANES), BF),
        ],
        cost_estimate=pl.CostEstimate(
            flops=20 * pairs * rows * masked * LANES, bytes_accessed=10 * rows * pairs * LANES, transcendentals=2 * pairs * rows * masked
        ),
        name="attend_back",
    )(q_rows, grad_rows, qkv, qkv, cos, sin, row_cos, row_sin)


def rotary_lanes(positions):
    cosine, sine = rotary_tables(positions)
    reps = LANES // HEAD_DIM
    return (
        jnp.concatenate([cosine, cosine] * reps, axis=1),
        jnp.concatenate([-sine, sine] * reps, axis=1),
    )


def window_shards(
    tokens,
    norm1_gain,
    norm1_bias,
    w_query,
    w_key,
    w_value,
    w_out,
    norm2_gain,
    norm2_bias,
    w_gate,
    w_up,
    w_down,
    out_grad,
    masked_rows,
    window_counts,
):
    rows_local, windows, width = tokens.shape
    n_seq, n_ten = lax.axis_size("seq"), lax.axis_size("tensor")
    n_dp = lax.axis_size("dp")
    seq_index, ten_index = lax.axis_index("seq"), lax.axis_index("tensor")
    shard_index = lax.axis_index("dp") * n_seq + seq_index
    half = windows // n_seq
    length = rows_local * n_seq * n_ten
    share = length // n_ten
    hw = w_query.shape[1]
    block = 3 * hw
    slots = masked_rows.shape[1]
    part = slots // n_ten

    tok = jnp.swapaxes(tokens, 0, 1).reshape(n_seq, half, rows_local, width)
    own_tok = lax.all_to_all(
        tok[:, :n_ten].reshape(n_seq * n_ten, rows_local, width), ("seq", "tensor"), 0, 0, tiled=True
    ).reshape(length, width)
    left_x = lax.all_to_all(tok[:, n_ten], "seq", 0, 0, tiled=True)
    left_tok = lax.all_gather(left_x, "tensor", axis=1, tiled=False).reshape(length, width)

    def cut(w, count):
        size = w.shape[0] // count
        return lax.dynamic_slice_in_dim(w, shard_index * size, size, axis=0)

    shards_xy = n_dp * n_seq

    def gather_columns(w):
        w = lax.all_gather(cut(w, shards_xy), "tensor", axis=1, tiled=True)
        return lax.all_gather(w, ("dp", "seq"), axis=0, tiled=True)

    def gather_rows(w):
        own = cut(w, shards_xy)
        w = lax.all_gather(own, "tensor", axis=0, tiled=False)
        w = lax.all_gather(w, ("dp", "seq"), axis=0, tiled=False)
        return jnp.swapaxes(w, 0, 1).reshape(-1, w.shape[-1])

    w_joined = jnp.concatenate([w_query, w_key, w_value], axis=1)
    all_joined = gather_columns(w_joined)
    all_out = gather_rows(w_out)
    all_gate = gather_columns(w_gate)
    all_up = gather_columns(w_up)
    all_down = gather_rows(w_down)

    live = jnp.arange(windows) < window_counts[0]
    valid = (masked_rows < length) & live[:, None]
    total = lax.psum(jnp.sum(valid.astype(jnp.int32)), "dp")
    loss_weight = LOSS_SCALE / total.astype(F32)
    first_window = seq_index * half
    my_rows = lax.dynamic_slice_in_dim(masked_rows, first_window, half, 0)
    my_valid = lax.dynamic_slice_in_dim(valid, first_window, half, 0)
    cot = lax.dynamic_slice_in_dim(out_grad, first_window, half, 0).astype(F32) * loss_weight
    cot = jnp.where(my_valid[:, :, None], cot, 0.0)
    cot_low = cot.astype(BF)
    own_rows = lax.dynamic_index_in_dim(my_rows, ten_index, 0, keepdims=False)
    own_valid = lax.dynamic_index_in_dim(my_valid, ten_index, 0, keepdims=False)
    own_cot = lax.dynamic_index_in_dim(cot, ten_index, 0, keepdims=False)
    left_rows, left_valid, left_cot = my_rows[n_ten], my_valid[n_ten], cot[n_ten]
    every = jnp.arange(length)
    own_pick = ((own_rows[:, None] == every[None, :]) & own_valid[:, None]).astype(BF)
    left_pick = ((left_rows[:, None] == every[None, :]) & left_valid[:, None]).astype(BF)

    cos, sin = rotary_lanes(every)
    own_cos, own_sin = rotary_lanes(own_rows)
    left_cos, left_sin = rotary_lanes(left_rows)

    def norm(x, gain, bias):
        normed, inv_std = layer_stats(x)
        return normed, inv_std, (normed * gain + bias).astype(BF)

    _, _, left_first = norm(left_tok.astype(F32), norm1_gain, norm1_bias)
    left_qkv = qkv_project(left_first, w_joined, cos, sin, block)
    left_att = attend(left_qkv, block)
    _, _, own_first = norm(own_tok.astype(F32), norm1_gain, norm1_bias)
    own_qkv = qkv_project(own_first, all_joined, cos, sin, block)
    own_att = attend(own_qkv, block)

    def spread(x):
        x = x.reshape(n_seq, n_ten, rows_local, x.shape[-1])
        x = lax.all_to_all(x, "tensor", 1, 1, tiled=True)
        return jnp.swapaxes(x, 1, 2).reshape(n_seq * rows_local, -1)

    def my_part(x):
        x = x.reshape(n_seq, n_ten, rows_local, x.shape[-1])
        return lax.dynamic_index_in_dim(x, ten_index, 1, keepdims=False).reshape(n_seq * rows_local, -1)

    left_att_part = spread(left_att)

    pick_rows = lambda pick, x: dot_n(pick, x).astype(BF)
    own_att_m = pick_rows(own_pick, own_att)
    left_att_m = pick_rows(left_pick, left_att)
    own_res_m = pick_rows(own_pick, own_tok).astype(F32) + dot_n(own_att_m, all_out)
    own_normed2, own_inv2, own_second = norm(own_res_m, norm2_gain, norm2_bias)
    sent = lax.all_gather(jnp.concatenate([own_second, left_att_m], axis=1), "tensor", axis=0, tiled=False)
    left_att_full = jnp.swapaxes(sent[:, :, width:], 0, 1).reshape(slots, -1)
    left_res_m = pick_rows(left_pick, left_tok).astype(F32) + dot_n(left_att_full, all_out)
    left_normed2, left_inv2, left_second = norm(left_res_m, norm2_gain, norm2_bias)
    second = jnp.concatenate([sent[:, :, :width].reshape(n_ten * slots, width), left_second], axis=0)

    gate = dot_n(second, w_gate)
    up = dot_n(second, w_up)
    down_in = cot_low.reshape(half * slots, width)
    grad_hidden = dot_t(down_in, w_down)
    sig = jax.nn.sigmoid(gate)
    silu = gate * sig
    hidden_m = (silu * up).astype(BF)
    grad_gate = (grad_hidden * up * sig * (1.0 + gate * (1.0 - sig))).astype(BF)
    grad_up = (grad_hidden * silu).astype(BF)
    grad_second = (dot_t(grad_gate, w_gate) + dot_t(grad_up, w_up)).astype(BF)
    grad_second = jnp.concatenate(
        [
            grad_second[: n_ten * slots].reshape(n_ten, slots, width),
            grad_second[n_ten * slots :].reshape(n_ten, part, width),
        ],
        axis=1,
    ).reshape(n_ten * (slots + part), width)
    grad_second = lax.psum_scatter(grad_second, "tensor", scatter_dimension=0, tiled=True)
    left_grad_second = lax.all_gather(grad_second[slots:], "tensor", axis=0, tiled=True).astype(F32)
    own_grad_second = grad_second[:slots].astype(F32)
    grad_w_down = t_dot(hidden_m, down_in).astype(BF)
    grad_w_gate = t_dot(second, grad_gate).astype(BF)
    grad_w_up = t_dot(second, grad_up).astype(BF)

    mine = lambda x: lax.dynamic_slice_in_dim(x, ten_index * part, part, 0)
    grad_norm2_gain = jnp.sum(own_grad_second * own_normed2, axis=0) + jnp.sum(
        mine(left_grad_second * left_normed2), axis=0
    )
    grad_norm2_bias = jnp.sum(own_grad_second, axis=0) + jnp.sum(mine(left_grad_second), axis=0)
    own_gr2 = (own_cot + norm_back(own_grad_second, own_normed2, own_inv2, norm2_gain)).astype(BF)
    left_gr2 = (left_cot + norm_back(left_grad_second, left_normed2, left_inv2, norm2_gain)).astype(BF)

    own_gatt = dot_t(own_gr2, all_out).astype(BF)
    left_gatt = dot_t(left_gr2, w_out).astype(BF)
    on_tensor = (jnp.arange(n_ten) == ten_index).astype(BF)
    left_att_wide = (left_att_m[:, None, :] * on_tensor[None, :, None]).reshape(slots, width)
    grad_w_out = t_dot(
        jnp.concatenate([own_att_m, left_att_wide], axis=0), jnp.concatenate([own_gr2, left_gr2], axis=0)
    ).astype(BF)

    def queries_of(pick, qkv):
        groups = qkv.shape[1] // block
        q = qkv.reshape(length, groups, block)[:, :, :hw].reshape(length, groups * hw)
        return pick_rows(pick, q)

    own_dq, own_dk, own_dv = attend_back(
        queries_of(own_pick, own_qkv), own_gatt, own_qkv, block, cos, sin, own_cos, own_sin
    )
    left_dq, left_dk, left_dv = attend_back(
        queries_of(left_pick, left_qkv), left_gatt, left_qkv, block, cos, sin, left_cos, left_sin
    )

    def join(pick, dq, dk, dv):
        groups = dk.shape[1] // hw
        dense_q = t_dot(pick, dq).astype(BF)
        parts = [x.reshape(length, groups, 1, hw) for x in (dense_q, dk, dv)]
        return jnp.concatenate(parts, axis=2).reshape(length, groups * block)

    own_grads = join(own_pick, own_dq, own_dk, own_dv)
    left_grads = join(left_pick, left_dq, left_dk, left_dv)
    left_grads_part = spread(left_grads)
    grad_first = jnp.concatenate([dot_t(own_grads, all_joined), dot_t(left_grads_part, all_joined)], axis=0)
    grad_w_all = t_dot(own_first, own_grads)
    left_block = t_dot(left_first, left_grads)
    grad_w_all = (grad_w_all.reshape(width, n_ten, block) + left_block[:, None, :] * on_tensor.astype(F32)[None, :, None]).reshape(
        width, n_ten * block
    ).astype(BF)

    both_tok = jnp.concatenate([own_tok, my_part(left_tok)], axis=0)
    normed1, inv_std1 = layer_stats(both_tok.astype(F32))
    grad_norm1_gain = jnp.sum(grad_first * normed1, axis=0)
    grad_norm1_bias = jnp.sum(grad_first, axis=0)
    gr2_dense = jnp.concatenate([t_dot(own_pick, own_gr2), dot_n(my_part(left_pick.T), left_gr2)], axis=0)
    grad_both = (gr2_dense + norm_back(grad_first, normed1, inv_std1, norm1_gain)).astype(BF)

    att = jnp.concatenate([own_att, left_att_part], axis=0)
    residual2 = both_tok.astype(F32) + dot_n(att, all_out)
    _, _, second_low = norm(residual2, norm2_gain, norm2_bias)
    hidden = (jax.nn.silu(dot_n(second_low, all_gate)) * dot_n(second_low, all_up)).astype(BF)
    out_both = (residual2 + dot_n(hidden, all_down)).astype(BF)

    def send_back(x):
        own = lax.all_to_all(
            x[:length].reshape(n_seq * n_ten, rows_local, width), ("seq", "tensor"), 0, 0, tiled=True
        ).reshape(n_seq, n_ten, rows_local, width)
        left = lax.all_to_all(x[length:].reshape(n_seq, rows_local, width), "seq", 0, 0, tiled=True)
        both = jnp.concatenate([own, left[:, None]], axis=1).reshape(windows, rows_local, width)
        return jnp.swapaxes(both, 0, 1)

    output = send_back(out_both)
    grad_tokens = send_back(grad_both).astype(F32)

    def summed(x, dim):
        return lax.psum_scatter(x, ("dp", "seq"), scatter_dimension=dim, tiled=True)

    gw_all = lax.psum_scatter(summed(grad_w_all, 0), "tensor", scatter_dimension=1, tiled=True).astype(F32)
    gw_out = lax.psum_scatter(summed(grad_w_out, 1), "tensor", scatter_dimension=0, tiled=True).astype(F32)
    gw_gate, gw_up = summed(grad_w_gate, 0).astype(F32), summed(grad_w_up, 0).astype(F32)
    gw_down = summed(grad_w_down, 1).astype(F32)
    vectors = [
        lax.psum_scatter(v, ("dp", "seq", "tensor"), scatter_dimension=0, tiled=True)
        for v in (grad_norm1_gain, grad_norm1_bias, grad_norm2_gain, grad_norm2_bias)
    ]
    return (
        output,
        grad_tokens,
        vectors[0],
        vectors[1],
        gw_all[:, :hw],
        gw_all[:, hw : 2 * hw],
        gw_all[:, 2 * hw :],
        gw_out,
        vectors[2],
        vectors[3],
        gw_gate,
        gw_up,
        gw_down,
    )


def shards(tokens, *rest):
    n_seq, n_ten = lax.axis_size("seq"), lax.axis_size("tensor")
    whole = tokens.shape[1] % n_seq == 0 and tokens.shape[1] // n_seq == n_ten + 1
    return (window_shards if whole else block_shards)(tokens, *rest)


def solution(mesh):
    return jax.shard_map(
        shards,
        mesh=mesh,
        in_specs=(
            P(("seq", "tensor"), "dp", None),
            P(),
            P(),
            P(None, "tensor"),
            P(None, "tensor"),
            P(None, "tensor"),
            P("tensor", None),
            P(),
            P(),
            P(None, "tensor"),
            P(None, "tensor"),
            P("tensor", None),
            P("dp", None, None),
            P("dp", None),
            P("dp"),
        ),
        out_specs=(
            P(("seq", "tensor"), "dp", None),
            P(("seq", "tensor"), "dp", None),
            P(("dp", "seq", "tensor")),
            P(("dp", "seq", "tensor")),
            P(("dp", "seq"), "tensor"),
            P(("dp", "seq"), "tensor"),
            P(("dp", "seq"), "tensor"),
            P("tensor", ("dp", "seq")),
            P(("dp", "seq", "tensor")),
            P(("dp", "seq", "tensor")),
            P(("dp", "seq"), "tensor"),
            P(("dp", "seq"), "tensor"),
            P("tensor", ("dp", "seq")),
        ),
        check_vma=False,
    )
```

```python
import math

import functools

import jax
import jax.numpy as jnp
from jax import lax
from jax.experimental import pallas as pl
from jax.experimental.pallas import tpu as pltpu
from jax.sharding import PartitionSpec as P

HEAD_DIM = 64
L = 1024
LOSS_SCALE = 1024


epsilon = 1e-05


def layer_stats(inputs):
    row_mean = jnp.mean(inputs, axis=-1, keepdims=True)
    centred = inputs - row_mean
    inv_std = lax.rsqrt(jnp.mean(centred * centred, axis=-1, keepdims=True) + epsilon)
    return (centred * inv_std, inv_std)


def norm_back(grad_norm, normed, inv_std, gain_vec):
    scaled = grad_norm * gain_vec
    return inv_std * (
        scaled
        - jnp.mean(scaled, axis=-1, keepdims=True)
        - normed * jnp.mean(scaled * normed, axis=-1, keepdims=True)
    )


def rotary_tables(positions):
    half_dim = HEAD_DIM // 2
    inv_freq = 10000.0 ** (-jnp.arange(half_dim, dtype=jnp.float32) * 2.0 / HEAD_DIM)
    angles = positions.astype(jnp.float32)[:, None] * inv_freq[None, :]
    return (jnp.cos(angles), jnp.sin(angles))


def rotate(values, cosine, sine):
    half_dim = values.shape[-1] // 2
    first_half = values[..., :half_dim]
    second_half = values[..., half_dim:]
    cos_b = cosine[:, None, None, :]
    sin_b = sine[:, None, None, :]
    return jnp.concatenate(
        [first_half * cos_b - second_half * sin_b, second_half * cos_b + first_half * sin_b],
        axis=-1,
    )


def unrotate(grads, cosine, sine):
    half_dim = grads.shape[-1] // 2
    first_half = grads[..., :half_dim]
    second_half = grads[..., half_dim:]
    cos_b = cosine[:, None, None, :]
    sin_b = sine[:, None, None, :]
    return jnp.concatenate(
        [first_half * cos_b + second_half * sin_b, second_half * cos_b - first_half * sin_b],
        axis=-1,
    )


def block_shards(
    tokens,
    norm1_gain,
    norm1_bias,
    w_query,
    w_key,
    w_value,
    w_out,
    norm2_gain,
    norm2_bias,
    w_gate,
    w_up,
    w_down,
    out_grad,
    masked_rows,
    window_counts,
):
    rows_local, windows, model_width = tokens.shape
    span_rows = rows_local * lax.axis_size("tensor")
    seq_index = lax.axis_index("seq")
    tensor_index = lax.axis_index("tensor")
    head_width = w_query.shape[1]
    heads_local = head_width // HEAD_DIM
    score_scale = 1.0 / math.sqrt(HEAD_DIM)
    head_shape = (span_rows, windows, heads_local, HEAD_DIM)
    residual = tokens.astype(jnp.float32)
    normed1, inv_std1 = layer_stats(residual)
    first_low = (normed1 * norm1_gain + norm1_bias).astype(jnp.bfloat16)
    first_full = lax.all_gather(first_low, "tensor", axis=0, tiled=True)
    w_joined = jnp.concatenate([w_query, w_key, w_value], axis=1)
    projected = jnp.einsum("rwd,de->rwe", first_full, w_joined, preferred_element_type=jnp.float32)
    positions = seq_index * span_rows + jnp.arange(span_rows)
    cosine, sine = rotary_tables(positions)
    queries = rotate(projected[..., :head_width].reshape(head_shape), cosine, sine).astype(
        jnp.bfloat16
    )
    keys_rot = (
        rotate(projected[..., head_width : 2 * head_width].reshape(head_shape), cosine, sine)
        .astype(jnp.bfloat16)
        .reshape(span_rows, windows, head_width)
    )
    values_own = projected[..., 2 * head_width :].astype(jnp.bfloat16)
    keys_all, values_all = (
        lax.all_gather(keys_rot, "seq", axis=0, tiled=True),
        lax.all_gather(values_own, "seq", axis=0, tiled=True),
    )
    key_heads = keys_all.reshape(-1, windows, heads_local, HEAD_DIM)
    value_heads = values_all.reshape(-1, windows, heads_local, HEAD_DIM)
    scores = (
        jnp.einsum("qwhd,kwhd->whqk", queries, key_heads, preferred_element_type=jnp.float32)
        * score_scale
    )
    row_max = jnp.max(scores, axis=-1, keepdims=True)
    row_sum = jnp.sum(jnp.exp(scores - row_max), axis=-1, keepdims=True)
    log_norm = row_max + jnp.log(row_sum)
    attn_prob = jnp.exp(scores - log_norm)
    prob_low = attn_prob.astype(jnp.bfloat16)
    attended = (
        jnp.einsum("whqk,kwhd->qwhd", prob_low, value_heads, preferred_element_type=jnp.float32)
        .reshape(span_rows, windows, head_width)
        .astype(jnp.bfloat16)
    )
    block_part = attended
    attn_branch = lax.psum_scatter(
        jnp.einsum("rwe,ed->rwd", block_part, w_out, preferred_element_type=jnp.float32).astype(
            jnp.bfloat16
        ),
        "tensor",
        scatter_dimension=0,
        tiled=True,
    ).astype(jnp.float32)
    residual2 = residual + attn_branch
    normed2, inv_std2 = layer_stats(residual2)
    second_low = (normed2 * norm2_gain + norm2_bias).astype(jnp.bfloat16)
    second_full = lax.all_gather(second_low, "tensor", axis=0, tiled=True)
    gate_proj = jnp.einsum("rwd,df->rwf", second_full, w_gate, preferred_element_type=jnp.float32)
    up_proj = jnp.einsum("rwd,df->rwf", second_full, w_up, preferred_element_type=jnp.float32)
    hidden = (jax.nn.silu(gate_proj) * up_proj).astype(jnp.bfloat16)
    block_part = hidden
    ffn_branch = lax.psum_scatter(
        jnp.einsum("rwf,fd->rwd", block_part, w_down, preferred_element_type=jnp.float32).astype(
            jnp.bfloat16
        ),
        "tensor",
        scatter_dimension=0,
        tiled=True,
    ).astype(jnp.float32)
    output = (residual2 + ffn_branch).astype(jnp.bfloat16)
    live_slot = jnp.arange(windows) < window_counts[0]
    valid_slot = (masked_rows < L) & live_slot[:, None]
    local_masked = jnp.sum(jnp.where(valid_slot, 1, 0)).astype(jnp.int32)
    total_masked = lax.psum(local_masked, "dp")
    loss_weight = LOSS_SCALE / total_masked.astype(jnp.float32)
    own_positions = seq_index * span_rows + tensor_index * rows_local + jnp.arange(rows_local)
    matches = (masked_rows[:, None, :] == own_positions[None, :, None]) & live_slot[:, None, None]
    picked = jnp.einsum(
        "wrm,wmd->rwd", matches.astype(jnp.bfloat16), out_grad, preferred_element_type=jnp.float32
    )
    grad_out = picked * loss_weight
    grad_down_in = lax.all_gather(grad_out.astype(jnp.bfloat16), "tensor", axis=0, tiled=True)
    grad_w_down = jnp.einsum(
        "rwf,rwd->fd", hidden, grad_down_in, preferred_element_type=jnp.float32
    )
    grad_hidden = jnp.einsum(
        "rwd,fd->rwf", grad_down_in, w_down, preferred_element_type=jnp.float32
    )
    sigmoid_gate = jax.nn.sigmoid(gate_proj)
    silu_gate = gate_proj * sigmoid_gate
    grad_gate = (
        grad_hidden * up_proj * sigmoid_gate * (1.0 + gate_proj * (1.0 - sigmoid_gate))
    ).astype(jnp.bfloat16)
    grad_up = (grad_hidden * silu_gate).astype(jnp.bfloat16)
    grad_w_gate = jnp.einsum(
        "rwd,rwf->df", second_full, grad_gate, preferred_element_type=jnp.float32
    )
    grad_w_up = jnp.einsum("rwd,rwf->df", second_full, grad_up, preferred_element_type=jnp.float32)
    grad_second = lax.psum_scatter(
        (
            jnp.einsum("rwf,df->rwd", grad_gate, w_gate, preferred_element_type=jnp.float32)
            + jnp.einsum("rwf,df->rwd", grad_up, w_up, preferred_element_type=jnp.float32)
        ).astype(jnp.bfloat16),
        "tensor",
        scatter_dimension=0,
        tiled=True,
    ).astype(jnp.float32)
    grad_norm2_gain = jnp.sum(grad_second * normed2, axis=(0, 1))
    grad_norm2_bias = jnp.sum(grad_second, axis=(0, 1))
    grad_residual2 = grad_out + norm_back(grad_second, normed2, inv_std2, norm2_gain)
    grad_attn_in = lax.all_gather(grad_residual2.astype(jnp.bfloat16), "tensor", axis=0, tiled=True)
    grad_w_out = jnp.einsum(
        "rwe,rwd->ed", attended, grad_attn_in, preferred_element_type=jnp.float32
    )
    grad_attended = jnp.einsum(
        "rwd,ed->rwe", grad_attn_in, w_out, preferred_element_type=jnp.float32
    ).astype(jnp.bfloat16)
    grad_att_heads = grad_attended.reshape(head_shape)
    scores_again = (
        jnp.einsum("qwhd,kwhd->whqk", queries, key_heads, preferred_element_type=jnp.float32)
        * score_scale
    )
    probs_again = jnp.exp(scores_again - log_norm)
    grad_probs = jnp.einsum(
        "qwhd,kwhd->whqk", grad_att_heads, value_heads, preferred_element_type=jnp.float32
    )
    row_delta = jnp.sum(probs_again * grad_probs, axis=-1, keepdims=True)
    grad_scores = (probs_again * (grad_probs - row_delta)).astype(jnp.bfloat16)
    grad_queries = (
        jnp.einsum("whqk,kwhd->qwhd", grad_scores, key_heads, preferred_element_type=jnp.float32)
        * score_scale
    )
    grad_key_all = (
        jnp.einsum("whqk,qwhd->kwhd", grad_scores, queries, preferred_element_type=jnp.float32)
        * score_scale
    ).reshape(-1, windows, head_width)
    grad_value_all = jnp.einsum(
        "whqk,qwhd->kwhd",
        probs_again.astype(jnp.bfloat16),
        grad_att_heads,
        preferred_element_type=jnp.float32,
    ).reshape(-1, windows, head_width)
    grad_keys, grad_values = (
        lax.psum_scatter(
            grad_key_all.astype(jnp.bfloat16), "seq", scatter_dimension=0, tiled=True
        ).astype(jnp.float32),
        lax.psum_scatter(
            grad_value_all.astype(jnp.bfloat16), "seq", scatter_dimension=0, tiled=True
        ).astype(jnp.float32),
    )
    grad_query_lin = (
        unrotate(grad_queries, cosine, sine)
        .reshape(span_rows, windows, head_width)
        .astype(jnp.bfloat16)
    )
    grad_key_lin = (
        unrotate(grad_keys.reshape(head_shape), cosine, sine)
        .reshape(span_rows, windows, head_width)
        .astype(jnp.bfloat16)
    )
    grad_value_lin = grad_values.astype(jnp.bfloat16)
    grad_joined = jnp.concatenate([grad_query_lin, grad_key_lin, grad_value_lin], axis=-1)
    grad_w_joined = jnp.einsum(
        "rwd,rwe->de", first_full, grad_joined, preferred_element_type=jnp.float32
    )
    grad_w_query = grad_w_joined[:, :head_width]
    grad_w_key = grad_w_joined[:, head_width : 2 * head_width]
    grad_w_value = grad_w_joined[:, 2 * head_width :]
    block_part = grad_joined
    grad_first = lax.psum_scatter(
        jnp.einsum("rwe,de->rwd", block_part, w_joined, preferred_element_type=jnp.float32).astype(
            jnp.bfloat16
        ),
        "tensor",
        scatter_dimension=0,
        tiled=True,
    ).astype(jnp.float32)
    grad_norm1_gain = jnp.sum(grad_first * normed1, axis=(0, 1))
    grad_norm1_bias = jnp.sum(grad_first, axis=(0, 1))
    grad_tokens = grad_residual2 + norm_back(grad_first, normed1, inv_std1, norm1_gain)
    summed = (
        lax.psum_scatter(
            grad_w_query.astype(jnp.bfloat16), ("dp", "seq"), scatter_dimension=0, tiled=True
        ).astype(jnp.float32),
        lax.psum_scatter(
            grad_w_key.astype(jnp.bfloat16), ("dp", "seq"), scatter_dimension=0, tiled=True
        ).astype(jnp.float32),
        lax.psum_scatter(
            grad_w_value.astype(jnp.bfloat16), ("dp", "seq"), scatter_dimension=0, tiled=True
        ).astype(jnp.float32),
        lax.psum_scatter(
            grad_w_out.astype(jnp.bfloat16), ("dp", "seq"), scatter_dimension=1, tiled=True
        ).astype(jnp.float32),
        lax.psum_scatter(
            grad_w_gate.astype(jnp.bfloat16), ("dp", "seq"), scatter_dimension=0, tiled=True
        ).astype(jnp.float32),
        lax.psum_scatter(
            grad_w_up.astype(jnp.bfloat16), ("dp", "seq"), scatter_dimension=0, tiled=True
        ).astype(jnp.float32),
        lax.psum_scatter(
            grad_w_down.astype(jnp.bfloat16), ("dp", "seq"), scatter_dimension=1, tiled=True
        ).astype(jnp.float32),
    )
    norm_sums = (
        lax.psum_scatter(grad_norm1_gain, ("dp", "seq", "tensor"), scatter_dimension=0, tiled=True),
        lax.psum_scatter(grad_norm1_bias, ("dp", "seq", "tensor"), scatter_dimension=0, tiled=True),
        lax.psum_scatter(grad_norm2_gain, ("dp", "seq", "tensor"), scatter_dimension=0, tiled=True),
        lax.psum_scatter(grad_norm2_bias, ("dp", "seq", "tensor"), scatter_dimension=0, tiled=True),
    )
    return (
        output,
        grad_tokens,
        norm_sums[0],
        norm_sums[1],
        summed[0],
        summed[1],
        summed[2],
        summed[3],
        norm_sums[2],
        norm_sums[3],
        summed[4],
        summed[5],
        summed[6],
    )


BF = jnp.bfloat16
F32 = jnp.float32
LANES = 128


def dot_t(a, b):
    return lax.dot_general(a, b, (((1,), (1,)), ((), ())), preferred_element_type=F32)


def dot_n(a, b):
    return lax.dot_general(a, b, (((1,), (0,)), ((), ())), preferred_element_type=F32)


def t_dot(a, b):
    return lax.dot_general(a, b, (((0,), (0,)), ((), ())), preferred_element_type=F32)


def swap_halves(x):
    half = HEAD_DIM // 2
    lane = lax.broadcasted_iota(jnp.int32, x.shape, 1)
    down = pltpu.roll(x, half, 1)
    up = pltpu.roll(x, LANES - half, 1)
    return jnp.where(lane % HEAD_DIM < half, up, down)


def head_mask(h):
    lane = lax.broadcasted_iota(jnp.int32, (1, LANES), 1)
    return jnp.where(lane // HEAD_DIM == h, 1.0, 0.0).astype(BF)


MESH = pl.DeviceIdType.MESH


def any_spec():
    return pl.BlockSpec(memory_space=pl.ANY)


def greet(peers):
    barrier = pltpu.get_barrier_semaphore()
    for peer in peers:
        pl.semaphore_signal(barrier, inc=1, device_id=peer, device_id_type=MESH)
    pl.semaphore_wait(barrier, len(peers))


def remote(src, dst, send, recv, peer):
    return pltpu.make_async_remote_copy(
        src_ref=src, dst_ref=dst, send_sem=send, recv_sem=recv, device_id=peer, device_id_type=MESH
    )


def start_all(copies):
    for copy in copies:
        copy.start()


def wait_all(copies):
    for copy in copies:
        copy.wait()


def exchange_in_kernel(
    sizes, tok_ref, wq_ref, wk_ref, wv_ref, wo_ref, x_ref, q_ref, k_ref, v_ref, o_ref,
    tok_send, tok_recv, w_send, w_recv, local_sem,
):
    n_seq, n_ten, half, rows, slices = sizes
    dp, sx, t = lax.axis_index("dp"), lax.axis_index("seq"), lax.axis_index("tensor")
    y, c = dp // 2, dp % 2
    me = sx * n_ten + t
    group = n_seq * n_ten
    others = []
    for i in range(1, group):
        g = (me + i) % group
        others.append((g // n_ten, g % n_ten))
    y_peer, c_peer, x_peer = {"dp": (dp + 2) % 4}, {"dp": 2 * y + 1 - c}, {"seq": 1 - sx}
    greet([{"seq": a, "tensor": b} for a, b in others] + [y_peer, c_peer])

    hw = wq_ref.shape[1]
    srow, orow = wq_ref.shape[0] // slices, hw // slices
    s_xy, s_yx = c * 4 + y * 2 + sx, c * 4 + sx * 2 + y
    weights = ((wq_ref, q_ref, s_xy, 0), (wk_ref, k_ref, s_xy, 0), (wv_ref, v_ref, s_yx, 0), (wo_ref, o_ref, s_yx, 1))

    def block(out, by_rows, base, count, which):
        if by_rows:
            return out.at[pl.ds(pl.multiple_of(which * hw + base * orow, orow), count * orow), :]
        return out.at[
            pl.ds(pl.multiple_of(base * srow, srow), count * srow), pl.ds(pl.multiple_of(which * hw, hw), hw)
        ]

    stage = [[], [], [], []]
    n = 0
    for j in range(1, n_ten):
        peer = {"tensor": (t + j) % n_ten}
        for w_ref, out, s, by_rows in weights:
            size = orow if by_rows else srow
            src = w_ref.at[pl.ds(pl.multiple_of(s * size, size), size), :]
            stage[0].append(remote(src, block(out, by_rows, s, 1, t), w_send.at[0, n], w_recv.at[0, n], peer))
            n += 1
    n = 0
    for j in range(1, n_ten):
        which = (t + j) % n_ten
        for w_ref, out, s, by_rows in weights:
            xy = s is s_xy
            hops = (
                (1, x_peer if xy else y_peer, s, 1),
                (2, y_peer if xy else x_peer, s // 2 * 2, 2),
                (3, c_peer, c * 4, 4),
            )
            for k, peer, base, count in hops:
                ref = block(out, by_rows, base, count, which)
                stage[k].append(remote(ref, ref, w_send.at[k, n], w_recv.at[k, n], peer))
            n += 1
    start_all(stage[0])

    tokens = []
    for i, (a, b) in enumerate(others):
        tokens.append(
            remote(
                tok_ref.at[a * half + b],
                x_ref.at[pl.ds(pl.multiple_of(me * rows, rows), rows), :],
                tok_send.at[i], tok_recv.at[i], {"seq": a, "tensor": b},
            )
        )
    tokens.append(
        remote(
            tok_ref.at[(1 - sx) * half + n_ten],
            x_ref.at[pl.ds(pl.multiple_of((group + sx) * rows, rows), rows), :],
            tok_send.at[group - 1], tok_recv.at[group - 1], x_peer,
        )
    )
    start_all(tokens)
    local = [
        pltpu.make_async_copy(
            tok_ref.at[sx * half + t], x_ref.at[pl.ds(pl.multiple_of(me * rows, rows), rows), :], local_sem.at[0]
        ),
        pltpu.make_async_copy(
            tok_ref.at[sx * half + n_ten],
            x_ref.at[pl.ds(pl.multiple_of((group + sx) * rows, rows), rows), :],
            local_sem.at[1],
        ),
    ]
    for i, (w_ref, out, s, by_rows) in enumerate(weights):
        local.append(pltpu.make_async_copy(w_ref, block(out, by_rows, 0, slices, t), local_sem.at[2 + i]))
    start_all(local)
    for k in range(1, 4):
        for earlier in stage[k - 1]:
            earlier.wait_recv()
        start_all(stage[k])
    for copy in stage[3]:
        copy.wait_recv()
    for copies in stage:
        for copy in copies:
            copy.wait_send()
    wait_all(local)
    wait_all(tokens)


def exchange_in(tok, w_query, w_key, w_value, w_out, n_dp, n_seq, n_ten):
    windows, rows, width = tok.shape
    slices = n_dp * n_seq
    vmem = pl.BlockSpec(memory_space=pltpu.VMEM)
    square = jax.ShapeDtypeStruct((width, width), BF)
    group = n_seq * n_ten
    return pl.pallas_call(
        functools.partial(exchange_in_kernel, (n_seq, n_ten, windows // n_seq, rows, slices)),
        in_specs=[vmem] * 5,
        out_specs=[any_spec()] * 5,
        out_shape=[jax.ShapeDtypeStruct(((group + n_seq) * rows, width), BF)] + [square] * 4,
        scratch_shapes=[
            pltpu.SemaphoreType.DMA((group,)),
            pltpu.SemaphoreType.DMA((group,)),
            pltpu.SemaphoreType.DMA((4, 4 * (n_ten - 1))),
            pltpu.SemaphoreType.DMA((4, 4 * (n_ten - 1))),
            pltpu.SemaphoreType.DMA((6,)),
        ],
        compiler_params=pltpu.CompilerParams(collective_id=0, has_side_effects=True),
        name="exchange_in",
    )(tok, w_query, w_key, w_value, w_out)


def qkv_kernel(x_ref, wq_ref, wk_ref, wv_ref, cos_ref, sin_ref, q_ref, k_ref, v_ref):
    x = x_ref[...]
    cos, sin = cos_ref[...], sin_ref[...]
    for w_ref, out_ref, scale in ((wq_ref, q_ref, 1.0 / math.sqrt(HEAD_DIM)), (wk_ref, k_ref, 1.0), (wv_ref, v_ref, None)):
        acc = dot_n(x, w_ref[...])
        for c in range(acc.shape[1] // LANES):
            part = acc[:, c * LANES : (c + 1) * LANES]
            if scale is not None:
                part = (part * cos + swap_halves(part) * sin) * scale
            out_ref[:, c * LANES : (c + 1) * LANES] = part.astype(BF)


def qkv_project(x, w_query, w_key, w_value, cos, sin):
    rows, width = x.shape
    tile, cols = 256, 512
    w_spec = pl.BlockSpec((width, cols), lambda t, r: (0, t))
    out_spec = pl.BlockSpec((tile, cols), lambda t, r: (r, t))
    table = pl.BlockSpec((tile, LANES), lambda t, r: (r, 0))
    return pl.pallas_call(
        qkv_kernel,
        grid=(width // cols, rows // tile),
        in_specs=[pl.BlockSpec((tile, width), lambda t, r: (r, 0)), w_spec, w_spec, w_spec, table, table],
        out_specs=[out_spec] * 3,
        out_shape=[jax.ShapeDtypeStruct((rows, width), BF)] * 3,
        cost_estimate=pl.CostEstimate(flops=6 * rows * width * width, bytes_accessed=8 * rows * width, transcendentals=0),
        name="qkv_project",
    )(x, w_query, w_key, w_value, cos, sin)


def attend_body(q_ref, k_ref, v_ref, o_ref):
    q, k, v = q_ref[...], k_ref[...], v_ref[...]
    outs = []
    for h in range(LANES // HEAD_DIM):
        s = dot_t(q * head_mask(h), k)
        p = jnp.exp(s - jnp.max(s, axis=1, keepdims=True))
        norm = jnp.sum(p, axis=1, keepdims=True)
        outs.append(dot_n(p.astype(BF), v) / norm)
    lane = lax.broadcasted_iota(jnp.int32, outs[0].shape, 1)
    o_ref[...] = jnp.where(lane < HEAD_DIM, outs[0], outs[1]).astype(BF)


def attend_specs(rows, tile):
    return [
        pl.BlockSpec((tile, LANES), lambda p, r: (r, p)),
        pl.BlockSpec((rows, LANES), lambda p, r: (0, p)),
        pl.BlockSpec((rows, LANES), lambda p, r: (0, p)),
    ]


def attend_cost(rows, pairs):
    return pl.CostEstimate(
        flops=16 * pairs * rows * rows * LANES, bytes_accessed=8 * rows * pairs * LANES, transcendentals=2 * pairs * rows * rows
    )


def attend(q, k, v):
    rows, width = q.shape
    tile, pairs = 512, width // LANES
    return pl.pallas_call(
        attend_body,
        grid=(pairs, rows // tile),
        in_specs=attend_specs(rows, tile),
        out_specs=pl.BlockSpec((tile, LANES), lambda p, r: (r, p)),
        out_shape=jax.ShapeDtypeStruct((rows, width), BF),
        cost_estimate=attend_cost(rows, pairs),
        name="attend",
    )(q, k, v)


def swap_part(refs, outs, send, recv, local_sem, n_ten, base):
    t = lax.axis_index("tensor")
    share, hw = outs[0].shape[0] // n_ten, outs[0].shape[1]
    copies, local = [], []
    rows = pl.ds(base, share)
    mine = pl.ds(pl.multiple_of(t * share, share), share)
    for i, (ref, out) in enumerate(zip(refs, outs, strict=True)):
        for j in range(1, n_ten):
            to = (t + j) % n_ten
            src = ref.at[rows, pl.ds(pl.multiple_of(to * hw, hw), hw)]
            copies.append(remote(src, out.at[mine, :], send.at[i, j - 1], recv.at[i, j - 1], {"tensor": to}))
        src = ref.at[rows, pl.ds(pl.multiple_of(t * hw, hw), hw)]
        local.append(pltpu.make_async_copy(src, out.at[mine, :], local_sem.at[i]))
    return copies, local


def attend_swap_kernel(
    n_ten, length, q_ref, k_ref, v_ref, q_all, k_all, v_all, o_ref, lq_ref, lk_ref, lv_ref, send, recv, local_sem
):
    t = lax.axis_index("tensor")
    step = pl.program_id(0) * pl.num_programs(1) + pl.program_id(1)
    copies, local = swap_part(
        (q_all, k_all, v_all), (lq_ref, lk_ref, lv_ref), send, recv, local_sem, n_ten, length
    )

    @pl.when(step == 0)
    def _():
        greet([{"tensor": (t + j) % n_ten} for j in range(1, n_ten)])
        start_all(copies + local)

    attend_body(q_ref, k_ref, v_ref, o_ref)

    @pl.when(step == pl.num_programs(0) * pl.num_programs(1) - 1)
    def _():
        wait_all(copies + local)


def attend_swap(q, k, v, length, n_ten):
    width = q.shape[1]
    tile, pairs, hw = 512, width // LANES, width // n_ten
    left = jax.ShapeDtypeStruct((length, hw), BF)
    return pl.pallas_call(
        functools.partial(attend_swap_kernel, n_ten, length),
        grid=(pairs, length // tile),
        in_specs=attend_specs(length, tile) + [any_spec()] * 3,
        out_specs=[pl.BlockSpec((tile, LANES), lambda p, r: (r, p))] + [any_spec()] * 3,
        out_shape=[jax.ShapeDtypeStruct((length, width), BF), left, left, left],
        scratch_shapes=[
            pltpu.SemaphoreType.DMA((3, n_ten - 1)),
            pltpu.SemaphoreType.DMA((3, n_ten - 1)),
            pltpu.SemaphoreType.DMA((3,)),
        ],
        compiler_params=pltpu.CompilerParams(collective_id=1, has_side_effects=True),
        cost_estimate=attend_cost(length, pairs),
        name="attend_swap",
    )(q, k, v, q, k, v)


def back_body(q_ref, g_ref, k_ref, v_ref, pick_ref, cos_ref, sin_ref, qcos_ref, qsin_ref):
    g, k, v, pick = g_ref[...], k_ref[...], v_ref[...], pick_ref[...]
    q = dot_n(pick, q_ref[...]).astype(BF)
    dq = []
    all_p, all_ds, all_q, all_g = [], [], [], []
    for h in range(LANES // HEAD_DIM):
        mask = head_mask(h)
        qh, gh = q * mask, g * mask
        s = dot_t(qh, k)
        p = jnp.exp(s - jnp.max(s, axis=1, keepdims=True))
        p = p / jnp.sum(p, axis=1, keepdims=True)
        dp = dot_t(gh, v)
        ds = (p * (dp - jnp.sum(p * dp, axis=1, keepdims=True))).astype(BF)
        dq.append(dot_n(ds, k))
        all_p.append(p.astype(BF))
        all_ds.append(ds)
        all_q.append(qh)
        all_g.append(gh)
    lane = lax.broadcasted_iota(jnp.int32, dq[0].shape, 1)
    dq = jnp.where(lane < HEAD_DIM, dq[0], dq[1]) * (1.0 / math.sqrt(HEAD_DIM))
    dq = (dq * qcos_ref[...] - swap_halves(dq) * qsin_ref[...]).astype(BF)
    dq = t_dot(pick, dq).astype(BF)
    dk = t_dot(jnp.concatenate(all_ds, axis=0), jnp.concatenate(all_q, axis=0))
    dk = (dk * cos_ref[...] - swap_halves(dk) * sin_ref[...]).astype(BF)
    dv = t_dot(jnp.concatenate(all_p, axis=0), jnp.concatenate(all_g, axis=0)).astype(BF)
    return dq, dk, dv


def back_kernel(q_ref, g_ref, k_ref, v_ref, pick_ref, cos_ref, sin_ref, qcos_ref, qsin_ref, dq_ref, dk_ref, dv_ref):
    dq_ref[...], dk_ref[...], dv_ref[...] = back_body(
        q_ref, g_ref, k_ref, v_ref, pick_ref, cos_ref, sin_ref, qcos_ref, qsin_ref
    )


def back_specs(length, masked):
    full = pl.BlockSpec((length, LANES), lambda p: (0, p))
    same = pl.BlockSpec((length, LANES), lambda p: (0, 0))
    row_same = pl.BlockSpec((masked, LANES), lambda p: (0, 0))
    return [
        full, pl.BlockSpec((masked, LANES), lambda p: (0, p)), full, full,
        pl.BlockSpec((masked, length), lambda p: (0, 0)), same, same, row_same, row_same,
    ]


def back_cost(length, masked, pairs):
    return pl.CostEstimate(
        flops=24 * pairs * length * masked * LANES, bytes_accessed=12 * length * pairs * LANES, transcendentals=2 * pairs * length * masked
    )


def attend_back(q, grad_rows, k, v, pick, tables):
    masked, length = pick.shape
    width = q.shape[1]
    full = pl.BlockSpec((length, LANES), lambda p: (0, p))
    return pl.pallas_call(
        back_kernel,
        grid=(width // LANES,),
        in_specs=back_specs(length, masked),
        out_specs=[full] * 3,
        out_shape=[jax.ShapeDtypeStruct((length, width), BF)] * 3,
        cost_estimate=back_cost(length, masked, width // LANES),
        name="attend_back",
    )(q, grad_rows, k, v, pick, *tables)


def back_swap_kernel(
    n_ten, q_ref, g_ref, k_ref, v_ref, pick_ref, cos_ref, sin_ref, qcos_ref, qsin_ref, lq_ref, lk_ref, lv_ref,
    dq_ref, dk_ref, dv_ref, buf, out_sem, send, recv, local_sem,
):
    t = lax.axis_index("tensor")
    step, steps = pl.program_id(0), pl.num_programs(0)
    length = q_ref.shape[0]
    share, hw = lq_ref.shape[0] // n_ten, lq_ref.shape[1]
    outs = (dq_ref, dk_ref, dv_ref)
    copies, local = [], []
    mine = pl.ds(pl.multiple_of(t * hw, hw), hw)
    for i, (ref, out) in enumerate(zip((lq_ref, lk_ref, lv_ref), outs, strict=True)):
        dst = out.at[pl.ds(length, share), mine]
        for j in range(1, n_ten):
            to = (t + j) % n_ten
            src = ref.at[pl.ds(pl.multiple_of(to * share, share), share), :]
            copies.append(remote(src, dst, send.at[i, j - 1], recv.at[i, j - 1], {"tensor": to}))
        src = ref.at[pl.ds(pl.multiple_of(t * share, share), share), :]
        local.append(pltpu.make_async_copy(src, dst, local_sem.at[i]))

    def out_copy(at, i):
        slot = at % 2
        columns = pl.ds(pl.multiple_of(at * LANES, LANES), LANES)
        return pltpu.make_async_copy(buf.at[slot, i], outs[i].at[pl.ds(0, length), columns], out_sem.at[slot, i])

    @pl.when(step == 0)
    def _():
        greet([{"tensor": (t + j) % n_ten} for j in range(1, n_ten)])
        start_all(copies + local)

    @pl.when(step >= 2)
    def _():
        for i in range(3):
            out_copy(step - 2, i).wait()

    results = back_body(q_ref, g_ref, k_ref, v_ref, pick_ref, cos_ref, sin_ref, qcos_ref, qsin_ref)
    for i in range(3):
        buf[step % 2, i] = results[i]
        out_copy(step, i).start()

    @pl.when(step == steps - 1)
    def _():
        for i in range(3):
            out_copy(step - 1, i).wait()
            out_copy(step, i).wait()
        wait_all(copies + local)


def back_swap(q, grad_rows, k, v, pick, tables, left, n_ten):
    masked, length = pick.shape
    width = q.shape[1]
    share = left[0].shape[0] // n_ten
    return pl.pallas_call(
        functools.partial(back_swap_kernel, n_ten),
        grid=(width // LANES,),
        in_specs=back_specs(length, masked) + [any_spec()] * 3,
        out_specs=[any_spec()] * 3,
        out_shape=[jax.ShapeDtypeStruct((length + share, width), BF)] * 3,
        scratch_shapes=[
            pltpu.VMEM((2, 3, length, LANES), BF),
            pltpu.SemaphoreType.DMA((2, 3)),
            pltpu.SemaphoreType.DMA((3, n_ten - 1)),
            pltpu.SemaphoreType.DMA((3, n_ten - 1)),
            pltpu.SemaphoreType.DMA((3,)),
        ],
        compiler_params=pltpu.CompilerParams(collective_id=2, has_side_effects=True),
        cost_estimate=back_cost(length, masked, width // LANES),
        name="back_swap",
    )(q, grad_rows, k, v, pick, *tables, *left)


def feed_kernel(x_ref, res_ref, gu_ref, down_ref, out_ref, acc_ref):
    step = pl.program_id(0)
    x = x_ref[...]
    unit = down_ref.shape[1]
    parts = []
    for p in range(gu_ref.shape[0]):
        both = dot_n(x, gu_ref[p])
        gate, up = both[:, :unit], both[:, unit:]
        parts.append((gate * jax.nn.sigmoid(gate) * up).astype(BF))
    hidden = jnp.concatenate(parts, axis=1)
    down = down_ref[...].reshape(-1, down_ref.shape[2])
    new = dot_n(hidden, down)

    @pl.when(step == 0)
    def _():
        acc_ref[...] = res_ref[...] + new

    @pl.when(step > 0)
    def _():
        acc_ref[...] += new

    @pl.when(step == pl.num_programs(0) - 1)
    def _():
        out_ref[...] = acc_ref[...].astype(BF)


def feed_forward(x, res, gate_up, down):
    rows, width = x.shape
    pieces, unit = down.shape[:2]
    per = 2
    whole = lambda i: (0, 0)
    return pl.pallas_call(
        feed_kernel,
        grid=(pieces // per,),
        in_specs=[
            pl.BlockSpec((rows, width), whole, pipeline_mode=pl.Buffered(1)),
            pl.BlockSpec((rows, width), whole, pipeline_mode=pl.Buffered(1)),
            pl.BlockSpec((per, width, 2 * unit), lambda i: (i, 0, 0)),
            pl.BlockSpec((per, unit, width), lambda i: (i, 0, 0)),
        ],
        out_specs=pl.BlockSpec((rows, width), whole),
        out_shape=jax.ShapeDtypeStruct((rows, width), BF),
        scratch_shapes=[pltpu.VMEM((rows, width), F32)],
        cost_estimate=pl.CostEstimate(
            flops=6 * rows * width * pieces * unit, bytes_accessed=6 * width * pieces * unit, transcendentals=rows * pieces * unit
        ),
        name="feed_forward",
    )(x, res, gate_up, down)


def rotary_lanes(positions):
    cosine, sine = rotary_tables(positions)
    reps = LANES // HEAD_DIM
    return (
        jnp.concatenate([cosine, cosine] * reps, axis=1),
        jnp.concatenate([-sine, sine] * reps, axis=1),
    )


def window_shards(
    tokens,
    norm1_gain,
    norm1_bias,
    w_query,
    w_key,
    w_value,
    w_out,
    norm2_gain,
    norm2_bias,
    w_gate,
    w_up,
    w_down,
    out_grad,
    masked_rows,
    window_counts,
):
    rows_local, windows, width = tokens.shape
    n_dp, n_seq, n_ten = lax.axis_size("dp"), lax.axis_size("seq"), lax.axis_size("tensor")
    seq_index, ten_index = lax.axis_index("seq"), lax.axis_index("tensor")
    shard_index = lax.axis_index("dp") * n_seq + seq_index
    half = windows // n_seq
    length = rows_local * n_seq * n_ten
    share = length // n_ten
    hw = w_query.shape[1]
    slots = masked_rows.shape[1]
    part = slots // n_ten
    units = w_down.shape[0] // (n_dp * n_seq)

    cut = lambda w, axis: lax.dynamic_slice_in_dim(w, shard_index * units, units, axis)
    everywhere = ("dp", "seq", "tensor")
    gate_up = lax.all_gather(jnp.concatenate([cut(w_gate, 1), cut(w_up, 1)], axis=1), everywhere, axis=0, tiled=False)
    down = lax.all_gather(cut(w_down, 0), everywhere, axis=0, tiled=False)

    both_tok, all_q, all_k, all_v, all_out = exchange_in(
        jnp.swapaxes(tokens, 0, 1), w_query, w_key, w_value, w_out, n_dp, n_seq, n_ten
    )

    live = jnp.arange(windows) < window_counts[0]
    valid = (masked_rows < length) & live[:, None]
    total = lax.psum(jnp.sum(valid.astype(jnp.int32)), "dp")
    loss_weight = LOSS_SCALE / total.astype(F32)
    first_window = seq_index * half
    my_rows = lax.dynamic_slice_in_dim(masked_rows, first_window, half, 0)
    my_valid = lax.dynamic_slice_in_dim(valid, first_window, half, 0)
    cot = lax.dynamic_slice_in_dim(out_grad, first_window, half, 0).astype(F32) * loss_weight
    cot = jnp.where(my_valid[:, :, None], cot, 0.0)
    cot_low = cot.astype(BF)
    own_rows = lax.dynamic_index_in_dim(my_rows, ten_index, 0, keepdims=False)
    own_valid = lax.dynamic_index_in_dim(my_valid, ten_index, 0, keepdims=False)
    own_cot = lax.dynamic_index_in_dim(cot, ten_index, 0, keepdims=False)
    left_rows, left_valid, left_cot = my_rows[n_ten], my_valid[n_ten], cot[n_ten]
    every = jnp.arange(length)
    left_every = jnp.swapaxes(every.reshape(n_seq, n_ten, rows_local), 0, 1).reshape(n_ten, share)
    my_left = lax.dynamic_index_in_dim(left_every, ten_index, 0, keepdims=False)
    left_every = left_every.reshape(length)
    own_pick = ((own_rows[:, None] == every[None, :]) & own_valid[:, None]).astype(BF)
    left_pick = ((left_rows[:, None] == left_every[None, :]) & left_valid[:, None]).astype(BF)
    part_pick = ((left_rows[:, None] == my_left[None, :]) & left_valid[:, None]).astype(BF)

    own_tables = rotary_lanes(every) + rotary_lanes(own_rows)
    left_tables = rotary_lanes(left_every) + rotary_lanes(left_rows)
    part_tables = rotary_lanes(my_left)
    cos, sin = [jnp.concatenate([a, b], axis=0) for a, b in zip(own_tables[:2], part_tables, strict=True)]

    def norm(x, gain, bias):
        normed, inv_std = layer_stats(x)
        return normed, inv_std, (normed * gain + bias).astype(BF)

    pick_rows = lambda pick, x: dot_n(pick, x).astype(BF)
    left_tok_m = lax.all_gather(pick_rows(part_pick, both_tok[length:]), "tensor", axis=0, tiled=False)
    _, _, first = norm(both_tok.astype(F32), norm1_gain, norm1_bias)
    q, k, v = qkv_project(first, all_q, all_k, all_v, cos, sin)
    own_att, left_q, left_k, left_v = attend_swap(q, k, v, length, n_ten)
    left_att = attend(left_q, left_k, left_v)
    left_att_part = lax.all_to_all(left_att.reshape(n_ten, share, hw), "tensor", 0, 0, tiled=True)
    left_att_part = jnp.swapaxes(left_att_part, 0, 1).reshape(share, width)

    own_att_m = pick_rows(own_pick, own_att)
    left_att_m = pick_rows(left_pick, left_att)
    own_res_m = pick_rows(own_pick, both_tok[:length]).astype(F32) + dot_n(own_att_m, all_out)
    own_normed2, own_inv2, own_second = norm(own_res_m, norm2_gain, norm2_bias)
    sent = lax.all_gather(jnp.concatenate([own_second, left_att_m], axis=1), "tensor", axis=0, tiled=False)
    left_att_full = jnp.swapaxes(sent[:, :, width:], 0, 1).reshape(slots, width)
    left_tok_full = jnp.sum(left_tok_m.astype(F32), axis=0)
    left_res_m = left_tok_full + dot_n(left_att_full, all_out)
    left_normed2, left_inv2, left_second = norm(left_res_m, norm2_gain, norm2_bias)
    second = jnp.concatenate([sent[:, :, :width].reshape(n_ten * slots, width), left_second], axis=0)

    gate = dot_n(second, w_gate)
    up = dot_n(second, w_up)
    down_in = cot_low.reshape(half * slots, width)
    grad_hidden = dot_t(down_in, w_down)
    sig = jax.nn.sigmoid(gate)
    silu = gate * sig
    hidden_m = (silu * up).astype(BF)
    grad_gate = (grad_hidden * up * sig * (1.0 + gate * (1.0 - sig))).astype(BF)
    grad_up = (grad_hidden * silu).astype(BF)
    grad_second = (dot_t(grad_gate, w_gate) + dot_t(grad_up, w_up)).astype(BF)
    grad_second = jnp.concatenate(
        [
            grad_second[: n_ten * slots].reshape(n_ten, slots, width),
            grad_second[n_ten * slots :].reshape(n_ten, part, width),
        ],
        axis=1,
    ).reshape(n_ten * (slots + part), width)
    grad_second = lax.psum_scatter(grad_second, "tensor", scatter_dimension=0, tiled=True)
    left_grad_second = lax.all_gather(grad_second[slots:], "tensor", axis=0, tiled=True).astype(F32)
    own_grad_second = grad_second[:slots].astype(F32)
    grad_w_ffn = jnp.concatenate(
        [t_dot(second, grad_gate).astype(BF), t_dot(second, grad_up).astype(BF), t_dot(down_in, hidden_m).astype(BF)], axis=1
    )

    mine = lambda x: lax.dynamic_slice_in_dim(x, ten_index * part, part, 0)
    grad_norm2_gain = jnp.sum(own_grad_second * own_normed2, axis=0) + jnp.sum(
        mine(left_grad_second * left_normed2), axis=0
    )
    grad_norm2_bias = jnp.sum(own_grad_second, axis=0) + jnp.sum(mine(left_grad_second), axis=0)
    own_gr2 = (own_cot + norm_back(own_grad_second, own_normed2, own_inv2, norm2_gain)).astype(BF)
    left_gr2 = (left_cot + norm_back(left_grad_second, left_normed2, left_inv2, norm2_gain)).astype(BF)

    own_gatt = dot_t(own_gr2, all_out).astype(BF)
    left_gatt = dot_t(left_gr2, w_out).astype(BF)
    on_tensor = (jnp.arange(n_ten) == ten_index).astype(BF)
    left_att_wide = (left_att_m[:, None, :] * on_tensor[None, :, None]).reshape(slots, width)
    grad_w_out = t_dot(
        jnp.concatenate([own_att_m, left_att_wide], axis=0), jnp.concatenate([own_gr2, left_gr2], axis=0)
    ).astype(BF)
    left_back = attend_back(left_q, left_gatt, left_k, left_v, left_pick, left_tables)
    dq, dk, dv = back_swap(q, own_gatt, k, v, own_pick, own_tables, left_back, n_ten)
    grad_first = dot_t(dq, all_q) + dot_t(dk, all_k) + dot_t(dv, all_v)
    grad_w_query, grad_w_key, grad_w_value = [t_dot(first, d).astype(BF) for d in (dq, dk, dv)]

    normed1, inv_std1 = layer_stats(both_tok.astype(F32))
    grad_norm1_gain = jnp.sum(grad_first * normed1, axis=0)
    grad_norm1_bias = jnp.sum(grad_first, axis=0)
    gr2_dense = jnp.concatenate([t_dot(own_pick, own_gr2), t_dot(part_pick, left_gr2)], axis=0)
    grad_both = (gr2_dense + norm_back(grad_first, normed1, inv_std1, norm1_gain)).astype(BF)

    att = jnp.concatenate([own_att, left_att_part], axis=0)
    residual2 = both_tok.astype(F32) + dot_n(att, all_out)
    _, _, second_low = norm(residual2, norm2_gain, norm2_bias)
    out_both = feed_forward(second_low, residual2, gate_up, down)

    def send_back(x):
        own = lax.all_to_all(
            x[:length].reshape(n_seq * n_ten, rows_local, width), ("seq", "tensor"), 0, 0, tiled=True
        ).reshape(n_seq, n_ten, rows_local, width)
        left = lax.all_to_all(x[length:].reshape(n_seq, rows_local, width), "seq", 0, 0, tiled=True)
        both = jnp.concatenate([own, left[:, None]], axis=1).reshape(windows, rows_local, width)
        return jnp.swapaxes(both, 0, 1)

    output = send_back(out_both)
    grad_tokens = send_back(grad_both).astype(F32)

    def summed(x, dim):
        return lax.psum_scatter(x, ("dp", "seq"), scatter_dimension=dim, tiled=True)

    gw_all = summed(jnp.concatenate([grad_w_query, grad_w_key, grad_w_value], axis=1), 0)
    gw_q, gw_k, gw_v = [
        lax.psum_scatter(gw_all[:, i * width : (i + 1) * width], "tensor", scatter_dimension=1, tiled=True).astype(F32)
        for i in range(3)
    ]
    gw_out = lax.psum_scatter(summed(grad_w_out, 1), "tensor", scatter_dimension=0, tiled=True).astype(F32)
    gw_ffn = summed(grad_w_ffn, 0).astype(F32)
    hidden_units = w_gate.shape[1]
    gw_gate, gw_up = gw_ffn[:, :hidden_units], gw_ffn[:, hidden_units : 2 * hidden_units]
    gw_down = gw_ffn[:, 2 * hidden_units :].T
    vectors = [
        lax.psum_scatter(v, ("dp", "seq", "tensor"), scatter_dimension=0, tiled=True)
        for v in (grad_norm1_gain, grad_norm1_bias, grad_norm2_gain, grad_norm2_bias)
    ]
    return (
        output,
        grad_tokens,
        vectors[0],
        vectors[1],
        gw_q,
        gw_k,
        gw_v,
        gw_out,
        vectors[2],
        vectors[3],
        gw_gate,
        gw_up,
        gw_down,
    )


def shards(tokens, *rest):
    n_dp, n_seq, n_ten = lax.axis_size("dp"), lax.axis_size("seq"), lax.axis_size("tensor")
    whole = n_dp == 4 and n_seq == 2 and tokens.shape[1] == n_seq * (n_ten + 1)
    return (window_shards if whole else block_shards)(tokens, *rest)


def solution(mesh):
    return jax.shard_map(
        shards,
        mesh=mesh,
        in_specs=(
            P(("seq", "tensor"), "dp", None),
            P(),
            P(),
            P(None, "tensor"),
            P(None, "tensor"),
            P(None, "tensor"),
            P("tensor", None),
            P(),
            P(),
            P(None, "tensor"),
            P(None, "tensor"),
            P("tensor", None),
            P("dp", None, None),
            P("dp", None),
            P("dp"),
        ),
        out_specs=(
            P(("seq", "tensor"), "dp", None),
            P(("seq", "tensor"), "dp", None),
            P(("dp", "seq", "tensor")),
            P(("dp", "seq", "tensor")),
            P(("dp", "seq"), "tensor"),
            P(("dp", "seq"), "tensor"),
            P(("dp", "seq"), "tensor"),
            P("tensor", ("dp", "seq")),
            P(("dp", "seq", "tensor")),
            P(("dp", "seq", "tensor")),
            P(("dp", "seq"), "tensor"),
            P(("dp", "seq"), "tensor"),
            P("tensor", ("dp", "seq")),
        ),
        check_vma=False,
    )
```

```python
import math

import functools

import jax
import jax.numpy as jnp
import numpy as np
from jax import lax
from jax.experimental import pallas as pl
from jax.experimental.pallas import tpu as pltpu
from jax.sharding import PartitionSpec as P

HEAD_DIM = 64
L = 1024
LOSS_SCALE = 1024


epsilon = 1e-05


def layer_stats(inputs):
    row_mean = jnp.mean(inputs, axis=-1, keepdims=True)
    centred = inputs - row_mean
    inv_std = lax.rsqrt(jnp.mean(centred * centred, axis=-1, keepdims=True) + epsilon)
    return (centred * inv_std, inv_std)


def norm_back(grad_norm, normed, inv_std, gain_vec):
    scaled = grad_norm * gain_vec
    return inv_std * (
        scaled
        - jnp.mean(scaled, axis=-1, keepdims=True)
        - normed * jnp.mean(scaled * normed, axis=-1, keepdims=True)
    )


def rotary_tables(positions):
    half_dim = HEAD_DIM // 2
    inv_freq = 10000.0 ** (-jnp.arange(half_dim, dtype=jnp.float32) * 2.0 / HEAD_DIM)
    angles = positions.astype(jnp.float32)[:, None] * inv_freq[None, :]
    return (jnp.cos(angles), jnp.sin(angles))


def rotate(values, cosine, sine):
    half_dim = values.shape[-1] // 2
    first_half = values[..., :half_dim]
    second_half = values[..., half_dim:]
    cos_b = cosine[:, None, None, :]
    sin_b = sine[:, None, None, :]
    return jnp.concatenate(
        [first_half * cos_b - second_half * sin_b, second_half * cos_b + first_half * sin_b],
        axis=-1,
    )


def unrotate(grads, cosine, sine):
    half_dim = grads.shape[-1] // 2
    first_half = grads[..., :half_dim]
    second_half = grads[..., half_dim:]
    cos_b = cosine[:, None, None, :]
    sin_b = sine[:, None, None, :]
    return jnp.concatenate(
        [first_half * cos_b + second_half * sin_b, second_half * cos_b - first_half * sin_b],
        axis=-1,
    )


def block_shards(
    tokens,
    norm1_gain,
    norm1_bias,
    w_query,
    w_key,
    w_value,
    w_out,
    norm2_gain,
    norm2_bias,
    w_gate,
    w_up,
    w_down,
    out_grad,
    masked_rows,
    window_counts,
):
    rows_local, windows, model_width = tokens.shape
    span_rows = rows_local * lax.axis_size("tensor")
    seq_index = lax.axis_index("seq")
    tensor_index = lax.axis_index("tensor")
    head_width = w_query.shape[1]
    heads_local = head_width // HEAD_DIM
    score_scale = 1.0 / math.sqrt(HEAD_DIM)
    head_shape = (span_rows, windows, heads_local, HEAD_DIM)
    residual = tokens.astype(jnp.float32)
    normed1, inv_std1 = layer_stats(residual)
    first_low = (normed1 * norm1_gain + norm1_bias).astype(jnp.bfloat16)
    first_full = lax.all_gather(first_low, "tensor", axis=0, tiled=True)
    w_joined = jnp.concatenate([w_query, w_key, w_value], axis=1)
    projected = jnp.einsum("rwd,de->rwe", first_full, w_joined, preferred_element_type=jnp.float32)
    positions = seq_index * span_rows + jnp.arange(span_rows)
    cosine, sine = rotary_tables(positions)
    queries = rotate(projected[..., :head_width].reshape(head_shape), cosine, sine).astype(
        jnp.bfloat16
    )
    keys_rot = (
        rotate(projected[..., head_width : 2 * head_width].reshape(head_shape), cosine, sine)
        .astype(jnp.bfloat16)
        .reshape(span_rows, windows, head_width)
    )
    values_own = projected[..., 2 * head_width :].astype(jnp.bfloat16)
    keys_all, values_all = (
        lax.all_gather(keys_rot, "seq", axis=0, tiled=True),
        lax.all_gather(values_own, "seq", axis=0, tiled=True),
    )
    key_heads = keys_all.reshape(-1, windows, heads_local, HEAD_DIM)
    value_heads = values_all.reshape(-1, windows, heads_local, HEAD_DIM)
    scores = (
        jnp.einsum("qwhd,kwhd->whqk", queries, key_heads, preferred_element_type=jnp.float32)
        * score_scale
    )
    row_max = jnp.max(scores, axis=-1, keepdims=True)
    row_sum = jnp.sum(jnp.exp(scores - row_max), axis=-1, keepdims=True)
    log_norm = row_max + jnp.log(row_sum)
    attn_prob = jnp.exp(scores - log_norm)
    prob_low = attn_prob.astype(jnp.bfloat16)
    attended = (
        jnp.einsum("whqk,kwhd->qwhd", prob_low, value_heads, preferred_element_type=jnp.float32)
        .reshape(span_rows, windows, head_width)
        .astype(jnp.bfloat16)
    )
    block_part = attended
    attn_branch = lax.psum_scatter(
        jnp.einsum("rwe,ed->rwd", block_part, w_out, preferred_element_type=jnp.float32).astype(
            jnp.bfloat16
        ),
        "tensor",
        scatter_dimension=0,
        tiled=True,
    ).astype(jnp.float32)
    residual2 = residual + attn_branch
    normed2, inv_std2 = layer_stats(residual2)
    second_low = (normed2 * norm2_gain + norm2_bias).astype(jnp.bfloat16)
    second_full = lax.all_gather(second_low, "tensor", axis=0, tiled=True)
    gate_proj = jnp.einsum("rwd,df->rwf", second_full, w_gate, preferred_element_type=jnp.float32)
    up_proj = jnp.einsum("rwd,df->rwf", second_full, w_up, preferred_element_type=jnp.float32)
    hidden = (jax.nn.silu(gate_proj) * up_proj).astype(jnp.bfloat16)
    block_part = hidden
    ffn_branch = lax.psum_scatter(
        jnp.einsum("rwf,fd->rwd", block_part, w_down, preferred_element_type=jnp.float32).astype(
            jnp.bfloat16
        ),
        "tensor",
        scatter_dimension=0,
        tiled=True,
    ).astype(jnp.float32)
    output = (residual2 + ffn_branch).astype(jnp.bfloat16)
    live_slot = jnp.arange(windows) < window_counts[0]
    valid_slot = (masked_rows < L) & live_slot[:, None]
    local_masked = jnp.sum(jnp.where(valid_slot, 1, 0)).astype(jnp.int32)
    total_masked = lax.psum(local_masked, "dp")
    loss_weight = LOSS_SCALE / total_masked.astype(jnp.float32)
    own_positions = seq_index * span_rows + tensor_index * rows_local + jnp.arange(rows_local)
    matches = (masked_rows[:, None, :] == own_positions[None, :, None]) & live_slot[:, None, None]
    picked = jnp.einsum(
        "wrm,wmd->rwd", matches.astype(jnp.bfloat16), out_grad, preferred_element_type=jnp.float32
    )
    grad_out = picked * loss_weight
    grad_down_in = lax.all_gather(grad_out.astype(jnp.bfloat16), "tensor", axis=0, tiled=True)
    grad_w_down = jnp.einsum(
        "rwf,rwd->fd", hidden, grad_down_in, preferred_element_type=jnp.float32
    )
    grad_hidden = jnp.einsum(
        "rwd,fd->rwf", grad_down_in, w_down, preferred_element_type=jnp.float32
    )
    sigmoid_gate = jax.nn.sigmoid(gate_proj)
    silu_gate = gate_proj * sigmoid_gate
    grad_gate = (
        grad_hidden * up_proj * sigmoid_gate * (1.0 + gate_proj * (1.0 - sigmoid_gate))
    ).astype(jnp.bfloat16)
    grad_up = (grad_hidden * silu_gate).astype(jnp.bfloat16)
    grad_w_gate = jnp.einsum(
        "rwd,rwf->df", second_full, grad_gate, preferred_element_type=jnp.float32
    )
    grad_w_up = jnp.einsum("rwd,rwf->df", second_full, grad_up, preferred_element_type=jnp.float32)
    grad_second = lax.psum_scatter(
        (
            jnp.einsum("rwf,df->rwd", grad_gate, w_gate, preferred_element_type=jnp.float32)
            + jnp.einsum("rwf,df->rwd", grad_up, w_up, preferred_element_type=jnp.float32)
        ).astype(jnp.bfloat16),
        "tensor",
        scatter_dimension=0,
        tiled=True,
    ).astype(jnp.float32)
    grad_norm2_gain = jnp.sum(grad_second * normed2, axis=(0, 1))
    grad_norm2_bias = jnp.sum(grad_second, axis=(0, 1))
    grad_residual2 = grad_out + norm_back(grad_second, normed2, inv_std2, norm2_gain)
    grad_attn_in = lax.all_gather(grad_residual2.astype(jnp.bfloat16), "tensor", axis=0, tiled=True)
    grad_w_out = jnp.einsum(
        "rwe,rwd->ed", attended, grad_attn_in, preferred_element_type=jnp.float32
    )
    grad_attended = jnp.einsum(
        "rwd,ed->rwe", grad_attn_in, w_out, preferred_element_type=jnp.float32
    ).astype(jnp.bfloat16)
    grad_att_heads = grad_attended.reshape(head_shape)
    scores_again = (
        jnp.einsum("qwhd,kwhd->whqk", queries, key_heads, preferred_element_type=jnp.float32)
        * score_scale
    )
    probs_again = jnp.exp(scores_again - log_norm)
    grad_probs = jnp.einsum(
        "qwhd,kwhd->whqk", grad_att_heads, value_heads, preferred_element_type=jnp.float32
    )
    row_delta = jnp.sum(probs_again * grad_probs, axis=-1, keepdims=True)
    grad_scores = (probs_again * (grad_probs - row_delta)).astype(jnp.bfloat16)
    grad_queries = (
        jnp.einsum("whqk,kwhd->qwhd", grad_scores, key_heads, preferred_element_type=jnp.float32)
        * score_scale
    )
    grad_key_all = (
        jnp.einsum("whqk,qwhd->kwhd", grad_scores, queries, preferred_element_type=jnp.float32)
        * score_scale
    ).reshape(-1, windows, head_width)
    grad_value_all = jnp.einsum(
        "whqk,qwhd->kwhd",
        probs_again.astype(jnp.bfloat16),
        grad_att_heads,
        preferred_element_type=jnp.float32,
    ).reshape(-1, windows, head_width)
    grad_keys, grad_values = (
        lax.psum_scatter(
            grad_key_all.astype(jnp.bfloat16), "seq", scatter_dimension=0, tiled=True
        ).astype(jnp.float32),
        lax.psum_scatter(
            grad_value_all.astype(jnp.bfloat16), "seq", scatter_dimension=0, tiled=True
        ).astype(jnp.float32),
    )
    grad_query_lin = (
        unrotate(grad_queries, cosine, sine)
        .reshape(span_rows, windows, head_width)
        .astype(jnp.bfloat16)
    )
    grad_key_lin = (
        unrotate(grad_keys.reshape(head_shape), cosine, sine)
        .reshape(span_rows, windows, head_width)
        .astype(jnp.bfloat16)
    )
    grad_value_lin = grad_values.astype(jnp.bfloat16)
    grad_joined = jnp.concatenate([grad_query_lin, grad_key_lin, grad_value_lin], axis=-1)
    grad_w_joined = jnp.einsum(
        "rwd,rwe->de", first_full, grad_joined, preferred_element_type=jnp.float32
    )
    grad_w_query = grad_w_joined[:, :head_width]
    grad_w_key = grad_w_joined[:, head_width : 2 * head_width]
    grad_w_value = grad_w_joined[:, 2 * head_width :]
    block_part = grad_joined
    grad_first = lax.psum_scatter(
        jnp.einsum("rwe,de->rwd", block_part, w_joined, preferred_element_type=jnp.float32).astype(
            jnp.bfloat16
        ),
        "tensor",
        scatter_dimension=0,
        tiled=True,
    ).astype(jnp.float32)
    grad_norm1_gain = jnp.sum(grad_first * normed1, axis=(0, 1))
    grad_norm1_bias = jnp.sum(grad_first, axis=(0, 1))
    grad_tokens = grad_residual2 + norm_back(grad_first, normed1, inv_std1, norm1_gain)
    summed = (
        lax.psum_scatter(
            grad_w_query.astype(jnp.bfloat16), ("dp", "seq"), scatter_dimension=0, tiled=True
        ).astype(jnp.float32),
        lax.psum_scatter(
            grad_w_key.astype(jnp.bfloat16), ("dp", "seq"), scatter_dimension=0, tiled=True
        ).astype(jnp.float32),
        lax.psum_scatter(
            grad_w_value.astype(jnp.bfloat16), ("dp", "seq"), scatter_dimension=0, tiled=True
        ).astype(jnp.float32),
        lax.psum_scatter(
            grad_w_out.astype(jnp.bfloat16), ("dp", "seq"), scatter_dimension=1, tiled=True
        ).astype(jnp.float32),
        lax.psum_scatter(
            grad_w_gate.astype(jnp.bfloat16), ("dp", "seq"), scatter_dimension=0, tiled=True
        ).astype(jnp.float32),
        lax.psum_scatter(
            grad_w_up.astype(jnp.bfloat16), ("dp", "seq"), scatter_dimension=0, tiled=True
        ).astype(jnp.float32),
        lax.psum_scatter(
            grad_w_down.astype(jnp.bfloat16), ("dp", "seq"), scatter_dimension=1, tiled=True
        ).astype(jnp.float32),
    )
    norm_sums = (
        lax.psum_scatter(grad_norm1_gain, ("dp", "seq", "tensor"), scatter_dimension=0, tiled=True),
        lax.psum_scatter(grad_norm1_bias, ("dp", "seq", "tensor"), scatter_dimension=0, tiled=True),
        lax.psum_scatter(grad_norm2_gain, ("dp", "seq", "tensor"), scatter_dimension=0, tiled=True),
        lax.psum_scatter(grad_norm2_bias, ("dp", "seq", "tensor"), scatter_dimension=0, tiled=True),
    )
    return (
        output,
        grad_tokens,
        norm_sums[0],
        norm_sums[1],
        summed[0],
        summed[1],
        summed[2],
        summed[3],
        norm_sums[2],
        norm_sums[3],
        summed[4],
        summed[5],
        summed[6],
    )


BF = jnp.bfloat16
F32 = jnp.float32
LANES = 128


def dot_t(a, b):
    return lax.dot_general(a, b, (((1,), (1,)), ((), ())), preferred_element_type=F32)


def dot_n(a, b):
    return lax.dot_general(a, b, (((1,), (0,)), ((), ())), preferred_element_type=F32)


def t_dot(a, b):
    return lax.dot_general(a, b, (((0,), (0,)), ((), ())), preferred_element_type=F32)


def swap_halves(x):
    half = HEAD_DIM // 2
    lane = lax.broadcasted_iota(jnp.int32, x.shape, 1)
    down = pltpu.roll(x, half, 1)
    up = pltpu.roll(x, LANES - half, 1)
    return jnp.where(lane % HEAD_DIM < half, up, down)


def head_mask(h):
    lane = lax.broadcasted_iota(jnp.int32, (1, LANES), 1)
    return jnp.where(lane // HEAD_DIM == h, 1.0, 0.0).astype(BF)


MESH = pl.DeviceIdType.MESH


def any_spec():
    return pl.BlockSpec(memory_space=pl.ANY)


def greet(peers):
    barrier = pltpu.get_barrier_semaphore()
    for peer in peers:
        pl.semaphore_signal(barrier, inc=1, device_id=peer, device_id_type=MESH)
    pl.semaphore_wait(barrier, len(peers))


def remote(src, dst, send, recv, peer):
    return pltpu.make_async_remote_copy(
        src_ref=src, dst_ref=dst, send_sem=send, recv_sem=recv, device_id=peer, device_id_type=MESH
    )


def start_all(copies):
    for copy in copies:
        copy.start()


def wait_all(copies):
    for copy in copies:
        copy.wait()


def exchange_in_kernel(
    sizes, tok_ref, wq_ref, wk_ref, wv_ref, wo_ref, count_ref, x_ref, q_ref, k_ref, v_ref, o_ref, counts_ref,
    tok_send, tok_recv, w_send, w_recv, count_send, count_recv, local_sem,
):
    n_seq, n_ten, half, rows, slices = sizes
    dp, sx, t = lax.axis_index("dp"), lax.axis_index("seq"), lax.axis_index("tensor")
    y, c = dp // 2, dp % 2
    me = sx * n_ten + t
    group = n_seq * n_ten
    others = []
    for i in range(1, group):
        g = (me + i) % group
        others.append((g // n_ten, g % n_ten))
    y_peer, c_peer, x_peer = {"dp": (dp + 2) % 4}, {"dp": 2 * y + 1 - c}, {"seq": 1 - sx}
    dp_peers = [{"dp": (dp + i) % 4} for i in range(1, 4)]
    greet([{"seq": a, "tensor": b} for a, b in others] + dp_peers)
    counts = [
        remote(count_ref, counts_ref.at[dp], count_send.at[i], count_recv.at[i], peer) for i, peer in enumerate(dp_peers)
    ]
    start_all(counts)

    hw = wq_ref.shape[1]
    srow, orow = wq_ref.shape[0] // slices, hw // slices
    s_xy, s_yx = c * 4 + y * 2 + sx, c * 4 + sx * 2 + y
    weights = ((wq_ref, q_ref, s_xy, 0), (wk_ref, k_ref, s_xy, 0), (wv_ref, v_ref, s_yx, 0), (wo_ref, o_ref, s_yx, 1))

    def block(out, by_rows, base, count, which):
        if by_rows:
            return out.at[pl.ds(pl.multiple_of(which * hw + base * orow, orow), count * orow), :]
        return out.at[
            pl.ds(pl.multiple_of(base * srow, srow), count * srow), pl.ds(pl.multiple_of(which * hw, hw), hw)
        ]

    stage = [[], [], [], []]
    n = 0
    for j in range(1, n_ten):
        peer = {"tensor": (t + j) % n_ten}
        for w_ref, out, s, by_rows in weights:
            size = orow if by_rows else srow
            src = w_ref.at[pl.ds(pl.multiple_of(s * size, size), size), :]
            stage[0].append(remote(src, block(out, by_rows, s, 1, t), w_send.at[0, n], w_recv.at[0, n], peer))
            n += 1
    n = 0
    for j in range(1, n_ten):
        which = (t + j) % n_ten
        for w_ref, out, s, by_rows in weights:
            xy = s is s_xy
            hops = (
                (1, x_peer if xy else y_peer, s, 1),
                (2, y_peer if xy else x_peer, s // 2 * 2, 2),
                (3, c_peer, c * 4, 4),
            )
            for k, peer, base, count in hops:
                ref = block(out, by_rows, base, count, which)
                stage[k].append(remote(ref, ref, w_send.at[k, n], w_recv.at[k, n], peer))
            n += 1
    start_all(stage[0])

    tokens = []
    for i, (a, b) in enumerate(others):
        tokens.append(
            remote(
                tok_ref.at[a * half + b],
                x_ref.at[pl.ds(pl.multiple_of(me * rows, rows), rows), :],
                tok_send.at[i], tok_recv.at[i], {"seq": a, "tensor": b},
            )
        )
    tokens.append(
        remote(
            tok_ref.at[(1 - sx) * half + n_ten],
            x_ref.at[pl.ds(pl.multiple_of((group + sx) * rows, rows), rows), :],
            tok_send.at[group - 1], tok_recv.at[group - 1], x_peer,
        )
    )
    start_all(tokens)
    local = [
        pltpu.make_async_copy(
            tok_ref.at[sx * half + t], x_ref.at[pl.ds(pl.multiple_of(me * rows, rows), rows), :], local_sem.at[0]
        ),
        pltpu.make_async_copy(
            tok_ref.at[sx * half + n_ten],
            x_ref.at[pl.ds(pl.multiple_of((group + sx) * rows, rows), rows), :],
            local_sem.at[1],
        ),
    ]
    for i, (w_ref, out, s, by_rows) in enumerate(weights):
        local.append(pltpu.make_async_copy(w_ref, block(out, by_rows, 0, slices, t), local_sem.at[2 + i]))
    local.append(pltpu.make_async_copy(count_ref, counts_ref.at[dp], local_sem.at[6]))
    start_all(local)
    for k in range(1, 4):
        for earlier in stage[k - 1]:
            earlier.wait_recv()
        start_all(stage[k])
    for copy in stage[3]:
        copy.wait_recv()
    for copies in stage:
        for copy in copies:
            copy.wait_send()
    wait_all(local)
    wait_all(counts)
    wait_all(tokens)


def exchange_in(tok, w_query, w_key, w_value, w_out, count, n_dp, n_seq, n_ten):
    windows, rows, width = tok.shape
    slices = n_dp * n_seq
    vmem = pl.BlockSpec(memory_space=pltpu.VMEM)
    square = jax.ShapeDtypeStruct((width, width), BF)
    group = n_seq * n_ten
    return pl.pallas_call(
        functools.partial(exchange_in_kernel, (n_seq, n_ten, windows // n_seq, rows, slices)),
        in_specs=[vmem] * 6,
        out_specs=[any_spec()] * 6,
        out_shape=[jax.ShapeDtypeStruct(((group + n_seq) * rows, width), BF)]
        + [square] * 4
        + [jax.ShapeDtypeStruct((n_dp,) + count.shape, count.dtype)],
        scratch_shapes=[
            pltpu.SemaphoreType.DMA((group,)),
            pltpu.SemaphoreType.DMA((group,)),
            pltpu.SemaphoreType.DMA((4, 4 * (n_ten - 1))),
            pltpu.SemaphoreType.DMA((4, 4 * (n_ten - 1))),
            pltpu.SemaphoreType.DMA((3,)),
            pltpu.SemaphoreType.DMA((3,)),
            pltpu.SemaphoreType.DMA((7,)),
        ],
        compiler_params=pltpu.CompilerParams(collective_id=0, has_side_effects=True),
        name="exchange_in",
    )(tok, w_query, w_key, w_value, w_out, count)


def qkv_kernel(
    x_ref, gain_ref, bias_ref, wq_ref, wk_ref, wv_ref, cos_ref, sin_ref, part_cos_ref, part_sin_ref,
    first_ref, q_ref, k_ref, v_ref,
):
    shared = pl.program_id(0) == pl.num_programs(0) - 1
    normed, _ = layer_stats(x_ref[...].astype(F32))
    first_ref[...] = (normed * gain_ref[...] + bias_ref[...]).astype(BF)
    cos = jnp.where(shared, part_cos_ref[...], cos_ref[...])
    sin = jnp.where(shared, part_sin_ref[...], sin_ref[...])
    wide = 256
    for w_ref, out_ref, scale in ((wq_ref, q_ref, 1.0 / math.sqrt(HEAD_DIM)), (wk_ref, k_ref, 1.0), (wv_ref, v_ref, None)):
        for at in range(0, w_ref.shape[1], wide):
            acc = dot_n(first_ref[...], w_ref[:, at : at + wide])
            for c in range(0, wide, LANES):
                part = acc[:, c : c + LANES]
                if scale is not None:
                    part = (part * cos + swap_halves(part) * sin) * scale
                out_ref[:, at + c : at + c + LANES] = part.astype(BF)


def once(shape):
    return pl.BlockSpec(shape, lambda *_: (0,) * len(shape), pipeline_mode=pl.Buffered(1))


def norm_qkv(x, gain, bias, w_query, w_key, w_value, tables, part_tables):
    rows, width = x.shape
    tile = 256
    row = pl.BlockSpec((tile, width), lambda r: (r, 0))
    own = tables[0].shape[0] // tile
    table = pl.BlockSpec((tile, LANES), lambda r: (jnp.minimum(r, own - 1), 0))
    return pl.pallas_call(
        qkv_kernel,
        grid=(rows // tile,),
        in_specs=[row, once((1, width)), once((1, width))] + [once((width, width))] * 3 + [table, table] + [once((tile, LANES))] * 2,
        out_specs=[row] * 4,
        out_shape=[jax.ShapeDtypeStruct((rows, width), BF)] * 4,
        cost_estimate=pl.CostEstimate(flops=6 * rows * width * width, bytes_accessed=16 * rows * width, transcendentals=0),
        name="norm_qkv",
    )(x, gain.reshape(1, width), bias.reshape(1, width), w_query, w_key, w_value, *tables, *part_tables)


def attend_body(q_ref, k_ref, v_ref):
    q, k, v = q_ref[...], k_ref[...], v_ref[...]
    outs = []
    for h in range(LANES // HEAD_DIM):
        s = dot_t(q * head_mask(h), k)
        p = jnp.exp(s - jnp.max(s, axis=1, keepdims=True))
        norm = jnp.sum(p, axis=1, keepdims=True)
        outs.append(dot_n(p.astype(BF), v) / norm)
    lane = lax.broadcasted_iota(jnp.int32, outs[0].shape, 1)
    return jnp.where(lane < HEAD_DIM, outs[0], outs[1]).astype(BF)


def attend_specs(rows, tile):
    return [
        pl.BlockSpec((tile, LANES), lambda p, r: (r, p)),
        pl.BlockSpec((rows, LANES), lambda p, r: (0, p)),
        pl.BlockSpec((rows, LANES), lambda p, r: (0, p)),
    ]


def attend_cost(rows, pairs):
    return pl.CostEstimate(
        flops=16 * pairs * rows * rows * LANES, bytes_accessed=8 * rows * pairs * LANES, transcendentals=2 * pairs * rows * rows
    )


def attend_left_kernel(n_ten, q_ref, k_ref, v_ref, part_ref, buf, send, recv, local_sem):
    t = lax.axis_index("tensor")
    r, p = pl.program_id(0), pl.program_id(1)
    last_pair = p == pl.num_programs(1) - 1
    hw = buf.shape[2]
    heads = pl.ds(pl.multiple_of(t * hw, hw), hw)
    dst = part_ref.at[:, heads]

    @pl.when((p == 0) & (r == 0))
    def _():
        greet([{"tensor": (t + j) % n_ten} for j in range(1, n_ten)])

    buf[r, :, pl.ds(pl.multiple_of(p * LANES, LANES), LANES)] = attend_body(q_ref, k_ref, v_ref)

    def copy_to(j):
        to = (t + j) % n_ten
        return remote(buf.at[to], dst, send.at[j - 1], recv.at[j - 1], {"tensor": to})

    own = pltpu.make_async_copy(buf.at[t], dst, local_sem.at[0])
    for j in range(1, n_ten):

        @pl.when(last_pair & (r == (t + j) % n_ten))
        def _(j=j):
            copy_to(j).start()

    @pl.when(last_pair & (r == t))
    def _():
        own.start()

    @pl.when(last_pair & (r == n_ten - 1))
    def _():
        wait_all([copy_to(j) for j in range(1, n_ten)])
        own.wait()


def attend_left(q, k, v, n_ten):
    rows, hw = q.shape
    tile, pairs = rows // n_ten, hw // LANES
    column = pl.BlockSpec((rows, LANES), lambda r, p: (0, p))
    return pl.pallas_call(
        functools.partial(attend_left_kernel, n_ten),
        grid=(n_ten, pairs),
        in_specs=[pl.BlockSpec((tile, LANES), lambda r, p: (r, p)), column, column],
        out_specs=any_spec(),
        out_shape=jax.ShapeDtypeStruct((tile, n_ten * hw), BF),
        scratch_shapes=[pltpu.VMEM((n_ten, tile, hw), BF)]
        + [pltpu.SemaphoreType.DMA((n_ten - 1,))] * 2
        + [pltpu.SemaphoreType.DMA((1,))],
        compiler_params=pltpu.CompilerParams(collective_id=3, has_side_effects=True),
        cost_estimate=attend_cost(rows, pairs),
        name="attend_left",
    )(q, k, v)


def swap_part(refs, outs, send, recv, local_sem, n_ten, base):
    t = lax.axis_index("tensor")
    share, hw = outs[0].shape[0] // n_ten, outs[0].shape[1]
    copies, local = [], []
    rows = pl.ds(base, share)
    mine = pl.ds(pl.multiple_of(t * share, share), share)
    for i, (ref, out) in enumerate(zip(refs, outs, strict=True)):
        for j in range(1, n_ten):
            to = (t + j) % n_ten
            src = ref.at[rows, pl.ds(pl.multiple_of(to * hw, hw), hw)]
            copies.append(remote(src, out.at[mine, :], send.at[i, j - 1], recv.at[i, j - 1], {"tensor": to}))
        src = ref.at[rows, pl.ds(pl.multiple_of(t * hw, hw), hw)]
        local.append(pltpu.make_async_copy(src, out.at[mine, :], local_sem.at[i]))
    return copies, local


def attend_swap_kernel(
    n_ten, length, q_ref, k_ref, v_ref, q_all, k_all, v_all, o_ref, lq_ref, lk_ref, lv_ref, send, recv, local_sem
):
    t = lax.axis_index("tensor")
    step = pl.program_id(0) * pl.num_programs(1) + pl.program_id(1)
    copies, local = swap_part(
        (q_all, k_all, v_all), (lq_ref, lk_ref, lv_ref), send, recv, local_sem, n_ten, length
    )

    @pl.when(step == 0)
    def _():
        greet([{"tensor": (t + j) % n_ten} for j in range(1, n_ten)])
        start_all(copies + local)

    o_ref[...] = attend_body(q_ref, k_ref, v_ref)

    @pl.when(step == pl.num_programs(0) * pl.num_programs(1) - 1)
    def _():
        wait_all(copies + local)


def attend_swap(q, k, v, length, n_ten):
    width = q.shape[1]
    tile, pairs, hw = 512, width // LANES, width // n_ten
    left = jax.ShapeDtypeStruct((length, hw), BF)
    return pl.pallas_call(
        functools.partial(attend_swap_kernel, n_ten, length),
        grid=(pairs, length // tile),
        in_specs=attend_specs(length, tile) + [any_spec()] * 3,
        out_specs=[pl.BlockSpec((tile, LANES), lambda p, r: (r, p))] + [any_spec()] * 3,
        out_shape=[jax.ShapeDtypeStruct((length, width), BF), left, left, left],
        scratch_shapes=[
            pltpu.SemaphoreType.DMA((3, n_ten - 1)),
            pltpu.SemaphoreType.DMA((3, n_ten - 1)),
            pltpu.SemaphoreType.DMA((3,)),
        ],
        compiler_params=pltpu.CompilerParams(collective_id=1, has_side_effects=True),
        cost_estimate=attend_cost(length, pairs),
        name="attend_swap",
    )(q, k, v, q, k, v)


def back_body(q_ref, g_ref, k_ref, v_ref, pick_ref, cos_ref, sin_ref, qcos_ref, qsin_ref):
    g, k, v, pick = g_ref[...], k_ref[...], v_ref[...], pick_ref[...]
    q = dot_n(pick, q_ref[...]).astype(BF)
    dq = []
    all_p, all_ds, all_q, all_g = [], [], [], []
    for h in range(LANES // HEAD_DIM):
        mask = head_mask(h)
        qh, gh = q * mask, g * mask
        s = dot_t(qh, k)
        p = jnp.exp(s - jnp.max(s, axis=1, keepdims=True))
        p = p / jnp.sum(p, axis=1, keepdims=True)
        dp = dot_t(gh, v)
        ds = (p * (dp - jnp.sum(p * dp, axis=1, keepdims=True))).astype(BF)
        dq.append(dot_n(ds, k))
        all_p.append(p.astype(BF))
        all_ds.append(ds)
        all_q.append(qh)
        all_g.append(gh)
    lane = lax.broadcasted_iota(jnp.int32, dq[0].shape, 1)
    dq = jnp.where(lane < HEAD_DIM, dq[0], dq[1]) * (1.0 / math.sqrt(HEAD_DIM))
    dq = (dq * qcos_ref[...] - swap_halves(dq) * qsin_ref[...]).astype(BF)
    dq = t_dot(pick, dq).astype(BF)
    dk = t_dot(jnp.concatenate(all_ds, axis=0), jnp.concatenate(all_q, axis=0))
    dk = (dk * cos_ref[...] - swap_halves(dk) * sin_ref[...]).astype(BF)
    dv = t_dot(jnp.concatenate(all_p, axis=0), jnp.concatenate(all_g, axis=0)).astype(BF)
    return dq, dk, dv


def back_left_kernel(
    n_ten, q_ref, g_ref, k_ref, v_ref, pick_ref, cos_ref, sin_ref, qcos_ref, qsin_ref, dq_ref, dk_ref, dv_ref,
    parts, total, send, recv,
):
    t = lax.axis_index("tensor")
    p = pl.program_id(0)
    hw = total.shape[1]

    @pl.when(p == 0)
    def _():
        peers = [(t + j) % n_ten for j in range(1, n_ten)]
        greet([{"tensor": to} for to in peers])
        copies = [
            remote(
                g_ref.at[:, pl.ds(pl.multiple_of(to * hw, hw), hw)], parts.at[j], send.at[j], recv.at[j], {"tensor": to}
            )
            for j, to in enumerate(peers)
        ]
        start_all(copies)
        wait_all(copies)
        whole = g_ref[:, pl.ds(pl.multiple_of(t * hw, hw), hw)].astype(F32)
        for j in range(n_ten - 1):
            whole = whole + parts[j].astype(F32)
        total[...] = whole.astype(BF)

    g_view = total.at[:, pl.ds(pl.multiple_of(p * LANES, LANES), LANES)]
    dq_ref[...], dk_ref[...], dv_ref[...] = back_body(
        q_ref, g_view, k_ref, v_ref, pick_ref, cos_ref, sin_ref, qcos_ref, qsin_ref
    )


def back_specs(length, masked):
    full = pl.BlockSpec((length, LANES), lambda p: (0, p))
    same = pl.BlockSpec((length, LANES), lambda p: (0, 0))
    row_same = pl.BlockSpec((masked, LANES), lambda p: (0, 0))
    return [
        full, pl.BlockSpec((masked, LANES), lambda p: (0, p)), full, full,
        pl.BlockSpec((masked, length), lambda p: (0, 0)), same, same, row_same, row_same,
    ]


def back_cost(length, masked, pairs):
    return pl.CostEstimate(
        flops=24 * pairs * length * masked * LANES, bytes_accessed=12 * length * pairs * LANES, transcendentals=2 * pairs * length * masked
    )


def back_left(q, grad_rows, k, v, pick, tables, n_ten):
    masked, length = pick.shape
    width = q.shape[1]
    full = pl.BlockSpec((length, LANES), lambda p: (0, p))
    specs = back_specs(length, masked)
    specs[1] = once(grad_rows.shape)
    return pl.pallas_call(
        functools.partial(back_left_kernel, n_ten),
        grid=(width // LANES,),
        in_specs=specs,
        out_specs=[full] * 3,
        out_shape=[jax.ShapeDtypeStruct((length, width), BF)] * 3,
        scratch_shapes=[
            pltpu.VMEM((n_ten - 1, masked, width), BF),
            pltpu.VMEM((masked, width), BF),
            pltpu.SemaphoreType.DMA((n_ten - 1,)),
            pltpu.SemaphoreType.DMA((n_ten - 1,)),
        ],
        compiler_params=pltpu.CompilerParams(collective_id=6, has_side_effects=True),
        cost_estimate=back_cost(length, masked, width // LANES),
        name="back_left",
    )(q, grad_rows, k, v, pick, *tables)


def back_swap_kernel(
    n_ten, q_ref, g_ref, k_ref, v_ref, pick_ref, cos_ref, sin_ref, qcos_ref, qsin_ref, lq_ref, lk_ref, lv_ref,
    dq_ref, dk_ref, dv_ref, buf, out_sem, send, recv, local_sem,
):
    t = lax.axis_index("tensor")
    step, steps = pl.program_id(0), pl.num_programs(0)
    length = q_ref.shape[0]
    share, hw = lq_ref.shape[0] // n_ten, lq_ref.shape[1]
    outs = (dq_ref, dk_ref, dv_ref)
    copies, local = [], []
    mine = pl.ds(pl.multiple_of(t * hw, hw), hw)
    for i, (ref, out) in enumerate(zip((lq_ref, lk_ref, lv_ref), outs, strict=True)):
        dst = out.at[pl.ds(length, share), mine]
        for j in range(1, n_ten):
            to = (t + j) % n_ten
            src = ref.at[pl.ds(pl.multiple_of(to * share, share), share), :]
            copies.append(remote(src, dst, send.at[i, j - 1], recv.at[i, j - 1], {"tensor": to}))
        src = ref.at[pl.ds(pl.multiple_of(t * share, share), share), :]
        local.append(pltpu.make_async_copy(src, dst, local_sem.at[i]))

    def out_copy(at, i):
        slot = at % 2
        columns = pl.ds(pl.multiple_of(at * LANES, LANES), LANES)
        return pltpu.make_async_copy(buf.at[slot, i], outs[i].at[pl.ds(0, length), columns], out_sem.at[slot, i])

    @pl.when(step == 0)
    def _():
        greet([{"tensor": (t + j) % n_ten} for j in range(1, n_ten)])
        start_all(copies + local)

    @pl.when(step >= 2)
    def _():
        for i in range(3):
            out_copy(step - 2, i).wait()

    results = back_body(q_ref, g_ref, k_ref, v_ref, pick_ref, cos_ref, sin_ref, qcos_ref, qsin_ref)
    for i in range(3):
        buf[step % 2, i] = results[i]
        out_copy(step, i).start()

    @pl.when(step == steps - 1)
    def _():
        for i in range(3):
            out_copy(step - 1, i).wait()
            out_copy(step, i).wait()
        wait_all(copies + local)


def back_swap(q, grad_rows, k, v, pick, tables, left, n_ten):
    masked, length = pick.shape
    width = q.shape[1]
    share = left[0].shape[0] // n_ten
    return pl.pallas_call(
        functools.partial(back_swap_kernel, n_ten),
        grid=(width // LANES,),
        in_specs=back_specs(length, masked) + [any_spec()] * 3,
        out_specs=[any_spec()] * 3,
        out_shape=[jax.ShapeDtypeStruct((length + share, width), BF)] * 3,
        scratch_shapes=[
            pltpu.VMEM((2, 3, length, LANES), BF),
            pltpu.SemaphoreType.DMA((2, 3)),
            pltpu.SemaphoreType.DMA((3, n_ten - 1)),
            pltpu.SemaphoreType.DMA((3, n_ten - 1)),
            pltpu.SemaphoreType.DMA((3,)),
        ],
        compiler_params=pltpu.CompilerParams(collective_id=2, has_side_effects=True),
        cost_estimate=back_cost(length, masked, width // LANES),
        name="back_swap",
    )(q, grad_rows, k, v, pick, *tables, *left)


def weight_hops(gathered, n_ten, sems):
    dp, sx, t = lax.axis_index("dp"), lax.axis_index("seq"), lax.axis_index("tensor")
    y, c = dp // 2, dp % 2
    gate_ref, up_ref, down_ref = gathered
    width, units = gate_ref.shape[0], gate_ref.shape[1] // n_ten
    size, cols = width // 8, width // 2
    s_xy, s_yx = c * 4 + y * 2 + sx, c * 4 + sx * 2 + y
    x_peer, y_peer, c_peer = {"seq": 1 - sx}, {"dp": (dp + 2) % 4}, {"dp": 2 * y + 1 - c}
    send, recv = sems

    def shard(ref, k, first, count, which):
        rows = pl.multiple_of(first * (size if k < 2 else units // 8), 16)
        if k < 2:
            at = 0 if which is None else pl.multiple_of(which * units, units)
            return ref.at[pl.ds(rows, count * size), pl.ds(at, units)]
        at = rows if which is None else pl.multiple_of(which * units + rows, 16)
        return ref.at[pl.ds(at, count * (units // 8)), pl.ds((k - 2) * cols, cols)]

    refs = (gate_ref, up_ref, down_ref, down_ref)
    slices = (s_xy, s_yx, s_xy, s_yx)

    def along(which, peer_t, slot, number, own=None):
        copies = []
        for k in range(4):
            dst = shard(refs[k], k, slices[k], 1, which)
            src = dst if own is None else shard(own[min(k, 2)], k, slices[k], 1, None)
            copies.append(remote(src, dst, send.at[number, k], recv.at[slot, k], {"tensor": peer_t}))
        return copies

    def across(hop, which, order):
        copies = []
        for k in range(4):
            xy = k % 2 == 0
            peer, first, count = (
                (x_peer if xy else y_peer, slices[k], 1),
                (y_peer if xy else x_peer, slices[k] // 2 * 2, 2),
                (c_peer, c * 4, 4),
            )[hop]
            ref = shard(refs[k], k, first, count, which)
            copies.append(remote(ref, ref, send.at[5 + 3 * order + hop, k], recv.at[4 + 3 * order + hop, k], peer))
        return copies

    return along, across


def feed_kernel(
    n_ten, tok_ref, att_ref, left_ref, wo_ref, gain_ref, bias_ref, pick_ref, part_pick_ref, cot_ref, wg_ref, wu_ref, wd_ref,
    out_ref, att_m_ref, gr2_ref, gatt_ref, vec_ref, x_m_ref, ag_ref, au_ref, ad_ref,
    x_ref, acc_ref, normed_ref, inv_ref, grad_ref, g_buf, u_buf, d_buf, buf_sem, send, recv,
):
    dp, sx, t = lax.axis_index("dp"), lax.axis_index("seq"), lax.axis_index("tensor")
    step, steps = pl.program_id(0), pl.num_programs(0)
    rows, width = tok_ref.shape
    length = att_ref.shape[0]
    masked = cot_ref.shape[0]
    slots = masked // 2
    unit = g_buf.shape[2]
    units = wg_ref.shape[1]
    per = units // unit
    gain = gain_ref[...]
    own = (wg_ref, wu_ref, wd_ref)

    side = t // 2
    middle = jnp.minimum(t, n_ten - 1 - t)
    mirror = lambda k: k + side * (n_ten - 1 - 2 * k)
    order = [mirror(k) for k in (middle, 1 - middle, 2, 3)]
    inward, outward = mirror(middle + 1), mirror(0)
    along, across = weight_hops((ag_ref, au_ref, ad_ref), n_ten, (send, recv))
    to_in = along(t, inward, 1 + middle, 0, own)
    to_out = along(t, outward, 1, 1, own)
    in_far = along(mirror(0), inward, 3, 2)
    out_two = along(mirror(2), outward, 2, 3)
    out_three = along(mirror(3), outward, 3, 4)
    is_middle, is_end = middle == 1, middle == 0
    hop = [[across(h, order[i], i - 1) for h in range(3)] for i in (1, 2, 3)]

    def arrived(i):
        for copy in along(order[i], inward, i, 0):
            copy.wait_recv()

    def got(copies):
        for copy in copies:
            copy.wait_recv()

    def fetch(at):
        slot, i, b = at % 2, at // per, at % per

        def make(refs, shard_at):
            base = pl.multiple_of(shard_at * units + b * unit, unit)
            return [
                pltpu.make_async_copy(refs[0].at[:, pl.ds(base, unit)], g_buf.at[slot], buf_sem.at[slot, 0]),
                pltpu.make_async_copy(refs[1].at[:, pl.ds(base, unit)], u_buf.at[slot], buf_sem.at[slot, 1]),
                pltpu.make_async_copy(refs[2].at[pl.ds(base, unit), :], d_buf.at[slot], buf_sem.at[slot, 2]),
            ]

        @pl.when(i == 0)
        def _():
            start_all(make(own, 0))

        @pl.when(i > 0)
        def _():
            which = order[1] * (i == 1) + order[2] * (i == 2) + order[3] * (i == 3)
            start_all(make((ag_ref, au_ref, ad_ref), which))

    def fetched(at):
        slot = at % 2
        wait_all(
            [
                pltpu.make_async_copy(wg_ref.at[:, pl.ds(0, unit)], g_buf.at[slot], buf_sem.at[slot, 0]),
                pltpu.make_async_copy(wu_ref.at[:, pl.ds(0, unit)], u_buf.at[slot], buf_sem.at[slot, 1]),
                pltpu.make_async_copy(wd_ref.at[pl.ds(0, unit), :], d_buf.at[slot], buf_sem.at[slot, 2]),
            ]
        )

    def norm(res):
        normed, inv_std = layer_stats(res)
        return normed, inv_std, (normed * gain + bias_ref[...]).astype(BF)

    @pl.when(step == 0)
    def _():
        peers = [{"tensor": (t + j) % n_ten} for j in range(1, n_ten)]
        greet(peers + [{"seq": 1 - sx}] + [{"dp": (dp + 2) % 4}, {"dp": dp // 2 * 2 + 1 - dp % 2}])
        start_all(to_in)

        @pl.when(is_middle)
        def _():
            start_all(to_out)

        fetch(0)
        tile = rows - length
        for i, (pick, att, tok) in enumerate(
            ((pick_ref[...], att_ref[...], tok_ref[:length, :]), (part_pick_ref[...], left_ref[...], tok_ref[length:, :]))
        ):
            here = slice(i * slots, (i + 1) * slots)
            att_m = dot_n(pick, att).astype(BF)
            att_m_ref[here, :] = att_m
            normed, inv_std, low = norm(dot_n(pick, tok) + dot_n(att_m, wo_ref[...]))
            normed_ref[here, :] = normed
            inv_ref[here, :] = jnp.broadcast_to(inv_std, (slots, LANES))
            here_too = jnp.sum(pick.astype(F32), axis=1, keepdims=True) > 0.0
            low = jnp.where(here_too, low.astype(F32), 0.0).astype(BF)
            x_ref[rows + i * slots : rows + (i + 1) * slots, :] = low
            x_m_ref[here, :] = low
        for at in range(0, rows, tile):
            att = att_ref[at : at + tile, :] if at < length else left_ref[...]
            res = tok_ref[at : at + tile, :].astype(F32) + dot_n(att, wo_ref[...])
            x_ref[at : at + tile, :] = norm(res)[2]
            acc_ref[at : at + tile, :] = res
        grad_ref[...] = jnp.zeros_like(grad_ref)

    fetched(step)

    @pl.when((step + 1 < steps) & ((step + 1) % per != 0))
    def _():
        fetch(step + 1)

    slot = step % 2
    x = x_ref[...]
    w_g, w_u, w_d = g_buf[slot], u_buf[slot], d_buf[slot]
    gate, up = dot_n(x, w_g), dot_n(x, w_u)
    sig = jax.nn.sigmoid(gate)
    act = gate * sig
    hidden = (act[:rows] * up[:rows]).astype(BF)
    for at in range(0, width, unit):
        acc_ref[:, at : at + unit] += dot_n(hidden, w_d[:, at : at + unit])
    back = dot_t(cot_ref[...].astype(BF), w_d)
    gate, up, sig, act = gate[rows:], up[rows:], sig[rows:], act[rows:]
    grad_gate = (back * up * sig * (1.0 + gate * (1.0 - sig))).astype(BF)
    grad_up = (back * act).astype(BF)
    grad_ref[...] += dot_t(grad_gate, w_g) + dot_t(grad_up, w_u)

    @pl.when(step == per - 1)
    def _():
        arrived(1)
        start_all(hop[0][0])

        @pl.when(is_middle)
        def _():
            arrived(2)
            start_all(in_far)
            start_all(out_two)

        got(hop[0][0])
        start_all(hop[0][1])

        @pl.when(is_end)
        def _():
            arrived(2)

        @pl.when(is_middle)
        def _():
            arrived(3)
            start_all(out_three)

        start_all(hop[1][0])
        got(hop[0][1])
        start_all(hop[0][2])
        got(hop[0][2])

    @pl.when(step == per)
    def _():
        got(hop[1][0])
        start_all(hop[1][1])

    @pl.when(step == per + 1)
    def _():
        @pl.when(is_end)
        def _():
            arrived(3)

        start_all(hop[2][0])

    @pl.when(step == 2 * per - 1)
    def _():
        got(hop[1][1])
        start_all(hop[1][2])
        got(hop[2][0])
        start_all(hop[2][1])
        got(hop[1][2])

    @pl.when(step == 3 * per - 1)
    def _():
        got(hop[2][1])
        start_all(hop[2][2])
        got(hop[2][2])

    @pl.when((step + 1 < steps) & ((step + 1) % per == 0))
    def _():
        fetch(step + 1)

    @pl.when(step == steps - 1)
    def _():
        out_ref[...] = acc_ref[...].astype(BF)
        grad, normed = grad_ref[...], normed_ref[...]
        vec_ref[...] = jnp.concatenate(
            [jnp.sum(grad * normed, axis=0, keepdims=True), jnp.sum(grad, axis=0, keepdims=True)], axis=0
        )
        gr2 = (cot_ref[...] + norm_back(grad, normed, inv_ref[:, :1], gain)).astype(BF)
        gr2_ref[...] = gr2
        gatt_ref[...] = dot_t(gr2, wo_ref[...]).astype(BF)
        for copy in to_in:
            copy.wait_send()

        @pl.when(is_middle)
        def _():
            for copy in to_out + in_far + out_two + out_three:
                copy.wait_send()

        for shard_hops in hop:
            for copies in shard_hops:
                for copy in copies:
                    copy.wait_send()


def feed_forward(tok, att, left_att, w_out, gain, bias, pick, part_pick, cot, w_gate, w_up, w_down, n_ten):
    rows, width = tok.shape
    units = w_gate.shape[1]
    masked = cot.shape[0]
    unit = 256
    whole = lambda *shape: pl.BlockSpec(shape, lambda i: (0,) * len(shape))
    low = jax.ShapeDtypeStruct((masked, width), BF)
    return pl.pallas_call(
        functools.partial(feed_kernel, n_ten),
        grid=(n_ten * units // unit,),
        in_specs=[once(x.shape) for x in (tok, att, left_att, w_out)]
        + [once((1, width)), once((1, width)), once(pick.shape), once(part_pick.shape), once(cot.shape)]
        + [any_spec()] * 3,
        out_specs=[whole(rows, width)] + [whole(masked, width)] * 3 + [whole(2, width), whole(masked, width)] + [any_spec()] * 3,
        out_shape=[
            jax.ShapeDtypeStruct((rows, width), BF), low, low, low,
            jax.ShapeDtypeStruct((2, width), F32), low,
            jax.ShapeDtypeStruct((width, n_ten * units), BF),
            jax.ShapeDtypeStruct((width, n_ten * units), BF),
            jax.ShapeDtypeStruct((n_ten * units, width), BF),
        ],
        scratch_shapes=[
            pltpu.VMEM((rows + masked, width), BF),
            pltpu.VMEM((rows, width), F32),
            pltpu.VMEM((masked, width), F32),
            pltpu.VMEM((masked, LANES), F32),
            pltpu.VMEM((masked, width), F32),
            pltpu.VMEM((2, width, unit), BF),
            pltpu.VMEM((2, width, unit), BF),
            pltpu.VMEM((2, unit, width), BF),
            pltpu.SemaphoreType.DMA((2, 3)),
            pltpu.SemaphoreType.DMA((14, 4)),
            pltpu.SemaphoreType.DMA((13, 4)),
        ],
        compiler_params=pltpu.CompilerParams(collective_id=5, has_side_effects=True),
        cost_estimate=pl.CostEstimate(
            flops=8 * rows * width * n_ten * units, bytes_accessed=6 * width * n_ten * units, transcendentals=rows * n_ten * units
        ),
        name="feed_forward",
    )(tok, att, left_att, w_out, gain.reshape(1, width), bias.reshape(1, width), pick, part_pick, cot, w_gate, w_up, w_down)[:6]


def token_back_kernel(
    tok_ref, dq_ref, dk_ref, dv_ref, wq_ref, wk_ref, wv_ref, gain_ref, pick_ref, rows_ref, out_ref, vec_ref
):
    acc = dot_t(dq_ref[...], wq_ref[...]) + dot_t(dk_ref[...], wk_ref[...]) + dot_t(dv_ref[...], wv_ref[...])
    normed, inv_std = layer_stats(tok_ref[...].astype(F32))
    direct = t_dot(pick_ref[...], rows_ref[0])
    out_ref[...] = (direct + norm_back(acc, normed, inv_std, gain_ref[...])).astype(BF)
    sums = jnp.concatenate([jnp.sum(acc * normed, axis=0, keepdims=True), jnp.sum(acc, axis=0, keepdims=True)], axis=0)

    @pl.when(pl.program_id(0) == 0)
    def _():
        vec_ref[...] = sums

    @pl.when(pl.program_id(0) > 0)
    def _():
        vec_ref[...] += sums


def token_back(tok, grads, weights, gain, pick, rows_m):
    rows, width = tok.shape
    slots = pick.shape[0]
    tile = 256
    row = pl.BlockSpec((tile, width), lambda r: (r, 0))
    own = rows // tile - 1
    return pl.pallas_call(
        token_back_kernel,
        grid=(rows // tile,),
        in_specs=[row] * 4
        + [once((width, width))] * 3
        + [
            once((1, width)),
            pl.BlockSpec((slots, tile), lambda r: (0, r)),
            pl.BlockSpec((1, slots, width), lambda r: (r // own, 0, 0)),
        ],
        out_specs=[row, pl.BlockSpec((2, width), lambda r: (0, 0))],
        out_shape=[jax.ShapeDtypeStruct((rows, width), BF), jax.ShapeDtypeStruct((2, width), F32)],
        cost_estimate=pl.CostEstimate(flops=6 * rows * width * width, bytes_accessed=16 * rows * width, transcendentals=0),
        name="token_back",
    )(tok, *grads, *weights, gain.reshape(1, width), pick, rows_m)


def exchange_out_kernel(
    sizes, gq_ref, gk_ref, gv_ref, go_ref, grad_ref, vec_ref, w_ref, tok_ref, vec_out,
    buf1, sum1, buf2, sum2, buf3, sum3, buf4, vec_buf, vec_sum,
    tok_send, tok_recv, send1, recv1, send2, recv2, send3, recv3, send4, recv4, vec_send, vec_recv, local_sem,
):
    n_seq, n_ten, half, rows = sizes
    dp, sx, t = lax.axis_index("dp"), lax.axis_index("seq"), lax.axis_index("tensor")
    y, c = dp // 2, dp % 2
    me = sx * n_ten + t
    group = n_seq * n_ten
    others = []
    for i in range(1, group):
        g = (me + i) % group
        others.append((g // n_ten, g % n_ten))
    y_peer, c_peer, x_peer = {"dp": (dp + 2) % 4}, {"dp": 2 * y + 1 - c}, {"seq": 1 - sx}
    z_peers = [{"tensor": (t + j) % n_ten} for j in range(1, n_ten)]
    greet([{"seq": a, "tensor": b} for a, b in others] + [y_peer, c_peer])
    grads = (gq_ref, gk_ref, gv_ref, go_ref)
    count = len(grads)
    height = gq_ref.shape[0]
    hw = height // n_ten

    def columns(b_y, b_c, b_x):
        return pl.ds(pl.multiple_of((b_y * 4 + b_c * 2 + b_x) * LANES, LANES), LANES)

    def add_rows(out, first, second):
        def body(i, carry):
            at = pl.ds(pl.multiple_of(i * hw, hw), hw)
            out[at, :] = (first[at, :].astype(F32) + second[at, :].astype(F32)).astype(BF)
            return carry

        lax.fori_loop(0, height // hw, body, 0)

    stage1 = []
    for a in range(count):
        stage1.append(
            [
                remote(
                    grads[a].at[:, columns(b_y, 1 - c, b_x)], buf1.at[a, b_y, b_x],
                    send1.at[a, 2 * b_y + b_x], recv1.at[a, 2 * b_y + b_x], c_peer,
                )
                for b_y in range(2)
                for b_x in range(2)
            ]
        )
    for copies in stage1:
        start_all(copies)

    vec_hops = []
    hops = [c_peer, x_peer, y_peer]
    vec_sum[0] = vec_ref[...]
    for i, peer in enumerate(hops):
        vec_hops.append([remote(vec_sum.at[i], vec_buf.at[i], vec_send.at[i], vec_recv.at[i], peer)])
    vec_hops.append(
        [
            remote(vec_sum.at[3], vec_buf.at[3 + j], vec_send.at[3 + j], vec_recv.at[3 + j], peer)
            for j, peer in enumerate(z_peers)
        ]
    )
    start_all(vec_hops[0])

    tokens = []
    for i, (a, b) in enumerate(others):
        tokens.append(
            remote(
                grad_ref.at[pl.ds(pl.multiple_of((a * n_ten + b) * rows, rows), rows), :],
                tok_ref.at[sx * half + t],
                tok_send.at[i], tok_recv.at[i], {"seq": a, "tensor": b},
            )
        )
    tokens.append(
        remote(
            grad_ref.at[pl.ds(pl.multiple_of((group + 1 - sx) * rows, rows), rows), :],
            tok_ref.at[sx * half + n_ten],
            tok_send.at[group - 1], tok_recv.at[group - 1], x_peer,
        )
    )
    start_all(tokens)
    local = [
        pltpu.make_async_copy(
            grad_ref.at[pl.ds(pl.multiple_of(me * rows, rows), rows), :], tok_ref.at[sx * half + t], local_sem.at[0]
        ),
        pltpu.make_async_copy(
            grad_ref.at[pl.ds(pl.multiple_of((group + sx) * rows, rows), rows), :],
            tok_ref.at[sx * half + n_ten],
            local_sem.at[1],
        ),
    ]
    start_all(local)

    stage2 = []
    for a in range(count):
        for copy in stage1[a]:
            copy.wait_recv()
        for b_y in range(2):
            for b_x in range(2):
                add_rows(sum1.at[a, b_y, b_x], grads[a].at[:, columns(b_y, c, b_x)], buf1.at[a, b_y, b_x])
        copies = []
        for b in range(2):
            src, peer = (sum1.at[a, b, 1 - sx], x_peer) if a % 2 == 0 else (sum1.at[a, 1 - y, b], y_peer)
            copies.append(remote(src, buf2.at[a, b], send2.at[a, b], recv2.at[a, b], peer))
        start_all(copies)
        stage2.append(copies)
    vec_hops[0][0].wait_recv()
    vec_sum[1] = vec_sum[0] + vec_buf[0]
    start_all(vec_hops[1])
    stage3 = []
    for a in range(count):
        for copy in stage2[a]:
            copy.wait_recv()
        for b in range(2):
            own = sum1.at[a, b, sx] if a % 2 == 0 else sum1.at[a, y, b]
            add_rows(sum2.at[a, b], own, buf2.at[a, b])
        src, peer = (sum2.at[a, 1 - y], y_peer) if a % 2 == 0 else (sum2.at[a, 1 - sx], x_peer)
        copy = remote(src, buf3.at[a], send3.at[a], recv3.at[a], peer)
        copy.start()
        stage3.append(copy)
    vec_hops[1][0].wait_recv()
    vec_sum[2] = vec_sum[1] + vec_buf[1]
    start_all(vec_hops[2])
    stage4 = []
    for a in range(count):
        stage3[a].wait_recv()
        add_rows(sum3.at[a], sum2.at[a, y] if a % 2 == 0 else sum2.at[a, sx], buf3.at[a])
        copies = []
        for j, peer in enumerate(z_peers):
            to = (t + 1 + j) % n_ten
            src = sum3.at[a, pl.ds(pl.multiple_of(to * hw, hw), hw), :]
            copies.append(remote(src, buf4.at[a, j], send4.at[a, j], recv4.at[a, j], peer))
        start_all(copies)
        stage4.append(copies)
    vec_hops[2][0].wait_recv()
    vec_sum[3] = vec_sum[2] + vec_buf[2]
    start_all(vec_hops[3])
    for a in range(count):
        total = sum3[a, pl.ds(pl.multiple_of(t * hw, hw), hw), :].astype(F32)
        for j, copy in enumerate(stage4[a]):
            copy.wait_recv()
            total = total + buf4[a, j].astype(F32)
        w_ref[a] = total
    total = vec_sum[3]
    for j, copy in enumerate(vec_hops[3]):
        copy.wait_recv()
        total = total + vec_buf[3 + j]
    vec_out[...] = total
    for copies in stage1 + stage2 + stage4 + [stage3] + vec_hops:
        for copy in copies:
            copy.wait_send()
    wait_all(local)
    wait_all(tokens)


def exchange_out(grads, grad_tok, vectors, n_seq, n_ten, half, rows):
    height, width = grads[0].shape
    hw, count, group = height // n_ten, len(grads), n_seq * n_ten
    vmem = pl.BlockSpec(memory_space=pltpu.VMEM)
    dma = pltpu.SemaphoreType.DMA
    hops = 3 + n_ten - 1
    return pl.pallas_call(
        functools.partial(exchange_out_kernel, (n_seq, n_ten, half, rows)),
        in_specs=[vmem] * 6,
        out_specs=[vmem, any_spec(), vmem],
        out_shape=[
            jax.ShapeDtypeStruct((count, hw, LANES), F32),
            jax.ShapeDtypeStruct((n_seq * half, rows, width), BF),
            jax.ShapeDtypeStruct(vectors.shape, F32),
        ],
        scratch_shapes=[
            pltpu.VMEM((count, 2, 2, height, LANES), BF),
            pltpu.VMEM((count, 2, 2, height, LANES), BF),
            pltpu.VMEM((count, 2, height, LANES), BF),
            pltpu.VMEM((count, 2, height, LANES), BF),
            pltpu.VMEM((count, height, LANES), BF),
            pltpu.VMEM((count, height, LANES), BF),
            pltpu.VMEM((count, n_ten - 1, hw, LANES), BF),
            pltpu.VMEM((hops,) + vectors.shape, F32),
            pltpu.VMEM((4,) + vectors.shape, F32),
            dma((group,)), dma((group,)),
            dma((count, 4)), dma((count, 4)),
            dma((count, 2)), dma((count, 2)),
            dma((count,)), dma((count,)),
            dma((count, n_ten - 1)), dma((count, n_ten - 1)),
            dma((hops,)), dma((hops,)),
            dma((2,)),
        ],
        compiler_params=pltpu.CompilerParams(collective_id=4, has_side_effects=True),
        name="exchange_out",
    )(*grads, grad_tok, vectors)


def rotary_lanes(cosine, sine):
    reps = LANES // HEAD_DIM
    return jnp.concatenate([cosine, cosine] * reps, axis=1), jnp.concatenate([-sine, sine] * reps, axis=1)


def position_tables(length):
    half_dim = HEAD_DIM // 2
    inv_freq = np.float32(10000.0) ** (-np.arange(half_dim, dtype=np.float32) * np.float32(2.0 / HEAD_DIM))
    angles = (np.arange(length, dtype=np.float32)[:, None] * inv_freq[None, :]).astype(np.float64)
    cosine, sine = np.cos(angles).astype(np.float32), np.sin(angles).astype(np.float32)
    reps = LANES // HEAD_DIM
    return np.concatenate([cosine, cosine] * reps, axis=1), np.concatenate([-sine, sine] * reps, axis=1)


def window_shards(
    tokens,
    norm1_gain,
    norm1_bias,
    w_query,
    w_key,
    w_value,
    w_out,
    norm2_gain,
    norm2_bias,
    w_gate,
    w_up,
    w_down,
    out_grad,
    masked_rows,
    window_counts,
):
    rows_local, windows, width = tokens.shape
    n_dp, n_seq, n_ten = lax.axis_size("dp"), lax.axis_size("seq"), lax.axis_size("tensor")
    seq_index, ten_index = lax.axis_index("seq"), lax.axis_index("tensor")
    shard_index = lax.axis_index("dp") * n_seq + seq_index
    half = windows // n_seq
    length = rows_local * n_seq * n_ten
    share = length // n_ten
    hw = w_query.shape[1]
    slots = masked_rows.shape[1]
    part = slots // n_ten

    live = jnp.arange(windows) < window_counts[0]
    valid = (masked_rows < length) & live[:, None]
    count = jnp.full((8, LANES), jnp.sum(valid.astype(jnp.int32)))
    both_tok, all_q, all_k, all_v, all_out, counts = exchange_in(
        jnp.swapaxes(tokens, 0, 1), w_query, w_key, w_value, w_out, count, n_dp, n_seq, n_ten
    )
    loss_weight = LOSS_SCALE / jnp.sum(counts[:, 0, 0]).astype(F32)
    first_window = seq_index * half
    my_rows = lax.dynamic_slice_in_dim(masked_rows, first_window, half, 0)
    my_valid = lax.dynamic_slice_in_dim(valid, first_window, half, 0)
    cot = lax.dynamic_slice_in_dim(out_grad, first_window, half, 0).astype(F32) * loss_weight
    cot = jnp.where(my_valid[:, :, None], cot, 0.0)
    own_rows = lax.dynamic_index_in_dim(my_rows, ten_index, 0, keepdims=False)
    own_valid = lax.dynamic_index_in_dim(my_valid, ten_index, 0, keepdims=False)
    left_rows, left_valid = my_rows[n_ten], my_valid[n_ten]
    every = jnp.arange(length)
    left_every = jnp.swapaxes(every.reshape(n_seq, n_ten, rows_local), 0, 1).reshape(n_ten, share)
    my_left = lax.dynamic_index_in_dim(left_every, ten_index, 0, keepdims=False)
    left_every = left_every.reshape(length)
    own_pick = ((own_rows[:, None] == every[None, :]) & own_valid[:, None]).astype(BF)
    left_pick = ((left_rows[:, None] == left_every[None, :]) & left_valid[:, None]).astype(BF)
    part_match = (left_rows[:, None] == my_left[None, :]) & left_valid[:, None]
    part_pick = part_match.astype(BF)
    my_cot = jnp.concatenate(
        [
            lax.dynamic_index_in_dim(cot, ten_index, 0, keepdims=False),
            jnp.where(jnp.any(part_match, axis=1, keepdims=True), cot[n_ten], 0.0),
        ],
        axis=0,
    )

    tables = [jnp.asarray(x) for x in position_tables(length)]
    by_block = [x.reshape(n_seq, n_ten, rows_local, LANES) for x in tables]
    part_tables = [lax.dynamic_index_in_dim(x, ten_index, 1, keepdims=False).reshape(share, LANES) for x in by_block]
    left_tables = [jnp.swapaxes(x, 0, 1).reshape(length, LANES) for x in by_block]
    own_tables = tables + list(rotary_lanes(*rotary_tables(own_rows)))
    left_tables = left_tables + list(rotary_lanes(*rotary_tables(left_rows)))

    first, q, k, v = norm_qkv(both_tok, norm1_gain, norm1_bias, all_q, all_k, all_v, tables, part_tables)
    own_att, left_q, left_k, left_v = attend_swap(q, k, v, length, n_ten)
    left_att_part = attend_left(left_q, left_k, left_v, n_ten)
    out_both, att_m, gr2, gatt, grad_norm2, second_m = feed_forward(
        both_tok, own_att, left_att_part, all_out, norm2_gain, norm2_bias, own_pick, part_pick, my_cot,
        w_gate, w_up, w_down, n_ten,
    )
    sent = lax.all_gather(second_m, "tensor", axis=0, tiled=False)

    second = jnp.concatenate(
        [sent[:, :slots].reshape(n_ten * slots, width), jnp.sum(sent[:, slots:].astype(F32), axis=0).astype(BF)], axis=0
    )
    gate = dot_n(second, w_gate)
    up = dot_n(second, w_up)
    down_in = cot.astype(BF).reshape(half * slots, width)
    grad_hidden = dot_t(down_in, w_down)
    sig = jax.nn.sigmoid(gate)
    silu = gate * sig
    hidden_m = (silu * up).astype(BF)
    grad_gate = (grad_hidden * up * sig * (1.0 + gate * (1.0 - sig))).astype(BF)
    grad_up = (grad_hidden * silu).astype(BF)
    grad_w_ffn = [
        t_dot(second, grad_gate).astype(BF), t_dot(second, grad_up).astype(BF), t_dot(down_in, hidden_m).astype(BF)
    ]

    grad_w_out = t_dot(att_m, gr2).astype(BF)
    left_back = back_left(left_q, gatt[slots:], left_k, left_v, left_pick, left_tables, n_ten)
    dq, dk, dv = back_swap(q, gatt[:slots], k, v, own_pick, own_tables, left_back, n_ten)
    grad_w_attn = [t_dot(d, first).astype(BF) for d in (dq, dk, dv)] + [grad_w_out]
    grad_both, grad_norm1 = token_back(
        both_tok, (dq, dk, dv), (all_q, all_k, all_v), norm1_gain,
        jnp.concatenate([own_pick, part_pick], axis=1), gr2.reshape(2, slots, width),
    )

    def send_back(x):
        own = lax.all_to_all(
            x[:length].reshape(n_seq * n_ten, rows_local, width), ("seq", "tensor"), 0, 0, tiled=True
        ).reshape(n_seq, n_ten, rows_local, width)
        left = lax.all_to_all(x[length:].reshape(n_seq, rows_local, width), "seq", 0, 0, tiled=True)
        both = jnp.concatenate([own, left[:, None]], axis=1).reshape(windows, rows_local, width)
        return jnp.swapaxes(both, 0, 1)

    output = send_back(out_both)
    vectors = jnp.concatenate(
        [grad_norm1, grad_norm2, jnp.zeros((4, width), F32)], axis=0
    )
    gw_attn, grad_tokens, vectors = exchange_out(grad_w_attn, grad_both, vectors, n_seq, n_ten, half, rows_local)
    grad_tokens = jnp.swapaxes(grad_tokens, 0, 1).astype(F32)
    small = width // (n_dp * n_seq * n_ten)
    vectors = lax.dynamic_slice_in_dim(vectors, (shard_index * n_ten + ten_index) * small, small, 1)

    gw_gate, gw_up, gw_down = [
        lax.psum_scatter(x, ("dp", "seq"), scatter_dimension=0, tiled=True).astype(F32) for x in grad_w_ffn
    ]
    return (
        output,
        grad_tokens,
        vectors[0],
        vectors[1],
        gw_attn[0].T,
        gw_attn[1].T,
        gw_attn[2].T,
        gw_attn[3],
        vectors[2],
        vectors[3],
        gw_gate,
        gw_up,
        gw_down.T,
    )


def shards(tokens, *rest):
    n_dp, n_seq, n_ten = lax.axis_size("dp"), lax.axis_size("seq"), lax.axis_size("tensor")
    whole = n_dp == 4 and n_seq == 2 and tokens.shape[1] == n_seq * (n_ten + 1)
    return (window_shards if whole else block_shards)(tokens, *rest)


def solution(mesh):
    return jax.shard_map(
        shards,
        mesh=mesh,
        in_specs=(
            P(("seq", "tensor"), "dp", None),
            P(),
            P(),
            P(None, "tensor"),
            P(None, "tensor"),
            P(None, "tensor"),
            P("tensor", None),
            P(),
            P(),
            P(None, "tensor"),
            P(None, "tensor"),
            P("tensor", None),
            P("dp", None, None),
            P("dp", None),
            P("dp"),
        ),
        out_specs=(
            P(("seq", "tensor"), "dp", None),
            P(("seq", "tensor"), "dp", None),
            P(("dp", "seq", "tensor")),
            P(("dp", "seq", "tensor")),
            P(("dp", "seq"), "tensor"),
            P(("dp", "seq"), "tensor"),
            P(("dp", "seq"), "tensor"),
            P("tensor", ("dp", "seq")),
            P(("dp", "seq", "tensor")),
            P(("dp", "seq", "tensor")),
            P(("dp", "seq"), "tensor"),
            P(("dp", "seq"), "tensor"),
            P("tensor", ("dp", "seq")),
        ),
        check_vma=False,
    )
```

```python
import math

import functools

import jax
import jax.numpy as jnp
import numpy as np
from jax import lax
from jax.experimental import pallas as pl
from jax.experimental.pallas import tpu as pltpu
from jax.sharding import PartitionSpec as P

HEAD_DIM = 64
L = 1024
LOSS_SCALE = 1024


epsilon = 1e-05


def layer_stats(inputs):
    row_mean = jnp.mean(inputs, axis=-1, keepdims=True)
    centred = inputs - row_mean
    inv_std = lax.rsqrt(jnp.mean(centred * centred, axis=-1, keepdims=True) + epsilon)
    return (centred * inv_std, inv_std)


def norm_back(grad_norm, normed, inv_std, gain_vec):
    scaled = grad_norm * gain_vec
    return inv_std * (
        scaled
        - jnp.mean(scaled, axis=-1, keepdims=True)
        - normed * jnp.mean(scaled * normed, axis=-1, keepdims=True)
    )


def rotary_tables(positions):
    half_dim = HEAD_DIM // 2
    inv_freq = 10000.0 ** (-jnp.arange(half_dim, dtype=jnp.float32) * 2.0 / HEAD_DIM)
    angles = positions.astype(jnp.float32)[:, None] * inv_freq[None, :]
    return (jnp.cos(angles), jnp.sin(angles))


def rotate(values, cosine, sine):
    half_dim = values.shape[-1] // 2
    first_half = values[..., :half_dim]
    second_half = values[..., half_dim:]
    cos_b = cosine[:, None, None, :]
    sin_b = sine[:, None, None, :]
    return jnp.concatenate(
        [first_half * cos_b - second_half * sin_b, second_half * cos_b + first_half * sin_b],
        axis=-1,
    )


def unrotate(grads, cosine, sine):
    half_dim = grads.shape[-1] // 2
    first_half = grads[..., :half_dim]
    second_half = grads[..., half_dim:]
    cos_b = cosine[:, None, None, :]
    sin_b = sine[:, None, None, :]
    return jnp.concatenate(
        [first_half * cos_b + second_half * sin_b, second_half * cos_b - first_half * sin_b],
        axis=-1,
    )


def block_shards(
    tokens,
    norm1_gain,
    norm1_bias,
    w_query,
    w_key,
    w_value,
    w_out,
    norm2_gain,
    norm2_bias,
    w_gate,
    w_up,
    w_down,
    out_grad,
    masked_rows,
    window_counts,
):
    rows_local, windows, model_width = tokens.shape
    span_rows = rows_local * lax.axis_size("tensor")
    seq_index = lax.axis_index("seq")
    tensor_index = lax.axis_index("tensor")
    head_width = w_query.shape[1]
    heads_local = head_width // HEAD_DIM
    score_scale = 1.0 / math.sqrt(HEAD_DIM)
    head_shape = (span_rows, windows, heads_local, HEAD_DIM)
    residual = tokens.astype(jnp.float32)
    normed1, inv_std1 = layer_stats(residual)
    first_low = (normed1 * norm1_gain + norm1_bias).astype(jnp.bfloat16)
    first_full = lax.all_gather(first_low, "tensor", axis=0, tiled=True)
    w_joined = jnp.concatenate([w_query, w_key, w_value], axis=1)
    projected = jnp.einsum("rwd,de->rwe", first_full, w_joined, preferred_element_type=jnp.float32)
    positions = seq_index * span_rows + jnp.arange(span_rows)
    cosine, sine = rotary_tables(positions)
    queries = rotate(projected[..., :head_width].reshape(head_shape), cosine, sine).astype(
        jnp.bfloat16
    )
    keys_rot = (
        rotate(projected[..., head_width : 2 * head_width].reshape(head_shape), cosine, sine)
        .astype(jnp.bfloat16)
        .reshape(span_rows, windows, head_width)
    )
    values_own = projected[..., 2 * head_width :].astype(jnp.bfloat16)
    keys_all, values_all = (
        lax.all_gather(keys_rot, "seq", axis=0, tiled=True),
        lax.all_gather(values_own, "seq", axis=0, tiled=True),
    )
    key_heads = keys_all.reshape(-1, windows, heads_local, HEAD_DIM)
    value_heads = values_all.reshape(-1, windows, heads_local, HEAD_DIM)
    scores = (
        jnp.einsum("qwhd,kwhd->whqk", queries, key_heads, preferred_element_type=jnp.float32)
        * score_scale
    )
    row_max = jnp.max(scores, axis=-1, keepdims=True)
    row_sum = jnp.sum(jnp.exp(scores - row_max), axis=-1, keepdims=True)
    log_norm = row_max + jnp.log(row_sum)
    attn_prob = jnp.exp(scores - log_norm)
    prob_low = attn_prob.astype(jnp.bfloat16)
    attended = (
        jnp.einsum("whqk,kwhd->qwhd", prob_low, value_heads, preferred_element_type=jnp.float32)
        .reshape(span_rows, windows, head_width)
        .astype(jnp.bfloat16)
    )
    block_part = attended
    attn_branch = lax.psum_scatter(
        jnp.einsum("rwe,ed->rwd", block_part, w_out, preferred_element_type=jnp.float32).astype(
            jnp.bfloat16
        ),
        "tensor",
        scatter_dimension=0,
        tiled=True,
    ).astype(jnp.float32)
    residual2 = residual + attn_branch
    normed2, inv_std2 = layer_stats(residual2)
    second_low = (normed2 * norm2_gain + norm2_bias).astype(jnp.bfloat16)
    second_full = lax.all_gather(second_low, "tensor", axis=0, tiled=True)
    gate_proj = jnp.einsum("rwd,df->rwf", second_full, w_gate, preferred_element_type=jnp.float32)
    up_proj = jnp.einsum("rwd,df->rwf", second_full, w_up, preferred_element_type=jnp.float32)
    hidden = (jax.nn.silu(gate_proj) * up_proj).astype(jnp.bfloat16)
    block_part = hidden
    ffn_branch = lax.psum_scatter(
        jnp.einsum("rwf,fd->rwd", block_part, w_down, preferred_element_type=jnp.float32).astype(
            jnp.bfloat16
        ),
        "tensor",
        scatter_dimension=0,
        tiled=True,
    ).astype(jnp.float32)
    output = (residual2 + ffn_branch).astype(jnp.bfloat16)
    live_slot = jnp.arange(windows) < window_counts[0]
    valid_slot = (masked_rows < L) & live_slot[:, None]
    local_masked = jnp.sum(jnp.where(valid_slot, 1, 0)).astype(jnp.int32)
    total_masked = lax.psum(local_masked, "dp")
    loss_weight = LOSS_SCALE / total_masked.astype(jnp.float32)
    own_positions = seq_index * span_rows + tensor_index * rows_local + jnp.arange(rows_local)
    matches = (masked_rows[:, None, :] == own_positions[None, :, None]) & live_slot[:, None, None]
    picked = jnp.einsum(
        "wrm,wmd->rwd", matches.astype(jnp.bfloat16), out_grad, preferred_element_type=jnp.float32
    )
    grad_out = picked * loss_weight
    grad_down_in = lax.all_gather(grad_out.astype(jnp.bfloat16), "tensor", axis=0, tiled=True)
    grad_w_down = jnp.einsum(
        "rwf,rwd->fd", hidden, grad_down_in, preferred_element_type=jnp.float32
    )
    grad_hidden = jnp.einsum(
        "rwd,fd->rwf", grad_down_in, w_down, preferred_element_type=jnp.float32
    )
    sigmoid_gate = jax.nn.sigmoid(gate_proj)
    silu_gate = gate_proj * sigmoid_gate
    grad_gate = (
        grad_hidden * up_proj * sigmoid_gate * (1.0 + gate_proj * (1.0 - sigmoid_gate))
    ).astype(jnp.bfloat16)
    grad_up = (grad_hidden * silu_gate).astype(jnp.bfloat16)
    grad_w_gate = jnp.einsum(
        "rwd,rwf->df", second_full, grad_gate, preferred_element_type=jnp.float32
    )
    grad_w_up = jnp.einsum("rwd,rwf->df", second_full, grad_up, preferred_element_type=jnp.float32)
    grad_second = lax.psum_scatter(
        (
            jnp.einsum("rwf,df->rwd", grad_gate, w_gate, preferred_element_type=jnp.float32)
            + jnp.einsum("rwf,df->rwd", grad_up, w_up, preferred_element_type=jnp.float32)
        ).astype(jnp.bfloat16),
        "tensor",
        scatter_dimension=0,
        tiled=True,
    ).astype(jnp.float32)
    grad_norm2_gain = jnp.sum(grad_second * normed2, axis=(0, 1))
    grad_norm2_bias = jnp.sum(grad_second, axis=(0, 1))
    grad_residual2 = grad_out + norm_back(grad_second, normed2, inv_std2, norm2_gain)
    grad_attn_in = lax.all_gather(grad_residual2.astype(jnp.bfloat16), "tensor", axis=0, tiled=True)
    grad_w_out = jnp.einsum(
        "rwe,rwd->ed", attended, grad_attn_in, preferred_element_type=jnp.float32
    )
    grad_attended = jnp.einsum(
        "rwd,ed->rwe", grad_attn_in, w_out, preferred_element_type=jnp.float32
    ).astype(jnp.bfloat16)
    grad_att_heads = grad_attended.reshape(head_shape)
    scores_again = (
        jnp.einsum("qwhd,kwhd->whqk", queries, key_heads, preferred_element_type=jnp.float32)
        * score_scale
    )
    probs_again = jnp.exp(scores_again - log_norm)
    grad_probs = jnp.einsum(
        "qwhd,kwhd->whqk", grad_att_heads, value_heads, preferred_element_type=jnp.float32
    )
    row_delta = jnp.sum(probs_again * grad_probs, axis=-1, keepdims=True)
    grad_scores = (probs_again * (grad_probs - row_delta)).astype(jnp.bfloat16)
    grad_queries = (
        jnp.einsum("whqk,kwhd->qwhd", grad_scores, key_heads, preferred_element_type=jnp.float32)
        * score_scale
    )
    grad_key_all = (
        jnp.einsum("whqk,qwhd->kwhd", grad_scores, queries, preferred_element_type=jnp.float32)
        * score_scale
    ).reshape(-1, windows, head_width)
    grad_value_all = jnp.einsum(
        "whqk,qwhd->kwhd",
        probs_again.astype(jnp.bfloat16),
        grad_att_heads,
        preferred_element_type=jnp.float32,
    ).reshape(-1, windows, head_width)
    grad_keys, grad_values = (
        lax.psum_scatter(
            grad_key_all.astype(jnp.bfloat16), "seq", scatter_dimension=0, tiled=True
        ).astype(jnp.float32),
        lax.psum_scatter(
            grad_value_all.astype(jnp.bfloat16), "seq", scatter_dimension=0, tiled=True
        ).astype(jnp.float32),
    )
    grad_query_lin = (
        unrotate(grad_queries, cosine, sine)
        .reshape(span_rows, windows, head_width)
        .astype(jnp.bfloat16)
    )
    grad_key_lin = (
        unrotate(grad_keys.reshape(head_shape), cosine, sine)
        .reshape(span_rows, windows, head_width)
        .astype(jnp.bfloat16)
    )
    grad_value_lin = grad_values.astype(jnp.bfloat16)
    grad_joined = jnp.concatenate([grad_query_lin, grad_key_lin, grad_value_lin], axis=-1)
    grad_w_joined = jnp.einsum(
        "rwd,rwe->de", first_full, grad_joined, preferred_element_type=jnp.float32
    )
    grad_w_query = grad_w_joined[:, :head_width]
    grad_w_key = grad_w_joined[:, head_width : 2 * head_width]
    grad_w_value = grad_w_joined[:, 2 * head_width :]
    block_part = grad_joined
    grad_first = lax.psum_scatter(
        jnp.einsum("rwe,de->rwd", block_part, w_joined, preferred_element_type=jnp.float32).astype(
            jnp.bfloat16
        ),
        "tensor",
        scatter_dimension=0,
        tiled=True,
    ).astype(jnp.float32)
    grad_norm1_gain = jnp.sum(grad_first * normed1, axis=(0, 1))
    grad_norm1_bias = jnp.sum(grad_first, axis=(0, 1))
    grad_tokens = grad_residual2 + norm_back(grad_first, normed1, inv_std1, norm1_gain)
    summed = (
        lax.psum_scatter(
            grad_w_query.astype(jnp.bfloat16), ("dp", "seq"), scatter_dimension=0, tiled=True
        ).astype(jnp.float32),
        lax.psum_scatter(
            grad_w_key.astype(jnp.bfloat16), ("dp", "seq"), scatter_dimension=0, tiled=True
        ).astype(jnp.float32),
        lax.psum_scatter(
            grad_w_value.astype(jnp.bfloat16), ("dp", "seq"), scatter_dimension=0, tiled=True
        ).astype(jnp.float32),
        lax.psum_scatter(
            grad_w_out.astype(jnp.bfloat16), ("dp", "seq"), scatter_dimension=1, tiled=True
        ).astype(jnp.float32),
        lax.psum_scatter(
            grad_w_gate.astype(jnp.bfloat16), ("dp", "seq"), scatter_dimension=0, tiled=True
        ).astype(jnp.float32),
        lax.psum_scatter(
            grad_w_up.astype(jnp.bfloat16), ("dp", "seq"), scatter_dimension=0, tiled=True
        ).astype(jnp.float32),
        lax.psum_scatter(
            grad_w_down.astype(jnp.bfloat16), ("dp", "seq"), scatter_dimension=1, tiled=True
        ).astype(jnp.float32),
    )
    norm_sums = (
        lax.psum_scatter(grad_norm1_gain, ("dp", "seq", "tensor"), scatter_dimension=0, tiled=True),
        lax.psum_scatter(grad_norm1_bias, ("dp", "seq", "tensor"), scatter_dimension=0, tiled=True),
        lax.psum_scatter(grad_norm2_gain, ("dp", "seq", "tensor"), scatter_dimension=0, tiled=True),
        lax.psum_scatter(grad_norm2_bias, ("dp", "seq", "tensor"), scatter_dimension=0, tiled=True),
    )
    return (
        output,
        grad_tokens,
        norm_sums[0],
        norm_sums[1],
        summed[0],
        summed[1],
        summed[2],
        summed[3],
        norm_sums[2],
        norm_sums[3],
        summed[4],
        summed[5],
        summed[6],
    )


BF = jnp.bfloat16
F32 = jnp.float32
LANES = 128
QUAD = 4


def dot_t(a, b):
    return lax.dot_general(a, b, (((1,), (1,)), ((), ())), preferred_element_type=F32)


def dot_n(a, b):
    return lax.dot_general(a, b, (((1,), (0,)), ((), ())), preferred_element_type=F32)


def t_dot(a, b):
    return lax.dot_general(a, b, (((0,), (0,)), ((), ())), preferred_element_type=F32)


def swap_halves(x):
    half = HEAD_DIM // 2
    lane = lax.broadcasted_iota(jnp.int32, x.shape, 1)
    down = pltpu.roll(x, half, 1)
    up = pltpu.roll(x, LANES - half, 1)
    return jnp.where(lane % HEAD_DIM < half, up, down)


def head_mask(h):
    lane = lax.broadcasted_iota(jnp.int32, (1, LANES), 1)
    return jnp.where(lane // HEAD_DIM == h, 1.0, 0.0).astype(BF)


MESH = pl.DeviceIdType.MESH


def any_spec():
    return pl.BlockSpec(memory_space=pl.ANY)


def greet(peers):
    barrier = pltpu.get_barrier_semaphore()
    for peer in peers:
        pl.semaphore_signal(barrier, inc=1, device_id=peer, device_id_type=MESH)
    pl.semaphore_wait(barrier, len(peers))


def remote(src, dst, send, recv, peer):
    return pltpu.make_async_remote_copy(
        src_ref=src, dst_ref=dst, send_sem=send, recv_sem=recv, device_id=peer, device_id_type=MESH
    )


def start_all(copies):
    for copy in copies:
        copy.start()


def wait_all(copies):
    for copy in copies:
        copy.wait()


def quad_place():
    dp, sx = lax.axis_index("dp"), lax.axis_index("seq")
    place = sx * 2 + dp % 2
    return place, lambda to: {"dp": dp // 2 * 2 + to % 2, "seq": to // 2}


def quad_peers():
    place, device = quad_place()
    return [device((place + j) % QUAD) for j in range(1, QUAD)]


class WeightRoute:
    def __init__(self, gathered, own, n_ten, send, recv):
        dp, sx, t = lax.axis_index("dp"), lax.axis_index("seq"), lax.axis_index("tensor")
        y, c = dp // 2, dp % 2
        gate_ref, up_ref, down_ref = gathered
        self.refs, self.own = (gate_ref, up_ref, down_ref), own
        self.width, self.units = gate_ref.shape[0], gate_ref.shape[1] // n_ten
        self.send, self.recv, self.c = send, recv, c
        s_xy, s_yx = c * 4 + y * 2 + sx, c * 4 + sx * 2 + y
        self.slices = (s_xy, s_yx, s_xy)
        self.x_peer, self.y_peer, self.c_peer = {"seq": 1 - sx}, {"dp": (dp + 2) % 4}, {"dp": 2 * y + 1 - c}
        side = t // 2
        middle = jnp.minimum(t, n_ten - 1 - t)
        mirror = lambda k: k + side * (n_ten - 1 - 2 * k)
        self.order = [mirror(k) for k in (middle, 1 - middle, 2, 3)]
        self.inward, self.outward = mirror(middle + 1), mirror(0)
        self.is_middle, self.is_end = middle == 1, middle == 0
        self.t, self.middle, self.mirror = t, middle, mirror

    def shard(self, ref, k, first, count, which):
        size, units = self.width // 8, self.units
        rows = pl.multiple_of(first * (size if k < 2 else units // 8), 16)
        if k < 2:
            at = 0 if which is None else pl.multiple_of(which * units, units)
            return ref.at[pl.ds(rows, count * size), pl.ds(at, units)]
        at = rows if which is None else pl.multiple_of(which * units + rows, 16)
        return ref.at[pl.ds(at, count * (units // 8)), :]

    def along(self, which, to, slot, number, own=False):
        copies = []
        for k in range(3):
            dst = self.shard(self.refs[k], k, self.slices[k], 1, which)
            src = self.shard(self.own[k], k, self.slices[k], 1, None) if own else dst
            copies.append(remote(src, dst, self.send.at[number, k], self.recv.at[slot, k], {"tensor": to}))
        return copies

    def to_in(self):
        return self.along(self.t, self.inward, 1 + self.middle, 0, True)

    def to_out(self):
        return self.along(self.t, self.outward, 1, 1, True)

    def in_far(self):
        return self.along(self.mirror(0), self.inward, 3, 2)

    def out_two(self):
        return self.along(self.mirror(2), self.outward, 2, 3)

    def out_three(self):
        return self.along(self.mirror(3), self.outward, 3, 4)

    def arrived(self, i):
        received(self.along(self.order[i], self.inward, i, 0))

    def hop(self, i, h):
        copies = []
        for k in range(3):
            xy = k != 1
            peer, first, count = (
                (self.x_peer if xy else self.y_peer, self.slices[k], 1),
                (self.y_peer if xy else self.x_peer, self.slices[k] // 2 * 2, 2),
                (self.c_peer, self.c * 4, 4),
            )[h]
            ref = self.shard(self.refs[k], k, first, count, self.order[i])
            copies.append(remote(ref, ref, self.send.at[2 + 3 * i + h, k], self.recv.at[1 + 3 * i + h, k], peer))
        return copies


def received(copies):
    for copy in copies:
        copy.wait_recv()


def sent_all(copies):
    for copy in copies:
        copy.wait_send()


def route_sems():
    return [pltpu.SemaphoreType.DMA((14, 3)), pltpu.SemaphoreType.DMA((13, 3))]


def exchange_in_kernel(
    sizes, tok_ref, wq_ref, wk_ref, wv_ref, wo_ref, count_ref, rows_ref, x_ref, q_ref, k_ref, v_ref, o_ref, counts_ref,
    peer_rows_ref, tok_send, tok_recv, w_send, w_recv, count_send, count_recv, rows_send, rows_recv, local_sem,
):
    n_seq, n_ten, half, rows, slices = sizes
    dp, sx, t = lax.axis_index("dp"), lax.axis_index("seq"), lax.axis_index("tensor")
    y, c = dp // 2, dp % 2
    me = sx * n_ten + t
    group = n_seq * n_ten
    others = []
    for i in range(1, group):
        g = (me + i) % group
        others.append((g // n_ten, g % n_ten))
    y_peer, c_peer, x_peer = {"dp": (dp + 2) % 4}, {"dp": 2 * y + 1 - c}, {"seq": 1 - sx}
    dp_peers = [{"dp": (dp + i) % 4} for i in range(1, 4)]
    beside = [{"dp": 2 * y + 1 - c, "tensor": (t + j) % n_ten} for j in range(1, n_ten)]
    greet([{"seq": a, "tensor": b} for a, b in others] + dp_peers + beside)
    counts = [
        remote(count_ref, counts_ref.at[dp], count_send.at[i], count_recv.at[i], peer) for i, peer in enumerate(dp_peers)
    ]
    start_all(counts)

    hw = wq_ref.shape[1]
    srow, orow = wq_ref.shape[0] // slices, hw // slices
    s_xy, s_yx = c * 4 + y * 2 + sx, c * 4 + sx * 2 + y
    weights = ((wq_ref, q_ref, s_xy, 0), (wk_ref, k_ref, s_xy, 0), (wv_ref, v_ref, s_yx, 0), (wo_ref, o_ref, s_yx, 1))

    def block(out, by_rows, base, count, which):
        if by_rows:
            return out.at[pl.ds(pl.multiple_of(which * hw + base * orow, orow), count * orow), :]
        return out.at[
            pl.ds(pl.multiple_of(base * srow, srow), count * srow), pl.ds(pl.multiple_of(which * hw, hw), hw)
        ]

    stage = [[], [], [], []]
    n = 0
    for j in range(1, n_ten):
        peer = {"tensor": (t + j) % n_ten}
        for w_ref, out, s, by_rows in weights:
            size = orow if by_rows else srow
            src = w_ref.at[pl.ds(pl.multiple_of(s * size, size), size), :]
            stage[0].append(remote(src, block(out, by_rows, s, 1, t), w_send.at[0, n], w_recv.at[0, n], peer))
            n += 1
    n = 0
    for j in range(1, n_ten):
        which = (t + j) % n_ten
        for w_ref, out, s, by_rows in weights:
            xy = s is s_xy
            hops = (
                (1, x_peer if xy else y_peer, s, 1),
                (2, y_peer if xy else x_peer, s // 2 * 2, 2),
                (3, c_peer, c * 4, 4),
            )
            for k, peer, base, count in hops:
                ref = block(out, by_rows, base, count, which)
                stage[k].append(remote(ref, ref, w_send.at[k, n], w_recv.at[k, n], peer))
            n += 1
    start_all(stage[0])

    tokens = []
    for i, (a, b) in enumerate(others):
        tokens.append(
            remote(
                tok_ref.at[a * half + b],
                x_ref.at[pl.ds(pl.multiple_of(me * rows, rows), rows), :],
                tok_send.at[i], tok_recv.at[i], {"seq": a, "tensor": b},
            )
        )
    shared = []
    for i in range(n_seq):
        src, dst = tok_ref.at[i * half + n_ten], x_ref.at[pl.ds(pl.multiple_of((group + t % 2) * rows, rows), rows), :]
        shared.append(
            (
                2 * c + i == t,
                remote(
                    src, dst, tok_send.at[group - 1 + i], tok_recv.at[group - 1 + t % 2],
                    {"dp": 2 * y + t // 2, "tensor": 2 * c + i},
                ),
                pltpu.make_async_copy(src, dst, local_sem.at[1]),
            )
        )
    arriving = [
        remote(
            tok_ref.at[n_ten], x_ref.at[pl.ds((group + i) * rows, rows), :],
            tok_send.at[group - 1], tok_recv.at[group - 1 + i], c_peer,
        )
        for i in range(n_seq)
    ]
    start_all(tokens)
    for here, away, near in shared:
        pl.when(here)(near.start)
        pl.when(jnp.logical_not(here))(away.start)
    peer_rows = [
        remote(rows_ref.at[i * half + n_ten], peer_rows_ref.at[i], rows_send.at[i], rows_recv.at[i], c_peer)
        for i in range(n_seq)
    ]
    start_all(peer_rows)
    local = [
        pltpu.make_async_copy(
            tok_ref.at[sx * half + t], x_ref.at[pl.ds(pl.multiple_of(me * rows, rows), rows), :], local_sem.at[0]
        ),
    ]
    for i, (w_ref, out, s, by_rows) in enumerate(weights):
        local.append(pltpu.make_async_copy(w_ref, block(out, by_rows, 0, slices, t), local_sem.at[2 + i]))
    local.append(pltpu.make_async_copy(count_ref, counts_ref.at[dp], local_sem.at[6]))
    start_all(local)
    for k in range(1, 4):
        for earlier in stage[k - 1]:
            earlier.wait_recv()
        start_all(stage[k])
    for copy in stage[3]:
        copy.wait_recv()
    for copies in stage:
        for copy in copies:
            copy.wait_send()
    wait_all(local)
    wait_all(counts)
    wait_all(peer_rows)
    wait_all(tokens)
    for here, away, near in shared:
        pl.when(here)(near.wait)
        pl.when(jnp.logical_not(here))(away.wait_send)
    for i in range(n_seq):
        pl.when(jnp.logical_not((t // 2 == c) & (t % 2 == i)))(arriving[i].wait_recv)


def exchange_in(tok, w_query, w_key, w_value, w_out, count, out_grad, n_dp, n_seq, n_ten):
    windows, rows, width = tok.shape
    slices = n_dp * n_seq
    vmem = pl.BlockSpec(memory_space=pltpu.VMEM)
    square = jax.ShapeDtypeStruct((width, width), BF)
    group = n_seq * n_ten
    return pl.pallas_call(
        functools.partial(exchange_in_kernel, (n_seq, n_ten, windows // n_seq, rows, slices)),
        in_specs=[vmem] * 6 + [any_spec()],
        out_specs=[any_spec()] * 7,
        out_shape=[jax.ShapeDtypeStruct(((group + n_seq) * rows, width), BF)]
        + [square] * 4
        + [jax.ShapeDtypeStruct((n_dp,) + count.shape, count.dtype)]
        + [jax.ShapeDtypeStruct((n_seq,) + out_grad.shape[1:], BF)],
        scratch_shapes=[
            pltpu.SemaphoreType.DMA((group + 1,)),
            pltpu.SemaphoreType.DMA((group + 1,)),
            pltpu.SemaphoreType.DMA((4, 4 * (n_ten - 1))),
            pltpu.SemaphoreType.DMA((4, 4 * (n_ten - 1))),
            pltpu.SemaphoreType.DMA((3,)),
            pltpu.SemaphoreType.DMA((3,)),
            pltpu.SemaphoreType.DMA((2,)),
            pltpu.SemaphoreType.DMA((2,)),
            pltpu.SemaphoreType.DMA((7,)),
        ],
        compiler_params=pltpu.CompilerParams(collective_id=0, has_side_effects=True),
        name="exchange_in",
    )(tok, w_query, w_key, w_value, w_out, count, out_grad)


def qkv_kernel(
    n_ten, x_ref, gain_ref, bias_ref, wq_ref, wk_ref, wv_ref, cos_ref, sin_ref, part_cos_ref, part_sin_ref,
    wg_ref, wu_ref, wd_ref, first_ref, q_ref, k_ref, v_ref, ag_ref, au_ref, ad_ref, send, recv,
):
    route = WeightRoute((ag_ref, au_ref, ad_ref), (wg_ref, wu_ref, wd_ref), n_ten, send, recv)

    @pl.when(pl.program_id(0) == 0)
    def _():
        greet([{"tensor": (route.t + j) % n_ten} for j in range(1, n_ten)])
        start_all(route.to_in())

        @pl.when(route.is_middle)
        def _():
            start_all(route.to_out())

    shared = pl.program_id(0) == pl.num_programs(0) - 1
    normed, _ = layer_stats(x_ref[...].astype(F32))
    first_ref[...] = (normed * gain_ref[...] + bias_ref[...]).astype(BF)
    cos = jnp.where(shared, part_cos_ref[...], cos_ref[...])
    sin = jnp.where(shared, part_sin_ref[...], sin_ref[...])
    wide = 256
    for w_ref, out_ref, scale in ((wq_ref, q_ref, 1.0 / math.sqrt(HEAD_DIM)), (wk_ref, k_ref, 1.0), (wv_ref, v_ref, None)):
        for at in range(0, w_ref.shape[1], wide):
            acc = dot_n(first_ref[...], w_ref[:, at : at + wide])
            for c in range(0, wide, LANES):
                part = acc[:, c : c + LANES]
                if scale is not None:
                    part = (part * cos + swap_halves(part) * sin) * scale
                out_ref[:, at + c : at + c + LANES] = part.astype(BF)

    @pl.when(shared)
    def _():
        route.arrived(1)
        sent_all(route.to_in())

        @pl.when(route.is_middle)
        def _():
            route.arrived(2)
            sent_all(route.to_out())


def once(shape):
    return pl.BlockSpec(shape, lambda *_: (0,) * len(shape), pipeline_mode=pl.Buffered(1))


def norm_qkv(x, gain, bias, w_query, w_key, w_value, tables, part_tables, ffn, n_ten):
    rows, width = x.shape
    tile = 256
    row = pl.BlockSpec((tile, width), lambda r: (r, 0))
    own = tables[0].shape[0] // tile
    table = pl.BlockSpec((tile, LANES), lambda r: (jnp.minimum(r, own - 1), 0))
    return pl.pallas_call(
        functools.partial(qkv_kernel, n_ten),
        grid=(rows // tile,),
        in_specs=[row, once((1, width)), once((1, width))] + [once((width, width))] * 3 + [table, table] + [once((tile, LANES))] * 2 + [any_spec()] * 3,
        out_specs=[row] * 4 + [any_spec()] * 3,
        out_shape=[jax.ShapeDtypeStruct((rows, width), BF)] * 4
        + [
            jax.ShapeDtypeStruct((width, n_ten * ffn[0].shape[1]), BF),
            jax.ShapeDtypeStruct((width, n_ten * ffn[1].shape[1]), BF),
            jax.ShapeDtypeStruct((n_ten * ffn[2].shape[0], width), BF),
        ],
        scratch_shapes=route_sems(),
        compiler_params=pltpu.CompilerParams(collective_id=7, has_side_effects=True),
        cost_estimate=pl.CostEstimate(flops=6 * rows * width * width, bytes_accessed=16 * rows * width, transcendentals=0),
        name="norm_qkv",
    )(x, gain.reshape(1, width), bias.reshape(1, width), w_query, w_key, w_value, *tables, *part_tables, *ffn)


def attend_body(q_ref, k_ref, v_ref):
    q, k, v = q_ref[...], k_ref[...], v_ref[...]
    outs = []
    for h in range(LANES // HEAD_DIM):
        s = dot_t(q * head_mask(h), k)
        p = jnp.exp(s - jnp.max(s, axis=1, keepdims=True))
        norm = jnp.sum(p, axis=1, keepdims=True)
        outs.append(dot_n(p.astype(BF), v) / norm)
    lane = lax.broadcasted_iota(jnp.int32, outs[0].shape, 1)
    return jnp.where(lane < HEAD_DIM, outs[0], outs[1]).astype(BF)


def attend_specs(rows, tile):
    return [
        pl.BlockSpec((tile, LANES), lambda p, r: (r, p)),
        pl.BlockSpec((rows, LANES), lambda p, r: (0, p)),
        pl.BlockSpec((rows, LANES), lambda p, r: (0, p)),
    ]


def attend_cost(rows, pairs):
    return pl.CostEstimate(
        flops=16 * pairs * rows * rows * LANES, bytes_accessed=8 * rows * pairs * LANES, transcendentals=2 * pairs * rows * rows
    )


def attend_left_kernel(
    n_ten, q_ref, k_ref, v_ref, ag_in, au_in, ad_in, part_ref, ag_ref, au_ref, ad_ref, buf, send, recv, local_sem,
    route_send, route_recv,
):
    place, device = quad_place()
    r, p = pl.program_id(0), pl.program_id(1)
    last_pair = p == pl.num_programs(1) - 1
    hw = buf.shape[2]
    dst = part_ref.at[:, pl.ds(pl.multiple_of(place * hw, hw), hw)]
    route = WeightRoute((ag_ref, au_ref, ad_ref), None, n_ten, route_send, route_recv)
    hops = route.hop(1, 2) + route.hop(2, 0)

    @pl.when((p == 0) & (r == 0))
    def _():
        greet(quad_peers() + [route.y_peer])
        start_all(hops)

    buf[r, :, pl.ds(pl.multiple_of(p * LANES, LANES), LANES)] = attend_body(q_ref, k_ref, v_ref)

    def copy_to(j):
        to = (place + j) % QUAD
        return remote(buf.at[to], dst, send.at[j - 1], recv.at[j - 1], device(to))

    own = pltpu.make_async_copy(buf.at[place], dst, local_sem.at[0])
    for j in range(1, QUAD):
        pl.when(last_pair & (r == (place + j) % QUAD))(copy_to(j).start)
    pl.when(last_pair & (r == place))(own.start)

    @pl.when(last_pair & (r == QUAD - 1))
    def _():
        wait_all([copy_to(j) for j in range(1, QUAD)])
        own.wait()
        wait_all(hops)


def attend_left(q, k, v, gathered, n_ten):
    rows, hw = q.shape
    tile, pairs = rows // QUAD, hw // LANES
    column = pl.BlockSpec((rows, LANES), lambda r, p: (0, p))
    return pl.pallas_call(
        functools.partial(attend_left_kernel, n_ten),
        grid=(QUAD, pairs),
        in_specs=[pl.BlockSpec((tile, LANES), lambda r, p: (r, p)), column, column] + [any_spec()] * 3,
        out_specs=[any_spec()] * 4,
        out_shape=[jax.ShapeDtypeStruct((tile, QUAD * hw), BF)] + [jax.ShapeDtypeStruct(w.shape, BF) for w in gathered],
        input_output_aliases={3: 1, 4: 2, 5: 3},
        scratch_shapes=[pltpu.VMEM((QUAD, tile, hw), BF)]
        + [pltpu.SemaphoreType.DMA((QUAD - 1,))] * 2
        + [pltpu.SemaphoreType.DMA((1,))]
        + route_sems(),
        compiler_params=pltpu.CompilerParams(collective_id=3, has_side_effects=True),
        cost_estimate=attend_cost(rows, pairs),
        name="attend_left",
    )(q, k, v, *gathered)


def swap_part(refs, outs, send, recv, local_sem, base):
    place, device = quad_place()
    share, hw = outs[0].shape[0] // QUAD, outs[0].shape[1]
    copies, local = [], []
    rows = pl.ds(base, share)
    mine = pl.ds(pl.multiple_of(place * share, share), share)
    for i, (ref, out) in enumerate(zip(refs, outs, strict=True)):
        for j in range(1, QUAD):
            to = (place + j) % QUAD
            src = ref.at[rows, pl.ds(pl.multiple_of(to * hw, hw), hw)]
            copies.append(remote(src, out.at[mine, :], send.at[i, j - 1], recv.at[i, j - 1], device(to)))
        src = ref.at[rows, pl.ds(pl.multiple_of(place * hw, hw), hw)]
        local.append(pltpu.make_async_copy(src, out.at[mine, :], local_sem.at[i]))
    return copies, local


def attend_swap_kernel(
    n_ten, length, q_ref, k_ref, v_ref, q_all, k_all, v_all, ag_in, au_in, ad_in, o_ref, lq_ref, lk_ref, lv_ref,
    ag_ref, au_ref, ad_ref, send, recv, local_sem, route_send, route_recv,
):
    step = pl.program_id(0) * pl.num_programs(1) + pl.program_id(1)
    steps = pl.num_programs(0) * pl.num_programs(1)
    copies, local = swap_part((q_all, k_all, v_all), (lq_ref, lk_ref, lv_ref), send, recv, local_sem, length)
    route = WeightRoute((ag_ref, au_ref, ad_ref), None, n_ten, route_send, route_recv)

    @pl.when(step == 0)
    def _():
        greet(quad_peers() + [route.y_peer] + [{"tensor": (route.t + j) % n_ten} for j in range(1, n_ten)])
        start_all(route.hop(1, 0))

        @pl.when(route.is_middle)
        def _():
            start_all(route.in_far())
            start_all(route.out_two())

        start_all(copies + local)

    o_ref[...] = attend_body(q_ref, k_ref, v_ref)

    @pl.when(step == steps // 4)
    def _():
        received(route.hop(1, 0))
        start_all(route.hop(1, 1))

    @pl.when(step == steps // 2)
    def _():
        @pl.when(route.is_middle)
        def _():
            route.arrived(3)
            start_all(route.out_three())

    @pl.when(step == steps - 1)
    def _():
        wait_all(copies + local)
        received(route.hop(1, 1))
        sent_all(route.hop(1, 0) + route.hop(1, 1))

        @pl.when(route.is_middle)
        def _():
            sent_all(route.in_far() + route.out_two() + route.out_three())

        @pl.when(route.is_end)
        def _():
            route.arrived(2)
            route.arrived(3)


def attend_swap(q, k, v, gathered, length, n_ten):
    width = q.shape[1]
    tile, pairs, hw = 512, width // LANES, width // QUAD
    left = jax.ShapeDtypeStruct((length, hw), BF)
    return pl.pallas_call(
        functools.partial(attend_swap_kernel, n_ten, length),
        grid=(pairs, length // tile),
        in_specs=attend_specs(length, tile) + [any_spec()] * 6,
        out_specs=[pl.BlockSpec((tile, LANES), lambda p, r: (r, p))] + [any_spec()] * 6,
        out_shape=[jax.ShapeDtypeStruct((length, width), BF), left, left, left]
        + [jax.ShapeDtypeStruct(w.shape, BF) for w in gathered],
        input_output_aliases={6: 4, 7: 5, 8: 6},
        scratch_shapes=[
            pltpu.SemaphoreType.DMA((3, QUAD - 1)),
            pltpu.SemaphoreType.DMA((3, QUAD - 1)),
            pltpu.SemaphoreType.DMA((3,)),
        ]
        + route_sems(),
        compiler_params=pltpu.CompilerParams(collective_id=1, has_side_effects=True),
        cost_estimate=attend_cost(length, pairs),
        name="attend_swap",
    )(q, k, v, q, k, v, *gathered)


def back_body(q_ref, g_ref, k_ref, v_ref, pick_ref, cos_ref, sin_ref, qcos_ref, qsin_ref):
    g, k, v, pick = g_ref[...], k_ref[...], v_ref[...], pick_ref[...]
    q = dot_n(pick, q_ref[...]).astype(BF)
    dq = []
    all_p, all_ds, all_q, all_g = [], [], [], []
    for h in range(LANES // HEAD_DIM):
        mask = head_mask(h)
        qh, gh = q * mask, g * mask
        s = dot_t(qh, k)
        p = jnp.exp(s - jnp.max(s, axis=1, keepdims=True))
        p = p / jnp.sum(p, axis=1, keepdims=True)
        dp = dot_t(gh, v)
        ds = (p * (dp - jnp.sum(p * dp, axis=1, keepdims=True))).astype(BF)
        dq.append(dot_n(ds, k))
        all_p.append(p.astype(BF))
        all_ds.append(ds)
        all_q.append(qh)
        all_g.append(gh)
    lane = lax.broadcasted_iota(jnp.int32, dq[0].shape, 1)
    dq = jnp.where(lane < HEAD_DIM, dq[0], dq[1]) * (1.0 / math.sqrt(HEAD_DIM))
    dq = (dq * qcos_ref[...] - swap_halves(dq) * qsin_ref[...]).astype(BF)
    dq = t_dot(pick, dq).astype(BF)
    dk = t_dot(jnp.concatenate(all_ds, axis=0), jnp.concatenate(all_q, axis=0))
    dk = (dk * cos_ref[...] - swap_halves(dk) * sin_ref[...]).astype(BF)
    dv = t_dot(jnp.concatenate(all_p, axis=0), jnp.concatenate(all_g, axis=0)).astype(BF)
    return dq, dk, dv


def back_kernel(q_ref, g_ref, k_ref, v_ref, pick_ref, cos_ref, sin_ref, qcos_ref, qsin_ref, dq_ref, dk_ref, dv_ref):
    dq_ref[...], dk_ref[...], dv_ref[...] = back_body(
        q_ref, g_ref, k_ref, v_ref, pick_ref, cos_ref, sin_ref, qcos_ref, qsin_ref
    )


def back_specs(length, masked):
    full = pl.BlockSpec((length, LANES), lambda p: (0, p))
    same = pl.BlockSpec((length, LANES), lambda p: (0, 0))
    row_same = pl.BlockSpec((masked, LANES), lambda p: (0, 0))
    return [
        full, pl.BlockSpec((masked, LANES), lambda p: (0, p)), full, full,
        pl.BlockSpec((masked, length), lambda p: (0, 0)), same, same, row_same, row_same,
    ]


def back_cost(length, masked, pairs):
    return pl.CostEstimate(
        flops=24 * pairs * length * masked * LANES, bytes_accessed=12 * length * pairs * LANES, transcendentals=2 * pairs * length * masked
    )


def back_left(q, grad_rows, k, v, pick, tables):
    masked, length = pick.shape
    width = q.shape[1]
    full = pl.BlockSpec((length, LANES), lambda p: (0, p))
    return pl.pallas_call(
        back_kernel,
        grid=(width // LANES,),
        in_specs=back_specs(length, masked),
        out_specs=[full] * 3,
        out_shape=[jax.ShapeDtypeStruct((length, width), BF)] * 3,
        cost_estimate=back_cost(length, masked, width // LANES),
        name="back_left",
    )(q, grad_rows, k, v, pick, *tables)


def back_swap_kernel(
    q_ref, g_ref, k_ref, v_ref, pick_ref, cos_ref, sin_ref, qcos_ref, qsin_ref, lq_ref, lk_ref, lv_ref,
    dq_ref, dk_ref, dv_ref, buf, out_sem, send, recv, local_sem,
):
    place, device = quad_place()
    step, steps = pl.program_id(0), pl.num_programs(0)
    length = q_ref.shape[0]
    share, hw = lq_ref.shape[0] // QUAD, lq_ref.shape[1]
    outs = (dq_ref, dk_ref, dv_ref)
    copies, local = [], []
    mine = pl.ds(pl.multiple_of(place * hw, hw), hw)
    for i, (ref, out) in enumerate(zip((lq_ref, lk_ref, lv_ref), outs, strict=True)):
        dst = out.at[pl.ds(length, share), mine]
        for j in range(1, QUAD):
            to = (place + j) % QUAD
            src = ref.at[pl.ds(pl.multiple_of(to * share, share), share), :]
            copies.append(remote(src, dst, send.at[i, j - 1], recv.at[i, j - 1], device(to)))
        src = ref.at[pl.ds(pl.multiple_of(place * share, share), share), :]
        local.append(pltpu.make_async_copy(src, dst, local_sem.at[i]))

    def out_copy(at, i):
        slot = at % 2
        columns = pl.ds(pl.multiple_of(at * LANES, LANES), LANES)
        return pltpu.make_async_copy(buf.at[slot, i], outs[i].at[pl.ds(0, length), columns], out_sem.at[slot, i])

    @pl.when(step == 0)
    def _():
        greet(quad_peers())
        start_all(copies + local)

    @pl.when(step >= 2)
    def _():
        for i in range(3):
            out_copy(step - 2, i).wait()

    results = back_body(q_ref, g_ref, k_ref, v_ref, pick_ref, cos_ref, sin_ref, qcos_ref, qsin_ref)
    for i in range(3):
        buf[step % 2, i] = results[i]
        out_copy(step, i).start()

    @pl.when(step == steps - 1)
    def _():
        for i in range(3):
            out_copy(step - 1, i).wait()
            out_copy(step, i).wait()
        wait_all(copies + local)


def back_swap(q, grad_rows, k, v, pick, tables, left):
    masked, length = pick.shape
    width = q.shape[1]
    share = left[0].shape[0] // QUAD
    return pl.pallas_call(
        back_swap_kernel,
        grid=(width // LANES,),
        in_specs=back_specs(length, masked) + [any_spec()] * 3,
        out_specs=[any_spec()] * 3,
        out_shape=[jax.ShapeDtypeStruct((length + share, width), BF)] * 3,
        scratch_shapes=[
            pltpu.VMEM((2, 3, length, LANES), BF),
            pltpu.SemaphoreType.DMA((2, 3)),
            pltpu.SemaphoreType.DMA((3, QUAD - 1)),
            pltpu.SemaphoreType.DMA((3, QUAD - 1)),
            pltpu.SemaphoreType.DMA((3,)),
        ],
        compiler_params=pltpu.CompilerParams(collective_id=2, has_side_effects=True),
        cost_estimate=back_cost(length, masked, width // LANES),
        name="back_swap",
    )(q, grad_rows, k, v, pick, *tables, *left)


def feed_kernel(
    n_ten, tok_ref, att_ref, left_ref, wo_ref, gain_ref, bias_ref, pick_ref, part_pick_ref, cot_ref, wg_ref, wu_ref, wd_ref,
    ag_in, au_in, ad_in, out_ref, att_m_ref, gr2_ref, gatt_ref, left_gatt_ref, vec_ref, all_own_ref, all_left_ref,
    ag_ref, au_ref, ad_ref,
    x_ref, acc_ref, normed_ref, inv_ref, grad_ref, g_buf, u_buf, d_buf, rows_buf, rows_parts, own_m, left_m, gatt_buf, gatt_parts,
    buf_sem, small_send, small_recv, line_send, line_recv, local_sem, send, recv,
):
    step, steps = pl.program_id(0), pl.num_programs(0)
    rows, width = tok_ref.shape
    length = att_ref.shape[0]
    masked = cot_ref.shape[0]
    slots = masked // 2
    unit = g_buf.shape[2]
    units = wg_ref.shape[1]
    per = units // unit
    part, hw = rows_buf.shape[1], gatt_parts.shape[2]
    gain = gain_ref[...]
    own = (wg_ref, wu_ref, wd_ref)
    route = WeightRoute((ag_ref, au_ref, ad_ref), own, n_ten, send, recv)
    order = route.order
    place, device = quad_place()
    rows_copies, gatt_copies = [], []
    for j in range(1, QUAD):
        to = (place + j) % QUAD
        rows_copies.append(
            remote(rows_buf.at[to], rows_parts.at[j - 1], small_send.at[0, j - 1], small_recv.at[0, j - 1], device(to))
        )
        src = gatt_buf.at[:, pl.ds(pl.multiple_of(to * hw, hw), hw)]
        gatt_copies.append(
            remote(src, gatt_parts.at[j - 1], small_send.at[1, j - 1], small_recv.at[1, j - 1], device(to))
        )

    line_copies = [[], []]
    local = []
    for n, (src, out) in enumerate(((own_m, all_own_ref), (left_m, all_left_ref))):
        for j in range(1, n_ten):
            to = (route.t + j) % n_ten
            line_copies[n].append(
                remote(src, out.at[route.t], line_send.at[n, j - 1], line_recv.at[n, j - 1], {"tensor": to})
            )
        local.append(pltpu.make_async_copy(src, out.at[route.t], local_sem.at[n]))

    def fetch(at):
        slot, i, b = at % 2, at // per, at % per

        def make(refs, shard_at):
            base = pl.multiple_of(shard_at * units + b * unit, unit)
            return [
                pltpu.make_async_copy(refs[0].at[:, pl.ds(base, unit)], g_buf.at[slot], buf_sem.at[slot, 0]),
                pltpu.make_async_copy(refs[1].at[:, pl.ds(base, unit)], u_buf.at[slot], buf_sem.at[slot, 1]),
                pltpu.make_async_copy(refs[2].at[pl.ds(base, unit), :], d_buf.at[slot], buf_sem.at[slot, 2]),
            ]

        @pl.when(i == 0)
        def _():
            start_all(make(own, 0))

        @pl.when(i > 0)
        def _():
            which = order[1] * (i == 1) + order[2] * (i == 2) + order[3] * (i == 3)
            start_all(make((ag_ref, au_ref, ad_ref), which))

    def fetched(at):
        slot = at % 2
        wait_all(
            [
                pltpu.make_async_copy(wg_ref.at[:, pl.ds(0, unit)], g_buf.at[slot], buf_sem.at[slot, 0]),
                pltpu.make_async_copy(wu_ref.at[:, pl.ds(0, unit)], u_buf.at[slot], buf_sem.at[slot, 1]),
                pltpu.make_async_copy(wd_ref.at[pl.ds(0, unit), :], d_buf.at[slot], buf_sem.at[slot, 2]),
            ]
        )

    def norm(res):
        normed, inv_std = layer_stats(res)
        return normed, inv_std, (normed * gain + bias_ref[...]).astype(BF)

    @pl.when(step == 0)
    def _():
        greet(quad_peers() + [route.y_peer] + [{"tensor": (route.t + j) % n_ten} for j in range(1, n_ten)])
        start_all(route.hop(2, 1))
        start_all(route.hop(3, 0))
        fetch(0)
        tile = rows - length
        for i, (pick, att, tok) in enumerate(
            ((pick_ref[...], att_ref[...], tok_ref[:length, :]), (part_pick_ref[...], left_ref[...], tok_ref[length:, :]))
        ):
            here = slice(i * slots, (i + 1) * slots)
            att_m = dot_n(pick, att).astype(BF)
            att_m_ref[here, :] = att_m
            normed, inv_std, low = norm(dot_n(pick, tok) + dot_n(att_m, wo_ref[...]))
            normed_ref[here, :] = normed
            inv_ref[here, :] = jnp.broadcast_to(inv_std, (slots, LANES))
            here_too = jnp.sum(pick.astype(F32), axis=1, keepdims=True) > 0.0
            low = jnp.where(here_too, low.astype(F32), 0.0)
            x_ref[rows + i * slots : rows + (i + 1) * slots, :] = low.astype(BF)
            if i == 0:
                own_m[...] = low.astype(BF)
            else:
                for k in range(QUAD):
                    rows_buf[k] = low[k * part : (k + 1) * part, :].astype(BF)
        for at in range(0, rows, tile):
            att = att_ref[at : at + tile, :] if at < length else left_ref[...]
            res = tok_ref[at : at + tile, :].astype(F32) + dot_n(att, wo_ref[...])
            x_ref[at : at + tile, :] = norm(res)[2]
            acc_ref[at : at + tile, :] = res
        grad_ref[...] = jnp.zeros_like(grad_ref)

    fetched(step)

    @pl.when((step + 1 < steps) & ((step + 1) % per != 0))
    def _():
        fetch(step + 1)

    slot = step % 2
    x = x_ref[...]
    w_g, w_u, w_d = g_buf[slot], u_buf[slot], d_buf[slot]
    gate, up = dot_n(x, w_g), dot_n(x, w_u)
    sig = jax.nn.sigmoid(gate)
    act = gate * sig
    hidden = (act[:rows] * up[:rows]).astype(BF)
    for at in range(0, width, unit):
        acc_ref[:, at : at + unit] += dot_n(hidden, w_d[:, at : at + unit])
    back = dot_t(cot_ref[...].astype(BF), w_d)
    gate, up, sig, act = gate[rows:], up[rows:], sig[rows:], act[rows:]
    grad_gate = (back * up * sig * (1.0 + gate * (1.0 - sig))).astype(BF)
    grad_up = (back * act).astype(BF)
    grad_ref[...] += dot_t(grad_gate, w_g) + dot_t(grad_up, w_u)

    @pl.when(step == 1)
    def _():
        start_all(rows_copies)
        start_all(line_copies[0])
        local[0].start()

    @pl.when(step == 3)
    def _():
        wait_all(rows_copies)
        whole = rows_buf[place].astype(F32)
        for j in range(QUAD - 1):
            whole = whole + rows_parts[j].astype(F32)
        left_m[...] = whole.astype(BF)

    @pl.when(step == 4)
    def _():
        start_all(line_copies[1])
        local[1].start()

    @pl.when(step == per + 1)
    def _():
        received(route.hop(2, 1))
        start_all(route.hop(2, 2))
        received(route.hop(3, 0))
        start_all(route.hop(3, 1))

    @pl.when(step == 2 * per - 1)
    def _():
        received(route.hop(2, 2))

    @pl.when(step == 2 * per + 2)
    def _():
        received(route.hop(3, 1))
        start_all(route.hop(3, 2))

    @pl.when(step == 3 * per - 1)
    def _():
        received(route.hop(3, 2))

    @pl.when((step + 1 < steps) & ((step + 1) % per == 0))
    def _():
        fetch(step + 1)

    @pl.when(step == steps - 1)
    def _():
        grad, normed = grad_ref[...], normed_ref[...]
        gr2 = (cot_ref[...] + norm_back(grad, normed, inv_ref[:, :1], gain)).astype(BF)
        gr2_ref[...] = gr2
        gatt = dot_t(gr2, wo_ref[...]).astype(BF)
        gatt_ref[...] = gatt[:slots]
        gatt_buf[...] = gatt[slots:]
        vec_ref[...] = jnp.concatenate(
            [jnp.sum(grad * normed, axis=0, keepdims=True), jnp.sum(grad, axis=0, keepdims=True)], axis=0
        )
        start_all(gatt_copies)
        out_ref[...] = acc_ref[...].astype(BF)
        sent_all(route.hop(2, 1) + route.hop(2, 2) + route.hop(3, 0) + route.hop(3, 1) + route.hop(3, 2))
        wait_all(gatt_copies)
        whole = gatt_buf[:, pl.ds(pl.multiple_of(place * hw, hw), hw)].astype(F32)
        for j in range(QUAD - 1):
            whole = whole + gatt_parts[j].astype(F32)
        left_gatt_ref[...] = whole.astype(BF)
        wait_all(line_copies[0] + line_copies[1])
        wait_all(local)


def feed_forward(tok, att, left_att, w_out, gain, bias, pick, part_pick, cot, ffn, gathered, n_ten):
    rows, width = tok.shape
    units = ffn[0].shape[1]
    masked = cot.shape[0]
    slots, hw = masked // 2, width // QUAD
    unit = 256
    whole = lambda *shape: pl.BlockSpec(shape, lambda i: (0,) * len(shape))
    low = jax.ShapeDtypeStruct((masked, width), BF)
    return pl.pallas_call(
        functools.partial(feed_kernel, n_ten),
        grid=(n_ten * units // unit,),
        in_specs=[once(x.shape) for x in (tok, att, left_att, w_out)]
        + [once((1, width)), once((1, width)), once(pick.shape), once(part_pick.shape), once(cot.shape)]
        + [any_spec()] * 6,
        out_specs=[whole(rows, width), whole(masked, width), whole(masked, width), whole(slots, width), whole(slots, hw)]
        + [whole(2, width)]
        + [any_spec()] * 5,
        out_shape=[
            jax.ShapeDtypeStruct((rows, width), BF), low, low,
            jax.ShapeDtypeStruct((slots, width), BF), jax.ShapeDtypeStruct((slots, hw), BF),
            jax.ShapeDtypeStruct((2, width), F32),
            jax.ShapeDtypeStruct((n_ten, slots, width), BF), jax.ShapeDtypeStruct((n_ten, slots // QUAD, width), BF),
        ]
        + [jax.ShapeDtypeStruct(w.shape, BF) for w in gathered],
        input_output_aliases={12: 8, 13: 9, 14: 10},
        scratch_shapes=[
            pltpu.VMEM((rows + masked, width), BF),
            pltpu.VMEM((rows, width), F32),
            pltpu.VMEM((masked, width), F32),
            pltpu.VMEM((masked, LANES), F32),
            pltpu.VMEM((masked, width), F32),
            pltpu.VMEM((2, width, unit), BF),
            pltpu.VMEM((2, width, unit), BF),
            pltpu.VMEM((2, unit, width), BF),
            pltpu.VMEM((QUAD, slots // QUAD, width), BF),
            pltpu.VMEM((QUAD - 1, slots // QUAD, width), BF),
            pltpu.VMEM((slots, width), BF),
            pltpu.VMEM((slots // QUAD, width), BF),
            pltpu.VMEM((slots, width), BF),
            pltpu.VMEM((QUAD - 1, slots, hw), BF),
            pltpu.SemaphoreType.DMA((2, 3)),
            pltpu.SemaphoreType.DMA((2, QUAD - 1)),
            pltpu.SemaphoreType.DMA((2, QUAD - 1)),
            pltpu.SemaphoreType.DMA((2, n_ten - 1)),
            pltpu.SemaphoreType.DMA((2, n_ten - 1)),
            pltpu.SemaphoreType.DMA((2,)),
        ]
        + route_sems(),
        compiler_params=pltpu.CompilerParams(collective_id=5, has_side_effects=True),
        cost_estimate=pl.CostEstimate(
            flops=8 * rows * width * n_ten * units, bytes_accessed=6 * width * n_ten * units, transcendentals=rows * n_ten * units
        ),
        name="feed_forward",
    )(tok, att, left_att, w_out, gain.reshape(1, width), bias.reshape(1, width), pick, part_pick, cot, *ffn, *gathered)[:8]


def token_back_kernel(
    tok_ref, dq_ref, dk_ref, dv_ref, wq_ref, wk_ref, wv_ref, gain_ref, pick_ref, rows_ref, out_ref, vec_ref
):
    acc = dot_t(dq_ref[...], wq_ref[...]) + dot_t(dk_ref[...], wk_ref[...]) + dot_t(dv_ref[...], wv_ref[...])
    normed, inv_std = layer_stats(tok_ref[...].astype(F32))
    direct = t_dot(pick_ref[...], rows_ref[0])
    out_ref[...] = (direct + norm_back(acc, normed, inv_std, gain_ref[...])).astype(BF)
    sums = jnp.concatenate([jnp.sum(acc * normed, axis=0, keepdims=True), jnp.sum(acc, axis=0, keepdims=True)], axis=0)

    @pl.when(pl.program_id(0) == 0)
    def _():
        vec_ref[...] = sums

    @pl.when(pl.program_id(0) > 0)
    def _():
        vec_ref[...] += sums


def token_back(tok, grads, weights, gain, pick, rows_m):
    rows, width = tok.shape
    slots = pick.shape[0]
    tile = 256
    row = pl.BlockSpec((tile, width), lambda r: (r, 0))
    own = rows // tile - 1
    return pl.pallas_call(
        token_back_kernel,
        grid=(rows // tile,),
        in_specs=[row] * 4
        + [once((width, width))] * 3
        + [
            once((1, width)),
            pl.BlockSpec((slots, tile), lambda r: (0, r)),
            pl.BlockSpec((1, slots, width), lambda r: (r // own, 0, 0)),
        ],
        out_specs=[row, pl.BlockSpec((2, width), lambda r: (0, 0))],
        out_shape=[jax.ShapeDtypeStruct((rows, width), BF), jax.ShapeDtypeStruct((2, width), F32)],
        cost_estimate=pl.CostEstimate(flops=6 * rows * width * width, bytes_accessed=16 * rows * width, transcendentals=0),
        name="token_back",
    )(tok, *grads, *weights, gain.reshape(1, width), pick, rows_m)


def exchange_out_kernel(
    sizes, go_ref, gq_ref, gk_ref, gv_ref, gg_ref, gu_ref, gd_ref, grad_ref, vec_ref, w_ref, ffn_ref, tok_ref, vec_out,
    buf1, buf2, buf3, buf4, vec_buf, vec_sum,
    tok_send, tok_recv, send1, recv1, send2, recv2, send3, recv3, send4, recv4, vec_send, vec_recv, local_sem,
):
    n_seq, n_ten, half, rows = sizes
    dp, sx, t = lax.axis_index("dp"), lax.axis_index("seq"), lax.axis_index("tensor")
    y, c = dp // 2, dp % 2
    me = sx * n_ten + t
    group = n_seq * n_ten
    others = []
    for i in range(1, group):
        g = (me + i) % group
        others.append((g // n_ten, g % n_ten))
    y_peer, c_peer, x_peer = {"dp": (dp + 2) % 4}, {"dp": 2 * y + 1 - c}, {"seq": 1 - sx}
    z_peers = [{"tensor": (t + j) % n_ten} for j in range(1, n_ten)]
    beside = [{"dp": 2 * y + 1 - c, "tensor": (t + j) % n_ten} for j in range(1, n_ten)]
    greet([{"seq": a, "tensor": b} for a, b in others] + [y_peer, c_peer] + beside)
    grads = (go_ref, gq_ref, gk_ref, gv_ref, gg_ref, gu_ref, gd_ref)
    count, attn = len(grads), w_ref.shape[0]
    x_first = (True, False, False, False, True, False, False)
    height = gq_ref.shape[0]
    hw = height // n_ten

    def columns(b_y, b_c, b_x):
        return pl.ds(pl.multiple_of((b_y * 4 + b_c * 2 + b_x) * LANES, LANES), LANES)

    def add_rows(out, first, second):
        def body(i, carry):
            at = pl.ds(pl.multiple_of(i * hw, hw), hw)
            out[at, :] = (first[at, :].astype(F32) + second[at, :].astype(F32)).astype(BF)
            return carry

        lax.fori_loop(0, height // hw, body, 0)

    stage1 = []
    for a in range(count):
        stage1.append(
            [
                remote(
                    grads[a].at[:, columns(b_y, 1 - c, b_x)], buf1.at[a, b_y, b_x],
                    send1.at[a, 2 * b_y + b_x], recv1.at[a, 2 * b_y + b_x], c_peer,
                )
                for b_y in range(2)
                for b_x in range(2)
            ]
        )
    for copies in stage1:
        start_all(copies)

    vec_hops = []
    hops = [c_peer, x_peer, y_peer]
    vec_sum[0] = vec_ref[...]
    for i, peer in enumerate(hops):
        vec_hops.append([remote(vec_sum.at[i], vec_buf.at[i], vec_send.at[i], vec_recv.at[i], peer)])
    vec_hops.append(
        [
            remote(vec_sum.at[3], vec_buf.at[3 + j], vec_send.at[3 + j], vec_recv.at[3 + j], peer)
            for j, peer in enumerate(z_peers)
        ]
    )
    start_all(vec_hops[0])

    tokens = []
    for i, (a, b) in enumerate(others):
        tokens.append(
            remote(
                grad_ref.at[pl.ds(pl.multiple_of((a * n_ten + b) * rows, rows), rows), :],
                tok_ref.at[sx * half + t],
                tok_send.at[i], tok_recv.at[i], {"seq": a, "tensor": b},
            )
        )
    shared = []
    for i in range(n_seq):
        src, dst = grad_ref.at[pl.ds((group + i) * rows, rows), :], tok_ref.at[t % 2 * half + n_ten]
        shared.append(
            (
                2 * c + i == t,
                remote(
                    src, dst, tok_send.at[group - 1 + i], tok_recv.at[group - 1 + t % 2],
                    {"dp": 2 * y + t // 2, "tensor": 2 * c + i},
                ),
                pltpu.make_async_copy(src, dst, local_sem.at[1]),
            )
        )
    arriving = [
        remote(
            grad_ref.at[pl.ds(0, rows), :], tok_ref.at[i * half + n_ten],
            tok_send.at[group - 1], tok_recv.at[group - 1 + i], c_peer,
        )
        for i in range(n_seq)
    ]
    start_all(tokens)
    for here, away, near in shared:
        pl.when(here)(near.start)
        pl.when(jnp.logical_not(here))(away.start)
    local = [
        pltpu.make_async_copy(
            grad_ref.at[pl.ds(pl.multiple_of(me * rows, rows), rows), :], tok_ref.at[sx * half + t], local_sem.at[0]
        ),
    ]
    start_all(local)

    stage2 = []
    for a in range(count):
        for copy in stage1[a]:
            copy.wait_recv()
        for b_y in range(2):
            for b_x in range(2):
                add_rows(buf1.at[a, b_y, b_x], grads[a].at[:, columns(b_y, c, b_x)], buf1.at[a, b_y, b_x])
        copies = []
        for b in range(2):
            src, peer = (buf1.at[a, b, 1 - sx], x_peer) if x_first[a] else (buf1.at[a, 1 - y, b], y_peer)
            copies.append(remote(src, buf2.at[a, b], send2.at[a, b], recv2.at[a, b], peer))
        start_all(copies)
        stage2.append(copies)
    vec_hops[0][0].wait_recv()
    vec_sum[1] = vec_sum[0] + vec_buf[0]
    start_all(vec_hops[1])
    stage3 = []
    for a in range(count):
        for copy in stage2[a]:
            copy.wait_recv()
        for b in range(2):
            own = buf1.at[a, b, sx] if x_first[a] else buf1.at[a, y, b]
            add_rows(buf2.at[a, b], own, buf2.at[a, b])
        src, peer = (buf2.at[a, 1 - y], y_peer) if x_first[a] else (buf2.at[a, 1 - sx], x_peer)
        copy = remote(src, buf3.at[a], send3.at[a], recv3.at[a], peer)
        copy.start()
        stage3.append(copy)
    vec_hops[1][0].wait_recv()
    vec_sum[2] = vec_sum[1] + vec_buf[1]
    start_all(vec_hops[2])
    stage4 = []
    for a in range(count):
        stage3[a].wait_recv()
        own = buf2.at[a, y] if x_first[a] else buf2.at[a, sx]
        if a >= attn:

            def final(i, carry, a=a, own=own):
                at = pl.ds(pl.multiple_of(i * hw, hw), hw)
                ffn_ref[a - attn, at, :] = own[at, :].astype(F32) + buf3[a, at, :].astype(F32)
                return carry

            lax.fori_loop(0, height // hw, final, 0)
            continue
        add_rows(buf3.at[a], own, buf3.at[a])
        copies = []
        for j, peer in enumerate(z_peers):
            to = (t + 1 + j) % n_ten
            src = buf3.at[a, pl.ds(pl.multiple_of(to * hw, hw), hw), :]
            copies.append(remote(src, buf4.at[a, j], send4.at[a, j], recv4.at[a, j], peer))
        start_all(copies)
        stage4.append(copies)
    vec_hops[2][0].wait_recv()
    vec_sum[3] = vec_sum[2] + vec_buf[2]
    start_all(vec_hops[3])
    for n, copies in enumerate(stage4):
        total = buf3[n, pl.ds(pl.multiple_of(t * hw, hw), hw), :].astype(F32)
        for j, copy in enumerate(copies):
            copy.wait_recv()
            total = total + buf4[n, j].astype(F32)
        w_ref[n] = total
    total = vec_sum[3]
    for j, copy in enumerate(vec_hops[3]):
        copy.wait_recv()
        total = total + vec_buf[3 + j]
    vec_out[...] = total
    for copies in stage1 + stage2 + stage4 + [stage3] + vec_hops:
        for copy in copies:
            copy.wait_send()
    wait_all(local)
    wait_all(tokens)
    for here, away, near in shared:
        pl.when(here)(near.wait)
        pl.when(jnp.logical_not(here))(away.wait_send)
    for i in range(n_seq):
        pl.when(jnp.logical_not(2 * c + i == t))(arriving[i].wait_recv)


def exchange_out(ffn_grads, attn_grads, grad_tok, vectors, n_seq, n_ten, half, rows):
    grads = (*attn_grads, *ffn_grads)
    ffn, attn = len(ffn_grads), len(attn_grads)
    height, width = grads[0].shape
    hw, count, group = height // n_ten, len(grads), n_seq * n_ten
    vmem = pl.BlockSpec(memory_space=pltpu.VMEM)
    dma = pltpu.SemaphoreType.DMA
    hops = 3 + n_ten - 1
    return pl.pallas_call(
        functools.partial(exchange_out_kernel, (n_seq, n_ten, half, rows)),
        in_specs=[vmem] * (count + 2),
        out_specs=[vmem, vmem, any_spec(), vmem],
        out_shape=[
            jax.ShapeDtypeStruct((attn, hw, LANES), F32),
            jax.ShapeDtypeStruct((ffn, height, LANES), F32),
            jax.ShapeDtypeStruct((n_seq * half, rows, width), BF),
            jax.ShapeDtypeStruct(vectors.shape, F32),
        ],
        scratch_shapes=[
            pltpu.VMEM((count, 2, 2, height, LANES), BF),
            pltpu.VMEM((count, 2, height, LANES), BF),
            pltpu.VMEM((count, height, LANES), BF),
            pltpu.VMEM((attn, n_ten - 1, hw, LANES), BF),
            pltpu.VMEM((hops,) + vectors.shape, F32),
            pltpu.VMEM((4,) + vectors.shape, F32),
            dma((group + 1,)), dma((group + 1,)),
            dma((count, 4)), dma((count, 4)),
            dma((count, 2)), dma((count, 2)),
            dma((count,)), dma((count,)),
            dma((attn, n_ten - 1)), dma((attn, n_ten - 1)),
            dma((hops,)), dma((hops,)),
            dma((2,)),
        ],
        compiler_params=pltpu.CompilerParams(collective_id=4, has_side_effects=True),
        name="exchange_out",
    )(*grads, grad_tok, vectors)


def rotary_lanes(cosine, sine):
    reps = LANES // HEAD_DIM
    return jnp.concatenate([cosine, cosine] * reps, axis=1), jnp.concatenate([-sine, sine] * reps, axis=1)


def position_tables(length):
    half_dim = HEAD_DIM // 2
    inv_freq = np.float32(10000.0) ** (-np.arange(half_dim, dtype=np.float32) * np.float32(2.0 / HEAD_DIM))
    angles = (np.arange(length, dtype=np.float32)[:, None] * inv_freq[None, :]).astype(np.float64)
    cosine, sine = np.cos(angles).astype(np.float32), np.sin(angles).astype(np.float32)
    reps = LANES // HEAD_DIM
    return np.concatenate([cosine, cosine] * reps, axis=1), np.concatenate([-sine, sine] * reps, axis=1)


def window_shards(
    tokens,
    norm1_gain,
    norm1_bias,
    w_query,
    w_key,
    w_value,
    w_out,
    norm2_gain,
    norm2_bias,
    w_gate,
    w_up,
    w_down,
    out_grad,
    masked_rows,
    window_counts,
):
    rows_local, windows, width = tokens.shape
    n_dp, n_seq, n_ten = lax.axis_size("dp"), lax.axis_size("seq"), lax.axis_size("tensor")
    dp_index, seq_index, ten_index = lax.axis_index("dp"), lax.axis_index("seq"), lax.axis_index("tensor")
    shard_index = dp_index * n_seq + seq_index
    core = dp_index % 2
    place = seq_index * 2 + core
    half = windows // n_seq
    length = rows_local * n_seq * n_ten
    share = length // QUAD
    hw = width // QUAD
    slots = masked_rows.shape[1]
    part = slots // QUAD

    live = jnp.arange(windows) < window_counts[0]
    valid = (masked_rows < length) & live[:, None]
    coded = jnp.where(valid, masked_rows, length)
    info = jnp.concatenate([coded, jnp.full((1, slots), jnp.sum(valid.astype(jnp.int32)))], axis=0)
    info = jnp.pad(info, ((0, -(windows + 1) % 8), (0, -slots % LANES)))
    both_tok, all_q, all_k, all_v, all_out, infos, peer_grad = exchange_in(
        jnp.swapaxes(tokens, 0, 1), w_query, w_key, w_value, w_out, info, out_grad, n_dp, n_seq, n_ten
    )
    loss_weight = LOSS_SCALE / jnp.sum(infos[:, windows, 0]).astype(F32)
    pick_one = lambda x, at: lax.dynamic_index_in_dim(x, at, 0, keepdims=False)
    first_window = seq_index * half
    my_coded = lax.dynamic_slice_in_dim(coded, first_window, n_ten, 0)
    my_grad = lax.dynamic_slice_in_dim(out_grad, first_window, n_ten, 0)
    pair_infos = lax.dynamic_slice_in_dim(infos, dp_index - core, 2, 0)
    left_coded = jnp.stack([pair_infos[i // n_seq, i % n_seq * half + n_ten, :slots] for i in range(n_ten)])
    own_left = jnp.stack([out_grad[i * half + n_ten] for i in range(n_seq)])
    left_grad = jnp.where(core == 0, jnp.concatenate([own_left, peer_grad]), jnp.concatenate([peer_grad, own_left]))
    weigh = lambda grad, rows: jnp.where((rows < length)[..., None], grad.astype(F32) * loss_weight, 0.0)

    own_rows, left_rows = pick_one(my_coded, ten_index), pick_one(left_coded, ten_index)
    every = jnp.arange(length)
    my_left = place * share + jnp.arange(share)
    own_pick = (own_rows[:, None] == every[None, :]).astype(BF)
    left_pick = (left_rows[:, None] == every[None, :]).astype(BF)
    part_match = left_rows[:, None] == my_left[None, :]
    part_pick = part_match.astype(BF)
    left_here = jnp.where(jnp.any(part_match, axis=1), left_rows, length)
    my_cot = jnp.concatenate(
        [weigh(pick_one(my_grad, ten_index), own_rows), weigh(pick_one(left_grad, ten_index), left_here)], axis=0
    )

    tables = [jnp.asarray(x) for x in position_tables(length)]
    part_tables = [lax.dynamic_slice_in_dim(x, place * share, share, 0) for x in tables]
    own_tables = tables + list(rotary_lanes(*rotary_tables(own_rows)))
    left_tables = tables + list(rotary_lanes(*rotary_tables(left_rows)))

    ffn = (w_gate, w_up, w_down)
    first, q, k, v, *gathered = norm_qkv(
        both_tok, norm1_gain, norm1_bias, all_q, all_k, all_v, tables, part_tables, ffn, n_ten
    )
    own_att, left_q, left_k, left_v, *gathered = attend_swap(q, k, v, gathered, length, n_ten)
    left_att_part, *gathered = attend_left(left_q, left_k, left_v, gathered, n_ten)
    out_both, att_m, gr2, own_gatt, left_gatt, grad_norm2, all_own, all_left = feed_forward(
        both_tok, own_att, left_att_part, all_out, norm2_gain, norm2_bias, own_pick, part_pick, my_cot, ffn, gathered, n_ten
    )

    grad_w_out = t_dot(att_m, gr2).astype(BF)
    left_back = back_left(left_q, left_gatt, left_k, left_v, left_pick, left_tables)
    dq, dk, dv = back_swap(q, own_gatt, k, v, own_pick, own_tables, left_back)
    all_own, dq, dk, dv = lax.optimization_barrier((all_own, dq, dk, dv))

    second = jnp.concatenate([all_own.reshape(-1, width), all_left.reshape(-1, width)], axis=0)
    part_of = lambda x: lax.dynamic_slice_in_dim(x, place * part, part, 1)
    down_in = jnp.concatenate(
        [
            weigh(my_grad, my_coded).reshape(n_ten * slots, width),
            weigh(part_of(left_grad), part_of(left_coded)).reshape(n_ten * part, width),
        ],
        axis=0,
    ).astype(BF)
    gate = dot_n(second, w_gate)
    up = dot_n(second, w_up)
    grad_hidden = dot_t(down_in, w_down)
    sig = jax.nn.sigmoid(gate)
    silu = gate * sig
    hidden_m = (silu * up).astype(BF)
    grad_gate = (grad_hidden * up * sig * (1.0 + gate * (1.0 - sig))).astype(BF)
    grad_up = (grad_hidden * silu).astype(BF)
    grad_w_ffn = [
        t_dot(grad_gate, second).astype(BF), t_dot(grad_up, second).astype(BF), t_dot(hidden_m, down_in).astype(BF)
    ]
    grad_w_attn = [grad_w_out] + [t_dot(d, first).astype(BF) for d in (dq, dk, dv)]
    grad_both, grad_norm1 = token_back(
        both_tok, (dq, dk, dv), (all_q, all_k, all_v), norm1_gain,
        jnp.concatenate([own_pick, part_pick], axis=1), gr2.reshape(2, slots, width),
    )

    own_out = lax.all_to_all(
        out_both[:length].reshape(n_seq * n_ten, rows_local, width), ("seq", "tensor"), 0, 0, tiled=True
    ).reshape(n_seq, n_ten, rows_local, width)
    left_chunks = out_both[length:].reshape(n_seq, rows_local, width)
    left_out = []
    for turn in range(2):
        perm = []
        for d in range(n_dp):
            for sx in range(n_seq):
                for p in range(n_ten):
                    to = d // 2 * 2 + p // 2, sx, d % 2 * 2 + (p % 2 ^ turn)
                    perm.append(((d * n_seq + sx) * n_ten + p, (to[0] * n_seq + to[1]) * n_ten + to[2]))
        left_out.append(lax.ppermute(pick_one(left_chunks, (ten_index + turn) % 2), ("dp", "seq", "tensor"), perm))
    even = ten_index % 2 == 0
    left_out = jnp.stack([jnp.where(even, left_out[0], left_out[1]), jnp.where(even, left_out[1], left_out[0])])
    output = jnp.concatenate([own_out, left_out[:, None]], axis=1).reshape(windows, rows_local, width)
    output = jnp.swapaxes(output, 0, 1)
    vectors = jnp.concatenate(
        [grad_norm1, grad_norm2, jnp.zeros((4, width), F32)], axis=0
    )
    gw_attn, gw_ffn, grad_tokens, vectors = exchange_out(
        grad_w_ffn, grad_w_attn, grad_both, vectors, n_seq, n_ten, half, rows_local
    )
    grad_tokens = jnp.swapaxes(grad_tokens, 0, 1).astype(F32)
    small = width // (n_dp * n_seq * n_ten)
    vectors = lax.dynamic_slice_in_dim(vectors, (shard_index * n_ten + ten_index) * small, small, 1)

    return (
        output,
        grad_tokens,
        vectors[0],
        vectors[1],
        gw_attn[1].T,
        gw_attn[2].T,
        gw_attn[3].T,
        gw_attn[0],
        vectors[2],
        vectors[3],
        gw_ffn[0].T,
        gw_ffn[1].T,
        gw_ffn[2],
    )


def shards(tokens, *rest):
    n_dp, n_seq, n_ten = lax.axis_size("dp"), lax.axis_size("seq"), lax.axis_size("tensor")
    whole = n_dp == 4 and n_seq == 2 and n_ten == 4 and tokens.shape[1] == n_seq * (n_ten + 1)
    return (window_shards if whole else block_shards)(tokens, *rest)


def solution(mesh):
    return jax.shard_map(
        shards,
        mesh=mesh,
        in_specs=(
            P(("seq", "tensor"), "dp", None),
            P(),
            P(),
            P(None, "tensor"),
            P(None, "tensor"),
            P(None, "tensor"),
            P("tensor", None),
            P(),
            P(),
            P(None, "tensor"),
            P(None, "tensor"),
            P("tensor", None),
            P("dp", None, None),
            P("dp", None),
            P("dp"),
        ),
        out_specs=(
            P(("seq", "tensor"), "dp", None),
            P(("seq", "tensor"), "dp", None),
            P(("dp", "seq", "tensor")),
            P(("dp", "seq", "tensor")),
            P(("dp", "seq"), "tensor"),
            P(("dp", "seq"), "tensor"),
            P(("dp", "seq"), "tensor"),
            P("tensor", ("dp", "seq")),
            P(("dp", "seq", "tensor")),
            P(("dp", "seq", "tensor")),
            P(("dp", "seq"), "tensor"),
            P(("dp", "seq"), "tensor"),
            P("tensor", ("dp", "seq")),
        ),
        check_vma=False,
    )
```

```python
import math

import functools

import jax
import jax.numpy as jnp
import numpy as np
from jax import lax
from jax.experimental import pallas as pl
from jax.experimental.pallas import tpu as pltpu
from jax.sharding import PartitionSpec as P

HEAD_DIM = 64
L = 1024
LOSS_SCALE = 1024


epsilon = 1e-05


def layer_stats(inputs):
    row_mean = jnp.mean(inputs, axis=-1, keepdims=True)
    centred = inputs - row_mean
    inv_std = lax.rsqrt(jnp.mean(centred * centred, axis=-1, keepdims=True) + epsilon)
    return (centred * inv_std, inv_std)


def norm_back(grad_norm, normed, inv_std, gain_vec):
    scaled = grad_norm * gain_vec
    return inv_std * (
        scaled
        - jnp.mean(scaled, axis=-1, keepdims=True)
        - normed * jnp.mean(scaled * normed, axis=-1, keepdims=True)
    )


def rotary_tables(positions):
    half_dim = HEAD_DIM // 2
    inv_freq = 10000.0 ** (-jnp.arange(half_dim, dtype=jnp.float32) * 2.0 / HEAD_DIM)
    angles = positions.astype(jnp.float32)[:, None] * inv_freq[None, :]
    return (jnp.cos(angles), jnp.sin(angles))


def rotate(values, cosine, sine):
    half_dim = values.shape[-1] // 2
    first_half = values[..., :half_dim]
    second_half = values[..., half_dim:]
    cos_b = cosine[:, None, None, :]
    sin_b = sine[:, None, None, :]
    return jnp.concatenate(
        [first_half * cos_b - second_half * sin_b, second_half * cos_b + first_half * sin_b],
        axis=-1,
    )


def unrotate(grads, cosine, sine):
    half_dim = grads.shape[-1] // 2
    first_half = grads[..., :half_dim]
    second_half = grads[..., half_dim:]
    cos_b = cosine[:, None, None, :]
    sin_b = sine[:, None, None, :]
    return jnp.concatenate(
        [first_half * cos_b + second_half * sin_b, second_half * cos_b - first_half * sin_b],
        axis=-1,
    )


def block_shards(
    tokens,
    norm1_gain,
    norm1_bias,
    w_query,
    w_key,
    w_value,
    w_out,
    norm2_gain,
    norm2_bias,
    w_gate,
    w_up,
    w_down,
    out_grad,
    masked_rows,
    window_counts,
):
    rows_local, windows, model_width = tokens.shape
    span_rows = rows_local * lax.axis_size("tensor")
    seq_index = lax.axis_index("seq")
    tensor_index = lax.axis_index("tensor")
    head_width = w_query.shape[1]
    heads_local = head_width // HEAD_DIM
    score_scale = 1.0 / math.sqrt(HEAD_DIM)
    head_shape = (span_rows, windows, heads_local, HEAD_DIM)
    residual = tokens.astype(jnp.float32)
    normed1, inv_std1 = layer_stats(residual)
    first_low = (normed1 * norm1_gain + norm1_bias).astype(jnp.bfloat16)
    first_full = lax.all_gather(first_low, "tensor", axis=0, tiled=True)
    w_joined = jnp.concatenate([w_query, w_key, w_value], axis=1)
    projected = jnp.einsum("rwd,de->rwe", first_full, w_joined, preferred_element_type=jnp.float32)
    positions = seq_index * span_rows + jnp.arange(span_rows)
    cosine, sine = rotary_tables(positions)
    queries = rotate(projected[..., :head_width].reshape(head_shape), cosine, sine).astype(
        jnp.bfloat16
    )
    keys_rot = (
        rotate(projected[..., head_width : 2 * head_width].reshape(head_shape), cosine, sine)
        .astype(jnp.bfloat16)
        .reshape(span_rows, windows, head_width)
    )
    values_own = projected[..., 2 * head_width :].astype(jnp.bfloat16)
    keys_all, values_all = (
        lax.all_gather(keys_rot, "seq", axis=0, tiled=True),
        lax.all_gather(values_own, "seq", axis=0, tiled=True),
    )
    key_heads = keys_all.reshape(-1, windows, heads_local, HEAD_DIM)
    value_heads = values_all.reshape(-1, windows, heads_local, HEAD_DIM)
    scores = (
        jnp.einsum("qwhd,kwhd->whqk", queries, key_heads, preferred_element_type=jnp.float32)
        * score_scale
    )
    row_max = jnp.max(scores, axis=-1, keepdims=True)
    row_sum = jnp.sum(jnp.exp(scores - row_max), axis=-1, keepdims=True)
    log_norm = row_max + jnp.log(row_sum)
    attn_prob = jnp.exp(scores - log_norm)
    prob_low = attn_prob.astype(jnp.bfloat16)
    attended = (
        jnp.einsum("whqk,kwhd->qwhd", prob_low, value_heads, preferred_element_type=jnp.float32)
        .reshape(span_rows, windows, head_width)
        .astype(jnp.bfloat16)
    )
    block_part = attended
    attn_branch = lax.psum_scatter(
        jnp.einsum("rwe,ed->rwd", block_part, w_out, preferred_element_type=jnp.float32).astype(
            jnp.bfloat16
        ),
        "tensor",
        scatter_dimension=0,
        tiled=True,
    ).astype(jnp.float32)
    residual2 = residual + attn_branch
    normed2, inv_std2 = layer_stats(residual2)
    second_low = (normed2 * norm2_gain + norm2_bias).astype(jnp.bfloat16)
    second_full = lax.all_gather(second_low, "tensor", axis=0, tiled=True)
    gate_proj = jnp.einsum("rwd,df->rwf", second_full, w_gate, preferred_element_type=jnp.float32)
    up_proj = jnp.einsum("rwd,df->rwf", second_full, w_up, preferred_element_type=jnp.float32)
    hidden = (jax.nn.silu(gate_proj) * up_proj).astype(jnp.bfloat16)
    block_part = hidden
    ffn_branch = lax.psum_scatter(
        jnp.einsum("rwf,fd->rwd", block_part, w_down, preferred_element_type=jnp.float32).astype(
            jnp.bfloat16
        ),
        "tensor",
        scatter_dimension=0,
        tiled=True,
    ).astype(jnp.float32)
    output = (residual2 + ffn_branch).astype(jnp.bfloat16)
    live_slot = jnp.arange(windows) < window_counts[0]
    valid_slot = (masked_rows < L) & live_slot[:, None]
    local_masked = jnp.sum(jnp.where(valid_slot, 1, 0)).astype(jnp.int32)
    total_masked = lax.psum(local_masked, "dp")
    loss_weight = LOSS_SCALE / total_masked.astype(jnp.float32)
    own_positions = seq_index * span_rows + tensor_index * rows_local + jnp.arange(rows_local)
    matches = (masked_rows[:, None, :] == own_positions[None, :, None]) & live_slot[:, None, None]
    picked = jnp.einsum(
        "wrm,wmd->rwd", matches.astype(jnp.bfloat16), out_grad, preferred_element_type=jnp.float32
    )
    grad_out = picked * loss_weight
    grad_down_in = lax.all_gather(grad_out.astype(jnp.bfloat16), "tensor", axis=0, tiled=True)
    grad_w_down = jnp.einsum(
        "rwf,rwd->fd", hidden, grad_down_in, preferred_element_type=jnp.float32
    )
    grad_hidden = jnp.einsum(
        "rwd,fd->rwf", grad_down_in, w_down, preferred_element_type=jnp.float32
    )
    sigmoid_gate = jax.nn.sigmoid(gate_proj)
    silu_gate = gate_proj * sigmoid_gate
    grad_gate = (
        grad_hidden * up_proj * sigmoid_gate * (1.0 + gate_proj * (1.0 - sigmoid_gate))
    ).astype(jnp.bfloat16)
    grad_up = (grad_hidden * silu_gate).astype(jnp.bfloat16)
    grad_w_gate = jnp.einsum(
        "rwd,rwf->df", second_full, grad_gate, preferred_element_type=jnp.float32
    )
    grad_w_up = jnp.einsum("rwd,rwf->df", second_full, grad_up, preferred_element_type=jnp.float32)
    grad_second = lax.psum_scatter(
        (
            jnp.einsum("rwf,df->rwd", grad_gate, w_gate, preferred_element_type=jnp.float32)
            + jnp.einsum("rwf,df->rwd", grad_up, w_up, preferred_element_type=jnp.float32)
        ).astype(jnp.bfloat16),
        "tensor",
        scatter_dimension=0,
        tiled=True,
    ).astype(jnp.float32)
    grad_norm2_gain = jnp.sum(grad_second * normed2, axis=(0, 1))
    grad_norm2_bias = jnp.sum(grad_second, axis=(0, 1))
    grad_residual2 = grad_out + norm_back(grad_second, normed2, inv_std2, norm2_gain)
    grad_attn_in = lax.all_gather(grad_residual2.astype(jnp.bfloat16), "tensor", axis=0, tiled=True)
    grad_w_out = jnp.einsum(
        "rwe,rwd->ed", attended, grad_attn_in, preferred_element_type=jnp.float32
    )
    grad_attended = jnp.einsum(
        "rwd,ed->rwe", grad_attn_in, w_out, preferred_element_type=jnp.float32
    ).astype(jnp.bfloat16)
    grad_att_heads = grad_attended.reshape(head_shape)
    scores_again = (
        jnp.einsum("qwhd,kwhd->whqk", queries, key_heads, preferred_element_type=jnp.float32)
        * score_scale
    )
    probs_again = jnp.exp(scores_again - log_norm)
    grad_probs = jnp.einsum(
        "qwhd,kwhd->whqk", grad_att_heads, value_heads, preferred_element_type=jnp.float32
    )
    row_delta = jnp.sum(probs_again * grad_probs, axis=-1, keepdims=True)
    grad_scores = (probs_again * (grad_probs - row_delta)).astype(jnp.bfloat16)
    grad_queries = (
        jnp.einsum("whqk,kwhd->qwhd", grad_scores, key_heads, preferred_element_type=jnp.float32)
        * score_scale
    )
    grad_key_all = (
        jnp.einsum("whqk,qwhd->kwhd", grad_scores, queries, preferred_element_type=jnp.float32)
        * score_scale
    ).reshape(-1, windows, head_width)
    grad_value_all = jnp.einsum(
        "whqk,qwhd->kwhd",
        probs_again.astype(jnp.bfloat16),
        grad_att_heads,
        preferred_element_type=jnp.float32,
    ).reshape(-1, windows, head_width)
    grad_keys, grad_values = (
        lax.psum_scatter(
            grad_key_all.astype(jnp.bfloat16), "seq", scatter_dimension=0, tiled=True
        ).astype(jnp.float32),
        lax.psum_scatter(
            grad_value_all.astype(jnp.bfloat16), "seq", scatter_dimension=0, tiled=True
        ).astype(jnp.float32),
    )
    grad_query_lin = (
        unrotate(grad_queries, cosine, sine)
        .reshape(span_rows, windows, head_width)
        .astype(jnp.bfloat16)
    )
    grad_key_lin = (
        unrotate(grad_keys.reshape(head_shape), cosine, sine)
        .reshape(span_rows, windows, head_width)
        .astype(jnp.bfloat16)
    )
    grad_value_lin = grad_values.astype(jnp.bfloat16)
    grad_joined = jnp.concatenate([grad_query_lin, grad_key_lin, grad_value_lin], axis=-1)
    grad_w_joined = jnp.einsum(
        "rwd,rwe->de", first_full, grad_joined, preferred_element_type=jnp.float32
    )
    grad_w_query = grad_w_joined[:, :head_width]
    grad_w_key = grad_w_joined[:, head_width : 2 * head_width]
    grad_w_value = grad_w_joined[:, 2 * head_width :]
    block_part = grad_joined
    grad_first = lax.psum_scatter(
        jnp.einsum("rwe,de->rwd", block_part, w_joined, preferred_element_type=jnp.float32).astype(
            jnp.bfloat16
        ),
        "tensor",
        scatter_dimension=0,
        tiled=True,
    ).astype(jnp.float32)
    grad_norm1_gain = jnp.sum(grad_first * normed1, axis=(0, 1))
    grad_norm1_bias = jnp.sum(grad_first, axis=(0, 1))
    grad_tokens = grad_residual2 + norm_back(grad_first, normed1, inv_std1, norm1_gain)
    summed = (
        lax.psum_scatter(
            grad_w_query.astype(jnp.bfloat16), ("dp", "seq"), scatter_dimension=0, tiled=True
        ).astype(jnp.float32),
        lax.psum_scatter(
            grad_w_key.astype(jnp.bfloat16), ("dp", "seq"), scatter_dimension=0, tiled=True
        ).astype(jnp.float32),
        lax.psum_scatter(
            grad_w_value.astype(jnp.bfloat16), ("dp", "seq"), scatter_dimension=0, tiled=True
        ).astype(jnp.float32),
        lax.psum_scatter(
            grad_w_out.astype(jnp.bfloat16), ("dp", "seq"), scatter_dimension=1, tiled=True
        ).astype(jnp.float32),
        lax.psum_scatter(
            grad_w_gate.astype(jnp.bfloat16), ("dp", "seq"), scatter_dimension=0, tiled=True
        ).astype(jnp.float32),
        lax.psum_scatter(
            grad_w_up.astype(jnp.bfloat16), ("dp", "seq"), scatter_dimension=0, tiled=True
        ).astype(jnp.float32),
        lax.psum_scatter(
            grad_w_down.astype(jnp.bfloat16), ("dp", "seq"), scatter_dimension=1, tiled=True
        ).astype(jnp.float32),
    )
    norm_sums = (
        lax.psum_scatter(grad_norm1_gain, ("dp", "seq", "tensor"), scatter_dimension=0, tiled=True),
        lax.psum_scatter(grad_norm1_bias, ("dp", "seq", "tensor"), scatter_dimension=0, tiled=True),
        lax.psum_scatter(grad_norm2_gain, ("dp", "seq", "tensor"), scatter_dimension=0, tiled=True),
        lax.psum_scatter(grad_norm2_bias, ("dp", "seq", "tensor"), scatter_dimension=0, tiled=True),
    )
    return (
        output,
        grad_tokens,
        norm_sums[0],
        norm_sums[1],
        summed[0],
        summed[1],
        summed[2],
        summed[3],
        norm_sums[2],
        norm_sums[3],
        summed[4],
        summed[5],
        summed[6],
    )


BF = jnp.bfloat16
F32 = jnp.float32
LANES = 128
QUAD = 4


def dot_t(a, b):
    return lax.dot_general(a, b, (((1,), (1,)), ((), ())), preferred_element_type=F32)


def dot_n(a, b):
    return lax.dot_general(a, b, (((1,), (0,)), ((), ())), preferred_element_type=F32)


def t_dot(a, b):
    return lax.dot_general(a, b, (((0,), (0,)), ((), ())), preferred_element_type=F32)


def swap_halves(x):
    half = HEAD_DIM // 2
    lane = lax.broadcasted_iota(jnp.int32, x.shape, 1)
    down = pltpu.roll(x, half, 1)
    up = pltpu.roll(x, LANES - half, 1)
    return jnp.where(lane % HEAD_DIM < half, up, down)


def head_mask(h):
    lane = lax.broadcasted_iota(jnp.int32, (1, LANES), 1)
    return jnp.where(lane // HEAD_DIM == h, 1.0, 0.0).astype(BF)


MESH = pl.DeviceIdType.MESH


def any_spec():
    return pl.BlockSpec(memory_space=pl.ANY)


def greet(peers):
    barrier = pltpu.get_barrier_semaphore()
    for peer in peers:
        pl.semaphore_signal(barrier, inc=1, device_id=peer, device_id_type=MESH)
    pl.semaphore_wait(barrier, len(peers))


def remote(src, dst, send, recv, peer):
    return pltpu.make_async_remote_copy(
        src_ref=src, dst_ref=dst, send_sem=send, recv_sem=recv, device_id=peer, device_id_type=MESH
    )


def start_all(copies):
    for copy in copies:
        copy.start()


def wait_all(copies):
    for copy in copies:
        copy.wait()


def quad_place():
    dp, sx = lax.axis_index("dp"), lax.axis_index("seq")
    place = sx * 2 + dp % 2
    return place, lambda to: {"dp": dp // 2 * 2 + to % 2, "seq": to // 2}


def quad_peers():
    place, device = quad_place()
    return [device((place + j) % QUAD) for j in range(1, QUAD)]


class WeightRoute:
    def __init__(self, gathered, own, n_ten, send, recv):
        dp, sx, t = lax.axis_index("dp"), lax.axis_index("seq"), lax.axis_index("tensor")
        y, c = dp // 2, dp % 2
        gate_ref, up_ref, down_ref = gathered
        self.refs, self.own = (gate_ref, up_ref, down_ref, down_ref), own
        self.width, self.units = gate_ref.shape[0], gate_ref.shape[1] // n_ten
        self.send, self.recv, self.c = send, recv, c
        s_xy, s_yx = c * 4 + y * 2 + sx, c * 4 + sx * 2 + y
        self.slices = (s_xy, s_yx, s_xy, s_yx)
        self.x_peer, self.y_peer, self.c_peer = {"seq": 1 - sx}, {"dp": (dp + 2) % 4}, {"dp": 2 * y + 1 - c}
        side = t // 2
        middle = jnp.minimum(t, n_ten - 1 - t)
        mirror = lambda k: k + side * (n_ten - 1 - 2 * k)
        self.order = [mirror(k) for k in (middle, 1 - middle, 2, 3)]
        self.inward, self.outward = mirror(middle + 1), mirror(0)
        self.is_middle, self.is_end = middle == 1, middle == 0
        self.t, self.middle, self.mirror = t, middle, mirror

    def shard(self, ref, k, first, count, which):
        size, cols, units = self.width // 8, self.width // 2, self.units
        rows = pl.multiple_of(first * (size if k < 2 else units // 8), 16)
        if k < 2:
            at = 0 if which is None else pl.multiple_of(which * units, units)
            return ref.at[pl.ds(rows, count * size), pl.ds(at, units)]
        at = rows if which is None else pl.multiple_of(which * units + rows, 16)
        return ref.at[pl.ds(at, count * (units // 8)), pl.ds((k - 2) * cols, cols)]

    def along(self, which, to, slot, number, own=False):
        copies = []
        for k in range(4):
            dst = self.shard(self.refs[k], k, self.slices[k], 1, which)
            src = self.shard(self.own[min(k, 2)], k, self.slices[k], 1, None) if own else dst
            copies.append(remote(src, dst, self.send.at[number, k], self.recv.at[slot, k], {"tensor": to}))
        return copies

    def to_in(self):
        return self.along(self.t, self.inward, 1 + self.middle, 0, True)

    def to_out(self):
        return self.along(self.t, self.outward, 1, 1, True)

    def in_far(self):
        return self.along(self.mirror(0), self.inward, 3, 2)

    def out_two(self):
        return self.along(self.mirror(2), self.outward, 2, 3)

    def out_three(self):
        return self.along(self.mirror(3), self.outward, 3, 4)

    def arrived(self, i):
        received(self.along(self.order[i], self.inward, i, 0))

    def hop(self, i, h):
        copies = []
        for k in range(4):
            xy = k % 2 == 0
            peer, first, count = (
                (self.x_peer if xy else self.y_peer, self.slices[k], 1),
                (self.y_peer if xy else self.x_peer, self.slices[k] // 2 * 2, 2),
                (self.c_peer, self.c * 4, 4),
            )[h]
            ref = self.shard(self.refs[k], k, first, count, self.order[i])
            copies.append(remote(ref, ref, self.send.at[2 + 3 * i + h, k], self.recv.at[1 + 3 * i + h, k], peer))
        return copies


def received(copies):
    for copy in copies:
        copy.wait_recv()


def sent_all(copies):
    for copy in copies:
        copy.wait_send()


def route_sems():
    return [pltpu.SemaphoreType.DMA((14, 4)), pltpu.SemaphoreType.DMA((13, 4))]


def exchange_in_kernel(
    sizes, tok_ref, wq_ref, wk_ref, wv_ref, wo_ref, count_ref, rows_ref, x_ref, q_ref, k_ref, v_ref, o_ref, counts_ref,
    peer_rows_ref, tok_send, tok_recv, w_send, w_recv, count_send, count_recv, rows_send, rows_recv, local_sem,
):
    n_seq, n_ten, half, rows, slices = sizes
    dp, sx, t = lax.axis_index("dp"), lax.axis_index("seq"), lax.axis_index("tensor")
    y, c = dp // 2, dp % 2
    me = sx * n_ten + t
    group = n_seq * n_ten
    others = []
    for i in range(1, group):
        g = (me + i) % group
        others.append((g // n_ten, g % n_ten))
    y_peer, c_peer, x_peer = {"dp": (dp + 2) % 4}, {"dp": 2 * y + 1 - c}, {"seq": 1 - sx}
    dp_peers = [{"dp": (dp + i) % 4} for i in range(1, 4)]
    beside = [{"dp": 2 * y + 1 - c, "tensor": (t + j) % n_ten} for j in range(1, n_ten)]
    greet([{"seq": a, "tensor": b} for a, b in others] + dp_peers + beside)
    counts = [
        remote(count_ref, counts_ref.at[dp], count_send.at[i], count_recv.at[i], peer) for i, peer in enumerate(dp_peers)
    ]
    start_all(counts)

    hw = wq_ref.shape[1]
    srow, orow = wq_ref.shape[0] // slices, hw // slices
    s_xy, s_yx = c * 4 + y * 2 + sx, c * 4 + sx * 2 + y
    weights = ((wq_ref, q_ref, s_xy, 0), (wk_ref, k_ref, s_xy, 0), (wv_ref, v_ref, s_yx, 0), (wo_ref, o_ref, s_yx, 1))

    def block(out, by_rows, base, count, which):
        if by_rows:
            return out.at[pl.ds(pl.multiple_of(which * hw + base * orow, orow), count * orow), :]
        return out.at[
            pl.ds(pl.multiple_of(base * srow, srow), count * srow), pl.ds(pl.multiple_of(which * hw, hw), hw)
        ]

    stage = [[], [], [], []]
    n = 0
    for j in range(1, n_ten):
        peer = {"tensor": (t + j) % n_ten}
        for w_ref, out, s, by_rows in weights:
            size = orow if by_rows else srow
            src = w_ref.at[pl.ds(pl.multiple_of(s * size, size), size), :]
            stage[0].append(remote(src, block(out, by_rows, s, 1, t), w_send.at[0, n], w_recv.at[0, n], peer))
            n += 1
    n = 0
    for j in range(1, n_ten):
        which = (t + j) % n_ten
        for w_ref, out, s, by_rows in weights:
            xy = s is s_xy
            hops = (
                (1, x_peer if xy else y_peer, s, 1),
                (2, y_peer if xy else x_peer, s // 2 * 2, 2),
                (3, c_peer, c * 4, 4),
            )
            for k, peer, base, count in hops:
                ref = block(out, by_rows, base, count, which)
                stage[k].append(remote(ref, ref, w_send.at[k, n], w_recv.at[k, n], peer))
            n += 1
    start_all(stage[0])

    tokens = []
    for i, (a, b) in enumerate(others):
        tokens.append(
            remote(
                tok_ref.at[a * half + b],
                x_ref.at[pl.ds(pl.multiple_of(me * rows, rows), rows), :],
                tok_send.at[i], tok_recv.at[i], {"seq": a, "tensor": b},
            )
        )
    shared = []
    for i in range(n_seq):
        src, dst = tok_ref.at[i * half + n_ten], x_ref.at[pl.ds(pl.multiple_of((group + t % 2) * rows, rows), rows), :]
        shared.append(
            (
                2 * c + i == t,
                remote(
                    src, dst, tok_send.at[group - 1 + i], tok_recv.at[group - 1 + t % 2],
                    {"dp": 2 * y + t // 2, "tensor": 2 * c + i},
                ),
                pltpu.make_async_copy(src, dst, local_sem.at[1]),
            )
        )
    arriving = [
        remote(
            tok_ref.at[n_ten], x_ref.at[pl.ds((group + i) * rows, rows), :],
            tok_send.at[group - 1], tok_recv.at[group - 1 + i], c_peer,
        )
        for i in range(n_seq)
    ]
    start_all(tokens)
    for here, away, near in shared:
        pl.when(here)(near.start)
        pl.when(jnp.logical_not(here))(away.start)
    peer_rows = [
        remote(rows_ref.at[i * half + n_ten], peer_rows_ref.at[2 * c + i], rows_send.at[i], rows_recv.at[i], c_peer)
        for i in range(n_seq)
    ]
    start_all(peer_rows)
    local = [
        pltpu.make_async_copy(
            tok_ref.at[sx * half + t], x_ref.at[pl.ds(pl.multiple_of(me * rows, rows), rows), :], local_sem.at[0]
        ),
    ]
    for i, (w_ref, out, s, by_rows) in enumerate(weights):
        local.append(pltpu.make_async_copy(w_ref, block(out, by_rows, 0, slices, t), local_sem.at[2 + i]))
    local.append(pltpu.make_async_copy(count_ref, counts_ref.at[dp], local_sem.at[6]))
    for i in range(n_seq):
        local.append(
            pltpu.make_async_copy(rows_ref.at[i * half + n_ten], peer_rows_ref.at[2 * c + i], local_sem.at[7 + i])
        )
    start_all(local)
    for k in range(1, 4):
        for earlier in stage[k - 1]:
            earlier.wait_recv()
        start_all(stage[k])
    for copy in stage[3]:
        copy.wait_recv()
    for copies in stage:
        for copy in copies:
            copy.wait_send()
    wait_all(local)
    wait_all(counts)
    wait_all(peer_rows)
    wait_all(tokens)
    for here, away, near in shared:
        pl.when(here)(near.wait)
        pl.when(jnp.logical_not(here))(away.wait_send)
    for i in range(n_seq):
        pl.when(jnp.logical_not((t // 2 == c) & (t % 2 == i)))(arriving[i].wait_recv)


def exchange_in(tok, w_query, w_key, w_value, w_out, count, out_grad, n_dp, n_seq, n_ten):
    windows, rows, width = tok.shape
    slices = n_dp * n_seq
    vmem = pl.BlockSpec(memory_space=pltpu.VMEM)
    square = jax.ShapeDtypeStruct((width, width), BF)
    group = n_seq * n_ten
    return pl.pallas_call(
        functools.partial(exchange_in_kernel, (n_seq, n_ten, windows // n_seq, rows, slices)),
        in_specs=[vmem] * 6 + [any_spec()],
        out_specs=[any_spec()] * 7,
        out_shape=[jax.ShapeDtypeStruct(((group + n_seq) * rows, width), BF)]
        + [square] * 4
        + [jax.ShapeDtypeStruct((n_dp,) + count.shape, count.dtype)]
        + [jax.ShapeDtypeStruct((2 * n_seq,) + out_grad.shape[1:], BF)],
        scratch_shapes=[
            pltpu.SemaphoreType.DMA((group + 1,)),
            pltpu.SemaphoreType.DMA((group + 1,)),
            pltpu.SemaphoreType.DMA((4, 4 * (n_ten - 1))),
            pltpu.SemaphoreType.DMA((4, 4 * (n_ten - 1))),
            pltpu.SemaphoreType.DMA((3,)),
            pltpu.SemaphoreType.DMA((3,)),
            pltpu.SemaphoreType.DMA((2,)),
            pltpu.SemaphoreType.DMA((2,)),
            pltpu.SemaphoreType.DMA((9,)),
        ],
        compiler_params=pltpu.CompilerParams(collective_id=0, has_side_effects=True),
        name="exchange_in",
    )(tok, w_query, w_key, w_value, w_out, count, out_grad)


def qkv_kernel(
    n_ten, x_ref, gain_ref, bias_ref, wq_ref, wk_ref, wv_ref, cos_ref, sin_ref, part_cos_ref, part_sin_ref,
    wg_ref, wu_ref, wd_ref, first_ref, q_ref, k_ref, v_ref, ag_ref, au_ref, ad_ref, send, recv,
):
    route = WeightRoute((ag_ref, au_ref, ad_ref), (wg_ref, wu_ref, wd_ref), n_ten, send, recv)

    @pl.when(pl.program_id(0) == 0)
    def _():
        greet([{"tensor": (route.t + j) % n_ten} for j in range(1, n_ten)])
        start_all(route.to_in())

        @pl.when(route.is_middle)
        def _():
            start_all(route.to_out())

    shared = pl.program_id(0) == pl.num_programs(0) - 1
    normed, _ = layer_stats(x_ref[...].astype(F32))
    first_ref[...] = (normed * gain_ref[...] + bias_ref[...]).astype(BF)
    cos = jnp.where(shared, part_cos_ref[...], cos_ref[...])
    sin = jnp.where(shared, part_sin_ref[...], sin_ref[...])
    wide = 256
    for w_ref, out_ref, scale in ((wq_ref, q_ref, 1.0 / math.sqrt(HEAD_DIM)), (wk_ref, k_ref, 1.0), (wv_ref, v_ref, None)):
        for at in range(0, w_ref.shape[1], wide):
            acc = dot_n(first_ref[...], w_ref[:, at : at + wide])
            for c in range(0, wide, LANES):
                part = acc[:, c : c + LANES]
                if scale is not None:
                    part = (part * cos + swap_halves(part) * sin) * scale
                out_ref[:, at + c : at + c + LANES] = part.astype(BF)

    @pl.when(shared)
    def _():
        route.arrived(1)
        sent_all(route.to_in())

        @pl.when(route.is_middle)
        def _():
            route.arrived(2)
            sent_all(route.to_out())


def once(shape):
    return pl.BlockSpec(shape, lambda *_: (0,) * len(shape), pipeline_mode=pl.Buffered(1))


def norm_qkv(x, gain, bias, w_query, w_key, w_value, tables, part_tables, ffn, n_ten):
    rows, width = x.shape
    tile = 256
    row = pl.BlockSpec((tile, width), lambda r: (r, 0))
    own = tables[0].shape[0] // tile
    table = pl.BlockSpec((tile, LANES), lambda r: (jnp.minimum(r, own - 1), 0))
    return pl.pallas_call(
        functools.partial(qkv_kernel, n_ten),
        grid=(rows // tile,),
        in_specs=[row, once((1, width)), once((1, width))] + [once((width, width))] * 3 + [table, table] + [once((tile, LANES))] * 2 + [any_spec()] * 3,
        out_specs=[row] * 4 + [any_spec()] * 3,
        out_shape=[jax.ShapeDtypeStruct((rows, width), BF)] * 4
        + [
            jax.ShapeDtypeStruct((width, n_ten * ffn[0].shape[1]), BF),
            jax.ShapeDtypeStruct((width, n_ten * ffn[1].shape[1]), BF),
            jax.ShapeDtypeStruct((n_ten * ffn[2].shape[0], width), BF),
        ],
        scratch_shapes=route_sems(),
        compiler_params=pltpu.CompilerParams(collective_id=7, has_side_effects=True),
        cost_estimate=pl.CostEstimate(flops=6 * rows * width * width, bytes_accessed=16 * rows * width, transcendentals=0),
        name="norm_qkv",
    )(x, gain.reshape(1, width), bias.reshape(1, width), w_query, w_key, w_value, *tables, *part_tables, *ffn)


def attend_body(q_ref, k_ref, v_ref):
    q, k, v = q_ref[...], k_ref[...], v_ref[...]
    outs = []
    for h in range(LANES // HEAD_DIM):
        s = dot_t(q * head_mask(h), k)
        p = jnp.exp(s - jnp.max(s, axis=1, keepdims=True))
        norm = jnp.sum(p, axis=1, keepdims=True)
        outs.append(dot_n(p.astype(BF), v) / norm)
    lane = lax.broadcasted_iota(jnp.int32, outs[0].shape, 1)
    return jnp.where(lane < HEAD_DIM, outs[0], outs[1]).astype(BF)


def attend_specs(rows, tile):
    return [
        pl.BlockSpec((tile, LANES), lambda p, r: (r, p)),
        pl.BlockSpec((rows, LANES), lambda p, r: (0, p)),
        pl.BlockSpec((rows, LANES), lambda p, r: (0, p)),
    ]


def attend_cost(rows, pairs):
    return pl.CostEstimate(
        flops=16 * pairs * rows * rows * LANES, bytes_accessed=8 * rows * pairs * LANES, transcendentals=2 * pairs * rows * rows
    )


def attend_left_kernel(
    n_ten, q_ref, k_ref, v_ref, ag_in, au_in, ad_in, part_ref, ag_ref, au_ref, ad_ref, buf, send, recv, local_sem,
    route_send, route_recv,
):
    place, device = quad_place()
    r, p = pl.program_id(0), pl.program_id(1)
    last_pair = p == pl.num_programs(1) - 1
    hw = buf.shape[2]
    dst = part_ref.at[:, pl.ds(pl.multiple_of(place * hw, hw), hw)]
    route = WeightRoute((ag_ref, au_ref, ad_ref), None, n_ten, route_send, route_recv)
    hops = route.hop(1, 2) + route.hop(2, 0)

    @pl.when((p == 0) & (r == 0))
    def _():
        greet(quad_peers() + [route.y_peer])
        start_all(hops)

    buf[r, :, pl.ds(pl.multiple_of(p * LANES, LANES), LANES)] = attend_body(q_ref, k_ref, v_ref)

    def copy_to(j):
        to = (place + j) % QUAD
        return remote(buf.at[to], dst, send.at[j - 1], recv.at[j - 1], device(to))

    own = pltpu.make_async_copy(buf.at[place], dst, local_sem.at[0])
    for j in range(1, QUAD):
        pl.when(last_pair & (r == (place + j) % QUAD))(copy_to(j).start)
    pl.when(last_pair & (r == place))(own.start)

    @pl.when(last_pair & (r == QUAD - 1))
    def _():
        wait_all([copy_to(j) for j in range(1, QUAD)])
        own.wait()
        wait_all(hops)


def attend_left(q, k, v, gathered, n_ten):
    rows, hw = q.shape
    tile, pairs = rows // QUAD, hw // LANES
    column = pl.BlockSpec((rows, LANES), lambda r, p: (0, p))
    return pl.pallas_call(
        functools.partial(attend_left_kernel, n_ten),
        grid=(QUAD, pairs),
        in_specs=[pl.BlockSpec((tile, LANES), lambda r, p: (r, p)), column, column] + [any_spec()] * 3,
        out_specs=[any_spec()] * 4,
        out_shape=[jax.ShapeDtypeStruct((tile, QUAD * hw), BF)] + [jax.ShapeDtypeStruct(w.shape, BF) for w in gathered],
        input_output_aliases={3: 1, 4: 2, 5: 3},
        scratch_shapes=[pltpu.VMEM((QUAD, tile, hw), BF)]
        + [pltpu.SemaphoreType.DMA((QUAD - 1,))] * 2
        + [pltpu.SemaphoreType.DMA((1,))]
        + route_sems(),
        compiler_params=pltpu.CompilerParams(collective_id=3, has_side_effects=True),
        cost_estimate=attend_cost(rows, pairs),
        name="attend_left",
    )(q, k, v, *gathered)


def swap_part(refs, outs, send, recv, local_sem, base):
    place, device = quad_place()
    share, hw = outs[0].shape[0] // QUAD, outs[0].shape[1]
    copies, local = [], []
    rows = pl.ds(base, share)
    mine = pl.ds(pl.multiple_of(place * share, share), share)
    for i, (ref, out) in enumerate(zip(refs, outs, strict=True)):
        for j in range(1, QUAD):
            to = (place + j) % QUAD
            src = ref.at[rows, pl.ds(pl.multiple_of(to * hw, hw), hw)]
            copies.append(remote(src, out.at[mine, :], send.at[i, j - 1], recv.at[i, j - 1], device(to)))
        src = ref.at[rows, pl.ds(pl.multiple_of(place * hw, hw), hw)]
        local.append(pltpu.make_async_copy(src, out.at[mine, :], local_sem.at[i]))
    return copies, local


def attend_swap_kernel(
    n_ten, length, q_ref, k_ref, v_ref, q_all, k_all, v_all, ag_in, au_in, ad_in, o_ref, lq_ref, lk_ref, lv_ref,
    ag_ref, au_ref, ad_ref, send, recv, local_sem, route_send, route_recv,
):
    step = pl.program_id(0) * pl.num_programs(1) + pl.program_id(1)
    steps = pl.num_programs(0) * pl.num_programs(1)
    copies, local = swap_part((q_all, k_all, v_all), (lq_ref, lk_ref, lv_ref), send, recv, local_sem, length)
    route = WeightRoute((ag_ref, au_ref, ad_ref), None, n_ten, route_send, route_recv)

    @pl.when(step == 0)
    def _():
        greet(quad_peers() + [route.y_peer] + [{"tensor": (route.t + j) % n_ten} for j in range(1, n_ten)])
        start_all(route.hop(1, 0))

        @pl.when(route.is_middle)
        def _():
            start_all(route.in_far())
            start_all(route.out_two())

        start_all(copies + local)

    o_ref[...] = attend_body(q_ref, k_ref, v_ref)

    @pl.when(step == steps // 4)
    def _():
        received(route.hop(1, 0))
        start_all(route.hop(1, 1))

    @pl.when(step == steps // 2)
    def _():
        @pl.when(route.is_middle)
        def _():
            route.arrived(3)
            start_all(route.out_three())

    @pl.when(step == steps - 1)
    def _():
        wait_all(copies + local)
        received(route.hop(1, 1))
        sent_all(route.hop(1, 0) + route.hop(1, 1))

        @pl.when(route.is_middle)
        def _():
            sent_all(route.in_far() + route.out_two() + route.out_three())

        @pl.when(route.is_end)
        def _():
            route.arrived(2)
            route.arrived(3)


def attend_swap(q, k, v, gathered, length, n_ten):
    width = q.shape[1]
    tile, pairs, hw = 512, width // LANES, width // QUAD
    left = jax.ShapeDtypeStruct((length, hw), BF)
    return pl.pallas_call(
        functools.partial(attend_swap_kernel, n_ten, length),
        grid=(pairs, length // tile),
        in_specs=attend_specs(length, tile) + [any_spec()] * 6,
        out_specs=[pl.BlockSpec((tile, LANES), lambda p, r: (r, p))] + [any_spec()] * 6,
        out_shape=[jax.ShapeDtypeStruct((length, width), BF), left, left, left]
        + [jax.ShapeDtypeStruct(w.shape, BF) for w in gathered],
        input_output_aliases={6: 4, 7: 5, 8: 6},
        scratch_shapes=[
            pltpu.SemaphoreType.DMA((3, QUAD - 1)),
            pltpu.SemaphoreType.DMA((3, QUAD - 1)),
            pltpu.SemaphoreType.DMA((3,)),
        ]
        + route_sems(),
        compiler_params=pltpu.CompilerParams(collective_id=1, has_side_effects=True),
        cost_estimate=attend_cost(length, pairs),
        name="attend_swap",
    )(q, k, v, q, k, v, *gathered)


def back_body(q_ref, g_ref, k_ref, v_ref, pick_ref, cos_ref, sin_ref, qcos_ref, qsin_ref):
    g, k, v, pick = g_ref[...], k_ref[...], v_ref[...], pick_ref[...]
    q = dot_n(pick, q_ref[...]).astype(BF)
    dq = []
    all_p, all_ds, all_q, all_g = [], [], [], []
    for h in range(LANES // HEAD_DIM):
        mask = head_mask(h)
        qh, gh = q * mask, g * mask
        s = dot_t(qh, k)
        p = jnp.exp(s - jnp.max(s, axis=1, keepdims=True))
        p = p / jnp.sum(p, axis=1, keepdims=True)
        dp = dot_t(gh, v)
        ds = (p * (dp - jnp.sum(p * dp, axis=1, keepdims=True))).astype(BF)
        dq.append(dot_n(ds, k))
        all_p.append(p.astype(BF))
        all_ds.append(ds)
        all_q.append(qh)
        all_g.append(gh)
    lane = lax.broadcasted_iota(jnp.int32, dq[0].shape, 1)
    dq = jnp.where(lane < HEAD_DIM, dq[0], dq[1]) * (1.0 / math.sqrt(HEAD_DIM))
    dq = (dq * qcos_ref[...] - swap_halves(dq) * qsin_ref[...]).astype(BF)
    dq = t_dot(pick, dq).astype(BF)
    dk = t_dot(jnp.concatenate(all_ds, axis=0), jnp.concatenate(all_q, axis=0))
    dk = (dk * cos_ref[...] - swap_halves(dk) * sin_ref[...]).astype(BF)
    dv = t_dot(jnp.concatenate(all_p, axis=0), jnp.concatenate(all_g, axis=0)).astype(BF)
    return dq, dk, dv


def back_kernel(q_ref, g_ref, k_ref, v_ref, pick_ref, cos_ref, sin_ref, qcos_ref, qsin_ref, dq_ref, dk_ref, dv_ref):
    dq_ref[...], dk_ref[...], dv_ref[...] = back_body(
        q_ref, g_ref, k_ref, v_ref, pick_ref, cos_ref, sin_ref, qcos_ref, qsin_ref
    )


def back_specs(length, masked):
    full = pl.BlockSpec((length, LANES), lambda p: (0, p))
    same = pl.BlockSpec((length, LANES), lambda p: (0, 0))
    row_same = pl.BlockSpec((masked, LANES), lambda p: (0, 0))
    return [
        full, pl.BlockSpec((masked, LANES), lambda p: (0, p)), full, full,
        pl.BlockSpec((masked, length), lambda p: (0, 0)), same, same, row_same, row_same,
    ]


def back_cost(length, masked, pairs):
    return pl.CostEstimate(
        flops=24 * pairs * length * masked * LANES, bytes_accessed=12 * length * pairs * LANES, transcendentals=2 * pairs * length * masked
    )


def back_left(q, grad_rows, k, v, pick, tables):
    masked, length = pick.shape
    width = q.shape[1]
    full = pl.BlockSpec((length, LANES), lambda p: (0, p))
    return pl.pallas_call(
        back_kernel,
        grid=(width // LANES,),
        in_specs=back_specs(length, masked),
        out_specs=[full] * 3,
        out_shape=[jax.ShapeDtypeStruct((length, width), BF)] * 3,
        cost_estimate=back_cost(length, masked, width // LANES),
        name="back_left",
    )(q, grad_rows, k, v, pick, *tables)


def back_swap_kernel(
    q_ref, g_ref, k_ref, v_ref, pick_ref, cos_ref, sin_ref, qcos_ref, qsin_ref, lq_ref, lk_ref, lv_ref,
    dq_ref, dk_ref, dv_ref, buf, out_sem, send, recv, local_sem,
):
    place, device = quad_place()
    step, steps = pl.program_id(0), pl.num_programs(0)
    length = q_ref.shape[0]
    share, hw = lq_ref.shape[0] // QUAD, lq_ref.shape[1]
    outs = (dq_ref, dk_ref, dv_ref)
    copies, local = [], []
    mine = pl.ds(pl.multiple_of(place * hw, hw), hw)
    for i, (ref, out) in enumerate(zip((lq_ref, lk_ref, lv_ref), outs, strict=True)):
        dst = out.at[pl.ds(length, share), mine]
        for j in range(1, QUAD):
            to = (place + j) % QUAD
            src = ref.at[pl.ds(pl.multiple_of(to * share, share), share), :]
            copies.append(remote(src, dst, send.at[i, j - 1], recv.at[i, j - 1], device(to)))
        src = ref.at[pl.ds(pl.multiple_of(place * share, share), share), :]
        local.append(pltpu.make_async_copy(src, dst, local_sem.at[i]))

    def out_copy(at, i):
        slot = at % 2
        columns = pl.ds(pl.multiple_of(at * LANES, LANES), LANES)
        return pltpu.make_async_copy(buf.at[slot, i], outs[i].at[pl.ds(0, length), columns], out_sem.at[slot, i])

    @pl.when(step == 0)
    def _():
        greet(quad_peers())
        start_all(copies + local)

    @pl.when(step >= 2)
    def _():
        for i in range(3):
            out_copy(step - 2, i).wait()

    results = back_body(q_ref, g_ref, k_ref, v_ref, pick_ref, cos_ref, sin_ref, qcos_ref, qsin_ref)
    for i in range(3):
        buf[step % 2, i] = results[i]
        out_copy(step, i).start()

    @pl.when(step == steps - 1)
    def _():
        for i in range(3):
            out_copy(step - 1, i).wait()
            out_copy(step, i).wait()
        wait_all(copies + local)


def back_swap(q, grad_rows, k, v, pick, tables, left):
    masked, length = pick.shape
    width = q.shape[1]
    share = left[0].shape[0] // QUAD
    return pl.pallas_call(
        back_swap_kernel,
        grid=(width // LANES,),
        in_specs=back_specs(length, masked) + [any_spec()] * 3,
        out_specs=[any_spec()] * 3,
        out_shape=[jax.ShapeDtypeStruct((length + share, width), BF)] * 3,
        scratch_shapes=[
            pltpu.VMEM((2, 3, length, LANES), BF),
            pltpu.SemaphoreType.DMA((2, 3)),
            pltpu.SemaphoreType.DMA((3, QUAD - 1)),
            pltpu.SemaphoreType.DMA((3, QUAD - 1)),
            pltpu.SemaphoreType.DMA((3,)),
        ],
        compiler_params=pltpu.CompilerParams(collective_id=2, has_side_effects=True),
        cost_estimate=back_cost(length, masked, width // LANES),
        name="back_swap",
    )(q, grad_rows, k, v, pick, *tables, *left)


def feed_kernel(
    n_ten, tok_ref, att_ref, left_ref, wo_ref, gain_ref, bias_ref, pick_ref, part_pick_ref, cot_ref, wg_ref, wu_ref, wd_ref,
    ag_in, au_in, ad_in, out_ref, out_left_ref, att_m_ref, gr2_ref, gatt_ref, left_gatt_ref, vec_ref, all_own_ref, all_left_ref,
    ag_ref, au_ref, ad_ref,
    x_ref, acc_ref, normed_ref, inv_ref, grad_ref, g_buf, u_buf, d_buf, rows_buf, rows_parts, own_m, left_m, gatt_buf, gatt_parts,
    buf_sem, small_send, small_recv, line_send, line_recv, local_sem, send, recv,
):
    step, steps = pl.program_id(0), pl.num_programs(0)
    rows, width = tok_ref.shape
    length = att_ref.shape[0]
    masked = cot_ref.shape[0]
    slots = masked // 2
    unit = g_buf.shape[2]
    units = wg_ref.shape[1]
    per = units // unit
    part, hw = rows_buf.shape[1], gatt_parts.shape[2]
    gain = gain_ref[...]
    own = (wg_ref, wu_ref, wd_ref)
    route = WeightRoute((ag_ref, au_ref, ad_ref), own, n_ten, send, recv)
    order = route.order
    place, device = quad_place()
    rows_copies, gatt_copies = [], []
    for j in range(1, QUAD):
        to = (place + j) % QUAD
        rows_copies.append(
            remote(rows_buf.at[to], rows_parts.at[j - 1], small_send.at[0, j - 1], small_recv.at[0, j - 1], device(to))
        )
        src = gatt_buf.at[:, pl.ds(pl.multiple_of(to * hw, hw), hw)]
        gatt_copies.append(
            remote(src, gatt_parts.at[j - 1], small_send.at[1, j - 1], small_recv.at[1, j - 1], device(to))
        )

    line_copies = [[], []]
    local = []
    for n, (src, out) in enumerate(((own_m, all_own_ref), (left_m, all_left_ref))):
        for j in range(1, n_ten):
            to = (route.t + j) % n_ten
            line_copies[n].append(
                remote(src, out.at[route.t], line_send.at[n, j - 1], line_recv.at[n, j - 1], {"tensor": to})
            )
        local.append(pltpu.make_async_copy(src, out.at[route.t], local_sem.at[n]))

    def fetch(at):
        slot, i, b = at % 2, at // per, at % per

        def make(refs, shard_at):
            base = pl.multiple_of(shard_at * units + b * unit, unit)
            return [
                pltpu.make_async_copy(refs[0].at[:, pl.ds(base, unit)], g_buf.at[slot], buf_sem.at[slot, 0]),
                pltpu.make_async_copy(refs[1].at[:, pl.ds(base, unit)], u_buf.at[slot], buf_sem.at[slot, 1]),
                pltpu.make_async_copy(refs[2].at[pl.ds(base, unit), :], d_buf.at[slot], buf_sem.at[slot, 2]),
            ]

        @pl.when(i == 0)
        def _():
            start_all(make(own, 0))

        @pl.when(i > 0)
        def _():
            which = order[1] * (i == 1) + order[2] * (i == 2) + order[3] * (i == 3)
            start_all(make((ag_ref, au_ref, ad_ref), which))

    def fetched(at):
        slot = at % 2
        wait_all(
            [
                pltpu.make_async_copy(wg_ref.at[:, pl.ds(0, unit)], g_buf.at[slot], buf_sem.at[slot, 0]),
                pltpu.make_async_copy(wu_ref.at[:, pl.ds(0, unit)], u_buf.at[slot], buf_sem.at[slot, 1]),
                pltpu.make_async_copy(wd_ref.at[pl.ds(0, unit), :], d_buf.at[slot], buf_sem.at[slot, 2]),
            ]
        )

    def norm(res):
        normed, inv_std = layer_stats(res)
        return normed, inv_std, (normed * gain + bias_ref[...]).astype(BF)

    @pl.when(step == 0)
    def _():
        greet(quad_peers() + [route.y_peer] + [{"tensor": (route.t + j) % n_ten} for j in range(1, n_ten)])
        start_all(route.hop(2, 1))
        start_all(route.hop(3, 0))
        fetch(0)
        tile = rows - length
        for i, (pick, att, tok) in enumerate(
            ((pick_ref[...], att_ref[...], tok_ref[:length, :]), (part_pick_ref[...], left_ref[...], tok_ref[length:, :]))
        ):
            here = slice(i * slots, (i + 1) * slots)
            att_m = dot_n(pick, att).astype(BF)
            att_m_ref[here, :] = att_m
            normed, inv_std, low = norm(dot_n(pick, tok) + dot_n(att_m, wo_ref[...]))
            normed_ref[here, :] = normed
            inv_ref[here, :] = jnp.broadcast_to(inv_std, (slots, LANES))
            here_too = jnp.sum(pick.astype(F32), axis=1, keepdims=True) > 0.0
            low = jnp.where(here_too, low.astype(F32), 0.0)
            x_ref[rows + i * slots : rows + (i + 1) * slots, :] = low.astype(BF)
            if i == 0:
                own_m[...] = low.astype(BF)
            else:
                for k in range(QUAD):
                    rows_buf[k] = low[k * part : (k + 1) * part, :].astype(BF)
        for at in range(0, rows, tile):
            att = att_ref[at : at + tile, :] if at < length else left_ref[...]
            res = tok_ref[at : at + tile, :].astype(F32) + dot_n(att, wo_ref[...])
            x_ref[at : at + tile, :] = norm(res)[2]
            acc_ref[at : at + tile, :] = res
        grad_ref[...] = jnp.zeros_like(grad_ref)

    fetched(step)

    @pl.when((step + 1 < steps) & ((step + 1) % per != 0))
    def _():
        fetch(step + 1)

    slot = step % 2
    x = x_ref[...]
    w_g, w_u, w_d = g_buf[slot], u_buf[slot], d_buf[slot]
    gate, up = dot_n(x, w_g), dot_n(x, w_u)
    sig = jax.nn.sigmoid(gate)
    act = gate * sig
    hidden = (act[:rows] * up[:rows]).astype(BF)
    for at in range(0, width, unit):
        acc_ref[:, at : at + unit] += dot_n(hidden, w_d[:, at : at + unit])
    back = dot_t(cot_ref[...].astype(BF), w_d)
    gate, up, sig, act = gate[rows:], up[rows:], sig[rows:], act[rows:]
    grad_gate = (back * up * sig * (1.0 + gate * (1.0 - sig))).astype(BF)
    grad_up = (back * act).astype(BF)
    grad_ref[...] += dot_t(grad_gate, w_g) + dot_t(grad_up, w_u)

    @pl.when(step == 1)
    def _():
        start_all(rows_copies)
        start_all(line_copies[0])
        local[0].start()

    @pl.when(step == 3)
    def _():
        wait_all(rows_copies)
        whole = rows_buf[place].astype(F32)
        for j in range(QUAD - 1):
            whole = whole + rows_parts[j].astype(F32)
        left_m[...] = whole.astype(BF)

    @pl.when(step == 4)
    def _():
        start_all(line_copies[1])
        local[1].start()

    @pl.when(step == per + 1)
    def _():
        received(route.hop(2, 1))
        start_all(route.hop(2, 2))
        received(route.hop(3, 0))
        start_all(route.hop(3, 1))

    @pl.when(step == 2 * per - 1)
    def _():
        received(route.hop(2, 2))

    @pl.when(step == 2 * per + 2)
    def _():
        received(route.hop(3, 1))
        start_all(route.hop(3, 2))

    @pl.when(step == 3 * per - 1)
    def _():
        received(route.hop(3, 2))

    @pl.when((step + 1 < steps) & ((step + 1) % per == 0))
    def _():
        fetch(step + 1)

    @pl.when(step == steps - 1)
    def _():
        grad, normed = grad_ref[...], normed_ref[...]
        gr2 = (cot_ref[...] + norm_back(grad, normed, inv_ref[:, :1], gain)).astype(BF)
        gr2_ref[...] = gr2
        gatt = dot_t(gr2, wo_ref[...]).astype(BF)
        gatt_ref[...] = gatt[:slots]
        gatt_buf[...] = gatt[slots:]
        vec_ref[...] = jnp.concatenate(
            [jnp.sum(grad * normed, axis=0, keepdims=True), jnp.sum(grad, axis=0, keepdims=True)], axis=0
        )
        start_all(gatt_copies)
        out_ref[...] = acc_ref[:length, :].astype(BF)
        chunk = out_left_ref.shape[1]
        for i in range(2):
            out_left_ref[(i + route.t) % 2] = acc_ref[length + i * chunk : length + (i + 1) * chunk, :].astype(BF)
        sent_all(route.hop(2, 1) + route.hop(2, 2) + route.hop(3, 0) + route.hop(3, 1) + route.hop(3, 2))
        wait_all(gatt_copies)
        whole = gatt_buf[:, pl.ds(pl.multiple_of(place * hw, hw), hw)].astype(F32)
        for j in range(QUAD - 1):
            whole = whole + gatt_parts[j].astype(F32)
        left_gatt_ref[...] = whole.astype(BF)
        wait_all(line_copies[0] + line_copies[1])
        wait_all(local)


def feed_forward(tok, att, left_att, w_out, gain, bias, pick, part_pick, cot, ffn, gathered, n_ten):
    rows, width = tok.shape
    units = ffn[0].shape[1]
    masked = cot.shape[0]
    slots, hw = masked // 2, width // QUAD
    unit = 256
    whole = lambda *shape: pl.BlockSpec(shape, lambda i: (0,) * len(shape))
    low = jax.ShapeDtypeStruct((masked, width), BF)
    return pl.pallas_call(
        functools.partial(feed_kernel, n_ten),
        grid=(n_ten * units // unit,),
        in_specs=[once(x.shape) for x in (tok, att, left_att, w_out)]
        + [once((1, width)), once((1, width)), once(pick.shape), once(part_pick.shape), once(cot.shape)]
        + [any_spec()] * 6,
        out_specs=[whole(*att.shape), whole(2, left_att.shape[0] // 2, width)]
        + [whole(masked, width), whole(masked, width), whole(slots, width), whole(slots, hw)]
        + [whole(2, width)]
        + [any_spec()] * 5,
        out_shape=[
            jax.ShapeDtypeStruct(att.shape, BF), jax.ShapeDtypeStruct((2, left_att.shape[0] // 2, width), BF), low, low,
            jax.ShapeDtypeStruct((slots, width), BF), jax.ShapeDtypeStruct((slots, hw), BF),
            jax.ShapeDtypeStruct((2, width), F32),
            jax.ShapeDtypeStruct((n_ten, slots, width), BF), jax.ShapeDtypeStruct((n_ten, slots // QUAD, width), BF),
        ]
        + [jax.ShapeDtypeStruct(w.shape, BF) for w in gathered],
        input_output_aliases={12: 9, 13: 10, 14: 11},
        scratch_shapes=[
            pltpu.VMEM((rows + masked, width), BF),
            pltpu.VMEM((rows, width), F32),
            pltpu.VMEM((masked, width), F32),
            pltpu.VMEM((masked, LANES), F32),
            pltpu.VMEM((masked, width), F32),
            pltpu.VMEM((2, width, unit), BF),
            pltpu.VMEM((2, width, unit), BF),
            pltpu.VMEM((2, unit, width), BF),
            pltpu.VMEM((QUAD, slots // QUAD, width), BF),
            pltpu.VMEM((QUAD - 1, slots // QUAD, width), BF),
            pltpu.VMEM((slots, width), BF),
            pltpu.VMEM((slots // QUAD, width), BF),
            pltpu.VMEM((slots, width), BF),
            pltpu.VMEM((QUAD - 1, slots, hw), BF),
            pltpu.SemaphoreType.DMA((2, 3)),
            pltpu.SemaphoreType.DMA((2, QUAD - 1)),
            pltpu.SemaphoreType.DMA((2, QUAD - 1)),
            pltpu.SemaphoreType.DMA((2, n_ten - 1)),
            pltpu.SemaphoreType.DMA((2, n_ten - 1)),
            pltpu.SemaphoreType.DMA((2,)),
        ]
        + route_sems(),
        compiler_params=pltpu.CompilerParams(collective_id=5, has_side_effects=True),
        cost_estimate=pl.CostEstimate(
            flops=8 * rows * width * n_ten * units, bytes_accessed=6 * width * n_ten * units, transcendentals=rows * n_ten * units
        ),
        name="feed_forward",
    )(tok, att, left_att, w_out, gain.reshape(1, width), bias.reshape(1, width), pick, part_pick, cot, *ffn, *gathered)[:9]


def token_back_kernel(
    tok_ref, dq_ref, dk_ref, dv_ref, wq_ref, wk_ref, wv_ref, gain_ref, pick_ref, rows_ref, out_ref, vec_ref
):
    acc = dot_t(dq_ref[...], wq_ref[...]) + dot_t(dk_ref[...], wk_ref[...]) + dot_t(dv_ref[...], wv_ref[...])
    normed, inv_std = layer_stats(tok_ref[...].astype(F32))
    direct = t_dot(pick_ref[...], rows_ref[0])
    out_ref[...] = (direct + norm_back(acc, normed, inv_std, gain_ref[...])).astype(BF)
    sums = jnp.concatenate([jnp.sum(acc * normed, axis=0, keepdims=True), jnp.sum(acc, axis=0, keepdims=True)], axis=0)

    @pl.when(pl.program_id(0) == 0)
    def _():
        vec_ref[...] = sums

    @pl.when(pl.program_id(0) > 0)
    def _():
        vec_ref[...] += sums


def token_back(tok, grads, weights, gain, pick, rows_m):
    rows, width = tok.shape
    slots = pick.shape[0]
    tile = 256
    row = pl.BlockSpec((tile, width), lambda r: (r, 0))
    own = rows // tile - 1
    return pl.pallas_call(
        token_back_kernel,
        grid=(rows // tile,),
        in_specs=[row] * 4
        + [once((width, width))] * 3
        + [
            once((1, width)),
            pl.BlockSpec((slots, tile), lambda r: (0, r)),
            pl.BlockSpec((1, slots, width), lambda r: (r // own, 0, 0)),
        ],
        out_specs=[row, pl.BlockSpec((2, width), lambda r: (0, 0))],
        out_shape=[jax.ShapeDtypeStruct((rows, width), BF), jax.ShapeDtypeStruct((2, width), F32)],
        cost_estimate=pl.CostEstimate(flops=6 * rows * width * width, bytes_accessed=16 * rows * width, transcendentals=0),
        name="token_back",
    )(tok, *grads, *weights, gain.reshape(1, width), pick, rows_m)


def exchange_out_kernel(
    sizes, go_ref, gq_ref, gk_ref, gv_ref, gg_ref, gu_ref, gd_ref, grad_ref, vec_ref, w_ref, ffn_ref, tok_ref, vec_out,
    buf1, buf2, buf3, buf4, vec_buf, vec_sum,
    tok_send, tok_recv, send1, recv1, send2, recv2, send3, recv3, send4, recv4, vec_send, vec_recv, local_sem,
):
    n_seq, n_ten, half, rows = sizes
    dp, sx, t = lax.axis_index("dp"), lax.axis_index("seq"), lax.axis_index("tensor")
    y, c = dp // 2, dp % 2
    me = sx * n_ten + t
    group = n_seq * n_ten
    others = []
    for i in range(1, group):
        g = (me + i) % group
        others.append((g // n_ten, g % n_ten))
    y_peer, c_peer, x_peer = {"dp": (dp + 2) % 4}, {"dp": 2 * y + 1 - c}, {"seq": 1 - sx}
    z_peers = [{"tensor": (t + j) % n_ten} for j in range(1, n_ten)]
    beside = [{"dp": 2 * y + 1 - c, "tensor": (t + j) % n_ten} for j in range(1, n_ten)]
    greet([{"seq": a, "tensor": b} for a, b in others] + [y_peer, c_peer] + beside)
    grads = (go_ref, gq_ref, gk_ref, gv_ref, gg_ref, gu_ref, gd_ref)
    count, attn = len(grads), w_ref.shape[0]
    x_first = (False, False, False, False, False, True, True)
    height = gq_ref.shape[0]
    hw = height // n_ten

    def columns(b_y, b_c, b_x):
        return pl.ds(pl.multiple_of((b_y * 4 + b_c * 2 + b_x) * LANES, LANES), LANES)

    def add_rows(out, first, second):
        def body(i, carry):
            at = pl.ds(pl.multiple_of(i * hw, hw), hw)
            out[at, :] = (first[at, :].astype(F32) + second[at, :].astype(F32)).astype(BF)
            return carry

        lax.fori_loop(0, height // hw, body, 0)

    stage1 = []
    for a in range(count):
        stage1.append(
            [
                remote(
                    grads[a].at[:, columns(b_y, 1 - c, b_x)], buf1.at[a, b_y, b_x],
                    send1.at[a, 2 * b_y + b_x], recv1.at[a, 2 * b_y + b_x], c_peer,
                )
                for b_y in range(2)
                for b_x in range(2)
            ]
        )
    for copies in stage1:
        start_all(copies)

    vec_hops = []
    hops = [c_peer, x_peer, y_peer]
    vec_sum[0] = vec_ref[...]
    for i, peer in enumerate(hops):
        vec_hops.append([remote(vec_sum.at[i], vec_buf.at[i], vec_send.at[i], vec_recv.at[i], peer)])
    vec_hops.append(
        [
            remote(vec_sum.at[3], vec_buf.at[3 + j], vec_send.at[3 + j], vec_recv.at[3 + j], peer)
            for j, peer in enumerate(z_peers)
        ]
    )
    start_all(vec_hops[0])

    tokens = []
    for i, (a, b) in enumerate(others):
        tokens.append(
            remote(
                grad_ref.at[pl.ds(pl.multiple_of((a * n_ten + b) * rows, rows), rows), :],
                tok_ref.at[sx * half + t],
                tok_send.at[i], tok_recv.at[i], {"seq": a, "tensor": b},
            )
        )
    shared = []
    for i in range(n_seq):
        src, dst = grad_ref.at[pl.ds((group + i) * rows, rows), :], tok_ref.at[t % 2 * half + n_ten]
        shared.append(
            (
                2 * c + i == t,
                remote(
                    src, dst, tok_send.at[group - 1 + i], tok_recv.at[group - 1 + t % 2],
                    {"dp": 2 * y + t // 2, "tensor": 2 * c + i},
                ),
                pltpu.make_async_copy(src, dst, local_sem.at[1]),
            )
        )
    arriving = [
        remote(
            grad_ref.at[pl.ds(0, rows), :], tok_ref.at[i * half + n_ten],
            tok_send.at[group - 1], tok_recv.at[group - 1 + i], c_peer,
        )
        for i in range(n_seq)
    ]
    start_all(tokens)
    for here, away, near in shared:
        pl.when(here)(near.start)
        pl.when(jnp.logical_not(here))(away.start)
    local = [
        pltpu.make_async_copy(
            grad_ref.at[pl.ds(pl.multiple_of(me * rows, rows), rows), :], tok_ref.at[sx * half + t], local_sem.at[0]
        ),
    ]
    start_all(local)

    stage2 = []
    for a in range(count):
        for copy in stage1[a]:
            copy.wait_recv()
        for b_y in range(2):
            for b_x in range(2):
                add_rows(buf1.at[a, b_y, b_x], grads[a].at[:, columns(b_y, c, b_x)], buf1.at[a, b_y, b_x])
        copies = []
        for b in range(2):
            src, peer = (buf1.at[a, b, 1 - sx], x_peer) if x_first[a] else (buf1.at[a, 1 - y, b], y_peer)
            copies.append(remote(src, buf2.at[a, b], send2.at[a, b], recv2.at[a, b], peer))
        start_all(copies)
        stage2.append(copies)
    vec_hops[0][0].wait_recv()
    vec_sum[1] = vec_sum[0] + vec_buf[0]
    start_all(vec_hops[1])
    stage3, stage4 = {}, {}

    def second(a):
        for copy in stage2[a]:
            copy.wait_recv()
        for b in range(2):
            own = buf1.at[a, b, sx] if x_first[a] else buf1.at[a, y, b]
            add_rows(buf2.at[a, b], own, buf2.at[a, b])
        src, peer = (buf2.at[a, 1 - y], y_peer) if x_first[a] else (buf2.at[a, 1 - sx], x_peer)
        stage3[a] = remote(src, buf3.at[a], send3.at[a], recv3.at[a], peer)
        stage3[a].start()

    def third(a):
        stage3[a].wait_recv()
        own = buf2.at[a, y] if x_first[a] else buf2.at[a, sx]
        if a >= attn:

            def final(i, carry):
                at = pl.ds(pl.multiple_of(i * hw, hw), hw)
                ffn_ref[a - attn, at, :] = own[at, :].astype(F32) + buf3[a, at, :].astype(F32)
                return carry

            lax.fori_loop(0, height // hw, final, 0)
            return
        add_rows(buf3.at[a], own, buf3.at[a])
        stage4[a] = []
        for j, peer in enumerate(z_peers):
            to = (t + 1 + j) % n_ten
            src = buf3.at[a, pl.ds(pl.multiple_of(to * hw, hw), hw), :]
            stage4[a].append(remote(src, buf4.at[a, j], send4.at[a, j], recv4.at[a, j], peer))
        start_all(stage4[a])

    vec_hops[1][0].wait_recv()
    vec_sum[2] = vec_sum[1] + vec_buf[1]
    start_all(vec_hops[2])
    for a in (0, 1, 2, 5, 3, 6):
        second(a)
    third(0)
    third(1)
    second(4)
    for a in (2, 3, 5, 6, 4):
        third(a)
    vec_hops[2][0].wait_recv()
    vec_sum[3] = vec_sum[2] + vec_buf[2]
    start_all(vec_hops[3])
    for n, copies in stage4.items():
        total = buf3[n, pl.ds(pl.multiple_of(t * hw, hw), hw), :].astype(F32)
        for j, copy in enumerate(copies):
            copy.wait_recv()
            total = total + buf4[n, j].astype(F32)
        w_ref[n] = total
    total = vec_sum[3]
    for j, copy in enumerate(vec_hops[3]):
        copy.wait_recv()
        total = total + vec_buf[3 + j]
    vec_out[...] = total
    for copies in stage1 + stage2 + list(stage4.values()) + [list(stage3.values())] + vec_hops:
        for copy in copies:
            copy.wait_send()
    wait_all(local)
    wait_all(tokens)
    for here, away, near in shared:
        pl.when(here)(near.wait)
        pl.when(jnp.logical_not(here))(away.wait_send)
    for i in range(n_seq):
        pl.when(jnp.logical_not(2 * c + i == t))(arriving[i].wait_recv)


def exchange_out(ffn_grads, attn_grads, grad_tok, vectors, n_seq, n_ten, half, rows):
    grads = (*attn_grads, *ffn_grads)
    ffn, attn = len(ffn_grads), len(attn_grads)
    height, width = grads[0].shape
    hw, count, group = height // n_ten, len(grads), n_seq * n_ten
    vmem = pl.BlockSpec(memory_space=pltpu.VMEM)
    dma = pltpu.SemaphoreType.DMA
    hops = 3 + n_ten - 1
    return pl.pallas_call(
        functools.partial(exchange_out_kernel, (n_seq, n_ten, half, rows)),
        in_specs=[vmem] * (count + 2),
        out_specs=[vmem, vmem, any_spec(), vmem],
        out_shape=[
            jax.ShapeDtypeStruct((attn, hw, LANES), F32),
            jax.ShapeDtypeStruct((ffn, height, LANES), F32),
            jax.ShapeDtypeStruct((n_seq * half, rows, width), BF),
            jax.ShapeDtypeStruct(vectors.shape, F32),
        ],
        scratch_shapes=[
            pltpu.VMEM((count, 2, 2, height, LANES), BF),
            pltpu.VMEM((count, 2, height, LANES), BF),
            pltpu.VMEM((count, height, LANES), BF),
            pltpu.VMEM((attn, n_ten - 1, hw, LANES), BF),
            pltpu.VMEM((hops,) + vectors.shape, F32),
            pltpu.VMEM((4,) + vectors.shape, F32),
            dma((group + 1,)), dma((group + 1,)),
            dma((count, 4)), dma((count, 4)),
            dma((count, 2)), dma((count, 2)),
            dma((count,)), dma((count,)),
            dma((attn, n_ten - 1)), dma((attn, n_ten - 1)),
            dma((hops,)), dma((hops,)),
            dma((2,)),
        ],
        compiler_params=pltpu.CompilerParams(collective_id=4, has_side_effects=True),
        name="exchange_out",
    )(*grads, grad_tok, vectors)


def rotary_lanes(cosine, sine):
    reps = LANES // HEAD_DIM
    return jnp.concatenate([cosine, cosine] * reps, axis=1), jnp.concatenate([-sine, sine] * reps, axis=1)


def position_tables(length):
    half_dim = HEAD_DIM // 2
    inv_freq = np.float32(10000.0) ** (-np.arange(half_dim, dtype=np.float32) * np.float32(2.0 / HEAD_DIM))
    angles = (np.arange(length, dtype=np.float32)[:, None] * inv_freq[None, :]).astype(np.float64)
    cosine, sine = np.cos(angles).astype(np.float32), np.sin(angles).astype(np.float32)
    reps = LANES // HEAD_DIM
    return np.concatenate([cosine, cosine] * reps, axis=1), np.concatenate([-sine, sine] * reps, axis=1)


def window_shards(
    tokens,
    norm1_gain,
    norm1_bias,
    w_query,
    w_key,
    w_value,
    w_out,
    norm2_gain,
    norm2_bias,
    w_gate,
    w_up,
    w_down,
    out_grad,
    masked_rows,
    window_counts,
):
    rows_local, windows, width = tokens.shape
    n_dp, n_seq, n_ten = lax.axis_size("dp"), lax.axis_size("seq"), lax.axis_size("tensor")
    dp_index, seq_index, ten_index = lax.axis_index("dp"), lax.axis_index("seq"), lax.axis_index("tensor")
    shard_index = dp_index * n_seq + seq_index
    core = dp_index % 2
    place = seq_index * 2 + core
    half = windows // n_seq
    length = rows_local * n_seq * n_ten
    share = length // QUAD
    hw = width // QUAD
    slots = masked_rows.shape[1]
    part = slots // QUAD

    live = jnp.arange(windows) < window_counts[0]
    valid = (masked_rows < length) & live[:, None]
    coded = jnp.where(valid, masked_rows, length)
    info = jnp.concatenate([coded, jnp.full((1, slots), jnp.sum(valid.astype(jnp.int32)))], axis=0)
    info = jnp.pad(info, ((0, -(windows + 1) % 8), (0, -slots % LANES)))
    both_tok, all_q, all_k, all_v, all_out, infos, left_grad = exchange_in(
        jnp.swapaxes(tokens, 0, 1), w_query, w_key, w_value, w_out, info, out_grad, n_dp, n_seq, n_ten
    )
    loss_weight = LOSS_SCALE / jnp.sum(infos[:, windows, 0]).astype(F32)
    pick_one = lambda x, at: lax.dynamic_index_in_dim(x, at, 0, keepdims=False)
    first_window = seq_index * half
    my_coded = lax.dynamic_slice_in_dim(coded, first_window, n_ten, 0)
    my_grad = lax.dynamic_slice_in_dim(out_grad, first_window, n_ten, 0)
    pair_infos = lax.dynamic_slice_in_dim(infos, dp_index - core, 2, 0)
    left_coded = jnp.stack([pair_infos[i // n_seq, i % n_seq * half + n_ten, :slots] for i in range(n_ten)])
    weigh = lambda grad, rows: jnp.where((rows < length)[..., None], grad.astype(F32) * loss_weight, 0.0)

    own_rows, left_rows = pick_one(my_coded, ten_index), pick_one(left_coded, ten_index)
    every = jnp.arange(length)
    my_left = place * share + jnp.arange(share)
    own_pick = (own_rows[:, None] == every[None, :]).astype(BF)
    left_pick = (left_rows[:, None] == every[None, :]).astype(BF)
    part_match = left_rows[:, None] == my_left[None, :]
    part_pick = part_match.astype(BF)
    left_here = jnp.where(jnp.any(part_match, axis=1), left_rows, length)
    my_cot = jnp.concatenate(
        [weigh(pick_one(my_grad, ten_index), own_rows), weigh(pick_one(left_grad, ten_index), left_here)], axis=0
    )

    tables = [jnp.asarray(x) for x in position_tables(length)]
    part_tables = [lax.dynamic_slice_in_dim(x, place * share, share, 0) for x in tables]
    own_tables = tables + list(rotary_lanes(*rotary_tables(own_rows)))
    left_tables = tables + list(rotary_lanes(*rotary_tables(left_rows)))

    ffn = (w_gate, w_up, w_down)
    first, q, k, v, *gathered = norm_qkv(
        both_tok, norm1_gain, norm1_bias, all_q, all_k, all_v, tables, part_tables, ffn, n_ten
    )
    own_att, left_q, left_k, left_v, *gathered = attend_swap(q, k, v, gathered, length, n_ten)
    left_att_part, *gathered = attend_left(left_q, left_k, left_v, gathered, n_ten)
    own_out, left_chunks, att_m, gr2, own_gatt, left_gatt, grad_norm2, all_own, all_left = feed_forward(
        both_tok, own_att, left_att_part, all_out, norm2_gain, norm2_bias, own_pick, part_pick, my_cot, ffn, gathered, n_ten
    )

    grad_w_out = t_dot(att_m, gr2).astype(BF)
    left_back = back_left(left_q, left_gatt, left_k, left_v, left_pick, left_tables)
    dq, dk, dv = back_swap(q, own_gatt, k, v, own_pick, own_tables, left_back)
    all_own, dq, dk, dv = lax.optimization_barrier((all_own, dq, dk, dv))

    second = jnp.concatenate([all_own.reshape(-1, width), all_left.reshape(-1, width)], axis=0)
    part_of = lambda x: lax.dynamic_slice_in_dim(x, place * part, part, 1)
    down_in = jnp.concatenate(
        [
            weigh(my_grad, my_coded).reshape(n_ten * slots, width),
            weigh(part_of(left_grad), part_of(left_coded)).reshape(n_ten * part, width),
        ],
        axis=0,
    ).astype(BF)
    gate = dot_n(second, w_gate)
    up = dot_n(second, w_up)
    grad_hidden = dot_t(down_in, w_down)
    sig = jax.nn.sigmoid(gate)
    silu = gate * sig
    hidden_m = (silu * up).astype(BF)
    grad_gate = (grad_hidden * up * sig * (1.0 + gate * (1.0 - sig))).astype(BF)
    grad_up = (grad_hidden * silu).astype(BF)
    grad_w_ffn = [
        t_dot(grad_gate, second).astype(BF), t_dot(grad_up, second).astype(BF), t_dot(hidden_m, down_in).astype(BF)
    ]
    grad_w_attn = [grad_w_out] + [t_dot(d, first).astype(BF) for d in (dq, dk, dv)]
    grad_both, grad_norm1 = token_back(
        both_tok, (dq, dk, dv), (all_q, all_k, all_v), norm1_gain,
        jnp.concatenate([own_pick, part_pick], axis=1), gr2.reshape(2, slots, width),
    )

    own_out = lax.all_to_all(
        own_out.reshape(n_seq * n_ten, rows_local, width), ("seq", "tensor"), 0, 0, tiled=True
    ).reshape(n_seq, n_ten, rows_local, width)
    left_out = []
    for turn in range(2):
        perm = []
        for d in range(n_dp):
            for sx in range(n_seq):
                for p in range(n_ten):
                    to = d // 2 * 2 + p // 2, sx, d % 2 * 2 + (p % 2 ^ turn)
                    perm.append(((d * n_seq + sx) * n_ten + p, (to[0] * n_seq + to[1]) * n_ten + to[2]))
        left_out.append(lax.ppermute(left_chunks[turn], ("dp", "seq", "tensor"), perm))
    even = ten_index % 2 == 0
    left_out = jnp.stack([jnp.where(even, left_out[0], left_out[1]), jnp.where(even, left_out[1], left_out[0])])
    output = jnp.concatenate([own_out, left_out[:, None]], axis=1).reshape(windows, rows_local, width)
    output = jnp.swapaxes(output, 0, 1)
    vectors = jnp.concatenate(
        [grad_norm1, grad_norm2, jnp.zeros((4, width), F32)], axis=0
    )
    gw_attn, gw_ffn, grad_tokens, vectors = exchange_out(
        grad_w_ffn, grad_w_attn, grad_both, vectors, n_seq, n_ten, half, rows_local
    )
    grad_tokens = jnp.swapaxes(grad_tokens, 0, 1).astype(F32)
    small = width // (n_dp * n_seq * n_ten)
    vectors = lax.dynamic_slice_in_dim(vectors, (shard_index * n_ten + ten_index) * small, small, 1)

    return (
        output,
        grad_tokens,
        vectors[0],
        vectors[1],
        gw_attn[1].T,
        gw_attn[2].T,
        gw_attn[3].T,
        gw_attn[0],
        vectors[2],
        vectors[3],
        gw_ffn[0].T,
        gw_ffn[1].T,
        gw_ffn[2],
    )


def shards(tokens, *rest):
    n_dp, n_seq, n_ten = lax.axis_size("dp"), lax.axis_size("seq"), lax.axis_size("tensor")
    whole = n_dp == 4 and n_seq == 2 and n_ten == 4 and tokens.shape[1] == n_seq * (n_ten + 1)
    return (window_shards if whole else block_shards)(tokens, *rest)


def solution(mesh):
    return jax.shard_map(
        shards,
        mesh=mesh,
        in_specs=(
            P(("seq", "tensor"), "dp", None),
            P(),
            P(),
            P(None, "tensor"),
            P(None, "tensor"),
            P(None, "tensor"),
            P("tensor", None),
            P(),
            P(),
            P(None, "tensor"),
            P(None, "tensor"),
            P("tensor", None),
            P("dp", None, None),
            P("dp", None),
            P("dp"),
        ),
        out_specs=(
            P(("seq", "tensor"), "dp", None),
            P(("seq", "tensor"), "dp", None),
            P(("dp", "seq", "tensor")),
            P(("dp", "seq", "tensor")),
            P(("dp", "seq"), "tensor"),
            P(("dp", "seq"), "tensor"),
            P(("dp", "seq"), "tensor"),
            P("tensor", ("dp", "seq")),
            P(("dp", "seq", "tensor")),
            P(("dp", "seq", "tensor")),
            P(("dp", "seq"), "tensor"),
            P(("dp", "seq"), "tensor"),
            P("tensor", ("dp", "seq")),
        ),
        check_vma=False,
    )
```

```python
import math

import functools

import jax
import jax.numpy as jnp
import numpy as np
from jax import lax
from jax.experimental import pallas as pl
from jax.experimental.pallas import tpu as pltpu
from jax.sharding import PartitionSpec as P

HEAD_DIM = 64
L = 1024
LOSS_SCALE = 1024


epsilon = 1e-05


def layer_stats(inputs):
    row_mean = jnp.mean(inputs, axis=-1, keepdims=True)
    centred = inputs - row_mean
    inv_std = lax.rsqrt(jnp.mean(centred * centred, axis=-1, keepdims=True) + epsilon)
    return (centred * inv_std, inv_std)


def norm_back(grad_norm, normed, inv_std, gain_vec):
    scaled = grad_norm * gain_vec
    return inv_std * (
        scaled
        - jnp.mean(scaled, axis=-1, keepdims=True)
        - normed * jnp.mean(scaled * normed, axis=-1, keepdims=True)
    )


def rotary_tables(positions):
    half_dim = HEAD_DIM // 2
    inv_freq = 10000.0 ** (-jnp.arange(half_dim, dtype=jnp.float32) * 2.0 / HEAD_DIM)
    angles = positions.astype(jnp.float32)[:, None] * inv_freq[None, :]
    return (jnp.cos(angles), jnp.sin(angles))


def rotate(values, cosine, sine):
    half_dim = values.shape[-1] // 2
    first_half = values[..., :half_dim]
    second_half = values[..., half_dim:]
    cos_b = cosine[:, None, None, :]
    sin_b = sine[:, None, None, :]
    return jnp.concatenate(
        [first_half * cos_b - second_half * sin_b, second_half * cos_b + first_half * sin_b],
        axis=-1,
    )


def unrotate(grads, cosine, sine):
    half_dim = grads.shape[-1] // 2
    first_half = grads[..., :half_dim]
    second_half = grads[..., half_dim:]
    cos_b = cosine[:, None, None, :]
    sin_b = sine[:, None, None, :]
    return jnp.concatenate(
        [first_half * cos_b + second_half * sin_b, second_half * cos_b - first_half * sin_b],
        axis=-1,
    )


def block_shards(
    tokens,
    norm1_gain,
    norm1_bias,
    w_query,
    w_key,
    w_value,
    w_out,
    norm2_gain,
    norm2_bias,
    w_gate,
    w_up,
    w_down,
    out_grad,
    masked_rows,
    window_counts,
):
    rows_local, windows, model_width = tokens.shape
    span_rows = rows_local * lax.axis_size("tensor")
    seq_index = lax.axis_index("seq")
    tensor_index = lax.axis_index("tensor")
    head_width = w_query.shape[1]
    heads_local = head_width // HEAD_DIM
    score_scale = 1.0 / math.sqrt(HEAD_DIM)
    head_shape = (span_rows, windows, heads_local, HEAD_DIM)
    residual = tokens.astype(jnp.float32)
    normed1, inv_std1 = layer_stats(residual)
    first_low = (normed1 * norm1_gain + norm1_bias).astype(jnp.bfloat16)
    first_full = lax.all_gather(first_low, "tensor", axis=0, tiled=True)
    w_joined = jnp.concatenate([w_query, w_key, w_value], axis=1)
    projected = jnp.einsum("rwd,de->rwe", first_full, w_joined, preferred_element_type=jnp.float32)
    positions = seq_index * span_rows + jnp.arange(span_rows)
    cosine, sine = rotary_tables(positions)
    queries = rotate(projected[..., :head_width].reshape(head_shape), cosine, sine).astype(
        jnp.bfloat16
    )
    keys_rot = (
        rotate(projected[..., head_width : 2 * head_width].reshape(head_shape), cosine, sine)
        .astype(jnp.bfloat16)
        .reshape(span_rows, windows, head_width)
    )
    values_own = projected[..., 2 * head_width :].astype(jnp.bfloat16)
    keys_all, values_all = (
        lax.all_gather(keys_rot, "seq", axis=0, tiled=True),
        lax.all_gather(values_own, "seq", axis=0, tiled=True),
    )
    key_heads = keys_all.reshape(-1, windows, heads_local, HEAD_DIM)
    value_heads = values_all.reshape(-1, windows, heads_local, HEAD_DIM)
    scores = (
        jnp.einsum("qwhd,kwhd->whqk", queries, key_heads, preferred_element_type=jnp.float32)
        * score_scale
    )
    row_max = jnp.max(scores, axis=-1, keepdims=True)
    row_sum = jnp.sum(jnp.exp(scores - row_max), axis=-1, keepdims=True)
    log_norm = row_max + jnp.log(row_sum)
    attn_prob = jnp.exp(scores - log_norm)
    prob_low = attn_prob.astype(jnp.bfloat16)
    attended = (
        jnp.einsum("whqk,kwhd->qwhd", prob_low, value_heads, preferred_element_type=jnp.float32)
        .reshape(span_rows, windows, head_width)
        .astype(jnp.bfloat16)
    )
    block_part = attended
    attn_branch = lax.psum_scatter(
        jnp.einsum("rwe,ed->rwd", block_part, w_out, preferred_element_type=jnp.float32).astype(
            jnp.bfloat16
        ),
        "tensor",
        scatter_dimension=0,
        tiled=True,
    ).astype(jnp.float32)
    residual2 = residual + attn_branch
    normed2, inv_std2 = layer_stats(residual2)
    second_low = (normed2 * norm2_gain + norm2_bias).astype(jnp.bfloat16)
    second_full = lax.all_gather(second_low, "tensor", axis=0, tiled=True)
    gate_proj = jnp.einsum("rwd,df->rwf", second_full, w_gate, preferred_element_type=jnp.float32)
    up_proj = jnp.einsum("rwd,df->rwf", second_full, w_up, preferred_element_type=jnp.float32)
    hidden = (jax.nn.silu(gate_proj) * up_proj).astype(jnp.bfloat16)
    block_part = hidden
    ffn_branch = lax.psum_scatter(
        jnp.einsum("rwf,fd->rwd", block_part, w_down, preferred_element_type=jnp.float32).astype(
            jnp.bfloat16
        ),
        "tensor",
        scatter_dimension=0,
        tiled=True,
    ).astype(jnp.float32)
    output = (residual2 + ffn_branch).astype(jnp.bfloat16)
    live_slot = jnp.arange(windows) < window_counts[0]
    valid_slot = (masked_rows < L) & live_slot[:, None]
    local_masked = jnp.sum(jnp.where(valid_slot, 1, 0)).astype(jnp.int32)
    total_masked = lax.psum(local_masked, "dp")
    loss_weight = LOSS_SCALE / total_masked.astype(jnp.float32)
    own_positions = seq_index * span_rows + tensor_index * rows_local + jnp.arange(rows_local)
    matches = (masked_rows[:, None, :] == own_positions[None, :, None]) & live_slot[:, None, None]
    picked = jnp.einsum(
        "wrm,wmd->rwd", matches.astype(jnp.bfloat16), out_grad, preferred_element_type=jnp.float32
    )
    grad_out = picked * loss_weight
    grad_down_in = lax.all_gather(grad_out.astype(jnp.bfloat16), "tensor", axis=0, tiled=True)
    grad_w_down = jnp.einsum(
        "rwf,rwd->fd", hidden, grad_down_in, preferred_element_type=jnp.float32
    )
    grad_hidden = jnp.einsum(
        "rwd,fd->rwf", grad_down_in, w_down, preferred_element_type=jnp.float32
    )
    sigmoid_gate = jax.nn.sigmoid(gate_proj)
    silu_gate = gate_proj * sigmoid_gate
    grad_gate = (
        grad_hidden * up_proj * sigmoid_gate * (1.0 + gate_proj * (1.0 - sigmoid_gate))
    ).astype(jnp.bfloat16)
    grad_up = (grad_hidden * silu_gate).astype(jnp.bfloat16)
    grad_w_gate = jnp.einsum(
        "rwd,rwf->df", second_full, grad_gate, preferred_element_type=jnp.float32
    )
    grad_w_up = jnp.einsum("rwd,rwf->df", second_full, grad_up, preferred_element_type=jnp.float32)
    grad_second = lax.psum_scatter(
        (
            jnp.einsum("rwf,df->rwd", grad_gate, w_gate, preferred_element_type=jnp.float32)
            + jnp.einsum("rwf,df->rwd", grad_up, w_up, preferred_element_type=jnp.float32)
        ).astype(jnp.bfloat16),
        "tensor",
        scatter_dimension=0,
        tiled=True,
    ).astype(jnp.float32)
    grad_norm2_gain = jnp.sum(grad_second * normed2, axis=(0, 1))
    grad_norm2_bias = jnp.sum(grad_second, axis=(0, 1))
    grad_residual2 = grad_out + norm_back(grad_second, normed2, inv_std2, norm2_gain)
    grad_attn_in = lax.all_gather(grad_residual2.astype(jnp.bfloat16), "tensor", axis=0, tiled=True)
    grad_w_out = jnp.einsum(
        "rwe,rwd->ed", attended, grad_attn_in, preferred_element_type=jnp.float32
    )
    grad_attended = jnp.einsum(
        "rwd,ed->rwe", grad_attn_in, w_out, preferred_element_type=jnp.float32
    ).astype(jnp.bfloat16)
    grad_att_heads = grad_attended.reshape(head_shape)
    scores_again = (
        jnp.einsum("qwhd,kwhd->whqk", queries, key_heads, preferred_element_type=jnp.float32)
        * score_scale
    )
    probs_again = jnp.exp(scores_again - log_norm)
    grad_probs = jnp.einsum(
        "qwhd,kwhd->whqk", grad_att_heads, value_heads, preferred_element_type=jnp.float32
    )
    row_delta = jnp.sum(probs_again * grad_probs, axis=-1, keepdims=True)
    grad_scores = (probs_again * (grad_probs - row_delta)).astype(jnp.bfloat16)
    grad_queries = (
        jnp.einsum("whqk,kwhd->qwhd", grad_scores, key_heads, preferred_element_type=jnp.float32)
        * score_scale
    )
    grad_key_all = (
        jnp.einsum("whqk,qwhd->kwhd", grad_scores, queries, preferred_element_type=jnp.float32)
        * score_scale
    ).reshape(-1, windows, head_width)
    grad_value_all = jnp.einsum(
        "whqk,qwhd->kwhd",
        probs_again.astype(jnp.bfloat16),
        grad_att_heads,
        preferred_element_type=jnp.float32,
    ).reshape(-1, windows, head_width)
    grad_keys, grad_values = (
        lax.psum_scatter(
            grad_key_all.astype(jnp.bfloat16), "seq", scatter_dimension=0, tiled=True
        ).astype(jnp.float32),
        lax.psum_scatter(
            grad_value_all.astype(jnp.bfloat16), "seq", scatter_dimension=0, tiled=True
        ).astype(jnp.float32),
    )
    grad_query_lin = (
        unrotate(grad_queries, cosine, sine)
        .reshape(span_rows, windows, head_width)
        .astype(jnp.bfloat16)
    )
    grad_key_lin = (
        unrotate(grad_keys.reshape(head_shape), cosine, sine)
        .reshape(span_rows, windows, head_width)
        .astype(jnp.bfloat16)
    )
    grad_value_lin = grad_values.astype(jnp.bfloat16)
    grad_joined = jnp.concatenate([grad_query_lin, grad_key_lin, grad_value_lin], axis=-1)
    grad_w_joined = jnp.einsum(
        "rwd,rwe->de", first_full, grad_joined, preferred_element_type=jnp.float32
    )
    grad_w_query = grad_w_joined[:, :head_width]
    grad_w_key = grad_w_joined[:, head_width : 2 * head_width]
    grad_w_value = grad_w_joined[:, 2 * head_width :]
    block_part = grad_joined
    grad_first = lax.psum_scatter(
        jnp.einsum("rwe,de->rwd", block_part, w_joined, preferred_element_type=jnp.float32).astype(
            jnp.bfloat16
        ),
        "tensor",
        scatter_dimension=0,
        tiled=True,
    ).astype(jnp.float32)
    grad_norm1_gain = jnp.sum(grad_first * normed1, axis=(0, 1))
    grad_norm1_bias = jnp.sum(grad_first, axis=(0, 1))
    grad_tokens = grad_residual2 + norm_back(grad_first, normed1, inv_std1, norm1_gain)
    summed = (
        lax.psum_scatter(
            grad_w_query.astype(jnp.bfloat16), ("dp", "seq"), scatter_dimension=0, tiled=True
        ).astype(jnp.float32),
        lax.psum_scatter(
            grad_w_key.astype(jnp.bfloat16), ("dp", "seq"), scatter_dimension=0, tiled=True
        ).astype(jnp.float32),
        lax.psum_scatter(
            grad_w_value.astype(jnp.bfloat16), ("dp", "seq"), scatter_dimension=0, tiled=True
        ).astype(jnp.float32),
        lax.psum_scatter(
            grad_w_out.astype(jnp.bfloat16), ("dp", "seq"), scatter_dimension=1, tiled=True
        ).astype(jnp.float32),
        lax.psum_scatter(
            grad_w_gate.astype(jnp.bfloat16), ("dp", "seq"), scatter_dimension=0, tiled=True
        ).astype(jnp.float32),
        lax.psum_scatter(
            grad_w_up.astype(jnp.bfloat16), ("dp", "seq"), scatter_dimension=0, tiled=True
        ).astype(jnp.float32),
        lax.psum_scatter(
            grad_w_down.astype(jnp.bfloat16), ("dp", "seq"), scatter_dimension=1, tiled=True
        ).astype(jnp.float32),
    )
    norm_sums = (
        lax.psum_scatter(grad_norm1_gain, ("dp", "seq", "tensor"), scatter_dimension=0, tiled=True),
        lax.psum_scatter(grad_norm1_bias, ("dp", "seq", "tensor"), scatter_dimension=0, tiled=True),
        lax.psum_scatter(grad_norm2_gain, ("dp", "seq", "tensor"), scatter_dimension=0, tiled=True),
        lax.psum_scatter(grad_norm2_bias, ("dp", "seq", "tensor"), scatter_dimension=0, tiled=True),
    )
    return (
        output,
        grad_tokens,
        norm_sums[0],
        norm_sums[1],
        summed[0],
        summed[1],
        summed[2],
        summed[3],
        norm_sums[2],
        norm_sums[3],
        summed[4],
        summed[5],
        summed[6],
    )


BF = jnp.bfloat16
F32 = jnp.float32
LANES = 128
QUAD = 4


def dot_t(a, b):
    return lax.dot_general(a, b, (((1,), (1,)), ((), ())), preferred_element_type=F32)


def dot_n(a, b):
    return lax.dot_general(a, b, (((1,), (0,)), ((), ())), preferred_element_type=F32)


def t_dot(a, b):
    return lax.dot_general(a, b, (((0,), (0,)), ((), ())), preferred_element_type=F32)


def swap_halves(x):
    half = HEAD_DIM // 2
    lane = lax.broadcasted_iota(jnp.int32, x.shape, 1)
    down = pltpu.roll(x, half, 1)
    up = pltpu.roll(x, LANES - half, 1)
    return jnp.where(lane % HEAD_DIM < half, up, down)


def head_mask(h):
    lane = lax.broadcasted_iota(jnp.int32, (1, LANES), 1)
    return jnp.where(lane // HEAD_DIM == h, 1.0, 0.0).astype(BF)


MESH = pl.DeviceIdType.MESH


def any_spec():
    return pl.BlockSpec(memory_space=pl.ANY)


def greet(peers):
    barrier = pltpu.get_barrier_semaphore()
    for peer in peers:
        pl.semaphore_signal(barrier, inc=1, device_id=peer, device_id_type=MESH)
    pl.semaphore_wait(barrier, len(peers))


def remote(src, dst, send, recv, peer):
    return pltpu.make_async_remote_copy(
        src_ref=src, dst_ref=dst, send_sem=send, recv_sem=recv, device_id=peer, device_id_type=MESH
    )


def start_all(copies):
    for copy in copies:
        copy.start()


def wait_all(copies):
    for copy in copies:
        copy.wait()


def quad_place():
    dp, sx = lax.axis_index("dp"), lax.axis_index("seq")
    place = sx * 2 + dp % 2
    return place, lambda to: {"dp": dp // 2 * 2 + to % 2, "seq": to // 2}


def quad_peers():
    place, device = quad_place()
    return [device((place + j) % QUAD) for j in range(1, QUAD)]


class WeightRoute:
    def __init__(self, gathered, own, n_ten, send, recv):
        dp, sx, t = lax.axis_index("dp"), lax.axis_index("seq"), lax.axis_index("tensor")
        y, c = dp // 2, dp % 2
        gate_ref, up_ref, down_ref = gathered
        self.refs, self.own = (gate_ref, up_ref, down_ref, down_ref), own
        self.width, self.units = gate_ref.shape[0], gate_ref.shape[1] // n_ten
        self.send, self.recv, self.c = send, recv, c
        s_xy, s_yx = c * 4 + y * 2 + sx, c * 4 + sx * 2 + y
        self.slices = (s_xy, s_yx, s_xy, s_yx)
        self.x_peer, self.y_peer, self.c_peer = {"seq": 1 - sx}, {"dp": (dp + 2) % 4}, {"dp": 2 * y + 1 - c}
        side = t // 2
        middle = jnp.minimum(t, n_ten - 1 - t)
        mirror = lambda k: k + side * (n_ten - 1 - 2 * k)
        self.order = [mirror(k) for k in (middle, 1 - middle, 2, 3)]
        self.inward, self.outward = mirror(middle + 1), mirror(0)
        self.is_middle, self.is_end = middle == 1, middle == 0
        self.t, self.middle, self.mirror = t, middle, mirror

    def shard(self, ref, k, first, count, which):
        size, cols, units = self.width // 8, self.width // 2, self.units
        rows = pl.multiple_of(first * (size if k < 2 else units // 8), 16)
        if k < 2:
            at = 0 if which is None else pl.multiple_of(which * units, units)
            return ref.at[pl.ds(rows, count * size), pl.ds(at, units)]
        at = rows if which is None else pl.multiple_of(which * units + rows, 16)
        return ref.at[pl.ds(at, count * (units // 8)), pl.ds((k - 2) * cols, cols)]

    def along(self, which, to, slot, number, own=False):
        copies = []
        for k in range(4):
            dst = self.shard(self.refs[k], k, self.slices[k], 1, which)
            src = self.shard(self.own[min(k, 2)], k, self.slices[k], 1, None) if own else dst
            copies.append(remote(src, dst, self.send.at[number, k], self.recv.at[slot, k], {"tensor": to}))
        return copies

    def to_in(self):
        return self.along(self.t, self.inward, 1 + self.middle, 0, True)

    def to_out(self):
        return self.along(self.t, self.outward, 1, 1, True)

    def in_far(self):
        return self.along(self.mirror(0), self.inward, 3, 2)

    def out_two(self):
        return self.along(self.mirror(2), self.outward, 2, 3)

    def out_three(self):
        return self.along(self.mirror(3), self.outward, 3, 4)

    def arrived(self, i):
        received(self.along(self.order[i], self.inward, i, 0))

    def hop(self, i, h):
        copies = []
        for k in range(4):
            xy = k % 2 == 0
            peer, first, count = (
                (self.x_peer if xy else self.y_peer, self.slices[k], 1),
                (self.y_peer if xy else self.x_peer, self.slices[k] // 2 * 2, 2),
                (self.c_peer, self.c * 4, 4),
            )[h]
            ref = self.shard(self.refs[k], k, first, count, self.order[i])
            copies.append(remote(ref, ref, self.send.at[2 + 3 * i + h, k], self.recv.at[1 + 3 * i + h, k], peer))
        return copies


def received(copies):
    for copy in copies:
        copy.wait_recv()


def sent_all(copies):
    for copy in copies:
        copy.wait_send()


def route_sems():
    return [pltpu.SemaphoreType.DMA((14, 4)), pltpu.SemaphoreType.DMA((13, 4))]


def exchange_in_kernel(
    sizes, tok_ref, wq_ref, wk_ref, wv_ref, wo_ref, count_ref, rows_ref, x_ref, q_ref, k_ref, v_ref, o_ref, counts_ref,
    peer_rows_ref, tok_send, tok_recv, w_send, w_recv, count_send, count_recv, rows_send, rows_recv, local_sem,
):
    n_seq, n_ten, half, rows, slices = sizes
    dp, sx, t = lax.axis_index("dp"), lax.axis_index("seq"), lax.axis_index("tensor")
    y, c = dp // 2, dp % 2
    me = sx * n_ten + t
    group = n_seq * n_ten
    others = []
    for i in range(1, group):
        g = (me + i) % group
        others.append((g // n_ten, g % n_ten))
    y_peer, c_peer, x_peer = {"dp": (dp + 2) % 4}, {"dp": 2 * y + 1 - c}, {"seq": 1 - sx}
    dp_peers = [{"dp": (dp + i) % 4} for i in range(1, 4)]
    beside = [{"dp": 2 * y + 1 - c, "tensor": (t + j) % n_ten} for j in range(1, n_ten)]
    greet([{"seq": a, "tensor": b} for a, b in others] + dp_peers + beside)
    counts = [
        remote(count_ref, counts_ref.at[dp], count_send.at[i], count_recv.at[i], peer) for i, peer in enumerate(dp_peers)
    ]
    start_all(counts)

    hw = wq_ref.shape[1]
    srow, orow = wq_ref.shape[0] // slices, hw // slices
    s_xy, s_yx = c * 4 + y * 2 + sx, c * 4 + sx * 2 + y
    weights = ((wq_ref, q_ref, s_xy, 0), (wk_ref, k_ref, s_xy, 0), (wv_ref, v_ref, s_yx, 0), (wo_ref, o_ref, s_yx, 1))

    def block(out, by_rows, base, count, which):
        if by_rows:
            return out.at[pl.ds(pl.multiple_of(which * hw + base * orow, orow), count * orow), :]
        return out.at[
            pl.ds(pl.multiple_of(base * srow, srow), count * srow), pl.ds(pl.multiple_of(which * hw, hw), hw)
        ]

    stage = [[], [], [], []]
    n = 0
    for j in range(1, n_ten):
        peer = {"tensor": (t + j) % n_ten}
        for w_ref, out, s, by_rows in weights:
            size = orow if by_rows else srow
            src = w_ref.at[pl.ds(pl.multiple_of(s * size, size), size), :]
            stage[0].append(remote(src, block(out, by_rows, s, 1, t), w_send.at[0, n], w_recv.at[0, n], peer))
            n += 1
    n = 0
    for j in range(1, n_ten):
        which = (t + j) % n_ten
        for w_ref, out, s, by_rows in weights:
            xy = s is s_xy
            hops = (
                (1, x_peer if xy else y_peer, s, 1),
                (2, y_peer if xy else x_peer, s // 2 * 2, 2),
                (3, c_peer, c * 4, 4),
            )
            for k, peer, base, count in hops:
                ref = block(out, by_rows, base, count, which)
                stage[k].append(remote(ref, ref, w_send.at[k, n], w_recv.at[k, n], peer))
            n += 1
    start_all(stage[0])

    tokens = []
    for i, (a, b) in enumerate(others):
        tokens.append(
            remote(
                tok_ref.at[a * half + b],
                x_ref.at[pl.ds(pl.multiple_of(me * rows, rows), rows), :],
                tok_send.at[i], tok_recv.at[i], {"seq": a, "tensor": b},
            )
        )
    shared = []
    for i in range(n_seq):
        src, dst = tok_ref.at[i * half + n_ten], x_ref.at[pl.ds(pl.multiple_of((group + t % 2) * rows, rows), rows), :]
        shared.append(
            (
                2 * c + i == t,
                remote(
                    src, dst, tok_send.at[group - 1 + i], tok_recv.at[group - 1 + t % 2],
                    {"dp": 2 * y + t // 2, "tensor": 2 * c + i},
                ),
                pltpu.make_async_copy(src, dst, local_sem.at[1]),
            )
        )
    arriving = [
        remote(
            tok_ref.at[n_ten], x_ref.at[pl.ds((group + i) * rows, rows), :],
            tok_send.at[group - 1], tok_recv.at[group - 1 + i], c_peer,
        )
        for i in range(n_seq)
    ]
    start_all(tokens)
    for here, away, near in shared:
        pl.when(here)(near.start)
        pl.when(jnp.logical_not(here))(away.start)
    peer_rows = [
        remote(rows_ref.at[i * half + n_ten], peer_rows_ref.at[2 * c + i], rows_send.at[i], rows_recv.at[i], c_peer)
        for i in range(n_seq)
    ]
    start_all(peer_rows)
    local = [
        pltpu.make_async_copy(
            tok_ref.at[sx * half + t], x_ref.at[pl.ds(pl.multiple_of(me * rows, rows), rows), :], local_sem.at[0]
        ),
    ]
    for i, (w_ref, out, s, by_rows) in enumerate(weights):
        local.append(pltpu.make_async_copy(w_ref, block(out, by_rows, 0, slices, t), local_sem.at[2 + i]))
    local.append(pltpu.make_async_copy(count_ref, counts_ref.at[dp], local_sem.at[6]))
    for i in range(n_seq):
        local.append(
            pltpu.make_async_copy(rows_ref.at[i * half + n_ten], peer_rows_ref.at[2 * c + i], local_sem.at[7 + i])
        )
    start_all(local)
    for k in range(1, 4):
        for earlier in stage[k - 1]:
            earlier.wait_recv()
        start_all(stage[k])
    for copy in stage[3]:
        copy.wait_recv()
    for copies in stage:
        for copy in copies:
            copy.wait_send()
    wait_all(local)
    wait_all(counts)
    wait_all(peer_rows)
    wait_all(tokens)
    for here, away, near in shared:
        pl.when(here)(near.wait)
        pl.when(jnp.logical_not(here))(away.wait_send)
    for i in range(n_seq):
        pl.when(jnp.logical_not((t // 2 == c) & (t % 2 == i)))(arriving[i].wait_recv)


def exchange_in(tok, w_query, w_key, w_value, w_out, count, out_grad, n_dp, n_seq, n_ten):
    windows, rows, width = tok.shape
    slices = n_dp * n_seq
    vmem = pl.BlockSpec(memory_space=pltpu.VMEM)
    square = jax.ShapeDtypeStruct((width, width), BF)
    group = n_seq * n_ten
    return pl.pallas_call(
        functools.partial(exchange_in_kernel, (n_seq, n_ten, windows // n_seq, rows, slices)),
        in_specs=[vmem] * 6 + [any_spec()],
        out_specs=[any_spec()] * 7,
        out_shape=[jax.ShapeDtypeStruct(((group + n_seq) * rows, width), BF)]
        + [square] * 4
        + [jax.ShapeDtypeStruct((n_dp,) + count.shape, count.dtype)]
        + [jax.ShapeDtypeStruct((2 * n_seq,) + out_grad.shape[1:], BF)],
        scratch_shapes=[
            pltpu.SemaphoreType.DMA((group + 1,)),
            pltpu.SemaphoreType.DMA((group + 1,)),
            pltpu.SemaphoreType.DMA((4, 4 * (n_ten - 1))),
            pltpu.SemaphoreType.DMA((4, 4 * (n_ten - 1))),
            pltpu.SemaphoreType.DMA((3,)),
            pltpu.SemaphoreType.DMA((3,)),
            pltpu.SemaphoreType.DMA((2,)),
            pltpu.SemaphoreType.DMA((2,)),
            pltpu.SemaphoreType.DMA((9,)),
        ],
        compiler_params=pltpu.CompilerParams(collective_id=0, has_side_effects=True),
        name="exchange_in",
    )(tok, w_query, w_key, w_value, w_out, count, out_grad)


def qkv_kernel(
    x_ref, gain_ref, bias_ref, wq_ref, wk_ref, wv_ref, cos_ref, sin_ref, part_cos_ref, part_sin_ref,
    first_ref, q_ref, k_ref, v_ref,
):
    shared = pl.program_id(0) == pl.num_programs(0) - 1
    normed, _ = layer_stats(x_ref[...].astype(F32))
    first_ref[...] = (normed * gain_ref[...] + bias_ref[...]).astype(BF)
    cos = jnp.where(shared, part_cos_ref[...], cos_ref[...])
    sin = jnp.where(shared, part_sin_ref[...], sin_ref[...])
    wide = 256
    for w_ref, out_ref, scale in ((wq_ref, q_ref, 1.0 / math.sqrt(HEAD_DIM)), (wk_ref, k_ref, 1.0), (wv_ref, v_ref, None)):
        for at in range(0, w_ref.shape[1], wide):
            acc = dot_n(first_ref[...], w_ref[:, at : at + wide])
            for c in range(0, wide, LANES):
                part = acc[:, c : c + LANES]
                if scale is not None:
                    part = (part * cos + swap_halves(part) * sin) * scale
                out_ref[:, at + c : at + c + LANES] = part.astype(BF)


def once(shape):
    return pl.BlockSpec(shape, lambda *_: (0,) * len(shape), pipeline_mode=pl.Buffered(1))


def norm_qkv(x, gain, bias, w_query, w_key, w_value, tables, part_tables):
    rows, width = x.shape
    tile = 256
    row = pl.BlockSpec((tile, width), lambda r: (r, 0))
    own = tables[0].shape[0] // tile
    table = pl.BlockSpec((tile, LANES), lambda r: (jnp.minimum(r, own - 1), 0))
    return pl.pallas_call(
        qkv_kernel,
        grid=(rows // tile,),
        in_specs=[row, once((1, width)), once((1, width))] + [once((width, width))] * 3 + [table, table] + [once((tile, LANES))] * 2,
        out_specs=[row] * 4,
        out_shape=[jax.ShapeDtypeStruct((rows, width), BF)] * 4,
        cost_estimate=pl.CostEstimate(flops=6 * rows * width * width, bytes_accessed=16 * rows * width, transcendentals=0),
        name="norm_qkv",
    )(x, gain.reshape(1, width), bias.reshape(1, width), w_query, w_key, w_value, *tables, *part_tables)


def attend_body(q_ref, k_ref, v_ref):
    q, k, v = q_ref[...], k_ref[...], v_ref[...]
    outs = []
    for h in range(LANES // HEAD_DIM):
        s = dot_t(q * head_mask(h), k)
        p = jnp.exp(s - jnp.max(s, axis=1, keepdims=True))
        norm = jnp.sum(p, axis=1, keepdims=True)
        outs.append(dot_n(p.astype(BF), v) / norm)
    lane = lax.broadcasted_iota(jnp.int32, outs[0].shape, 1)
    return jnp.where(lane < HEAD_DIM, outs[0], outs[1]).astype(BF)


def attend_specs(rows, tile):
    return [
        pl.BlockSpec((tile, LANES), lambda p, r: (r, p)),
        pl.BlockSpec((rows, LANES), lambda p, r: (0, p)),
        pl.BlockSpec((rows, LANES), lambda p, r: (0, p)),
    ]


def attend_cost(rows, pairs):
    return pl.CostEstimate(
        flops=16 * pairs * rows * rows * LANES, bytes_accessed=8 * rows * pairs * LANES, transcendentals=2 * pairs * rows * rows
    )


def attend_left_kernel(
    n_ten, q_ref, k_ref, v_ref, ag_in, au_in, ad_in, part_ref, ag_ref, au_ref, ad_ref, buf, send, recv, local_sem,
    route_send, route_recv,
):
    place, device = quad_place()
    r, p = pl.program_id(0), pl.program_id(1)
    last_pair = p == pl.num_programs(1) - 1
    hw = buf.shape[2]
    dst = part_ref.at[:, pl.ds(pl.multiple_of(place * hw, hw), hw)]
    route = WeightRoute((ag_ref, au_ref, ad_ref), None, n_ten, route_send, route_recv)
    hops = route.hop(1, 2) + route.hop(2, 0)

    @pl.when((p == 0) & (r == 0))
    def _():
        greet(quad_peers() + [route.y_peer] + [{"tensor": (route.t + j) % n_ten} for j in range(1, n_ten)])
        start_all(hops)
        pl.when(route.is_middle)(lambda: start_all(route.out_three()))

    buf[r, :, pl.ds(pl.multiple_of(p * LANES, LANES), LANES)] = attend_body(q_ref, k_ref, v_ref)

    def copy_to(j):
        to = (place + j) % QUAD
        return remote(buf.at[to], dst, send.at[j - 1], recv.at[j - 1], device(to))

    own = pltpu.make_async_copy(buf.at[place], dst, local_sem.at[0])
    for j in range(1, QUAD):
        pl.when(last_pair & (r == (place + j) % QUAD))(copy_to(j).start)
    pl.when(last_pair & (r == place))(own.start)

    @pl.when(last_pair & (r == QUAD - 1))
    def _():
        wait_all([copy_to(j) for j in range(1, QUAD)])
        own.wait()
        wait_all(hops)
        pl.when(route.is_middle)(lambda: sent_all(route.out_three()))
        pl.when(route.is_end)(lambda: route.arrived(3))


def attend_left(q, k, v, gathered, n_ten):
    rows, hw = q.shape
    tile, pairs = rows // QUAD, hw // LANES
    column = pl.BlockSpec((rows, LANES), lambda r, p: (0, p))
    return pl.pallas_call(
        functools.partial(attend_left_kernel, n_ten),
        grid=(QUAD, pairs),
        in_specs=[pl.BlockSpec((tile, LANES), lambda r, p: (r, p)), column, column] + [any_spec()] * 3,
        out_specs=[any_spec()] * 4,
        out_shape=[jax.ShapeDtypeStruct((tile, QUAD * hw), BF)] + [jax.ShapeDtypeStruct(w.shape, BF) for w in gathered],
        input_output_aliases={3: 1, 4: 2, 5: 3},
        scratch_shapes=[pltpu.VMEM((QUAD, tile, hw), BF)]
        + [pltpu.SemaphoreType.DMA((QUAD - 1,))] * 2
        + [pltpu.SemaphoreType.DMA((1,))]
        + route_sems(),
        compiler_params=pltpu.CompilerParams(collective_id=3, has_side_effects=True),
        cost_estimate=attend_cost(rows, pairs),
        name="attend_left",
    )(q, k, v, *gathered)


def swap_part(refs, outs, send, recv, local_sem, base):
    place, device = quad_place()
    share, hw = outs[0].shape[0] // QUAD, outs[0].shape[1]
    copies, local = [], []
    rows = pl.ds(base, share)
    mine = pl.ds(pl.multiple_of(place * share, share), share)
    for i, (ref, out) in enumerate(zip(refs, outs, strict=True)):
        for j in range(1, QUAD):
            to = (place + j) % QUAD
            src = ref.at[rows, pl.ds(pl.multiple_of(to * hw, hw), hw)]
            copies.append(remote(src, out.at[mine, :], send.at[i, j - 1], recv.at[i, j - 1], device(to)))
        src = ref.at[rows, pl.ds(pl.multiple_of(place * hw, hw), hw)]
        local.append(pltpu.make_async_copy(src, out.at[mine, :], local_sem.at[i]))
    return copies, local


def attend_swap_kernel(
    n_ten, length, q_ref, k_ref, v_ref, q_all, k_all, v_all, wg_ref, wu_ref, wd_ref, o_ref, lq_ref, lk_ref, lv_ref,
    ag_ref, au_ref, ad_ref, send, recv, local_sem, route_send, route_recv,
):
    step = pl.program_id(0) * pl.num_programs(1) + pl.program_id(1)
    steps = pl.num_programs(0) * pl.num_programs(1)
    copies, local = swap_part((q_all, k_all, v_all), (lq_ref, lk_ref, lv_ref), send, recv, local_sem, length)
    route = WeightRoute((ag_ref, au_ref, ad_ref), (wg_ref, wu_ref, wd_ref), n_ten, route_send, route_recv)

    @pl.when(step == 0)
    def _():
        greet(quad_peers() + [route.y_peer] + [{"tensor": (route.t + j) % n_ten} for j in range(1, n_ten)])
        start_all(route.to_in())
        pl.when(route.is_middle)(lambda: start_all(route.to_out()))
        start_all(copies + local)

    o_ref[...] = attend_body(q_ref, k_ref, v_ref)

    @pl.when(step == steps // 2)
    def _():
        route.arrived(1)
        start_all(route.hop(1, 0))

        @pl.when(route.is_middle)
        def _():
            route.arrived(2)
            start_all(route.in_far())
            start_all(route.out_two())

    @pl.when(step == steps * 3 // 4)
    def _():
        received(route.hop(1, 0))
        start_all(route.hop(1, 1))

    @pl.when(step == steps - 1)
    def _():
        wait_all(copies + local)
        received(route.hop(1, 1))
        sent_all(route.hop(1, 0) + route.hop(1, 1) + route.to_in())

        @pl.when(route.is_middle)
        def _():
            route.arrived(3)
            sent_all(route.to_out() + route.in_far() + route.out_two())

        @pl.when(route.is_end)
        def _():
            route.arrived(2)


def attend_swap(q, k, v, ffn, length, n_ten):
    width = q.shape[1]
    tile, pairs, hw = 512, width // LANES, width // QUAD
    left = jax.ShapeDtypeStruct((length, hw), BF)
    return pl.pallas_call(
        functools.partial(attend_swap_kernel, n_ten, length),
        grid=(pairs, length // tile),
        in_specs=attend_specs(length, tile) + [any_spec()] * 6,
        out_specs=[pl.BlockSpec((tile, LANES), lambda p, r: (r, p))] + [any_spec()] * 6,
        out_shape=[jax.ShapeDtypeStruct((length, width), BF), left, left, left]
        + [jax.ShapeDtypeStruct((width, n_ten * w.shape[1]), BF) for w in ffn[:2]]
        + [jax.ShapeDtypeStruct((n_ten * ffn[2].shape[0], width), BF)],
        scratch_shapes=[
            pltpu.SemaphoreType.DMA((3, QUAD - 1)),
            pltpu.SemaphoreType.DMA((3, QUAD - 1)),
            pltpu.SemaphoreType.DMA((3,)),
        ]
        + route_sems(),
        compiler_params=pltpu.CompilerParams(collective_id=1, has_side_effects=True),
        cost_estimate=attend_cost(length, pairs),
        name="attend_swap",
    )(q, k, v, q, k, v, *ffn)


def back_body(q_ref, g_ref, k_ref, v_ref, pick_ref, cos_ref, sin_ref, qcos_ref, qsin_ref):
    g, k, v, pick = g_ref[...], k_ref[...], v_ref[...], pick_ref[...]
    q = dot_n(pick, q_ref[...]).astype(BF)
    dq = []
    all_p, all_ds, all_q, all_g = [], [], [], []
    for h in range(LANES // HEAD_DIM):
        mask = head_mask(h)
        qh, gh = q * mask, g * mask
        s = dot_t(qh, k)
        p = jnp.exp(s - jnp.max(s, axis=1, keepdims=True))
        p = p / jnp.sum(p, axis=1, keepdims=True)
        dp = dot_t(gh, v)
        ds = (p * (dp - jnp.sum(p * dp, axis=1, keepdims=True))).astype(BF)
        dq.append(dot_n(ds, k))
        all_p.append(p.astype(BF))
        all_ds.append(ds)
        all_q.append(qh)
        all_g.append(gh)
    lane = lax.broadcasted_iota(jnp.int32, dq[0].shape, 1)
    dq = jnp.where(lane < HEAD_DIM, dq[0], dq[1]) * (1.0 / math.sqrt(HEAD_DIM))
    dq = (dq * qcos_ref[...] - swap_halves(dq) * qsin_ref[...]).astype(BF)
    dq = t_dot(pick, dq).astype(BF)
    dk = t_dot(jnp.concatenate(all_ds, axis=0), jnp.concatenate(all_q, axis=0))
    dk = (dk * cos_ref[...] - swap_halves(dk) * sin_ref[...]).astype(BF)
    dv = t_dot(jnp.concatenate(all_p, axis=0), jnp.concatenate(all_g, axis=0)).astype(BF)
    return dq, dk, dv


def back_kernel(q_ref, g_ref, k_ref, v_ref, pick_ref, cos_ref, sin_ref, qcos_ref, qsin_ref, dq_ref, dk_ref, dv_ref):
    dq_ref[...], dk_ref[...], dv_ref[...] = back_body(
        q_ref, g_ref, k_ref, v_ref, pick_ref, cos_ref, sin_ref, qcos_ref, qsin_ref
    )


def back_specs(length, masked):
    full = pl.BlockSpec((length, LANES), lambda p: (0, p))
    same = pl.BlockSpec((length, LANES), lambda p: (0, 0))
    row_same = pl.BlockSpec((masked, LANES), lambda p: (0, 0))
    return [
        full, pl.BlockSpec((masked, LANES), lambda p: (0, p)), full, full,
        pl.BlockSpec((masked, length), lambda p: (0, 0)), same, same, row_same, row_same,
    ]


def back_cost(length, masked, pairs):
    return pl.CostEstimate(
        flops=24 * pairs * length * masked * LANES, bytes_accessed=12 * length * pairs * LANES, transcendentals=2 * pairs * length * masked
    )


def back_left(q, grad_rows, k, v, pick, tables):
    masked, length = pick.shape
    width = q.shape[1]
    full = pl.BlockSpec((length, LANES), lambda p: (0, p))
    return pl.pallas_call(
        back_kernel,
        grid=(width // LANES,),
        in_specs=back_specs(length, masked),
        out_specs=[full] * 3,
        out_shape=[jax.ShapeDtypeStruct((length, width), BF)] * 3,
        cost_estimate=back_cost(length, masked, width // LANES),
        name="back_left",
    )(q, grad_rows, k, v, pick, *tables)


def back_swap_kernel(
    q_ref, g_ref, k_ref, v_ref, pick_ref, cos_ref, sin_ref, qcos_ref, qsin_ref, lq_ref, lk_ref, lv_ref,
    dq_ref, dk_ref, dv_ref, buf, out_sem, send, recv, local_sem,
):
    place, device = quad_place()
    step, steps = pl.program_id(0), pl.num_programs(0)
    length = q_ref.shape[0]
    share, hw = lq_ref.shape[0] // QUAD, lq_ref.shape[1]
    outs = (dq_ref, dk_ref, dv_ref)
    copies, local = [], []
    mine = pl.ds(pl.multiple_of(place * hw, hw), hw)
    for i, (ref, out) in enumerate(zip((lq_ref, lk_ref, lv_ref), outs, strict=True)):
        dst = out.at[pl.ds(length, share), mine]
        for j in range(1, QUAD):
            to = (place + j) % QUAD
            src = ref.at[pl.ds(pl.multiple_of(to * share, share), share), :]
            copies.append(remote(src, dst, send.at[i, j - 1], recv.at[i, j - 1], device(to)))
        src = ref.at[pl.ds(pl.multiple_of(place * share, share), share), :]
        local.append(pltpu.make_async_copy(src, dst, local_sem.at[i]))

    def out_copy(at, i):
        slot = at % 2
        columns = pl.ds(pl.multiple_of(at * LANES, LANES), LANES)
        return pltpu.make_async_copy(buf.at[slot, i], outs[i].at[pl.ds(0, length), columns], out_sem.at[slot, i])

    @pl.when(step == 0)
    def _():
        greet(quad_peers())
        start_all(copies + local)

    @pl.when(step >= 2)
    def _():
        for i in range(3):
            out_copy(step - 2, i).wait()

    results = back_body(q_ref, g_ref, k_ref, v_ref, pick_ref, cos_ref, sin_ref, qcos_ref, qsin_ref)
    for i in range(3):
        buf[step % 2, i] = results[i]
        out_copy(step, i).start()

    @pl.when(step == steps - 1)
    def _():
        for i in range(3):
            out_copy(step - 1, i).wait()
            out_copy(step, i).wait()
        wait_all(copies + local)


def back_swap(q, grad_rows, k, v, pick, tables, left):
    masked, length = pick.shape
    width = q.shape[1]
    share = left[0].shape[0] // QUAD
    return pl.pallas_call(
        back_swap_kernel,
        grid=(width // LANES,),
        in_specs=back_specs(length, masked) + [any_spec()] * 3,
        out_specs=[any_spec()] * 3,
        out_shape=[jax.ShapeDtypeStruct((length + share, width), BF)] * 3,
        scratch_shapes=[
            pltpu.VMEM((2, 3, length, LANES), BF),
            pltpu.SemaphoreType.DMA((2, 3)),
            pltpu.SemaphoreType.DMA((3, QUAD - 1)),
            pltpu.SemaphoreType.DMA((3, QUAD - 1)),
            pltpu.SemaphoreType.DMA((3,)),
        ],
        compiler_params=pltpu.CompilerParams(collective_id=2, has_side_effects=True),
        cost_estimate=back_cost(length, masked, width // LANES),
        name="back_swap",
    )(q, grad_rows, k, v, pick, *tables, *left)


def feed_kernel(
    n_ten, tok_ref, att_ref, left_ref, wo_ref, gain_ref, bias_ref, pick_ref, part_pick_ref, cot_ref, wg_ref, wu_ref, wd_ref,
    ag_in, au_in, ad_in, out_ref, out_left_ref, att_m_ref, gr2_ref, gatt_ref, left_gatt_ref, vec_ref, all_own_ref, all_left_ref,
    ag_ref, au_ref, ad_ref,
    x_ref, acc_ref, normed_ref, inv_ref, grad_ref, g_buf, u_buf, d_buf, rows_buf, rows_parts, own_m, left_m, gatt_buf, gatt_parts,
    buf_sem, small_send, small_recv, line_send, line_recv, local_sem, send, recv,
):
    step, steps = pl.program_id(0), pl.num_programs(0)
    rows, width = tok_ref.shape
    length = att_ref.shape[0]
    masked = cot_ref.shape[0]
    slots = masked // 2
    unit = g_buf.shape[2]
    units = wg_ref.shape[1]
    per = units // unit
    part, hw = rows_buf.shape[1], gatt_parts.shape[2]
    gain = gain_ref[...]
    own = (wg_ref, wu_ref, wd_ref)
    route = WeightRoute((ag_ref, au_ref, ad_ref), own, n_ten, send, recv)
    order = route.order
    place, device = quad_place()
    rows_copies, gatt_copies = [], []
    for j in range(1, QUAD):
        to = (place + j) % QUAD
        rows_copies.append(
            remote(rows_buf.at[to], rows_parts.at[j - 1], small_send.at[0, j - 1], small_recv.at[0, j - 1], device(to))
        )
        src = gatt_buf.at[:, pl.ds(pl.multiple_of(to * hw, hw), hw)]
        gatt_copies.append(
            remote(src, gatt_parts.at[j - 1], small_send.at[1, j - 1], small_recv.at[1, j - 1], device(to))
        )

    line_copies = [[], []]
    local = []
    for n, (src, out) in enumerate(((own_m, all_own_ref), (left_m, all_left_ref))):
        for j in range(1, n_ten):
            to = (route.t + j) % n_ten
            line_copies[n].append(
                remote(src, out.at[route.t], line_send.at[n, j - 1], line_recv.at[n, j - 1], {"tensor": to})
            )
        local.append(pltpu.make_async_copy(src, out.at[route.t], local_sem.at[n]))

    def fetch(at):
        slot, i, b = at % 2, at // per, at % per

        def make(refs, shard_at):
            base = pl.multiple_of(shard_at * units + b * unit, unit)
            return [
                pltpu.make_async_copy(refs[0].at[:, pl.ds(base, unit)], g_buf.at[slot], buf_sem.at[slot, 0]),
                pltpu.make_async_copy(refs[1].at[:, pl.ds(base, unit)], u_buf.at[slot], buf_sem.at[slot, 1]),
                pltpu.make_async_copy(refs[2].at[pl.ds(base, unit), :], d_buf.at[slot], buf_sem.at[slot, 2]),
            ]

        @pl.when(i == 0)
        def _():
            start_all(make(own, 0))

        @pl.when(i > 0)
        def _():
            which = order[1] * (i == 1) + order[2] * (i == 2) + order[3] * (i == 3)
            start_all(make((ag_ref, au_ref, ad_ref), which))

    def fetched(at):
        slot = at % 2
        wait_all(
            [
                pltpu.make_async_copy(wg_ref.at[:, pl.ds(0, unit)], g_buf.at[slot], buf_sem.at[slot, 0]),
                pltpu.make_async_copy(wu_ref.at[:, pl.ds(0, unit)], u_buf.at[slot], buf_sem.at[slot, 1]),
                pltpu.make_async_copy(wd_ref.at[pl.ds(0, unit), :], d_buf.at[slot], buf_sem.at[slot, 2]),
            ]
        )

    def norm(res):
        normed, inv_std = layer_stats(res)
        return normed, inv_std, (normed * gain + bias_ref[...]).astype(BF)

    @pl.when(step == 0)
    def _():
        greet(quad_peers() + [route.y_peer] + [{"tensor": (route.t + j) % n_ten} for j in range(1, n_ten)])
        start_all(route.hop(2, 1))
        start_all(route.hop(3, 0))
        fetch(0)
        tile = rows - length
        for i, (pick, att, tok) in enumerate(
            ((pick_ref[...], att_ref[...], tok_ref[:length, :]), (part_pick_ref[...], left_ref[...], tok_ref[length:, :]))
        ):
            here = slice(i * slots, (i + 1) * slots)
            att_m = dot_n(pick, att).astype(BF)
            att_m_ref[here, :] = att_m
            normed, inv_std, low = norm(dot_n(pick, tok) + dot_n(att_m, wo_ref[...]))
            normed_ref[here, :] = normed
            inv_ref[here, :] = jnp.broadcast_to(inv_std, (slots, LANES))
            here_too = jnp.sum(pick.astype(F32), axis=1, keepdims=True) > 0.0
            low = jnp.where(here_too, low.astype(F32), 0.0)
            x_ref[rows + i * slots : rows + (i + 1) * slots, :] = low.astype(BF)
            if i == 0:
                own_m[...] = low.astype(BF)
            else:
                for k in range(QUAD):
                    rows_buf[k] = low[k * part : (k + 1) * part, :].astype(BF)
        for at in range(0, rows, tile):
            att = att_ref[at : at + tile, :] if at < length else left_ref[...]
            res = tok_ref[at : at + tile, :].astype(F32) + dot_n(att, wo_ref[...])
            x_ref[at : at + tile, :] = norm(res)[2]
            acc_ref[at : at + tile, :] = res
        grad_ref[...] = jnp.zeros_like(grad_ref)

    fetched(step)

    @pl.when((step + 1 < steps) & ((step + 1) % per != 0))
    def _():
        fetch(step + 1)

    slot = step % 2
    x = x_ref[...]
    w_g, w_u, w_d = g_buf[slot], u_buf[slot], d_buf[slot]
    gate, up = dot_n(x, w_g), dot_n(x, w_u)
    sig = jax.nn.sigmoid(gate)
    act = gate * sig
    hidden = (act[:rows] * up[:rows]).astype(BF)
    for at in range(0, width, unit):
        acc_ref[:, at : at + unit] += dot_n(hidden, w_d[:, at : at + unit])
    back = dot_t(cot_ref[...].astype(BF), w_d)
    gate, up, sig, act = gate[rows:], up[rows:], sig[rows:], act[rows:]
    grad_gate = (back * up * sig * (1.0 + gate * (1.0 - sig))).astype(BF)
    grad_up = (back * act).astype(BF)
    grad_ref[...] += dot_t(grad_gate, w_g) + dot_t(grad_up, w_u)

    @pl.when(step == 1)
    def _():
        start_all(rows_copies)
        start_all(line_copies[0])
        local[0].start()

    @pl.when(step == 2 * per)
    def _():
        wait_all(rows_copies)
        whole = rows_buf[place].astype(F32)
        for j in range(QUAD - 1):
            whole = whole + rows_parts[j].astype(F32)
        left_m[...] = whole.astype(BF)

    @pl.when(step == 2 * per + 1)
    def _():
        start_all(line_copies[1])
        local[1].start()

    @pl.when(step == per + 1)
    def _():
        received(route.hop(2, 1))
        start_all(route.hop(2, 2))
        received(route.hop(3, 0))
        start_all(route.hop(3, 1))

    @pl.when(step == 2 * per - 1)
    def _():
        received(route.hop(2, 2))

    @pl.when(step == 2 * per + 2)
    def _():
        received(route.hop(3, 1))
        start_all(route.hop(3, 2))

    @pl.when(step == 3 * per - 1)
    def _():
        received(route.hop(3, 2))

    @pl.when((step + 1 < steps) & ((step + 1) % per == 0))
    def _():
        fetch(step + 1)

    @pl.when(step == steps - 1)
    def _():
        grad, normed = grad_ref[...], normed_ref[...]
        gr2 = (cot_ref[...] + norm_back(grad, normed, inv_ref[:, :1], gain)).astype(BF)
        gr2_ref[...] = gr2
        gatt = dot_t(gr2, wo_ref[...]).astype(BF)
        gatt_ref[...] = gatt[:slots]
        gatt_buf[...] = gatt[slots:]
        vec_ref[...] = jnp.concatenate(
            [jnp.sum(grad * normed, axis=0, keepdims=True), jnp.sum(grad, axis=0, keepdims=True)], axis=0
        )
        start_all(gatt_copies)
        out_ref[...] = acc_ref[:length, :].astype(BF)
        chunk = out_left_ref.shape[1]
        for i in range(2):
            out_left_ref[(i + route.t) % 2] = acc_ref[length + i * chunk : length + (i + 1) * chunk, :].astype(BF)
        sent_all(route.hop(2, 1) + route.hop(2, 2) + route.hop(3, 0) + route.hop(3, 1) + route.hop(3, 2))
        wait_all(gatt_copies)
        whole = gatt_buf[:, pl.ds(pl.multiple_of(place * hw, hw), hw)].astype(F32)
        for j in range(QUAD - 1):
            whole = whole + gatt_parts[j].astype(F32)
        left_gatt_ref[...] = whole.astype(BF)
        wait_all(line_copies[0] + line_copies[1])
        wait_all(local)


def feed_forward(tok, att, left_att, w_out, gain, bias, pick, part_pick, cot, ffn, gathered, n_ten):
    rows, width = tok.shape
    units = ffn[0].shape[1]
    masked = cot.shape[0]
    slots, hw = masked // 2, width // QUAD
    unit = 256
    whole = lambda *shape: pl.BlockSpec(shape, lambda i: (0,) * len(shape))
    low = jax.ShapeDtypeStruct((masked, width), BF)
    return pl.pallas_call(
        functools.partial(feed_kernel, n_ten),
        grid=(n_ten * units // unit,),
        in_specs=[once(x.shape) for x in (tok, att, left_att, w_out)]
        + [once((1, width)), once((1, width)), once(pick.shape), once(part_pick.shape), once(cot.shape)]
        + [any_spec()] * 6,
        out_specs=[whole(*att.shape), whole(2, left_att.shape[0] // 2, width)]
        + [whole(masked, width), whole(masked, width), whole(slots, width), whole(slots, hw)]
        + [whole(2, width)]
        + [any_spec()] * 5,
        out_shape=[
            jax.ShapeDtypeStruct(att.shape, BF), jax.ShapeDtypeStruct((2, left_att.shape[0] // 2, width), BF), low, low,
            jax.ShapeDtypeStruct((slots, width), BF), jax.ShapeDtypeStruct((slots, hw), BF),
            jax.ShapeDtypeStruct((2, width), F32),
            jax.ShapeDtypeStruct((n_ten, slots, width), BF), jax.ShapeDtypeStruct((n_ten, slots // QUAD, width), BF),
        ]
        + [jax.ShapeDtypeStruct(w.shape, BF) for w in gathered],
        input_output_aliases={12: 9, 13: 10, 14: 11},
        scratch_shapes=[
            pltpu.VMEM((rows + masked, width), BF),
            pltpu.VMEM((rows, width), F32),
            pltpu.VMEM((masked, width), F32),
            pltpu.VMEM((masked, LANES), F32),
            pltpu.VMEM((masked, width), F32),
            pltpu.VMEM((2, width, unit), BF),
            pltpu.VMEM((2, width, unit), BF),
            pltpu.VMEM((2, unit, width), BF),
            pltpu.VMEM((QUAD, slots // QUAD, width), BF),
            pltpu.VMEM((QUAD - 1, slots // QUAD, width), BF),
            pltpu.VMEM((slots, width), BF),
            pltpu.VMEM((slots // QUAD, width), BF),
            pltpu.VMEM((slots, width), BF),
            pltpu.VMEM((QUAD - 1, slots, hw), BF),
            pltpu.SemaphoreType.DMA((2, 3)),
            pltpu.SemaphoreType.DMA((2, QUAD - 1)),
            pltpu.SemaphoreType.DMA((2, QUAD - 1)),
            pltpu.SemaphoreType.DMA((2, n_ten - 1)),
            pltpu.SemaphoreType.DMA((2, n_ten - 1)),
            pltpu.SemaphoreType.DMA((2,)),
        ]
        + route_sems(),
        compiler_params=pltpu.CompilerParams(collective_id=5, has_side_effects=True),
        cost_estimate=pl.CostEstimate(
            flops=8 * rows * width * n_ten * units, bytes_accessed=6 * width * n_ten * units, transcendentals=rows * n_ten * units
        ),
        name="feed_forward",
    )(tok, att, left_att, w_out, gain.reshape(1, width), bias.reshape(1, width), pick, part_pick, cot, *ffn, *gathered)[:9]


def feed_grads_kernel(own_ref, left_ref, cot_ref, wg_ref, wu_ref, wd_ref, gg_ref, gu_ref, gd_ref, x_ref):
    @pl.when(pl.program_id(0) == 0)
    def _():
        x_ref[: own_ref.shape[0], :] = own_ref[...]
        x_ref[own_ref.shape[0] :, :] = left_ref[...]

    x, cot = x_ref[...], cot_ref[...]
    gate, up, back = dot_n(x, wg_ref[...]), dot_n(x, wu_ref[...]), dot_t(cot, wd_ref[...])
    sig = jax.nn.sigmoid(gate)
    act = gate * sig
    gg_ref[...] = t_dot((back * up * sig * (1.0 + gate * (1.0 - sig))).astype(BF), x).astype(BF)
    gu_ref[...] = t_dot((back * act).astype(BF), x).astype(BF)
    gd_ref[...] = t_dot((act * up).astype(BF), cot).astype(BF)


def feed_grads(own, left, cot, w_gate, w_up, w_down):
    rows, width = cot.shape
    units = w_gate.shape[1]
    unit = 256
    columns = pl.BlockSpec((width, unit), lambda i: (0, i))
    line = pl.BlockSpec((unit, width), lambda i: (i, 0))
    return pl.pallas_call(
        feed_grads_kernel,
        grid=(units // unit,),
        in_specs=[once(own.shape), once(left.shape), once(cot.shape), columns, columns, line],
        out_specs=[line] * 3,
        out_shape=[jax.ShapeDtypeStruct((units, width), BF)] * 3,
        scratch_shapes=[pltpu.VMEM((rows, width), BF)],
        cost_estimate=pl.CostEstimate(flops=12 * rows * width * units, bytes_accessed=12 * width * units, transcendentals=rows * units),
        name="feed_grads",
    )(own, left, cot, w_gate, w_up, w_down)


def token_back_kernel(
    tok_ref, dq_ref, dk_ref, dv_ref, wq_ref, wk_ref, wv_ref, gain_ref, pick_ref, rows_ref, out_ref, vec_ref
):
    acc = dot_t(dq_ref[...], wq_ref[...]) + dot_t(dk_ref[...], wk_ref[...]) + dot_t(dv_ref[...], wv_ref[...])
    normed, inv_std = layer_stats(tok_ref[...].astype(F32))
    direct = t_dot(pick_ref[...], rows_ref[0])
    out_ref[...] = (direct + norm_back(acc, normed, inv_std, gain_ref[...])).astype(BF)
    sums = jnp.concatenate([jnp.sum(acc * normed, axis=0, keepdims=True), jnp.sum(acc, axis=0, keepdims=True)], axis=0)

    @pl.when(pl.program_id(0) == 0)
    def _():
        vec_ref[...] = sums

    @pl.when(pl.program_id(0) > 0)
    def _():
        vec_ref[...] += sums


def token_back(tok, grads, weights, gain, pick, rows_m):
    rows, width = tok.shape
    slots = pick.shape[0]
    tile = 256
    row = pl.BlockSpec((tile, width), lambda r: (r, 0))
    own = rows // tile - 1
    return pl.pallas_call(
        token_back_kernel,
        grid=(rows // tile,),
        in_specs=[row] * 4
        + [once((width, width))] * 3
        + [
            once((1, width)),
            pl.BlockSpec((slots, tile), lambda r: (0, r)),
            pl.BlockSpec((1, slots, width), lambda r: (r // own, 0, 0)),
        ],
        out_specs=[row, pl.BlockSpec((2, width), lambda r: (0, 0))],
        out_shape=[jax.ShapeDtypeStruct((rows, width), BF), jax.ShapeDtypeStruct((2, width), F32)],
        cost_estimate=pl.CostEstimate(flops=6 * rows * width * width, bytes_accessed=16 * rows * width, transcendentals=0),
        name="token_back",
    )(tok, *grads, *weights, gain.reshape(1, width), pick, rows_m)


def exchange_out_kernel(
    sizes, go_ref, gq_ref, gk_ref, gv_ref, gg_ref, gu_ref, gd_ref, grad_ref, vec_ref, w_ref, ffn_ref, tok_ref, vec_out,
    buf1, buf2, buf3, buf4, vec_buf, vec_sum,
    tok_send, tok_recv, send1, recv1, send2, recv2, send3, recv3, send4, recv4, vec_send, vec_recv, local_sem,
):
    n_seq, n_ten, half, rows = sizes
    dp, sx, t = lax.axis_index("dp"), lax.axis_index("seq"), lax.axis_index("tensor")
    y, c = dp // 2, dp % 2
    me = sx * n_ten + t
    group = n_seq * n_ten
    others = []
    for i in range(1, group):
        g = (me + i) % group
        others.append((g // n_ten, g % n_ten))
    y_peer, c_peer, x_peer = {"dp": (dp + 2) % 4}, {"dp": 2 * y + 1 - c}, {"seq": 1 - sx}
    z_peers = [{"tensor": (t + j) % n_ten} for j in range(1, n_ten)]
    beside = [{"dp": 2 * y + 1 - c, "tensor": (t + j) % n_ten} for j in range(1, n_ten)]
    greet([{"seq": a, "tensor": b} for a, b in others] + [y_peer, c_peer] + beside)
    grads = (go_ref, gq_ref, gk_ref, gv_ref, gg_ref, gu_ref, gd_ref)
    count, attn = len(grads), w_ref.shape[0]
    x_first = (False, False, False, False, False, True, True)
    height = gq_ref.shape[0]
    hw = height // n_ten

    def columns(b_y, b_c, b_x):
        return pl.ds(pl.multiple_of((b_y * 4 + b_c * 2 + b_x) * LANES, LANES), LANES)

    def add_rows(out, first, second):
        def body(i, carry):
            at = pl.ds(pl.multiple_of(i * hw, hw), hw)
            out[at, :] = (first[at, :].astype(F32) + second[at, :].astype(F32)).astype(BF)
            return carry

        lax.fori_loop(0, height // hw, body, 0)

    stage1 = []
    for a in range(count):
        stage1.append(
            [
                remote(
                    grads[a].at[:, columns(b_y, 1 - c, b_x)], buf1.at[a, b_y, b_x],
                    send1.at[a, 2 * b_y + b_x], recv1.at[a, 2 * b_y + b_x], c_peer,
                )
                for b_y in range(2)
                for b_x in range(2)
            ]
        )
    for copies in stage1:
        start_all(copies)

    vec_hops = []
    hops = [c_peer, x_peer, y_peer]
    vec_sum[0] = vec_ref[...]
    for i, peer in enumerate(hops):
        vec_hops.append([remote(vec_sum.at[i], vec_buf.at[i], vec_send.at[i], vec_recv.at[i], peer)])
    vec_hops.append(
        [
            remote(vec_sum.at[3], vec_buf.at[3 + j], vec_send.at[3 + j], vec_recv.at[3 + j], peer)
            for j, peer in enumerate(z_peers)
        ]
    )
    start_all(vec_hops[0])

    tokens = []
    for i, (a, b) in enumerate(others):
        tokens.append(
            remote(
                grad_ref.at[pl.ds(pl.multiple_of((a * n_ten + b) * rows, rows), rows), :],
                tok_ref.at[sx * half + t],
                tok_send.at[i], tok_recv.at[i], {"seq": a, "tensor": b},
            )
        )
    shared = []
    for i in range(n_seq):
        src, dst = grad_ref.at[pl.ds((group + i) * rows, rows), :], tok_ref.at[t % 2 * half + n_ten]
        shared.append(
            (
                2 * c + i == t,
                remote(
                    src, dst, tok_send.at[group - 1 + i], tok_recv.at[group - 1 + t % 2],
                    {"dp": 2 * y + t // 2, "tensor": 2 * c + i},
                ),
                pltpu.make_async_copy(src, dst, local_sem.at[1]),
            )
        )
    arriving = [
        remote(
            grad_ref.at[pl.ds(0, rows), :], tok_ref.at[i * half + n_ten],
            tok_send.at[group - 1], tok_recv.at[group - 1 + i], c_peer,
        )
        for i in range(n_seq)
    ]
    start_all(tokens)
    for here, away, near in shared:
        pl.when(here)(near.start)
        pl.when(jnp.logical_not(here))(away.start)
    local = [
        pltpu.make_async_copy(
            grad_ref.at[pl.ds(pl.multiple_of(me * rows, rows), rows), :], tok_ref.at[sx * half + t], local_sem.at[0]
        ),
    ]
    start_all(local)

    stage2 = []
    for a in range(count):
        for copy in stage1[a]:
            copy.wait_recv()
        for b_y in range(2):
            for b_x in range(2):
                add_rows(buf1.at[a, b_y, b_x], grads[a].at[:, columns(b_y, c, b_x)], buf1.at[a, b_y, b_x])
        copies = []
        for b in range(2):
            src, peer = (buf1.at[a, b, 1 - sx], x_peer) if x_first[a] else (buf1.at[a, 1 - y, b], y_peer)
            copies.append(remote(src, buf2.at[a, b], send2.at[a, b], recv2.at[a, b], peer))
        start_all(copies)
        stage2.append(copies)
    vec_hops[0][0].wait_recv()
    vec_sum[1] = vec_sum[0] + vec_buf[0]
    start_all(vec_hops[1])
    stage3, stage4 = {}, {}

    def second(a):
        for copy in stage2[a]:
            copy.wait_recv()
        for b in range(2):
            own = buf1.at[a, b, sx] if x_first[a] else buf1.at[a, y, b]
            add_rows(buf2.at[a, b], own, buf2.at[a, b])
        src, peer = (buf2.at[a, 1 - y], y_peer) if x_first[a] else (buf2.at[a, 1 - sx], x_peer)
        stage3[a] = remote(src, buf3.at[a], send3.at[a], recv3.at[a], peer)
        stage3[a].start()

    def third(a):
        stage3[a].wait_recv()
        own = buf2.at[a, y] if x_first[a] else buf2.at[a, sx]
        if a >= attn:

            def final(i, carry):
                at = pl.ds(pl.multiple_of(i * hw, hw), hw)
                ffn_ref[a - attn, at, :] = own[at, :].astype(F32) + buf3[a, at, :].astype(F32)
                return carry

            lax.fori_loop(0, height // hw, final, 0)
            return
        add_rows(buf3.at[a], own, buf3.at[a])
        stage4[a] = []
        for j, peer in enumerate(z_peers):
            to = (t + 1 + j) % n_ten
            src = buf3.at[a, pl.ds(pl.multiple_of(to * hw, hw), hw), :]
            stage4[a].append(remote(src, buf4.at[a, j], send4.at[a, j], recv4.at[a, j], peer))
        start_all(stage4[a])

    vec_hops[1][0].wait_recv()
    vec_sum[2] = vec_sum[1] + vec_buf[1]
    start_all(vec_hops[2])
    for a in (0, 1, 2, 5, 3, 6):
        second(a)
    third(0)
    third(1)
    second(4)
    for a in (2, 3, 5, 6, 4):
        third(a)
    vec_hops[2][0].wait_recv()
    vec_sum[3] = vec_sum[2] + vec_buf[2]
    start_all(vec_hops[3])
    for n, copies in stage4.items():
        total = buf3[n, pl.ds(pl.multiple_of(t * hw, hw), hw), :].astype(F32)
        for j, copy in enumerate(copies):
            copy.wait_recv()
            total = total + buf4[n, j].astype(F32)
        w_ref[n] = total
    total = vec_sum[3]
    for j, copy in enumerate(vec_hops[3]):
        copy.wait_recv()
        total = total + vec_buf[3 + j]
    vec_out[...] = total
    for copies in stage1 + stage2 + list(stage4.values()) + [list(stage3.values())] + vec_hops:
        for copy in copies:
            copy.wait_send()
    wait_all(local)
    wait_all(tokens)
    for here, away, near in shared:
        pl.when(here)(near.wait)
        pl.when(jnp.logical_not(here))(away.wait_send)
    for i in range(n_seq):
        pl.when(jnp.logical_not(2 * c + i == t))(arriving[i].wait_recv)


def exchange_out(ffn_grads, attn_grads, grad_tok, vectors, n_seq, n_ten, half, rows):
    grads = (*attn_grads, *ffn_grads)
    ffn, attn = len(ffn_grads), len(attn_grads)
    height, width = grads[0].shape
    hw, count, group = height // n_ten, len(grads), n_seq * n_ten
    vmem = pl.BlockSpec(memory_space=pltpu.VMEM)
    dma = pltpu.SemaphoreType.DMA
    hops = 3 + n_ten - 1
    return pl.pallas_call(
        functools.partial(exchange_out_kernel, (n_seq, n_ten, half, rows)),
        in_specs=[vmem] * (count + 2),
        out_specs=[vmem, vmem, any_spec(), vmem],
        out_shape=[
            jax.ShapeDtypeStruct((attn, hw, LANES), F32),
            jax.ShapeDtypeStruct((ffn, height, LANES), F32),
            jax.ShapeDtypeStruct((n_seq * half, rows, width), BF),
            jax.ShapeDtypeStruct(vectors.shape, F32),
        ],
        scratch_shapes=[
            pltpu.VMEM((count, 2, 2, height, LANES), BF),
            pltpu.VMEM((count, 2, height, LANES), BF),
            pltpu.VMEM((count, height, LANES), BF),
            pltpu.VMEM((attn, n_ten - 1, hw, LANES), BF),
            pltpu.VMEM((hops,) + vectors.shape, F32),
            pltpu.VMEM((4,) + vectors.shape, F32),
            dma((group + 1,)), dma((group + 1,)),
            dma((count, 4)), dma((count, 4)),
            dma((count, 2)), dma((count, 2)),
            dma((count,)), dma((count,)),
            dma((attn, n_ten - 1)), dma((attn, n_ten - 1)),
            dma((hops,)), dma((hops,)),
            dma((2,)),
        ],
        compiler_params=pltpu.CompilerParams(collective_id=4, has_side_effects=True),
        name="exchange_out",
    )(*grads, grad_tok, vectors)


def rotary_lanes(cosine, sine):
    reps = LANES // HEAD_DIM
    return jnp.concatenate([cosine, cosine] * reps, axis=1), jnp.concatenate([-sine, sine] * reps, axis=1)


def position_tables(length):
    half_dim = HEAD_DIM // 2
    inv_freq = np.float32(10000.0) ** (-np.arange(half_dim, dtype=np.float32) * np.float32(2.0 / HEAD_DIM))
    angles = (np.arange(length, dtype=np.float32)[:, None] * inv_freq[None, :]).astype(np.float64)
    cosine, sine = np.cos(angles).astype(np.float32), np.sin(angles).astype(np.float32)
    reps = LANES // HEAD_DIM
    return np.concatenate([cosine, cosine] * reps, axis=1), np.concatenate([-sine, sine] * reps, axis=1)


def window_shards(
    tokens,
    norm1_gain,
    norm1_bias,
    w_query,
    w_key,
    w_value,
    w_out,
    norm2_gain,
    norm2_bias,
    w_gate,
    w_up,
    w_down,
    out_grad,
    masked_rows,
    window_counts,
):
    rows_local, windows, width = tokens.shape
    n_dp, n_seq, n_ten = lax.axis_size("dp"), lax.axis_size("seq"), lax.axis_size("tensor")
    dp_index, seq_index, ten_index = lax.axis_index("dp"), lax.axis_index("seq"), lax.axis_index("tensor")
    shard_index = dp_index * n_seq + seq_index
    core = dp_index % 2
    place = seq_index * 2 + core
    half = windows // n_seq
    length = rows_local * n_seq * n_ten
    share = length // QUAD
    hw = width // QUAD
    slots = masked_rows.shape[1]
    part = slots // QUAD

    live = jnp.arange(windows) < window_counts[0]
    valid = (masked_rows < length) & live[:, None]
    coded = jnp.where(valid, masked_rows, length)
    info = jnp.concatenate([coded, jnp.full((1, slots), jnp.sum(valid.astype(jnp.int32)))], axis=0)
    info = jnp.pad(info, ((0, -(windows + 1) % 8), (0, -slots % LANES)))
    both_tok, all_q, all_k, all_v, all_out, infos, left_grad = exchange_in(
        jnp.swapaxes(tokens, 0, 1), w_query, w_key, w_value, w_out, info, out_grad, n_dp, n_seq, n_ten
    )
    loss_weight = LOSS_SCALE / jnp.sum(infos[:, windows, 0]).astype(F32)
    pick_one = lambda x, at: lax.dynamic_index_in_dim(x, at, 0, keepdims=False)
    first_window = seq_index * half
    my_coded = lax.dynamic_slice_in_dim(coded, first_window, n_ten, 0)
    my_grad = lax.dynamic_slice_in_dim(out_grad, first_window, n_ten, 0)
    pair_infos = lax.dynamic_slice_in_dim(infos, dp_index - core, 2, 0)
    left_coded = jnp.stack([pair_infos[i // n_seq, i % n_seq * half + n_ten, :slots] for i in range(n_ten)])
    weigh = lambda grad, rows: jnp.where((rows < length)[..., None], grad.astype(F32) * loss_weight, 0.0)

    own_rows, left_rows = pick_one(my_coded, ten_index), pick_one(left_coded, ten_index)
    every = jnp.arange(length)
    my_left = place * share + jnp.arange(share)
    own_pick = (own_rows[:, None] == every[None, :]).astype(BF)
    left_pick = (left_rows[:, None] == every[None, :]).astype(BF)
    part_match = left_rows[:, None] == my_left[None, :]
    part_pick = part_match.astype(BF)
    left_here = jnp.where(jnp.any(part_match, axis=1), left_rows, length)
    my_cot = jnp.concatenate(
        [weigh(pick_one(my_grad, ten_index), own_rows), weigh(pick_one(left_grad, ten_index), left_here)], axis=0
    )

    tables = [jnp.asarray(x) for x in position_tables(length)]
    part_tables = [lax.dynamic_slice_in_dim(x, place * share, share, 0) for x in tables]
    own_tables = tables + list(rotary_lanes(*rotary_tables(own_rows)))
    left_tables = tables + list(rotary_lanes(*rotary_tables(left_rows)))

    ffn = (w_gate, w_up, w_down)
    first, q, k, v = norm_qkv(both_tok, norm1_gain, norm1_bias, all_q, all_k, all_v, tables, part_tables)
    own_att, left_q, left_k, left_v, *gathered = attend_swap(q, k, v, ffn, length, n_ten)
    left_att_part, *gathered = attend_left(left_q, left_k, left_v, gathered, n_ten)
    own_out, left_chunks, att_m, gr2, own_gatt, left_gatt, grad_norm2, all_own, all_left = feed_forward(
        both_tok, own_att, left_att_part, all_out, norm2_gain, norm2_bias, own_pick, part_pick, my_cot, ffn, gathered, n_ten
    )

    grad_w_out = t_dot(att_m, gr2).astype(BF)
    left_back = back_left(left_q, left_gatt, left_k, left_v, left_pick, left_tables)
    dq, dk, dv = back_swap(q, own_gatt, k, v, own_pick, own_tables, left_back)
    all_own, dq, dk, dv = lax.optimization_barrier((all_own, dq, dk, dv))

    part_of = lambda x: lax.dynamic_slice_in_dim(x, place * part, part, 1)
    down_in = jnp.concatenate(
        [
            weigh(my_grad, my_coded).reshape(n_ten * slots, width),
            weigh(part_of(left_grad), part_of(left_coded)).reshape(n_ten * part, width),
        ],
        axis=0,
    ).astype(BF)
    grad_w_ffn = feed_grads(all_own.reshape(-1, width), all_left.reshape(-1, width), down_in, *ffn)
    grad_w_attn = [grad_w_out] + [t_dot(d, first).astype(BF) for d in (dq, dk, dv)]
    grad_both, grad_norm1 = token_back(
        both_tok, (dq, dk, dv), (all_q, all_k, all_v), norm1_gain,
        jnp.concatenate([own_pick, part_pick], axis=1), gr2.reshape(2, slots, width),
    )

    own_out = lax.all_to_all(
        own_out.reshape(n_seq * n_ten, rows_local, width), ("seq", "tensor"), 0, 0, tiled=True
    ).reshape(n_seq, n_ten, rows_local, width)
    left_out = []
    for turn in range(2):
        perm = []
        for d in range(n_dp):
            for sx in range(n_seq):
                for p in range(n_ten):
                    to = d // 2 * 2 + p // 2, sx, d % 2 * 2 + (p % 2 ^ turn)
                    perm.append(((d * n_seq + sx) * n_ten + p, (to[0] * n_seq + to[1]) * n_ten + to[2]))
        left_out.append(lax.ppermute(left_chunks[turn], ("dp", "seq", "tensor"), perm))
    even = ten_index % 2 == 0
    left_out = jnp.stack([jnp.where(even, left_out[0], left_out[1]), jnp.where(even, left_out[1], left_out[0])])
    output = jnp.concatenate([own_out, left_out[:, None]], axis=1).reshape(windows, rows_local, width)
    output = jnp.swapaxes(output, 0, 1)
    vectors = jnp.concatenate(
        [grad_norm1, grad_norm2, jnp.zeros((4, width), F32)], axis=0
    )
    gw_attn, gw_ffn, grad_tokens, vectors = exchange_out(
        grad_w_ffn, grad_w_attn, grad_both, vectors, n_seq, n_ten, half, rows_local
    )
    grad_tokens = jnp.swapaxes(grad_tokens, 0, 1).astype(F32)
    small = width // (n_dp * n_seq * n_ten)
    vectors = lax.dynamic_slice_in_dim(vectors, (shard_index * n_ten + ten_index) * small, small, 1)

    return (
        output,
        grad_tokens,
        vectors[0],
        vectors[1],
        gw_attn[1].T,
        gw_attn[2].T,
        gw_attn[3].T,
        gw_attn[0],
        vectors[2],
        vectors[3],
        gw_ffn[0].T,
        gw_ffn[1].T,
        gw_ffn[2],
    )


def shards(tokens, *rest):
    n_dp, n_seq, n_ten = lax.axis_size("dp"), lax.axis_size("seq"), lax.axis_size("tensor")
    whole = n_dp == 4 and n_seq == 2 and n_ten == 4 and tokens.shape[1] == n_seq * (n_ten + 1)
    return (window_shards if whole else block_shards)(tokens, *rest)


def solution(mesh):
    return jax.shard_map(
        shards,
        mesh=mesh,
        in_specs=(
            P(("seq", "tensor"), "dp", None),
            P(),
            P(),
            P(None, "tensor"),
            P(None, "tensor"),
            P(None, "tensor"),
            P("tensor", None),
            P(),
            P(),
            P(None, "tensor"),
            P(None, "tensor"),
            P("tensor", None),
            P("dp", None, None),
            P("dp", None),
            P("dp"),
        ),
        out_specs=(
            P(("seq", "tensor"), "dp", None),
            P(("seq", "tensor"), "dp", None),
            P(("dp", "seq", "tensor")),
            P(("dp", "seq", "tensor")),
            P(("dp", "seq"), "tensor"),
            P(("dp", "seq"), "tensor"),
            P(("dp", "seq"), "tensor"),
            P("tensor", ("dp", "seq")),
            P(("dp", "seq", "tensor")),
            P(("dp", "seq", "tensor")),
            P(("dp", "seq"), "tensor"),
            P(("dp", "seq"), "tensor"),
            P("tensor", ("dp", "seq")),
        ),
        check_vma=False,
    )
```

```python
import math

import functools

import jax
import jax.numpy as jnp
import numpy as np
from jax import lax
from jax.experimental import pallas as pl
from jax.experimental.pallas import tpu as pltpu
from jax.sharding import PartitionSpec as P

HEAD_DIM = 64
L = 1024
LOSS_SCALE = 1024


epsilon = 1e-05


def layer_stats(inputs):
    row_mean = jnp.mean(inputs, axis=-1, keepdims=True)
    centred = inputs - row_mean
    inv_std = lax.rsqrt(jnp.mean(centred * centred, axis=-1, keepdims=True) + epsilon)
    return (centred * inv_std, inv_std)


def norm_back(grad_norm, normed, inv_std, gain_vec):
    scaled = grad_norm * gain_vec
    return inv_std * (
        scaled
        - jnp.mean(scaled, axis=-1, keepdims=True)
        - normed * jnp.mean(scaled * normed, axis=-1, keepdims=True)
    )


def rotary_tables(positions):
    half_dim = HEAD_DIM // 2
    inv_freq = 10000.0 ** (-jnp.arange(half_dim, dtype=jnp.float32) * 2.0 / HEAD_DIM)
    angles = positions.astype(jnp.float32)[:, None] * inv_freq[None, :]
    return (jnp.cos(angles), jnp.sin(angles))


def rotate(values, cosine, sine):
    half_dim = values.shape[-1] // 2
    first_half = values[..., :half_dim]
    second_half = values[..., half_dim:]
    cos_b = cosine[:, None, None, :]
    sin_b = sine[:, None, None, :]
    return jnp.concatenate(
        [first_half * cos_b - second_half * sin_b, second_half * cos_b + first_half * sin_b],
        axis=-1,
    )


def unrotate(grads, cosine, sine):
    half_dim = grads.shape[-1] // 2
    first_half = grads[..., :half_dim]
    second_half = grads[..., half_dim:]
    cos_b = cosine[:, None, None, :]
    sin_b = sine[:, None, None, :]
    return jnp.concatenate(
        [first_half * cos_b + second_half * sin_b, second_half * cos_b - first_half * sin_b],
        axis=-1,
    )


def block_shards(
    tokens,
    norm1_gain,
    norm1_bias,
    w_query,
    w_key,
    w_value,
    w_out,
    norm2_gain,
    norm2_bias,
    w_gate,
    w_up,
    w_down,
    out_grad,
    masked_rows,
    window_counts,
):
    rows_local, windows, model_width = tokens.shape
    span_rows = rows_local * lax.axis_size("tensor")
    seq_index = lax.axis_index("seq")
    tensor_index = lax.axis_index("tensor")
    head_width = w_query.shape[1]
    heads_local = head_width // HEAD_DIM
    score_scale = 1.0 / math.sqrt(HEAD_DIM)
    head_shape = (span_rows, windows, heads_local, HEAD_DIM)
    residual = tokens.astype(jnp.float32)
    normed1, inv_std1 = layer_stats(residual)
    first_low = (normed1 * norm1_gain + norm1_bias).astype(jnp.bfloat16)
    first_full = lax.all_gather(first_low, "tensor", axis=0, tiled=True)
    w_joined = jnp.concatenate([w_query, w_key, w_value], axis=1)
    projected = jnp.einsum("rwd,de->rwe", first_full, w_joined, preferred_element_type=jnp.float32)
    positions = seq_index * span_rows + jnp.arange(span_rows)
    cosine, sine = rotary_tables(positions)
    queries = rotate(projected[..., :head_width].reshape(head_shape), cosine, sine).astype(
        jnp.bfloat16
    )
    keys_rot = (
        rotate(projected[..., head_width : 2 * head_width].reshape(head_shape), cosine, sine)
        .astype(jnp.bfloat16)
        .reshape(span_rows, windows, head_width)
    )
    values_own = projected[..., 2 * head_width :].astype(jnp.bfloat16)
    keys_all, values_all = (
        lax.all_gather(keys_rot, "seq", axis=0, tiled=True),
        lax.all_gather(values_own, "seq", axis=0, tiled=True),
    )
    key_heads = keys_all.reshape(-1, windows, heads_local, HEAD_DIM)
    value_heads = values_all.reshape(-1, windows, heads_local, HEAD_DIM)
    scores = (
        jnp.einsum("qwhd,kwhd->whqk", queries, key_heads, preferred_element_type=jnp.float32)
        * score_scale
    )
    row_max = jnp.max(scores, axis=-1, keepdims=True)
    row_sum = jnp.sum(jnp.exp(scores - row_max), axis=-1, keepdims=True)
    log_norm = row_max + jnp.log(row_sum)
    attn_prob = jnp.exp(scores - log_norm)
    prob_low = attn_prob.astype(jnp.bfloat16)
    attended = (
        jnp.einsum("whqk,kwhd->qwhd", prob_low, value_heads, preferred_element_type=jnp.float32)
        .reshape(span_rows, windows, head_width)
        .astype(jnp.bfloat16)
    )
    block_part = attended
    attn_branch = lax.psum_scatter(
        jnp.einsum("rwe,ed->rwd", block_part, w_out, preferred_element_type=jnp.float32).astype(
            jnp.bfloat16
        ),
        "tensor",
        scatter_dimension=0,
        tiled=True,
    ).astype(jnp.float32)
    residual2 = residual + attn_branch
    normed2, inv_std2 = layer_stats(residual2)
    second_low = (normed2 * norm2_gain + norm2_bias).astype(jnp.bfloat16)
    second_full = lax.all_gather(second_low, "tensor", axis=0, tiled=True)
    gate_proj = jnp.einsum("rwd,df->rwf", second_full, w_gate, preferred_element_type=jnp.float32)
    up_proj = jnp.einsum("rwd,df->rwf", second_full, w_up, preferred_element_type=jnp.float32)
    hidden = (jax.nn.silu(gate_proj) * up_proj).astype(jnp.bfloat16)
    block_part = hidden
    ffn_branch = lax.psum_scatter(
        jnp.einsum("rwf,fd->rwd", block_part, w_down, preferred_element_type=jnp.float32).astype(
            jnp.bfloat16
        ),
        "tensor",
        scatter_dimension=0,
        tiled=True,
    ).astype(jnp.float32)
    output = (residual2 + ffn_branch).astype(jnp.bfloat16)
    live_slot = jnp.arange(windows) < window_counts[0]
    valid_slot = (masked_rows < L) & live_slot[:, None]
    local_masked = jnp.sum(jnp.where(valid_slot, 1, 0)).astype(jnp.int32)
    total_masked = lax.psum(local_masked, "dp")
    loss_weight = LOSS_SCALE / total_masked.astype(jnp.float32)
    own_positions = seq_index * span_rows + tensor_index * rows_local + jnp.arange(rows_local)
    matches = (masked_rows[:, None, :] == own_positions[None, :, None]) & live_slot[:, None, None]
    picked = jnp.einsum(
        "wrm,wmd->rwd", matches.astype(jnp.bfloat16), out_grad, preferred_element_type=jnp.float32
    )
    grad_out = picked * loss_weight
    grad_down_in = lax.all_gather(grad_out.astype(jnp.bfloat16), "tensor", axis=0, tiled=True)
    grad_w_down = jnp.einsum(
        "rwf,rwd->fd", hidden, grad_down_in, preferred_element_type=jnp.float32
    )
    grad_hidden = jnp.einsum(
        "rwd,fd->rwf", grad_down_in, w_down, preferred_element_type=jnp.float32
    )
    sigmoid_gate = jax.nn.sigmoid(gate_proj)
    silu_gate = gate_proj * sigmoid_gate
    grad_gate = (
        grad_hidden * up_proj * sigmoid_gate * (1.0 + gate_proj * (1.0 - sigmoid_gate))
    ).astype(jnp.bfloat16)
    grad_up = (grad_hidden * silu_gate).astype(jnp.bfloat16)
    grad_w_gate = jnp.einsum(
        "rwd,rwf->df", second_full, grad_gate, preferred_element_type=jnp.float32
    )
    grad_w_up = jnp.einsum("rwd,rwf->df", second_full, grad_up, preferred_element_type=jnp.float32)
    grad_second = lax.psum_scatter(
        (
            jnp.einsum("rwf,df->rwd", grad_gate, w_gate, preferred_element_type=jnp.float32)
            + jnp.einsum("rwf,df->rwd", grad_up, w_up, preferred_element_type=jnp.float32)
        ).astype(jnp.bfloat16),
        "tensor",
        scatter_dimension=0,
        tiled=True,
    ).astype(jnp.float32)
    grad_norm2_gain = jnp.sum(grad_second * normed2, axis=(0, 1))
    grad_norm2_bias = jnp.sum(grad_second, axis=(0, 1))
    grad_residual2 = grad_out + norm_back(grad_second, normed2, inv_std2, norm2_gain)
    grad_attn_in = lax.all_gather(grad_residual2.astype(jnp.bfloat16), "tensor", axis=0, tiled=True)
    grad_w_out = jnp.einsum(
        "rwe,rwd->ed", attended, grad_attn_in, preferred_element_type=jnp.float32
    )
    grad_attended = jnp.einsum(
        "rwd,ed->rwe", grad_attn_in, w_out, preferred_element_type=jnp.float32
    ).astype(jnp.bfloat16)
    grad_att_heads = grad_attended.reshape(head_shape)
    scores_again = (
        jnp.einsum("qwhd,kwhd->whqk", queries, key_heads, preferred_element_type=jnp.float32)
        * score_scale
    )
    probs_again = jnp.exp(scores_again - log_norm)
    grad_probs = jnp.einsum(
        "qwhd,kwhd->whqk", grad_att_heads, value_heads, preferred_element_type=jnp.float32
    )
    row_delta = jnp.sum(probs_again * grad_probs, axis=-1, keepdims=True)
    grad_scores = (probs_again * (grad_probs - row_delta)).astype(jnp.bfloat16)
    grad_queries = (
        jnp.einsum("whqk,kwhd->qwhd", grad_scores, key_heads, preferred_element_type=jnp.float32)
        * score_scale
    )
    grad_key_all = (
        jnp.einsum("whqk,qwhd->kwhd", grad_scores, queries, preferred_element_type=jnp.float32)
        * score_scale
    ).reshape(-1, windows, head_width)
    grad_value_all = jnp.einsum(
        "whqk,qwhd->kwhd",
        probs_again.astype(jnp.bfloat16),
        grad_att_heads,
        preferred_element_type=jnp.float32,
    ).reshape(-1, windows, head_width)
    grad_keys, grad_values = (
        lax.psum_scatter(
            grad_key_all.astype(jnp.bfloat16), "seq", scatter_dimension=0, tiled=True
        ).astype(jnp.float32),
        lax.psum_scatter(
            grad_value_all.astype(jnp.bfloat16), "seq", scatter_dimension=0, tiled=True
        ).astype(jnp.float32),
    )
    grad_query_lin = (
        unrotate(grad_queries, cosine, sine)
        .reshape(span_rows, windows, head_width)
        .astype(jnp.bfloat16)
    )
    grad_key_lin = (
        unrotate(grad_keys.reshape(head_shape), cosine, sine)
        .reshape(span_rows, windows, head_width)
        .astype(jnp.bfloat16)
    )
    grad_value_lin = grad_values.astype(jnp.bfloat16)
    grad_joined = jnp.concatenate([grad_query_lin, grad_key_lin, grad_value_lin], axis=-1)
    grad_w_joined = jnp.einsum(
        "rwd,rwe->de", first_full, grad_joined, preferred_element_type=jnp.float32
    )
    grad_w_query = grad_w_joined[:, :head_width]
    grad_w_key = grad_w_joined[:, head_width : 2 * head_width]
    grad_w_value = grad_w_joined[:, 2 * head_width :]
    block_part = grad_joined
    grad_first = lax.psum_scatter(
        jnp.einsum("rwe,de->rwd", block_part, w_joined, preferred_element_type=jnp.float32).astype(
            jnp.bfloat16
        ),
        "tensor",
        scatter_dimension=0,
        tiled=True,
    ).astype(jnp.float32)
    grad_norm1_gain = jnp.sum(grad_first * normed1, axis=(0, 1))
    grad_norm1_bias = jnp.sum(grad_first, axis=(0, 1))
    grad_tokens = grad_residual2 + norm_back(grad_first, normed1, inv_std1, norm1_gain)
    summed = (
        lax.psum_scatter(
            grad_w_query.astype(jnp.bfloat16), ("dp", "seq"), scatter_dimension=0, tiled=True
        ).astype(jnp.float32),
        lax.psum_scatter(
            grad_w_key.astype(jnp.bfloat16), ("dp", "seq"), scatter_dimension=0, tiled=True
        ).astype(jnp.float32),
        lax.psum_scatter(
            grad_w_value.astype(jnp.bfloat16), ("dp", "seq"), scatter_dimension=0, tiled=True
        ).astype(jnp.float32),
        lax.psum_scatter(
            grad_w_out.astype(jnp.bfloat16), ("dp", "seq"), scatter_dimension=1, tiled=True
        ).astype(jnp.float32),
        lax.psum_scatter(
            grad_w_gate.astype(jnp.bfloat16), ("dp", "seq"), scatter_dimension=0, tiled=True
        ).astype(jnp.float32),
        lax.psum_scatter(
            grad_w_up.astype(jnp.bfloat16), ("dp", "seq"), scatter_dimension=0, tiled=True
        ).astype(jnp.float32),
        lax.psum_scatter(
            grad_w_down.astype(jnp.bfloat16), ("dp", "seq"), scatter_dimension=1, tiled=True
        ).astype(jnp.float32),
    )
    norm_sums = (
        lax.psum_scatter(grad_norm1_gain, ("dp", "seq", "tensor"), scatter_dimension=0, tiled=True),
        lax.psum_scatter(grad_norm1_bias, ("dp", "seq", "tensor"), scatter_dimension=0, tiled=True),
        lax.psum_scatter(grad_norm2_gain, ("dp", "seq", "tensor"), scatter_dimension=0, tiled=True),
        lax.psum_scatter(grad_norm2_bias, ("dp", "seq", "tensor"), scatter_dimension=0, tiled=True),
    )
    return (
        output,
        grad_tokens,
        norm_sums[0],
        norm_sums[1],
        summed[0],
        summed[1],
        summed[2],
        summed[3],
        norm_sums[2],
        norm_sums[3],
        summed[4],
        summed[5],
        summed[6],
    )


BF = jnp.bfloat16
F32 = jnp.float32
LANES = 128
QUAD = 4


def dot_t(a, b):
    return lax.dot_general(a, b, (((1,), (1,)), ((), ())), preferred_element_type=F32)


def dot_n(a, b):
    return lax.dot_general(a, b, (((1,), (0,)), ((), ())), preferred_element_type=F32)


def t_dot(a, b):
    return lax.dot_general(a, b, (((0,), (0,)), ((), ())), preferred_element_type=F32)


def swap_halves(x):
    half = HEAD_DIM // 2
    lane = lax.broadcasted_iota(jnp.int32, x.shape, 1)
    down = pltpu.roll(x, half, 1)
    up = pltpu.roll(x, LANES - half, 1)
    return jnp.where(lane % HEAD_DIM < half, up, down)


def head_mask(h):
    lane = lax.broadcasted_iota(jnp.int32, (1, LANES), 1)
    return jnp.where(lane // HEAD_DIM == h, 1.0, 0.0).astype(BF)


MESH = pl.DeviceIdType.MESH


def any_spec():
    return pl.BlockSpec(memory_space=pl.ANY)


def greet(peers):
    barrier = pltpu.get_barrier_semaphore()
    for peer in peers:
        pl.semaphore_signal(barrier, inc=1, device_id=peer, device_id_type=MESH)
    pl.semaphore_wait(barrier, len(peers))


def remote(src, dst, send, recv, peer):
    return pltpu.make_async_remote_copy(
        src_ref=src, dst_ref=dst, send_sem=send, recv_sem=recv, device_id=peer, device_id_type=MESH
    )


def start_all(copies):
    for copy in copies:
        copy.start()


def wait_all(copies):
    for copy in copies:
        copy.wait()


def quad_place():
    dp, sx = lax.axis_index("dp"), lax.axis_index("seq")
    place = sx * 2 + dp % 2
    return place, lambda to: {"dp": dp // 2 * 2 + to % 2, "seq": to // 2}


def quad_peers():
    place, device = quad_place()
    return [device((place + j) % QUAD) for j in range(1, QUAD)]


class WeightRoute:
    def __init__(self, gathered, own, n_ten, send, recv):
        dp, sx, t = lax.axis_index("dp"), lax.axis_index("seq"), lax.axis_index("tensor")
        y, c = dp // 2, dp % 2
        gate_ref, up_ref, down_ref = gathered
        self.refs, self.own = (gate_ref, up_ref, down_ref, down_ref), own
        self.width, self.units = gate_ref.shape[0], gate_ref.shape[1] // n_ten
        self.send, self.recv, self.c = send, recv, c
        s_xy, s_yx = c * 4 + y * 2 + sx, c * 4 + sx * 2 + y
        self.slices = (s_xy, s_yx, s_xy, s_yx)
        self.x_peer, self.y_peer, self.c_peer = {"seq": 1 - sx}, {"dp": (dp + 2) % 4}, {"dp": 2 * y + 1 - c}
        side = t // 2
        middle = jnp.minimum(t, n_ten - 1 - t)
        mirror = lambda k: k + side * (n_ten - 1 - 2 * k)
        self.order = [mirror(k) for k in (middle, 1 - middle, 2, 3)]
        self.inward, self.outward = mirror(middle + 1), mirror(0)
        self.is_middle, self.is_end = middle == 1, middle == 0
        self.t, self.middle, self.mirror = t, middle, mirror

    def shard(self, ref, k, first, count, which):
        size, cols, units = self.width // 8, self.width // 2, self.units
        rows = pl.multiple_of(first * (size if k < 2 else units // 8), 16)
        if k < 2:
            at = 0 if which is None else pl.multiple_of(which * units, units)
            return ref.at[pl.ds(rows, count * size), pl.ds(at, units)]
        at = rows if which is None else pl.multiple_of(which * units + rows, 16)
        return ref.at[pl.ds(at, count * (units // 8)), pl.ds((k - 2) * cols, cols)]

    def along(self, which, to, slot, number, own=False):
        copies = []
        for k in range(4):
            dst = self.shard(self.refs[k], k, self.slices[k], 1, which)
            src = self.shard(self.own[min(k, 2)], k, self.slices[k], 1, None) if own else dst
            copies.append(remote(src, dst, self.send.at[number, k], self.recv.at[slot, k], {"tensor": to}))
        return copies

    def to_in(self):
        return self.along(self.t, self.inward, 1 + self.middle, 0, True)

    def to_out(self):
        return self.along(self.t, self.outward, 1, 1, True)

    def in_far(self):
        return self.along(self.mirror(0), self.inward, 3, 2)

    def out_two(self):
        return self.along(self.mirror(2), self.outward, 2, 3)

    def out_three(self):
        return self.along(self.mirror(3), self.outward, 3, 4)

    def arrived(self, i):
        received(self.along(self.order[i], self.inward, i, 0))

    def hop(self, i, h):
        copies = []
        for k in range(4):
            xy = k % 2 == 0
            peer, first, count = (
                (self.x_peer if xy else self.y_peer, self.slices[k], 1),
                (self.y_peer if xy else self.x_peer, self.slices[k] // 2 * 2, 2),
                (self.c_peer, self.c * 4, 4),
            )[h]
            ref = self.shard(self.refs[k], k, first, count, self.order[i])
            copies.append(remote(ref, ref, self.send.at[2 + 3 * i + h, k], self.recv.at[1 + 3 * i + h, k], peer))
        return copies


def received(copies):
    for copy in copies:
        copy.wait_recv()


def sent_all(copies):
    for copy in copies:
        copy.wait_send()


def route_sems():
    return [pltpu.SemaphoreType.DMA((14, 4)), pltpu.SemaphoreType.DMA((13, 4))]


def exchange_in_kernel(
    sizes, tok_ref, wq_ref, wk_ref, wv_ref, wo_ref, count_ref, rows_ref, x_ref, q_ref, k_ref, v_ref, o_ref, counts_ref,
    peer_rows_ref, tok_send, tok_recv, w_send, w_recv, count_send, count_recv, rows_send, rows_recv, local_sem,
):
    n_seq, n_ten, half, rows, slices = sizes
    dp, sx, t = lax.axis_index("dp"), lax.axis_index("seq"), lax.axis_index("tensor")
    y, c = dp // 2, dp % 2
    me = sx * n_ten + t
    group = n_seq * n_ten
    others = []
    for i in range(1, group):
        g = (me + i) % group
        others.append((g // n_ten, g % n_ten))
    y_peer, c_peer, x_peer = {"dp": (dp + 2) % 4}, {"dp": 2 * y + 1 - c}, {"seq": 1 - sx}
    dp_peers = [{"dp": (dp + i) % 4} for i in range(1, 4)]
    beside = [{"dp": 2 * y + 1 - c, "tensor": (t + j) % n_ten} for j in range(1, n_ten)]
    greet([{"seq": a, "tensor": b} for a, b in others] + dp_peers + beside)
    counts = [
        remote(count_ref, counts_ref.at[dp], count_send.at[i], count_recv.at[i], peer) for i, peer in enumerate(dp_peers)
    ]
    start_all(counts)

    hw = wq_ref.shape[1]
    srow, orow = wq_ref.shape[0] // slices, hw // slices
    s_xy, s_yx = c * 4 + y * 2 + sx, c * 4 + sx * 2 + y
    weights = ((wq_ref, q_ref, s_xy, 0), (wk_ref, k_ref, s_xy, 0), (wv_ref, v_ref, s_yx, 0), (wo_ref, o_ref, s_yx, 1))

    def block(out, by_rows, base, count, which):
        if by_rows:
            return out.at[pl.ds(pl.multiple_of(which * hw + base * orow, orow), count * orow), :]
        return out.at[
            pl.ds(pl.multiple_of(base * srow, srow), count * srow), pl.ds(pl.multiple_of(which * hw, hw), hw)
        ]

    stage = [[], [], [], []]
    n = 0
    for j in range(1, n_ten):
        peer = {"tensor": (t + j) % n_ten}
        for w_ref, out, s, by_rows in weights:
            size = orow if by_rows else srow
            src = w_ref.at[pl.ds(pl.multiple_of(s * size, size), size), :]
            stage[0].append(remote(src, block(out, by_rows, s, 1, t), w_send.at[0, n], w_recv.at[0, n], peer))
            n += 1
    n = 0
    for j in range(1, n_ten):
        which = (t + j) % n_ten
        for w_ref, out, s, by_rows in weights:
            xy = s is s_xy
            hops = (
                (1, x_peer if xy else y_peer, s, 1),
                (2, y_peer if xy else x_peer, s // 2 * 2, 2),
                (3, c_peer, c * 4, 4),
            )
            for k, peer, base, count in hops:
                ref = block(out, by_rows, base, count, which)
                stage[k].append(remote(ref, ref, w_send.at[k, n], w_recv.at[k, n], peer))
            n += 1
    start_all(stage[0])

    tokens = []
    for i, (a, b) in enumerate(others):
        tokens.append(
            remote(
                tok_ref.at[a * half + b],
                x_ref.at[pl.ds(pl.multiple_of(me * rows, rows), rows), :],
                tok_send.at[i], tok_recv.at[i], {"seq": a, "tensor": b},
            )
        )
    shared = []
    for i in range(n_seq):
        src, dst = tok_ref.at[i * half + n_ten], x_ref.at[pl.ds(pl.multiple_of((group + t % 2) * rows, rows), rows), :]
        shared.append(
            (
                2 * c + i == t,
                remote(
                    src, dst, tok_send.at[group - 1 + i], tok_recv.at[group - 1 + t % 2],
                    {"dp": 2 * y + t // 2, "tensor": 2 * c + i},
                ),
                pltpu.make_async_copy(src, dst, local_sem.at[1]),
            )
        )
    arriving = [
        remote(
            tok_ref.at[n_ten], x_ref.at[pl.ds((group + i) * rows, rows), :],
            tok_send.at[group - 1], tok_recv.at[group - 1 + i], c_peer,
        )
        for i in range(n_seq)
    ]
    start_all(tokens)
    for here, away, near in shared:
        pl.when(here)(near.start)
        pl.when(jnp.logical_not(here))(away.start)
    peer_rows = [
        remote(rows_ref.at[i * half + n_ten], peer_rows_ref.at[2 * c + i], rows_send.at[i], rows_recv.at[i], c_peer)
        for i in range(n_seq)
    ]
    start_all(peer_rows)
    local = [
        pltpu.make_async_copy(
            tok_ref.at[sx * half + t], x_ref.at[pl.ds(pl.multiple_of(me * rows, rows), rows), :], local_sem.at[0]
        ),
    ]
    for i, (w_ref, out, s, by_rows) in enumerate(weights):
        local.append(pltpu.make_async_copy(w_ref, block(out, by_rows, 0, slices, t), local_sem.at[2 + i]))
    local.append(pltpu.make_async_copy(count_ref, counts_ref.at[dp], local_sem.at[6]))
    for i in range(n_seq):
        local.append(
            pltpu.make_async_copy(rows_ref.at[i * half + n_ten], peer_rows_ref.at[2 * c + i], local_sem.at[7 + i])
        )
    start_all(local)
    for k in range(1, 4):
        for earlier in stage[k - 1]:
            earlier.wait_recv()
        start_all(stage[k])
    for copy in stage[3]:
        copy.wait_recv()
    for copies in stage:
        for copy in copies:
            copy.wait_send()
    wait_all(local)
    wait_all(counts)
    wait_all(peer_rows)
    wait_all(tokens)
    for here, away, near in shared:
        pl.when(here)(near.wait)
        pl.when(jnp.logical_not(here))(away.wait_send)
    for i in range(n_seq):
        pl.when(jnp.logical_not((t // 2 == c) & (t % 2 == i)))(arriving[i].wait_recv)


def exchange_in(tok, w_query, w_key, w_value, w_out, count, out_grad, n_dp, n_seq, n_ten):
    windows, rows, width = tok.shape
    slices = n_dp * n_seq
    vmem = pl.BlockSpec(memory_space=pltpu.VMEM)
    square = jax.ShapeDtypeStruct((width, width), BF)
    group = n_seq * n_ten
    return pl.pallas_call(
        functools.partial(exchange_in_kernel, (n_seq, n_ten, windows // n_seq, rows, slices)),
        in_specs=[vmem] * 6 + [any_spec()],
        out_specs=[any_spec()] * 7,
        out_shape=[jax.ShapeDtypeStruct(((group + n_seq) * rows, width), BF)]
        + [square] * 4
        + [jax.ShapeDtypeStruct((n_dp,) + count.shape, count.dtype)]
        + [jax.ShapeDtypeStruct((2 * n_seq,) + out_grad.shape[1:], BF)],
        scratch_shapes=[
            pltpu.SemaphoreType.DMA((group + 1,)),
            pltpu.SemaphoreType.DMA((group + 1,)),
            pltpu.SemaphoreType.DMA((4, 4 * (n_ten - 1))),
            pltpu.SemaphoreType.DMA((4, 4 * (n_ten - 1))),
            pltpu.SemaphoreType.DMA((3,)),
            pltpu.SemaphoreType.DMA((3,)),
            pltpu.SemaphoreType.DMA((2,)),
            pltpu.SemaphoreType.DMA((2,)),
            pltpu.SemaphoreType.DMA((9,)),
        ],
        compiler_params=pltpu.CompilerParams(collective_id=0, has_side_effects=True),
        name="exchange_in",
    )(tok, w_query, w_key, w_value, w_out, count, out_grad)


def qkv_kernel(
    x_ref, gain_ref, bias_ref, wq_ref, wk_ref, wv_ref, cos_ref, sin_ref, part_cos_ref, part_sin_ref,
    first_ref, q_ref, k_ref, v_ref,
):
    shared = pl.program_id(0) == pl.num_programs(0) - 1
    normed, _ = layer_stats(x_ref[...].astype(F32))
    first_ref[...] = (normed * gain_ref[...] + bias_ref[...]).astype(BF)
    cos = jnp.where(shared, part_cos_ref[...], cos_ref[...])
    sin = jnp.where(shared, part_sin_ref[...], sin_ref[...])
    wide = 256
    for w_ref, out_ref, scale in ((wq_ref, q_ref, 1.0 / math.sqrt(HEAD_DIM)), (wk_ref, k_ref, 1.0), (wv_ref, v_ref, None)):
        for at in range(0, w_ref.shape[1], wide):
            acc = dot_n(first_ref[...], w_ref[:, at : at + wide])
            for c in range(0, wide, LANES):
                part = acc[:, c : c + LANES]
                if scale is not None:
                    part = (part * cos + swap_halves(part) * sin) * scale
                out_ref[:, at + c : at + c + LANES] = part.astype(BF)


def once(shape):
    return pl.BlockSpec(shape, lambda *_: (0,) * len(shape), pipeline_mode=pl.Buffered(1))


def norm_qkv(x, gain, bias, w_query, w_key, w_value, tables, part_tables):
    rows, width = x.shape
    tile = 256
    row = pl.BlockSpec((tile, width), lambda r: (r, 0))
    own = tables[0].shape[0] // tile
    table = pl.BlockSpec((tile, LANES), lambda r: (jnp.minimum(r, own - 1), 0))
    return pl.pallas_call(
        qkv_kernel,
        grid=(rows // tile,),
        in_specs=[row, once((1, width)), once((1, width))] + [once((width, width))] * 3 + [table, table] + [once((tile, LANES))] * 2,
        out_specs=[row] * 4,
        out_shape=[jax.ShapeDtypeStruct((rows, width), BF)] * 4,
        cost_estimate=pl.CostEstimate(flops=6 * rows * width * width, bytes_accessed=16 * rows * width, transcendentals=0),
        name="norm_qkv",
    )(x, gain.reshape(1, width), bias.reshape(1, width), w_query, w_key, w_value, *tables, *part_tables)


def attend_body(q_ref, k_ref, v_ref):
    q, k, v = q_ref[...], k_ref[...], v_ref[...]
    outs = []
    for h in range(LANES // HEAD_DIM):
        s = dot_t(q * head_mask(h), k)
        p = jnp.exp(s - jnp.max(s, axis=1, keepdims=True))
        norm = jnp.sum(p, axis=1, keepdims=True)
        outs.append(dot_n(p.astype(BF), v) / norm)
    lane = lax.broadcasted_iota(jnp.int32, outs[0].shape, 1)
    return jnp.where(lane < HEAD_DIM, outs[0], outs[1]).astype(BF)


def attend_specs(rows, tile):
    return [
        pl.BlockSpec((tile, LANES), lambda p, r: (r, p)),
        pl.BlockSpec((rows, LANES), lambda p, r: (0, p)),
        pl.BlockSpec((rows, LANES), lambda p, r: (0, p)),
    ]


def attend_cost(rows, pairs):
    return pl.CostEstimate(
        flops=16 * pairs * rows * rows * LANES, bytes_accessed=8 * rows * pairs * LANES, transcendentals=2 * pairs * rows * rows
    )


def attend_left_kernel(
    n_ten, q_ref, k_ref, v_ref, ag_in, au_in, ad_in, part_ref, ag_ref, au_ref, ad_ref, buf, send, recv, local_sem,
    route_send, route_recv,
):
    place, device = quad_place()
    r, p = pl.program_id(0), pl.program_id(1)
    last_pair = p == pl.num_programs(1) - 1
    hw = buf.shape[2]
    dst = part_ref.at[:, pl.ds(pl.multiple_of(place * hw, hw), hw)]
    route = WeightRoute((ag_ref, au_ref, ad_ref), None, n_ten, route_send, route_recv)
    hops = route.hop(1, 2) + route.hop(2, 0)

    @pl.when((p == 0) & (r == 0))
    def _():
        greet(quad_peers() + [route.y_peer] + [{"tensor": (route.t + j) % n_ten} for j in range(1, n_ten)])
        start_all(hops)
        pl.when(route.is_middle)(lambda: start_all(route.out_three()))

    buf[r, :, pl.ds(pl.multiple_of(p * LANES, LANES), LANES)] = attend_body(q_ref, k_ref, v_ref)

    def copy_to(j):
        to = (place + j) % QUAD
        return remote(buf.at[to], dst, send.at[j - 1], recv.at[j - 1], device(to))

    own = pltpu.make_async_copy(buf.at[place], dst, local_sem.at[0])
    for j in range(1, QUAD):
        pl.when(last_pair & (r == (place + j) % QUAD))(copy_to(j).start)
    pl.when(last_pair & (r == place))(own.start)

    @pl.when(last_pair & (r == QUAD - 1))
    def _():
        wait_all([copy_to(j) for j in range(1, QUAD)])
        own.wait()
        wait_all(hops)
        pl.when(route.is_middle)(lambda: sent_all(route.out_three()))
        pl.when(route.is_end)(lambda: route.arrived(3))


def attend_left(q, k, v, gathered, n_ten):
    rows, hw = q.shape
    tile, pairs = rows // QUAD, hw // LANES
    column = pl.BlockSpec((rows, LANES), lambda r, p: (0, p))
    return pl.pallas_call(
        functools.partial(attend_left_kernel, n_ten),
        grid=(QUAD, pairs),
        in_specs=[pl.BlockSpec((tile, LANES), lambda r, p: (r, p)), column, column] + [any_spec()] * 3,
        out_specs=[any_spec()] * 4,
        out_shape=[jax.ShapeDtypeStruct((tile, QUAD * hw), BF)] + [jax.ShapeDtypeStruct(w.shape, BF) for w in gathered],
        input_output_aliases={3: 1, 4: 2, 5: 3},
        scratch_shapes=[pltpu.VMEM((QUAD, tile, hw), BF)]
        + [pltpu.SemaphoreType.DMA((QUAD - 1,))] * 2
        + [pltpu.SemaphoreType.DMA((1,))]
        + route_sems(),
        compiler_params=pltpu.CompilerParams(collective_id=3, has_side_effects=True),
        cost_estimate=attend_cost(rows, pairs),
        name="attend_left",
    )(q, k, v, *gathered)


def swap_part(refs, outs, send, recv, local_sem, base):
    place, device = quad_place()
    share, hw = outs[0].shape[0] // QUAD, outs[0].shape[1]
    copies, local = [], []
    rows = pl.ds(base, share)
    mine = pl.ds(pl.multiple_of(place * share, share), share)
    for i, (ref, out) in enumerate(zip(refs, outs, strict=True)):
        for j in range(1, QUAD):
            to = (place + j) % QUAD
            src = ref.at[rows, pl.ds(pl.multiple_of(to * hw, hw), hw)]
            copies.append(remote(src, out.at[mine, :], send.at[i, j - 1], recv.at[i, j - 1], device(to)))
        src = ref.at[rows, pl.ds(pl.multiple_of(place * hw, hw), hw)]
        local.append(pltpu.make_async_copy(src, out.at[mine, :], local_sem.at[i]))
    return copies, local


def attend_swap_kernel(
    n_ten, length, q_ref, k_ref, v_ref, q_all, k_all, v_all, wg_ref, wu_ref, wd_ref, o_ref, lq_ref, lk_ref, lv_ref,
    ag_ref, au_ref, ad_ref, send, recv, local_sem, route_send, route_recv,
):
    step = pl.program_id(0) * pl.num_programs(1) + pl.program_id(1)
    steps = pl.num_programs(0) * pl.num_programs(1)
    copies, local = swap_part((q_all, k_all, v_all), (lq_ref, lk_ref, lv_ref), send, recv, local_sem, length)
    route = WeightRoute((ag_ref, au_ref, ad_ref), (wg_ref, wu_ref, wd_ref), n_ten, route_send, route_recv)

    @pl.when(step == 0)
    def _():
        greet(quad_peers() + [route.y_peer] + [{"tensor": (route.t + j) % n_ten} for j in range(1, n_ten)])
        start_all(route.to_in())
        pl.when(route.is_middle)(lambda: start_all(route.to_out()))
        start_all(copies + local)

    o_ref[...] = attend_body(q_ref, k_ref, v_ref)

    @pl.when(step == steps // 2)
    def _():
        route.arrived(1)
        start_all(route.hop(1, 0))

        @pl.when(route.is_middle)
        def _():
            route.arrived(2)
            start_all(route.in_far())
            start_all(route.out_two())

    @pl.when(step == steps * 3 // 4)
    def _():
        received(route.hop(1, 0))
        start_all(route.hop(1, 1))

    @pl.when(step == steps - 1)
    def _():
        wait_all(copies + local)
        received(route.hop(1, 1))
        sent_all(route.hop(1, 0) + route.hop(1, 1) + route.to_in())

        @pl.when(route.is_middle)
        def _():
            route.arrived(3)
            sent_all(route.to_out() + route.in_far() + route.out_two())

        @pl.when(route.is_end)
        def _():
            route.arrived(2)


def attend_swap(q, k, v, ffn, length, n_ten):
    width = q.shape[1]
    tile, pairs, hw = 512, width // LANES, width // QUAD
    left = jax.ShapeDtypeStruct((length, hw), BF)
    return pl.pallas_call(
        functools.partial(attend_swap_kernel, n_ten, length),
        grid=(pairs, length // tile),
        in_specs=attend_specs(length, tile) + [any_spec()] * 6,
        out_specs=[pl.BlockSpec((tile, LANES), lambda p, r: (r, p))] + [any_spec()] * 6,
        out_shape=[jax.ShapeDtypeStruct((length, width), BF), left, left, left]
        + [jax.ShapeDtypeStruct((width, n_ten * w.shape[1]), BF) for w in ffn[:2]]
        + [jax.ShapeDtypeStruct((n_ten * ffn[2].shape[0], width), BF)],
        scratch_shapes=[
            pltpu.SemaphoreType.DMA((3, QUAD - 1)),
            pltpu.SemaphoreType.DMA((3, QUAD - 1)),
            pltpu.SemaphoreType.DMA((3,)),
        ]
        + route_sems(),
        compiler_params=pltpu.CompilerParams(collective_id=1, has_side_effects=True),
        cost_estimate=attend_cost(length, pairs),
        name="attend_swap",
    )(q, k, v, q, k, v, *ffn)


def back_body(q_ref, g_ref, k_ref, v_ref, pick_ref, cos_ref, sin_ref, qcos_ref, qsin_ref):
    g, k, v, pick = g_ref[...], k_ref[...], v_ref[...], pick_ref[...]
    q = dot_n(pick, q_ref[...]).astype(BF)
    dq = []
    all_p, all_ds, all_q, all_g = [], [], [], []
    for h in range(LANES // HEAD_DIM):
        mask = head_mask(h)
        qh, gh = q * mask, g * mask
        s = dot_t(qh, k)
        p = jnp.exp(s - jnp.max(s, axis=1, keepdims=True))
        p = p / jnp.sum(p, axis=1, keepdims=True)
        dp = dot_t(gh, v)
        ds = (p * (dp - jnp.sum(p * dp, axis=1, keepdims=True))).astype(BF)
        dq.append(dot_n(ds, k))
        all_p.append(p.astype(BF))
        all_ds.append(ds)
        all_q.append(qh)
        all_g.append(gh)
    lane = lax.broadcasted_iota(jnp.int32, dq[0].shape, 1)
    dq = jnp.where(lane < HEAD_DIM, dq[0], dq[1]) * (1.0 / math.sqrt(HEAD_DIM))
    dq = (dq * qcos_ref[...] - swap_halves(dq) * qsin_ref[...]).astype(BF)
    dq = t_dot(pick, dq).astype(BF)
    dk = t_dot(jnp.concatenate(all_ds, axis=0), jnp.concatenate(all_q, axis=0))
    dk = (dk * cos_ref[...] - swap_halves(dk) * sin_ref[...]).astype(BF)
    dv = t_dot(jnp.concatenate(all_p, axis=0), jnp.concatenate(all_g, axis=0)).astype(BF)
    return dq, dk, dv


def back_kernel(q_ref, g_ref, k_ref, v_ref, pick_ref, cos_ref, sin_ref, qcos_ref, qsin_ref, dq_ref, dk_ref, dv_ref):
    dq_ref[...], dk_ref[...], dv_ref[...] = back_body(
        q_ref, g_ref, k_ref, v_ref, pick_ref, cos_ref, sin_ref, qcos_ref, qsin_ref
    )


def back_specs(length, masked):
    full = pl.BlockSpec((length, LANES), lambda p: (0, p))
    same = pl.BlockSpec((length, LANES), lambda p: (0, 0))
    row_same = pl.BlockSpec((masked, LANES), lambda p: (0, 0))
    return [
        full, pl.BlockSpec((masked, LANES), lambda p: (0, p)), full, full,
        pl.BlockSpec((masked, length), lambda p: (0, 0)), same, same, row_same, row_same,
    ]


def back_cost(length, masked, pairs):
    return pl.CostEstimate(
        flops=24 * pairs * length * masked * LANES, bytes_accessed=12 * length * pairs * LANES, transcendentals=2 * pairs * length * masked
    )


def back_left(q, grad_rows, k, v, pick, tables):
    masked, length = pick.shape
    width = q.shape[1]
    full = pl.BlockSpec((length, LANES), lambda p: (0, p))
    return pl.pallas_call(
        back_kernel,
        grid=(width // LANES,),
        in_specs=back_specs(length, masked),
        out_specs=[full] * 3,
        out_shape=[jax.ShapeDtypeStruct((length, width), BF)] * 3,
        cost_estimate=back_cost(length, masked, width // LANES),
        name="back_left",
    )(q, grad_rows, k, v, pick, *tables)


def back_swap_kernel(
    q_ref, g_ref, k_ref, v_ref, pick_ref, cos_ref, sin_ref, qcos_ref, qsin_ref, lq_ref, lk_ref, lv_ref,
    dq_ref, dk_ref, dv_ref, buf, out_sem, send, recv, local_sem,
):
    place, device = quad_place()
    step, steps = pl.program_id(0), pl.num_programs(0)
    length = q_ref.shape[0]
    share, hw = lq_ref.shape[0] // QUAD, lq_ref.shape[1]
    outs = (dq_ref, dk_ref, dv_ref)
    copies, local = [], []
    mine = pl.ds(pl.multiple_of(place * hw, hw), hw)
    for i, (ref, out) in enumerate(zip((lq_ref, lk_ref, lv_ref), outs, strict=True)):
        dst = out.at[pl.ds(length, share), mine]
        for j in range(1, QUAD):
            to = (place + j) % QUAD
            src = ref.at[pl.ds(pl.multiple_of(to * share, share), share), :]
            copies.append(remote(src, dst, send.at[i, j - 1], recv.at[i, j - 1], device(to)))
        src = ref.at[pl.ds(pl.multiple_of(place * share, share), share), :]
        local.append(pltpu.make_async_copy(src, dst, local_sem.at[i]))

    def out_copy(at, i):
        slot = at % 2
        columns = pl.ds(pl.multiple_of(at * LANES, LANES), LANES)
        return pltpu.make_async_copy(buf.at[slot, i], outs[i].at[pl.ds(0, length), columns], out_sem.at[slot, i])

    @pl.when(step == 0)
    def _():
        greet(quad_peers())
        start_all(copies + local)

    @pl.when(step >= 2)
    def _():
        for i in range(3):
            out_copy(step - 2, i).wait()

    results = back_body(q_ref, g_ref, k_ref, v_ref, pick_ref, cos_ref, sin_ref, qcos_ref, qsin_ref)
    for i in range(3):
        buf[step % 2, i] = results[i]
        out_copy(step, i).start()

    @pl.when(step == steps - 1)
    def _():
        for i in range(3):
            out_copy(step - 1, i).wait()
            out_copy(step, i).wait()
        wait_all(copies + local)


def back_swap(q, grad_rows, k, v, pick, tables, left):
    masked, length = pick.shape
    width = q.shape[1]
    share = left[0].shape[0] // QUAD
    return pl.pallas_call(
        back_swap_kernel,
        grid=(width // LANES,),
        in_specs=back_specs(length, masked) + [any_spec()] * 3,
        out_specs=[any_spec()] * 3,
        out_shape=[jax.ShapeDtypeStruct((length + share, width), BF)] * 3,
        scratch_shapes=[
            pltpu.VMEM((2, 3, length, LANES), BF),
            pltpu.SemaphoreType.DMA((2, 3)),
            pltpu.SemaphoreType.DMA((3, QUAD - 1)),
            pltpu.SemaphoreType.DMA((3, QUAD - 1)),
            pltpu.SemaphoreType.DMA((3,)),
        ],
        compiler_params=pltpu.CompilerParams(collective_id=2, has_side_effects=True),
        cost_estimate=back_cost(length, masked, width // LANES),
        name="back_swap",
    )(q, grad_rows, k, v, pick, *tables, *left)


def feed_kernel(
    n_ten, tok_ref, att_ref, left_ref, wo_ref, gain_ref, bias_ref, pick_ref, part_pick_ref, cot_ref, wg_ref, wu_ref, wd_ref,
    ag_in, au_in, ad_in, out_ref, out_left_ref, att_m_ref, gr2_ref, gatt_ref, left_gatt_ref, vec_ref, all_own_ref, all_left_ref,
    ag_ref, au_ref, ad_ref,
    x_ref, acc_ref, normed_ref, inv_ref, grad_ref, g_buf, u_buf, d_buf, rows_buf, rows_parts, own_m, left_m, gatt_buf, gatt_parts,
    buf_sem, small_send, small_recv, line_send, line_recv, local_sem, send, recv,
):
    step, steps = pl.program_id(0), pl.num_programs(0)
    rows, width = tok_ref.shape
    length = att_ref.shape[0]
    masked = cot_ref.shape[0]
    slots = masked // 2
    unit = g_buf.shape[2]
    units = wg_ref.shape[1]
    per = units // unit
    part, hw = rows_buf.shape[1], gatt_parts.shape[2]
    gain = gain_ref[...]
    own = (wg_ref, wu_ref, wd_ref)
    route = WeightRoute((ag_ref, au_ref, ad_ref), own, n_ten, send, recv)
    order = route.order
    place, device = quad_place()
    rows_copies, gatt_copies = [], []
    for j in range(1, QUAD):
        to = (place + j) % QUAD
        rows_copies.append(
            remote(rows_buf.at[to], rows_parts.at[j - 1], small_send.at[0, j - 1], small_recv.at[0, j - 1], device(to))
        )
        src = gatt_buf.at[:, pl.ds(pl.multiple_of(to * hw, hw), hw)]
        gatt_copies.append(
            remote(src, gatt_parts.at[j - 1], small_send.at[1, j - 1], small_recv.at[1, j - 1], device(to))
        )

    line_copies = [[], []]
    local = []
    for n, (src, out) in enumerate(((own_m, all_own_ref), (left_m, all_left_ref))):
        for j in range(1, n_ten):
            to = (route.t + j) % n_ten
            line_copies[n].append(
                remote(src, out.at[route.t], line_send.at[n, j - 1], line_recv.at[n, j - 1], {"tensor": to})
            )
        local.append(pltpu.make_async_copy(src, out.at[route.t], local_sem.at[n]))

    def fetch(at):
        slot, i, b = at % 2, at // per, at % per

        def make(refs, shard_at):
            base = pl.multiple_of(shard_at * units + b * unit, unit)
            return [
                pltpu.make_async_copy(refs[0].at[:, pl.ds(base, unit)], g_buf.at[slot], buf_sem.at[slot, 0]),
                pltpu.make_async_copy(refs[1].at[:, pl.ds(base, unit)], u_buf.at[slot], buf_sem.at[slot, 1]),
                pltpu.make_async_copy(refs[2].at[pl.ds(base, unit), :], d_buf.at[slot], buf_sem.at[slot, 2]),
            ]

        @pl.when(i == 0)
        def _():
            start_all(make(own, 0))

        @pl.when(i > 0)
        def _():
            which = order[1] * (i == 1) + order[2] * (i == 2) + order[3] * (i == 3)
            start_all(make((ag_ref, au_ref, ad_ref), which))

    def fetched(at):
        slot = at % 2
        wait_all(
            [
                pltpu.make_async_copy(wg_ref.at[:, pl.ds(0, unit)], g_buf.at[slot], buf_sem.at[slot, 0]),
                pltpu.make_async_copy(wu_ref.at[:, pl.ds(0, unit)], u_buf.at[slot], buf_sem.at[slot, 1]),
                pltpu.make_async_copy(wd_ref.at[pl.ds(0, unit), :], d_buf.at[slot], buf_sem.at[slot, 2]),
            ]
        )

    def norm(res):
        normed, inv_std = layer_stats(res)
        return normed, inv_std, (normed * gain + bias_ref[...]).astype(BF)

    @pl.when(step == 0)
    def _():
        greet(quad_peers() + [route.y_peer] + [{"tensor": (route.t + j) % n_ten} for j in range(1, n_ten)])
        start_all(route.hop(2, 1))
        start_all(route.hop(3, 0))
        fetch(0)
        tile = rows - length
        for i, (pick, att, tok) in enumerate(
            ((pick_ref[...], att_ref[...], tok_ref[:length, :]), (part_pick_ref[...], left_ref[...], tok_ref[length:, :]))
        ):
            here = slice(i * slots, (i + 1) * slots)
            att_m = dot_n(pick, att).astype(BF)
            att_m_ref[here, :] = att_m
            normed, inv_std, low = norm(dot_n(pick, tok) + dot_n(att_m, wo_ref[...]))
            normed_ref[here, :] = normed
            inv_ref[here, :] = jnp.broadcast_to(inv_std, (slots, LANES))
            here_too = jnp.sum(pick.astype(F32), axis=1, keepdims=True) > 0.0
            low = jnp.where(here_too, low.astype(F32), 0.0)
            x_ref[rows + i * slots : rows + (i + 1) * slots, :] = low.astype(BF)
            if i == 0:
                own_m[...] = low.astype(BF)
            else:
                for k in range(QUAD):
                    rows_buf[k] = low[k * part : (k + 1) * part, :].astype(BF)
        for at in range(0, rows, tile):
            att = att_ref[at : at + tile, :] if at < length else left_ref[...]
            res = tok_ref[at : at + tile, :].astype(F32) + dot_n(att, wo_ref[...])
            x_ref[at : at + tile, :] = norm(res)[2]
            acc_ref[at : at + tile, :] = res
        grad_ref[...] = jnp.zeros_like(grad_ref)

    fetched(step)

    @pl.when((step + 1 < steps) & ((step + 1) % per != 0))
    def _():
        fetch(step + 1)

    slot = step % 2
    x = x_ref[...]
    w_g, w_u, w_d = g_buf[slot], u_buf[slot], d_buf[slot]
    gate, up = dot_n(x, w_g), dot_n(x, w_u)
    sig = jax.nn.sigmoid(gate)
    act = gate * sig
    hidden = (act[:rows] * up[:rows]).astype(BF)
    for at in range(0, width, unit):
        acc_ref[:, at : at + unit] += dot_n(hidden, w_d[:, at : at + unit])
    back = dot_t(cot_ref[...].astype(BF), w_d)
    gate, up, sig, act = gate[rows:], up[rows:], sig[rows:], act[rows:]
    grad_gate = (back * up * sig * (1.0 + gate * (1.0 - sig))).astype(BF)
    grad_up = (back * act).astype(BF)
    grad_ref[...] += dot_t(grad_gate, w_g) + dot_t(grad_up, w_u)

    @pl.when(step == 1)
    def _():
        start_all(rows_copies)
        start_all(line_copies[0])
        local[0].start()

    @pl.when(step == 2 * per)
    def _():
        wait_all(rows_copies)
        whole = rows_buf[place].astype(F32)
        for j in range(QUAD - 1):
            whole = whole + rows_parts[j].astype(F32)
        left_m[...] = whole.astype(BF)

    @pl.when(step == 2 * per + 1)
    def _():
        start_all(line_copies[1])
        local[1].start()

    @pl.when(step == per + 1)
    def _():
        received(route.hop(2, 1))
        start_all(route.hop(2, 2))
        received(route.hop(3, 0))
        start_all(route.hop(3, 1))

    @pl.when(step == 2 * per - 1)
    def _():
        received(route.hop(2, 2))

    @pl.when(step == 2 * per + 2)
    def _():
        received(route.hop(3, 1))
        start_all(route.hop(3, 2))

    @pl.when(step == 3 * per - 1)
    def _():
        received(route.hop(3, 2))

    @pl.when((step + 1 < steps) & ((step + 1) % per == 0))
    def _():
        fetch(step + 1)

    @pl.when(step == steps - 1)
    def _():
        grad, normed = grad_ref[...], normed_ref[...]
        gr2 = (cot_ref[...] + norm_back(grad, normed, inv_ref[:, :1], gain)).astype(BF)
        gr2_ref[...] = gr2
        gatt = dot_t(gr2, wo_ref[...]).astype(BF)
        gatt_ref[...] = gatt[:slots]
        gatt_buf[...] = gatt[slots:]
        vec_ref[...] = jnp.concatenate(
            [jnp.sum(grad * normed, axis=0, keepdims=True), jnp.sum(grad, axis=0, keepdims=True)], axis=0
        )
        start_all(gatt_copies)
        out_ref[...] = acc_ref[:length, :].astype(BF)
        chunk = out_left_ref.shape[1]
        for i in range(2):
            out_left_ref[(i + route.t) % 2] = acc_ref[length + i * chunk : length + (i + 1) * chunk, :].astype(BF)
        sent_all(route.hop(2, 1) + route.hop(2, 2) + route.hop(3, 0) + route.hop(3, 1) + route.hop(3, 2))
        wait_all(gatt_copies)
        whole = gatt_buf[:, pl.ds(pl.multiple_of(place * hw, hw), hw)].astype(F32)
        for j in range(QUAD - 1):
            whole = whole + gatt_parts[j].astype(F32)
        left_gatt_ref[...] = whole.astype(BF)
        wait_all(line_copies[0] + line_copies[1])
        wait_all(local)


def feed_forward(tok, att, left_att, w_out, gain, bias, pick, part_pick, cot, ffn, gathered, n_ten):
    rows, width = tok.shape
    units = ffn[0].shape[1]
    masked = cot.shape[0]
    slots, hw = masked // 2, width // QUAD
    unit = 256
    whole = lambda *shape: pl.BlockSpec(shape, lambda i: (0,) * len(shape))
    low = jax.ShapeDtypeStruct((masked, width), BF)
    return pl.pallas_call(
        functools.partial(feed_kernel, n_ten),
        grid=(n_ten * units // unit,),
        in_specs=[once(x.shape) for x in (tok, att, left_att, w_out)]
        + [once((1, width)), once((1, width)), once(pick.shape), once(part_pick.shape), once(cot.shape)]
        + [any_spec()] * 6,
        out_specs=[whole(*att.shape), whole(2, left_att.shape[0] // 2, width)]
        + [whole(masked, width), whole(masked, width), whole(slots, width), whole(slots, hw)]
        + [whole(2, width)]
        + [any_spec()] * 5,
        out_shape=[
            jax.ShapeDtypeStruct(att.shape, BF), jax.ShapeDtypeStruct((2, left_att.shape[0] // 2, width), BF), low, low,
            jax.ShapeDtypeStruct((slots, width), BF), jax.ShapeDtypeStruct((slots, hw), BF),
            jax.ShapeDtypeStruct((2, width), F32),
            jax.ShapeDtypeStruct((n_ten, slots, width), BF), jax.ShapeDtypeStruct((n_ten, slots // QUAD, width), BF),
        ]
        + [jax.ShapeDtypeStruct(w.shape, BF) for w in gathered],
        input_output_aliases={12: 9, 13: 10, 14: 11},
        scratch_shapes=[
            pltpu.VMEM((rows + masked, width), BF),
            pltpu.VMEM((rows, width), F32),
            pltpu.VMEM((masked, width), F32),
            pltpu.VMEM((masked, LANES), F32),
            pltpu.VMEM((masked, width), F32),
            pltpu.VMEM((2, width, unit), BF),
            pltpu.VMEM((2, width, unit), BF),
            pltpu.VMEM((2, unit, width), BF),
            pltpu.VMEM((QUAD, slots // QUAD, width), BF),
            pltpu.VMEM((QUAD - 1, slots // QUAD, width), BF),
            pltpu.VMEM((slots, width), BF),
            pltpu.VMEM((slots // QUAD, width), BF),
            pltpu.VMEM((slots, width), BF),
            pltpu.VMEM((QUAD - 1, slots, hw), BF),
            pltpu.SemaphoreType.DMA((2, 3)),
            pltpu.SemaphoreType.DMA((2, QUAD - 1)),
            pltpu.SemaphoreType.DMA((2, QUAD - 1)),
            pltpu.SemaphoreType.DMA((2, n_ten - 1)),
            pltpu.SemaphoreType.DMA((2, n_ten - 1)),
            pltpu.SemaphoreType.DMA((2,)),
        ]
        + route_sems(),
        compiler_params=pltpu.CompilerParams(collective_id=5, has_side_effects=True),
        cost_estimate=pl.CostEstimate(
            flops=8 * rows * width * n_ten * units, bytes_accessed=6 * width * n_ten * units, transcendentals=rows * n_ten * units
        ),
        name="feed_forward",
    )(tok, att, left_att, w_out, gain.reshape(1, width), bias.reshape(1, width), pick, part_pick, cot, *ffn, *gathered)[:9]


def feed_grads_kernel(own_ref, left_ref, cot_ref, wg_ref, wu_ref, wd_ref, gg_ref, gu_ref, gd_ref, x_ref):
    @pl.when(pl.program_id(0) == 0)
    def _():
        x_ref[: own_ref.shape[0], :] = own_ref[...]
        x_ref[own_ref.shape[0] :, :] = left_ref[...]

    x, cot = x_ref[...], cot_ref[...]
    gate, up, back = dot_n(x, wg_ref[...]), dot_n(x, wu_ref[...]), dot_t(cot, wd_ref[...])
    sig = jax.nn.sigmoid(gate)
    act = gate * sig
    gg_ref[...] = t_dot((back * up * sig * (1.0 + gate * (1.0 - sig))).astype(BF), x).astype(BF)
    gu_ref[...] = t_dot((back * act).astype(BF), x).astype(BF)
    gd_ref[...] = t_dot((act * up).astype(BF), cot).astype(BF)


def feed_grads(own, left, cot, w_gate, w_up, w_down):
    rows, width = cot.shape
    units = w_gate.shape[1]
    unit = 512
    columns = pl.BlockSpec((width, unit), lambda i: (0, i))
    line = pl.BlockSpec((unit, width), lambda i: (i, 0))
    return pl.pallas_call(
        feed_grads_kernel,
        grid=(units // unit,),
        in_specs=[once(own.shape), once(left.shape), once(cot.shape), columns, columns, line],
        out_specs=[line] * 3,
        out_shape=[jax.ShapeDtypeStruct((units, width), BF)] * 3,
        scratch_shapes=[pltpu.VMEM((rows, width), BF)],
        cost_estimate=pl.CostEstimate(flops=12 * rows * width * units, bytes_accessed=12 * width * units, transcendentals=rows * units),
        name="feed_grads",
    )(own, left, cot, w_gate, w_up, w_down)


def token_back_kernel(
    tok_ref, dq_ref, dk_ref, dv_ref, wq_ref, wk_ref, wv_ref, gain_ref, pick_ref, rows_ref, out_ref, vec_ref
):
    acc = dot_t(dq_ref[...], wq_ref[...]) + dot_t(dk_ref[...], wk_ref[...]) + dot_t(dv_ref[...], wv_ref[...])
    normed, inv_std = layer_stats(tok_ref[...].astype(F32))
    direct = t_dot(pick_ref[...], rows_ref[0])
    out_ref[...] = (direct + norm_back(acc, normed, inv_std, gain_ref[...])).astype(BF)
    sums = jnp.concatenate([jnp.sum(acc * normed, axis=0, keepdims=True), jnp.sum(acc, axis=0, keepdims=True)], axis=0)

    @pl.when(pl.program_id(0) == 0)
    def _():
        vec_ref[...] = sums

    @pl.when(pl.program_id(0) > 0)
    def _():
        vec_ref[...] += sums


def token_back(tok, grads, weights, gain, pick, rows_m):
    rows, width = tok.shape
    slots = pick.shape[0]
    tile = 256
    row = pl.BlockSpec((tile, width), lambda r: (r, 0))
    own = rows // tile - 1
    return pl.pallas_call(
        token_back_kernel,
        grid=(rows // tile,),
        in_specs=[row] * 4
        + [once((width, width))] * 3
        + [
            once((1, width)),
            pl.BlockSpec((slots, tile), lambda r: (0, r)),
            pl.BlockSpec((1, slots, width), lambda r: (r // own, 0, 0)),
        ],
        out_specs=[row, pl.BlockSpec((2, width), lambda r: (0, 0))],
        out_shape=[jax.ShapeDtypeStruct((rows, width), BF), jax.ShapeDtypeStruct((2, width), F32)],
        cost_estimate=pl.CostEstimate(flops=6 * rows * width * width, bytes_accessed=16 * rows * width, transcendentals=0),
        name="token_back",
    )(tok, *grads, *weights, gain.reshape(1, width), pick, rows_m)


def exchange_out_kernel(
    sizes, go_ref, gq_ref, gk_ref, gv_ref, gg_ref, gu_ref, gd_ref, grad_ref, vec_ref, w_ref, ffn_ref, tok_ref, vec_out,
    mine, buf1, buf2, buf3, buf4, vec_buf, vec_sum, mine_sem,
    tok_send, tok_recv, send1, recv1, send2, recv2, send3, recv3, send4, recv4, vec_send, vec_recv, local_sem,
):
    n_seq, n_ten, half, rows = sizes
    dp, sx, t = lax.axis_index("dp"), lax.axis_index("seq"), lax.axis_index("tensor")
    y, c = dp // 2, dp % 2
    me = sx * n_ten + t
    group = n_seq * n_ten
    others = []
    for i in range(1, group):
        g = (me + i) % group
        others.append((g // n_ten, g % n_ten))
    y_peer, c_peer, x_peer = {"dp": (dp + 2) % 4}, {"dp": 2 * y + 1 - c}, {"seq": 1 - sx}
    z_peers = [{"tensor": (t + j) % n_ten} for j in range(1, n_ten)]
    beside = [{"dp": 2 * y + 1 - c, "tensor": (t + j) % n_ten} for j in range(1, n_ten)]
    greet([{"seq": a, "tensor": b} for a, b in others] + [y_peer, c_peer] + beside)
    grads = (go_ref, gq_ref, gk_ref, gv_ref, gg_ref, gu_ref, gd_ref)
    count, attn = len(grads), w_ref.shape[0]
    x_first = (False, False, False, False, False, True, True)
    height = gq_ref.shape[0]
    hw = height // n_ten

    def columns(b_y, b_c, b_x):
        return pl.ds(pl.multiple_of((b_y * 4 + b_c * 2 + b_x) * LANES, LANES), LANES)

    def add_rows(out, first, second):
        def body(i, carry):
            at = pl.ds(pl.multiple_of(i * hw, hw), hw)
            out[at, :] = (first[at, :].astype(F32) + second[at, :].astype(F32)).astype(BF)
            return carry

        lax.fori_loop(0, height // hw, body, 0)

    stage1 = []
    for a in range(count):
        stage1.append(
            [
                remote(
                    grads[a].at[:, columns(b_y, 1 - c, b_x)], buf1.at[a, b_y, b_x],
                    send1.at[a, 2 * b_y + b_x], recv1.at[a, 2 * b_y + b_x], c_peer,
                )
                for b_y in range(2)
                for b_x in range(2)
            ]
        )
    for copies in stage1:
        start_all(copies)
    kept = [
        [
            pltpu.make_async_copy(
                grads[a].at[:, columns(b_y, c, b_x)], mine.at[a, b_y, b_x], mine_sem.at[a, 2 * b_y + b_x]
            )
            for b_y in range(2)
            for b_x in range(2)
        ]
        for a in range(count)
    ]
    for copies in kept:
        start_all(copies)

    vec_hops = []
    hops = [c_peer, x_peer, y_peer]
    vec_sum[0] = vec_ref[...]
    for i, peer in enumerate(hops):
        vec_hops.append([remote(vec_sum.at[i], vec_buf.at[i], vec_send.at[i], vec_recv.at[i], peer)])
    vec_hops.append(
        [
            remote(vec_sum.at[3], vec_buf.at[3 + j], vec_send.at[3 + j], vec_recv.at[3 + j], peer)
            for j, peer in enumerate(z_peers)
        ]
    )
    start_all(vec_hops[0])

    tokens = []
    for i, (a, b) in enumerate(others):
        tokens.append(
            remote(
                grad_ref.at[pl.ds(pl.multiple_of((a * n_ten + b) * rows, rows), rows), :],
                tok_ref.at[sx * half + t],
                tok_send.at[i], tok_recv.at[i], {"seq": a, "tensor": b},
            )
        )
    shared = []
    for i in range(n_seq):
        src, dst = grad_ref.at[pl.ds((group + i) * rows, rows), :], tok_ref.at[t % 2 * half + n_ten]
        shared.append(
            (
                2 * c + i == t,
                remote(
                    src, dst, tok_send.at[group - 1 + i], tok_recv.at[group - 1 + t % 2],
                    {"dp": 2 * y + t // 2, "tensor": 2 * c + i},
                ),
                pltpu.make_async_copy(src, dst, local_sem.at[1]),
            )
        )
    arriving = [
        remote(
            grad_ref.at[pl.ds(0, rows), :], tok_ref.at[i * half + n_ten],
            tok_send.at[group - 1], tok_recv.at[group - 1 + i], c_peer,
        )
        for i in range(n_seq)
    ]
    start_all(tokens)
    for here, away, near in shared:
        pl.when(here)(near.start)
        pl.when(jnp.logical_not(here))(away.start)
    local = [
        pltpu.make_async_copy(
            grad_ref.at[pl.ds(pl.multiple_of(me * rows, rows), rows), :], tok_ref.at[sx * half + t], local_sem.at[0]
        ),
    ]
    start_all(local)

    stage2 = []
    for a in range(count):
        wait_all(kept[a])
        for copy in stage1[a]:
            copy.wait_recv()
        for b_y in range(2):
            for b_x in range(2):
                add_rows(buf1.at[a, b_y, b_x], mine.at[a, b_y, b_x], buf1.at[a, b_y, b_x])
        copies = []
        for b in range(2):
            src, peer = (buf1.at[a, b, 1 - sx], x_peer) if x_first[a] else (buf1.at[a, 1 - y, b], y_peer)
            copies.append(remote(src, buf2.at[a, b], send2.at[a, b], recv2.at[a, b], peer))
        start_all(copies)
        stage2.append(copies)
    vec_hops[0][0].wait_recv()
    vec_sum[1] = vec_sum[0] + vec_buf[0]
    start_all(vec_hops[1])
    stage3, stage4 = {}, {}

    def second(a):
        for copy in stage2[a]:
            copy.wait_recv()
        for b in range(2):
            own = buf1.at[a, b, sx] if x_first[a] else buf1.at[a, y, b]
            add_rows(buf2.at[a, b], own, buf2.at[a, b])
        src, peer = (buf2.at[a, 1 - y], y_peer) if x_first[a] else (buf2.at[a, 1 - sx], x_peer)
        stage3[a] = remote(src, buf3.at[a], send3.at[a], recv3.at[a], peer)
        stage3[a].start()

    def third(a):
        stage3[a].wait_recv()
        own = buf2.at[a, y] if x_first[a] else buf2.at[a, sx]
        if a >= attn:

            def final(i, carry):
                at = pl.ds(pl.multiple_of(i * hw, hw), hw)
                ffn_ref[a - attn, at, :] = own[at, :].astype(F32) + buf3[a, at, :].astype(F32)
                return carry

            lax.fori_loop(0, height // hw, final, 0)
            return
        add_rows(buf3.at[a], own, buf3.at[a])
        stage4[a] = []
        for j, peer in enumerate(z_peers):
            to = (t + 1 + j) % n_ten
            src = buf3.at[a, pl.ds(pl.multiple_of(to * hw, hw), hw), :]
            stage4[a].append(remote(src, buf4.at[a, j], send4.at[a, j], recv4.at[a, j], peer))
        start_all(stage4[a])

    vec_hops[1][0].wait_recv()
    vec_sum[2] = vec_sum[1] + vec_buf[1]
    start_all(vec_hops[2])
    for a in (0, 1, 2, 5, 3, 6):
        second(a)
    third(0)
    third(1)
    second(4)
    for a in (2, 3, 5, 6, 4):
        third(a)
    vec_hops[2][0].wait_recv()
    vec_sum[3] = vec_sum[2] + vec_buf[2]
    start_all(vec_hops[3])
    for n, copies in stage4.items():
        total = buf3[n, pl.ds(pl.multiple_of(t * hw, hw), hw), :].astype(F32)
        for j, copy in enumerate(copies):
            copy.wait_recv()
            total = total + buf4[n, j].astype(F32)
        w_ref[n] = total
    total = vec_sum[3]
    for j, copy in enumerate(vec_hops[3]):
        copy.wait_recv()
        total = total + vec_buf[3 + j]
    vec_out[...] = total
    for copies in stage1 + stage2 + list(stage4.values()) + [list(stage3.values())] + vec_hops:
        for copy in copies:
            copy.wait_send()
    wait_all(local)
    wait_all(tokens)
    for here, away, near in shared:
        pl.when(here)(near.wait)
        pl.when(jnp.logical_not(here))(away.wait_send)
    for i in range(n_seq):
        pl.when(jnp.logical_not(2 * c + i == t))(arriving[i].wait_recv)


def exchange_out(ffn_grads, attn_grads, grad_tok, vectors, n_seq, n_ten, half, rows):
    grads = (*attn_grads, *ffn_grads)
    ffn, attn = len(ffn_grads), len(attn_grads)
    height, width = grads[0].shape
    hw, count, group = height // n_ten, len(grads), n_seq * n_ten
    vmem = pl.BlockSpec(memory_space=pltpu.VMEM)
    dma = pltpu.SemaphoreType.DMA
    hops = 3 + n_ten - 1
    return pl.pallas_call(
        functools.partial(exchange_out_kernel, (n_seq, n_ten, half, rows)),
        in_specs=[any_spec()] * (count + 1) + [vmem],
        out_specs=[vmem, vmem, any_spec(), vmem],
        out_shape=[
            jax.ShapeDtypeStruct((attn, hw, LANES), F32),
            jax.ShapeDtypeStruct((ffn, height, LANES), F32),
            jax.ShapeDtypeStruct((n_seq * half, rows, width), BF),
            jax.ShapeDtypeStruct(vectors.shape, F32),
        ],
        scratch_shapes=[
            pltpu.VMEM((count, 2, 2, height, LANES), BF),
            pltpu.VMEM((count, 2, 2, height, LANES), BF),
            pltpu.VMEM((count, 2, height, LANES), BF),
            pltpu.VMEM((count, height, LANES), BF),
            pltpu.VMEM((attn, n_ten - 1, hw, LANES), BF),
            pltpu.VMEM((hops,) + vectors.shape, F32),
            pltpu.VMEM((4,) + vectors.shape, F32),
            dma((count, 4)),
            dma((group + 1,)), dma((group + 1,)),
            dma((count, 4)), dma((count, 4)),
            dma((count, 2)), dma((count, 2)),
            dma((count,)), dma((count,)),
            dma((attn, n_ten - 1)), dma((attn, n_ten - 1)),
            dma((hops,)), dma((hops,)),
            dma((2,)),
        ],
        compiler_params=pltpu.CompilerParams(collective_id=4, has_side_effects=True),
        name="exchange_out",
    )(*grads, grad_tok, vectors)


def rotary_lanes(cosine, sine):
    reps = LANES // HEAD_DIM
    return jnp.concatenate([cosine, cosine] * reps, axis=1), jnp.concatenate([-sine, sine] * reps, axis=1)


def position_tables(length):
    half_dim = HEAD_DIM // 2
    inv_freq = np.float32(10000.0) ** (-np.arange(half_dim, dtype=np.float32) * np.float32(2.0 / HEAD_DIM))
    angles = (np.arange(length, dtype=np.float32)[:, None] * inv_freq[None, :]).astype(np.float64)
    cosine, sine = np.cos(angles).astype(np.float32), np.sin(angles).astype(np.float32)
    reps = LANES // HEAD_DIM
    return np.concatenate([cosine, cosine] * reps, axis=1), np.concatenate([-sine, sine] * reps, axis=1)


def window_shards(
    tokens,
    norm1_gain,
    norm1_bias,
    w_query,
    w_key,
    w_value,
    w_out,
    norm2_gain,
    norm2_bias,
    w_gate,
    w_up,
    w_down,
    out_grad,
    masked_rows,
    window_counts,
):
    rows_local, windows, width = tokens.shape
    n_dp, n_seq, n_ten = lax.axis_size("dp"), lax.axis_size("seq"), lax.axis_size("tensor")
    dp_index, seq_index, ten_index = lax.axis_index("dp"), lax.axis_index("seq"), lax.axis_index("tensor")
    shard_index = dp_index * n_seq + seq_index
    core = dp_index % 2
    place = seq_index * 2 + core
    half = windows // n_seq
    length = rows_local * n_seq * n_ten
    share = length // QUAD
    hw = width // QUAD
    slots = masked_rows.shape[1]
    part = slots // QUAD

    live = jnp.arange(windows) < window_counts[0]
    valid = (masked_rows < length) & live[:, None]
    coded = jnp.where(valid, masked_rows, length)
    info = jnp.concatenate([coded, jnp.full((1, slots), jnp.sum(valid.astype(jnp.int32)))], axis=0)
    info = jnp.pad(info, ((0, -(windows + 1) % 8), (0, -slots % LANES)))
    both_tok, all_q, all_k, all_v, all_out, infos, left_grad = exchange_in(
        jnp.swapaxes(tokens, 0, 1), w_query, w_key, w_value, w_out, info, out_grad, n_dp, n_seq, n_ten
    )
    loss_weight = LOSS_SCALE / jnp.sum(infos[:, windows, 0]).astype(F32)
    pick_one = lambda x, at: lax.dynamic_index_in_dim(x, at, 0, keepdims=False)
    first_window = seq_index * half
    my_coded = lax.dynamic_slice_in_dim(coded, first_window, n_ten, 0)
    my_grad = lax.dynamic_slice_in_dim(out_grad, first_window, n_ten, 0)
    pair_infos = lax.dynamic_slice_in_dim(infos, dp_index - core, 2, 0)
    left_coded = jnp.stack([pair_infos[i // n_seq, i % n_seq * half + n_ten, :slots] for i in range(n_ten)])
    weigh = lambda grad, rows: jnp.where((rows < length)[..., None], grad.astype(F32) * loss_weight, 0.0)

    own_rows, left_rows = pick_one(my_coded, ten_index), pick_one(left_coded, ten_index)
    every = jnp.arange(length)
    my_left = place * share + jnp.arange(share)
    own_pick = (own_rows[:, None] == every[None, :]).astype(BF)
    left_pick = (left_rows[:, None] == every[None, :]).astype(BF)
    part_match = left_rows[:, None] == my_left[None, :]
    part_pick = part_match.astype(BF)
    left_here = jnp.where(jnp.any(part_match, axis=1), left_rows, length)
    my_cot = jnp.concatenate(
        [weigh(pick_one(my_grad, ten_index), own_rows), weigh(pick_one(left_grad, ten_index), left_here)], axis=0
    )

    tables = [jnp.asarray(x) for x in position_tables(length)]
    part_tables = [lax.dynamic_slice_in_dim(x, place * share, share, 0) for x in tables]
    own_tables = tables + list(rotary_lanes(*rotary_tables(own_rows)))
    left_tables = tables + list(rotary_lanes(*rotary_tables(left_rows)))

    ffn = (w_gate, w_up, w_down)
    first, q, k, v = norm_qkv(both_tok, norm1_gain, norm1_bias, all_q, all_k, all_v, tables, part_tables)
    own_att, left_q, left_k, left_v, *gathered = attend_swap(q, k, v, ffn, length, n_ten)
    left_att_part, *gathered = attend_left(left_q, left_k, left_v, gathered, n_ten)
    own_out, left_chunks, att_m, gr2, own_gatt, left_gatt, grad_norm2, all_own, all_left = feed_forward(
        both_tok, own_att, left_att_part, all_out, norm2_gain, norm2_bias, own_pick, part_pick, my_cot, ffn, gathered, n_ten
    )

    grad_w_out = t_dot(att_m, gr2).astype(BF)
    left_back = back_left(left_q, left_gatt, left_k, left_v, left_pick, left_tables)
    dq, dk, dv = back_swap(q, own_gatt, k, v, own_pick, own_tables, left_back)
    all_own, dq, dk, dv = lax.optimization_barrier((all_own, dq, dk, dv))

    part_of = lambda x: lax.dynamic_slice_in_dim(x, place * part, part, 1)
    down_in = jnp.concatenate(
        [
            weigh(my_grad, my_coded).reshape(n_ten * slots, width),
            weigh(part_of(left_grad), part_of(left_coded)).reshape(n_ten * part, width),
        ],
        axis=0,
    ).astype(BF)
    grad_w_ffn = feed_grads(all_own.reshape(-1, width), all_left.reshape(-1, width), down_in, *ffn)
    grad_w_attn = [grad_w_out] + [t_dot(d, first).astype(BF) for d in (dq, dk, dv)]
    grad_both, grad_norm1 = token_back(
        both_tok, (dq, dk, dv), (all_q, all_k, all_v), norm1_gain,
        jnp.concatenate([own_pick, part_pick], axis=1), gr2.reshape(2, slots, width),
    )

    own_out = lax.all_to_all(
        own_out.reshape(n_seq * n_ten, rows_local, width), ("seq", "tensor"), 0, 0, tiled=True
    ).reshape(n_seq, n_ten, rows_local, width)
    left_out = []
    for turn in range(2):
        perm = []
        for d in range(n_dp):
            for sx in range(n_seq):
                for p in range(n_ten):
                    to = d // 2 * 2 + p // 2, sx, d % 2 * 2 + (p % 2 ^ turn)
                    perm.append(((d * n_seq + sx) * n_ten + p, (to[0] * n_seq + to[1]) * n_ten + to[2]))
        left_out.append(lax.ppermute(left_chunks[turn], ("dp", "seq", "tensor"), perm))
    even = ten_index % 2 == 0
    left_out = jnp.stack([jnp.where(even, left_out[0], left_out[1]), jnp.where(even, left_out[1], left_out[0])])
    output = jnp.concatenate([own_out, left_out[:, None]], axis=1).reshape(windows, rows_local, width)
    output = jnp.swapaxes(output, 0, 1)
    vectors = jnp.concatenate(
        [grad_norm1, grad_norm2, jnp.zeros((4, width), F32)], axis=0
    )
    gw_attn, gw_ffn, grad_tokens, vectors = exchange_out(
        grad_w_ffn, grad_w_attn, grad_both, vectors, n_seq, n_ten, half, rows_local
    )
    grad_tokens = jnp.swapaxes(grad_tokens, 0, 1).astype(F32)
    small = width // (n_dp * n_seq * n_ten)
    vectors = lax.dynamic_slice_in_dim(vectors, (shard_index * n_ten + ten_index) * small, small, 1)

    return (
        output,
        grad_tokens,
        vectors[0],
        vectors[1],
        gw_attn[1].T,
        gw_attn[2].T,
        gw_attn[3].T,
        gw_attn[0],
        vectors[2],
        vectors[3],
        gw_ffn[0].T,
        gw_ffn[1].T,
        gw_ffn[2],
    )


def shards(tokens, *rest):
    n_dp, n_seq, n_ten = lax.axis_size("dp"), lax.axis_size("seq"), lax.axis_size("tensor")
    whole = n_dp == 4 and n_seq == 2 and n_ten == 4 and tokens.shape[1] == n_seq * (n_ten + 1)
    return (window_shards if whole else block_shards)(tokens, *rest)


def solution(mesh):
    return jax.shard_map(
        shards,
        mesh=mesh,
        in_specs=(
            P(("seq", "tensor"), "dp", None),
            P(),
            P(),
            P(None, "tensor"),
            P(None, "tensor"),
            P(None, "tensor"),
            P("tensor", None),
            P(),
            P(),
            P(None, "tensor"),
            P(None, "tensor"),
            P("tensor", None),
            P("dp", None, None),
            P("dp", None),
            P("dp"),
        ),
        out_specs=(
            P(("seq", "tensor"), "dp", None),
            P(("seq", "tensor"), "dp", None),
            P(("dp", "seq", "tensor")),
            P(("dp", "seq", "tensor")),
            P(("dp", "seq"), "tensor"),
            P(("dp", "seq"), "tensor"),
            P(("dp", "seq"), "tensor"),
            P("tensor", ("dp", "seq")),
            P(("dp", "seq", "tensor")),
            P(("dp", "seq", "tensor")),
            P(("dp", "seq"), "tensor"),
            P(("dp", "seq"), "tensor"),
            P("tensor", ("dp", "seq")),
        ),
        check_vma=False,
    )
```

```python
import math

import functools

import jax
import jax.numpy as jnp
import numpy as np
from jax import lax
from jax.experimental import pallas as pl
from jax.experimental.pallas import tpu as pltpu
from jax.sharding import PartitionSpec as P

HEAD_DIM = 64
L = 1024
LOSS_SCALE = 1024


epsilon = 1e-05


def layer_stats(inputs):
    row_mean = jnp.mean(inputs, axis=-1, keepdims=True)
    centred = inputs - row_mean
    inv_std = lax.rsqrt(jnp.mean(centred * centred, axis=-1, keepdims=True) + epsilon)
    return (centred * inv_std, inv_std)


def norm_back(grad_norm, normed, inv_std, gain_vec):
    scaled = grad_norm * gain_vec
    return inv_std * (
        scaled
        - jnp.mean(scaled, axis=-1, keepdims=True)
        - normed * jnp.mean(scaled * normed, axis=-1, keepdims=True)
    )


def rotary_tables(positions):
    half_dim = HEAD_DIM // 2
    inv_freq = 10000.0 ** (-jnp.arange(half_dim, dtype=jnp.float32) * 2.0 / HEAD_DIM)
    angles = positions.astype(jnp.float32)[:, None] * inv_freq[None, :]
    return (jnp.cos(angles), jnp.sin(angles))


def rotate(values, cosine, sine):
    half_dim = values.shape[-1] // 2
    first_half = values[..., :half_dim]
    second_half = values[..., half_dim:]
    cos_b = cosine[:, None, None, :]
    sin_b = sine[:, None, None, :]
    return jnp.concatenate(
        [first_half * cos_b - second_half * sin_b, second_half * cos_b + first_half * sin_b],
        axis=-1,
    )


def unrotate(grads, cosine, sine):
    half_dim = grads.shape[-1] // 2
    first_half = grads[..., :half_dim]
    second_half = grads[..., half_dim:]
    cos_b = cosine[:, None, None, :]
    sin_b = sine[:, None, None, :]
    return jnp.concatenate(
        [first_half * cos_b + second_half * sin_b, second_half * cos_b - first_half * sin_b],
        axis=-1,
    )


def block_shards(
    tokens,
    norm1_gain,
    norm1_bias,
    w_query,
    w_key,
    w_value,
    w_out,
    norm2_gain,
    norm2_bias,
    w_gate,
    w_up,
    w_down,
    out_grad,
    masked_rows,
    window_counts,
):
    rows_local, windows, model_width = tokens.shape
    span_rows = rows_local * lax.axis_size("tensor")
    seq_index = lax.axis_index("seq")
    tensor_index = lax.axis_index("tensor")
    head_width = w_query.shape[1]
    heads_local = head_width // HEAD_DIM
    score_scale = 1.0 / math.sqrt(HEAD_DIM)
    head_shape = (span_rows, windows, heads_local, HEAD_DIM)
    residual = tokens.astype(jnp.float32)
    normed1, inv_std1 = layer_stats(residual)
    first_low = (normed1 * norm1_gain + norm1_bias).astype(jnp.bfloat16)
    first_full = lax.all_gather(first_low, "tensor", axis=0, tiled=True)
    w_joined = jnp.concatenate([w_query, w_key, w_value], axis=1)
    projected = jnp.einsum("rwd,de->rwe", first_full, w_joined, preferred_element_type=jnp.float32)
    positions = seq_index * span_rows + jnp.arange(span_rows)
    cosine, sine = rotary_tables(positions)
    queries = rotate(projected[..., :head_width].reshape(head_shape), cosine, sine).astype(
        jnp.bfloat16
    )
    keys_rot = (
        rotate(projected[..., head_width : 2 * head_width].reshape(head_shape), cosine, sine)
        .astype(jnp.bfloat16)
        .reshape(span_rows, windows, head_width)
    )
    values_own = projected[..., 2 * head_width :].astype(jnp.bfloat16)
    keys_all, values_all = (
        lax.all_gather(keys_rot, "seq", axis=0, tiled=True),
        lax.all_gather(values_own, "seq", axis=0, tiled=True),
    )
    key_heads = keys_all.reshape(-1, windows, heads_local, HEAD_DIM)
    value_heads = values_all.reshape(-1, windows, heads_local, HEAD_DIM)
    scores = (
        jnp.einsum("qwhd,kwhd->whqk", queries, key_heads, preferred_element_type=jnp.float32)
        * score_scale
    )
    row_max = jnp.max(scores, axis=-1, keepdims=True)
    row_sum = jnp.sum(jnp.exp(scores - row_max), axis=-1, keepdims=True)
    log_norm = row_max + jnp.log(row_sum)
    attn_prob = jnp.exp(scores - log_norm)
    prob_low = attn_prob.astype(jnp.bfloat16)
    attended = (
        jnp.einsum("whqk,kwhd->qwhd", prob_low, value_heads, preferred_element_type=jnp.float32)
        .reshape(span_rows, windows, head_width)
        .astype(jnp.bfloat16)
    )
    block_part = attended
    attn_branch = lax.psum_scatter(
        jnp.einsum("rwe,ed->rwd", block_part, w_out, preferred_element_type=jnp.float32).astype(
            jnp.bfloat16
        ),
        "tensor",
        scatter_dimension=0,
        tiled=True,
    ).astype(jnp.float32)
    residual2 = residual + attn_branch
    normed2, inv_std2 = layer_stats(residual2)
    second_low = (normed2 * norm2_gain + norm2_bias).astype(jnp.bfloat16)
    second_full = lax.all_gather(second_low, "tensor", axis=0, tiled=True)
    gate_proj = jnp.einsum("rwd,df->rwf", second_full, w_gate, preferred_element_type=jnp.float32)
    up_proj = jnp.einsum("rwd,df->rwf", second_full, w_up, preferred_element_type=jnp.float32)
    hidden = (jax.nn.silu(gate_proj) * up_proj).astype(jnp.bfloat16)
    block_part = hidden
    ffn_branch = lax.psum_scatter(
        jnp.einsum("rwf,fd->rwd", block_part, w_down, preferred_element_type=jnp.float32).astype(
            jnp.bfloat16
        ),
        "tensor",
        scatter_dimension=0,
        tiled=True,
    ).astype(jnp.float32)
    output = (residual2 + ffn_branch).astype(jnp.bfloat16)
    live_slot = jnp.arange(windows) < window_counts[0]
    valid_slot = (masked_rows < L) & live_slot[:, None]
    local_masked = jnp.sum(jnp.where(valid_slot, 1, 0)).astype(jnp.int32)
    total_masked = lax.psum(local_masked, "dp")
    loss_weight = LOSS_SCALE / total_masked.astype(jnp.float32)
    own_positions = seq_index * span_rows + tensor_index * rows_local + jnp.arange(rows_local)
    matches = (masked_rows[:, None, :] == own_positions[None, :, None]) & live_slot[:, None, None]
    picked = jnp.einsum(
        "wrm,wmd->rwd", matches.astype(jnp.bfloat16), out_grad, preferred_element_type=jnp.float32
    )
    grad_out = picked * loss_weight
    grad_down_in = lax.all_gather(grad_out.astype(jnp.bfloat16), "tensor", axis=0, tiled=True)
    grad_w_down = jnp.einsum(
        "rwf,rwd->fd", hidden, grad_down_in, preferred_element_type=jnp.float32
    )
    grad_hidden = jnp.einsum(
        "rwd,fd->rwf", grad_down_in, w_down, preferred_element_type=jnp.float32
    )
    sigmoid_gate = jax.nn.sigmoid(gate_proj)
    silu_gate = gate_proj * sigmoid_gate
    grad_gate = (
        grad_hidden * up_proj * sigmoid_gate * (1.0 + gate_proj * (1.0 - sigmoid_gate))
    ).astype(jnp.bfloat16)
    grad_up = (grad_hidden * silu_gate).astype(jnp.bfloat16)
    grad_w_gate = jnp.einsum(
        "rwd,rwf->df", second_full, grad_gate, preferred_element_type=jnp.float32
    )
    grad_w_up = jnp.einsum("rwd,rwf->df", second_full, grad_up, preferred_element_type=jnp.float32)
    grad_second = lax.psum_scatter(
        (
            jnp.einsum("rwf,df->rwd", grad_gate, w_gate, preferred_element_type=jnp.float32)
            + jnp.einsum("rwf,df->rwd", grad_up, w_up, preferred_element_type=jnp.float32)
        ).astype(jnp.bfloat16),
        "tensor",
        scatter_dimension=0,
        tiled=True,
    ).astype(jnp.float32)
    grad_norm2_gain = jnp.sum(grad_second * normed2, axis=(0, 1))
    grad_norm2_bias = jnp.sum(grad_second, axis=(0, 1))
    grad_residual2 = grad_out + norm_back(grad_second, normed2, inv_std2, norm2_gain)
    grad_attn_in = lax.all_gather(grad_residual2.astype(jnp.bfloat16), "tensor", axis=0, tiled=True)
    grad_w_out = jnp.einsum(
        "rwe,rwd->ed", attended, grad_attn_in, preferred_element_type=jnp.float32
    )
    grad_attended = jnp.einsum(
        "rwd,ed->rwe", grad_attn_in, w_out, preferred_element_type=jnp.float32
    ).astype(jnp.bfloat16)
    grad_att_heads = grad_attended.reshape(head_shape)
    scores_again = (
        jnp.einsum("qwhd,kwhd->whqk", queries, key_heads, preferred_element_type=jnp.float32)
        * score_scale
    )
    probs_again = jnp.exp(scores_again - log_norm)
    grad_probs = jnp.einsum(
        "qwhd,kwhd->whqk", grad_att_heads, value_heads, preferred_element_type=jnp.float32
    )
    row_delta = jnp.sum(probs_again * grad_probs, axis=-1, keepdims=True)
    grad_scores = (probs_again * (grad_probs - row_delta)).astype(jnp.bfloat16)
    grad_queries = (
        jnp.einsum("whqk,kwhd->qwhd", grad_scores, key_heads, preferred_element_type=jnp.float32)
        * score_scale
    )
    grad_key_all = (
        jnp.einsum("whqk,qwhd->kwhd", grad_scores, queries, preferred_element_type=jnp.float32)
        * score_scale
    ).reshape(-1, windows, head_width)
    grad_value_all = jnp.einsum(
        "whqk,qwhd->kwhd",
        probs_again.astype(jnp.bfloat16),
        grad_att_heads,
        preferred_element_type=jnp.float32,
    ).reshape(-1, windows, head_width)
    grad_keys, grad_values = (
        lax.psum_scatter(
            grad_key_all.astype(jnp.bfloat16), "seq", scatter_dimension=0, tiled=True
        ).astype(jnp.float32),
        lax.psum_scatter(
            grad_value_all.astype(jnp.bfloat16), "seq", scatter_dimension=0, tiled=True
        ).astype(jnp.float32),
    )
    grad_query_lin = (
        unrotate(grad_queries, cosine, sine)
        .reshape(span_rows, windows, head_width)
        .astype(jnp.bfloat16)
    )
    grad_key_lin = (
        unrotate(grad_keys.reshape(head_shape), cosine, sine)
        .reshape(span_rows, windows, head_width)
        .astype(jnp.bfloat16)
    )
    grad_value_lin = grad_values.astype(jnp.bfloat16)
    grad_joined = jnp.concatenate([grad_query_lin, grad_key_lin, grad_value_lin], axis=-1)
    grad_w_joined = jnp.einsum(
        "rwd,rwe->de", first_full, grad_joined, preferred_element_type=jnp.float32
    )
    grad_w_query = grad_w_joined[:, :head_width]
    grad_w_key = grad_w_joined[:, head_width : 2 * head_width]
    grad_w_value = grad_w_joined[:, 2 * head_width :]
    block_part = grad_joined
    grad_first = lax.psum_scatter(
        jnp.einsum("rwe,de->rwd", block_part, w_joined, preferred_element_type=jnp.float32).astype(
            jnp.bfloat16
        ),
        "tensor",
        scatter_dimension=0,
        tiled=True,
    ).astype(jnp.float32)
    grad_norm1_gain = jnp.sum(grad_first * normed1, axis=(0, 1))
    grad_norm1_bias = jnp.sum(grad_first, axis=(0, 1))
    grad_tokens = grad_residual2 + norm_back(grad_first, normed1, inv_std1, norm1_gain)
    summed = (
        lax.psum_scatter(
            grad_w_query.astype(jnp.bfloat16), ("dp", "seq"), scatter_dimension=0, tiled=True
        ).astype(jnp.float32),
        lax.psum_scatter(
            grad_w_key.astype(jnp.bfloat16), ("dp", "seq"), scatter_dimension=0, tiled=True
        ).astype(jnp.float32),
        lax.psum_scatter(
            grad_w_value.astype(jnp.bfloat16), ("dp", "seq"), scatter_dimension=0, tiled=True
        ).astype(jnp.float32),
        lax.psum_scatter(
            grad_w_out.astype(jnp.bfloat16), ("dp", "seq"), scatter_dimension=1, tiled=True
        ).astype(jnp.float32),
        lax.psum_scatter(
            grad_w_gate.astype(jnp.bfloat16), ("dp", "seq"), scatter_dimension=0, tiled=True
        ).astype(jnp.float32),
        lax.psum_scatter(
            grad_w_up.astype(jnp.bfloat16), ("dp", "seq"), scatter_dimension=0, tiled=True
        ).astype(jnp.float32),
        lax.psum_scatter(
            grad_w_down.astype(jnp.bfloat16), ("dp", "seq"), scatter_dimension=1, tiled=True
        ).astype(jnp.float32),
    )
    norm_sums = (
        lax.psum_scatter(grad_norm1_gain, ("dp", "seq", "tensor"), scatter_dimension=0, tiled=True),
        lax.psum_scatter(grad_norm1_bias, ("dp", "seq", "tensor"), scatter_dimension=0, tiled=True),
        lax.psum_scatter(grad_norm2_gain, ("dp", "seq", "tensor"), scatter_dimension=0, tiled=True),
        lax.psum_scatter(grad_norm2_bias, ("dp", "seq", "tensor"), scatter_dimension=0, tiled=True),
    )
    return (
        output,
        grad_tokens,
        norm_sums[0],
        norm_sums[1],
        summed[0],
        summed[1],
        summed[2],
        summed[3],
        norm_sums[2],
        norm_sums[3],
        summed[4],
        summed[5],
        summed[6],
    )


BF = jnp.bfloat16
F32 = jnp.float32
LANES = 128
QUAD = 4


def dot_t(a, b):
    return lax.dot_general(a, b, (((1,), (1,)), ((), ())), preferred_element_type=F32)


def dot_n(a, b):
    return lax.dot_general(a, b, (((1,), (0,)), ((), ())), preferred_element_type=F32)


def t_dot(a, b):
    return lax.dot_general(a, b, (((0,), (0,)), ((), ())), preferred_element_type=F32)


def swap_halves(x):
    half = HEAD_DIM // 2
    lane = lax.broadcasted_iota(jnp.int32, x.shape, 1)
    down = pltpu.roll(x, half, 1)
    up = pltpu.roll(x, LANES - half, 1)
    return jnp.where(lane % HEAD_DIM < half, up, down)


def head_mask(h):
    lane = lax.broadcasted_iota(jnp.int32, (1, LANES), 1)
    return jnp.where(lane // HEAD_DIM == h, 1.0, 0.0).astype(BF)


MESH = pl.DeviceIdType.MESH


def any_spec():
    return pl.BlockSpec(memory_space=pl.ANY)


def greet(peers):
    barrier = pltpu.get_barrier_semaphore()
    for peer in peers:
        pl.semaphore_signal(barrier, inc=1, device_id=peer, device_id_type=MESH)
    pl.semaphore_wait(barrier, len(peers))


def remote(src, dst, send, recv, peer):
    return pltpu.make_async_remote_copy(
        src_ref=src, dst_ref=dst, send_sem=send, recv_sem=recv, device_id=peer, device_id_type=MESH
    )


def start_all(copies):
    for copy in copies:
        copy.start()


def wait_all(copies):
    for copy in copies:
        copy.wait()


def quad_place():
    dp, sx = lax.axis_index("dp"), lax.axis_index("seq")
    place = sx * 2 + dp % 2
    return place, lambda to: {"dp": dp // 2 * 2 + to % 2, "seq": to // 2}


def quad_peers():
    place, device = quad_place()
    return [device((place + j) % QUAD) for j in range(1, QUAD)]


class WeightRoute:
    def __init__(self, gathered, own, n_ten, send, recv):
        dp, sx, t = lax.axis_index("dp"), lax.axis_index("seq"), lax.axis_index("tensor")
        y, c = dp // 2, dp % 2
        gate_ref, up_ref, down_ref = gathered
        self.refs, self.own = (gate_ref, up_ref, down_ref, down_ref), own
        self.width, self.units = gate_ref.shape[0], gate_ref.shape[1] // n_ten
        self.send, self.recv, self.c = send, recv, c
        s_xy, s_yx = c * 4 + y * 2 + sx, c * 4 + sx * 2 + y
        self.slices = (s_xy, s_yx, s_xy, s_yx)
        self.x_peer, self.y_peer, self.c_peer = {"seq": 1 - sx}, {"dp": (dp + 2) % 4}, {"dp": 2 * y + 1 - c}
        side = t // 2
        middle = jnp.minimum(t, n_ten - 1 - t)
        mirror = lambda k: k + side * (n_ten - 1 - 2 * k)
        self.order = [mirror(k) for k in (middle, 1 - middle, 2, 3)]
        self.inward, self.outward = mirror(middle + 1), mirror(0)
        self.is_middle, self.is_end = middle == 1, middle == 0
        self.t, self.middle, self.mirror = t, middle, mirror

    def shard(self, ref, k, first, count, which):
        size, cols, units = self.width // 8, self.width // 2, self.units
        rows = pl.multiple_of(first * (size if k < 2 else units // 8), 16)
        if k < 2:
            at = 0 if which is None else pl.multiple_of(which * units, units)
            return ref.at[pl.ds(rows, count * size), pl.ds(at, units)]
        at = rows if which is None else pl.multiple_of(which * units + rows, 16)
        return ref.at[pl.ds(at, count * (units // 8)), pl.ds((k - 2) * cols, cols)]

    def along(self, which, to, slot, number, own=False):
        copies = []
        for k in range(4):
            dst = self.shard(self.refs[k], k, self.slices[k], 1, which)
            src = self.shard(self.own[min(k, 2)], k, self.slices[k], 1, None) if own else dst
            copies.append(remote(src, dst, self.send.at[number, k], self.recv.at[slot, k], {"tensor": to}))
        return copies

    def to_in(self):
        return self.along(self.t, self.inward, 1 + self.middle, 0, True)

    def to_out(self):
        return self.along(self.t, self.outward, 1, 1, True)

    def in_far(self):
        return self.along(self.mirror(0), self.inward, 3, 2)

    def out_two(self):
        return self.along(self.mirror(2), self.outward, 2, 3)

    def out_three(self):
        return self.along(self.mirror(3), self.outward, 3, 4)

    def arrived(self, i):
        received(self.along(self.order[i], self.inward, i, 0))

    def hop(self, i, h):
        copies = []
        for k in range(4):
            xy = k % 2 == 0
            peer, first, count = (
                (self.x_peer if xy else self.y_peer, self.slices[k], 1),
                (self.y_peer if xy else self.x_peer, self.slices[k] // 2 * 2, 2),
                (self.c_peer, self.c * 4, 4),
            )[h]
            ref = self.shard(self.refs[k], k, first, count, self.order[i])
            copies.append(remote(ref, ref, self.send.at[2 + 3 * i + h, k], self.recv.at[1 + 3 * i + h, k], peer))
        return copies


def received(copies):
    for copy in copies:
        copy.wait_recv()


def sent_all(copies):
    for copy in copies:
        copy.wait_send()


def route_sems():
    return [pltpu.SemaphoreType.DMA((14, 4)), pltpu.SemaphoreType.DMA((13, 4))]


def exchange_in_kernel(
    sizes, tok_ref, wq_ref, wk_ref, wv_ref, wo_ref, count_ref, rows_ref, x_ref, q_ref, k_ref, v_ref, o_ref, counts_ref,
    peer_rows_ref, tok_send, tok_recv, w_send, w_recv, count_send, count_recv, rows_send, rows_recv, local_sem,
):
    n_seq, n_ten, half, rows, slices = sizes
    dp, sx, t = lax.axis_index("dp"), lax.axis_index("seq"), lax.axis_index("tensor")
    y, c = dp // 2, dp % 2
    me = sx * n_ten + t
    group = n_seq * n_ten
    others = []
    for i in range(1, group):
        g = (me + i) % group
        others.append((g // n_ten, g % n_ten))
    y_peer, c_peer, x_peer = {"dp": (dp + 2) % 4}, {"dp": 2 * y + 1 - c}, {"seq": 1 - sx}
    dp_peers = [{"dp": (dp + i) % 4} for i in range(1, 4)]
    beside = [{"dp": 2 * y + 1 - c, "tensor": (t + j) % n_ten} for j in range(1, n_ten)]
    greet([{"seq": a, "tensor": b} for a, b in others] + dp_peers + beside)
    counts = [
        remote(count_ref, counts_ref.at[dp], count_send.at[i], count_recv.at[i], peer) for i, peer in enumerate(dp_peers)
    ]
    start_all(counts)

    hw = wq_ref.shape[1]
    srow, orow = wq_ref.shape[0] // slices, hw // slices
    s_xy, s_yx = c * 4 + y * 2 + sx, c * 4 + sx * 2 + y
    weights = ((wq_ref, q_ref, s_xy, 0), (wk_ref, k_ref, s_xy, 0), (wv_ref, v_ref, s_yx, 0), (wo_ref, o_ref, s_yx, 1))

    def block(out, by_rows, base, count, which):
        if by_rows:
            return out.at[pl.ds(pl.multiple_of(which * hw + base * orow, orow), count * orow), :]
        return out.at[
            pl.ds(pl.multiple_of(base * srow, srow), count * srow), pl.ds(pl.multiple_of(which * hw, hw), hw)
        ]

    stage = [[], [], [], []]
    n = 0
    for j in range(1, n_ten):
        peer = {"tensor": (t + j) % n_ten}
        for w_ref, out, s, by_rows in weights:
            size = orow if by_rows else srow
            src = w_ref.at[pl.ds(pl.multiple_of(s * size, size), size), :]
            stage[0].append(remote(src, block(out, by_rows, s, 1, t), w_send.at[0, n], w_recv.at[0, n], peer))
            n += 1
    n = 0
    for j in range(1, n_ten):
        which = (t + j) % n_ten
        for w_ref, out, s, by_rows in weights:
            xy = s is s_xy
            hops = (
                (1, x_peer if xy else y_peer, s, 1),
                (2, y_peer if xy else x_peer, s // 2 * 2, 2),
                (3, c_peer, c * 4, 4),
            )
            for k, peer, base, count in hops:
                ref = block(out, by_rows, base, count, which)
                stage[k].append(remote(ref, ref, w_send.at[k, n], w_recv.at[k, n], peer))
            n += 1
    start_all(stage[0])

    tokens = []
    for i, (a, b) in enumerate(others):
        tokens.append(
            remote(
                tok_ref.at[a * half + b],
                x_ref.at[pl.ds(pl.multiple_of(me * rows, rows), rows), :],
                tok_send.at[i], tok_recv.at[i], {"seq": a, "tensor": b},
            )
        )
    shared = []
    for i in range(n_seq):
        src, dst = tok_ref.at[i * half + n_ten], x_ref.at[pl.ds(pl.multiple_of((group + t % 2) * rows, rows), rows), :]
        shared.append(
            (
                2 * c + i == t,
                remote(
                    src, dst, tok_send.at[group - 1 + i], tok_recv.at[group - 1 + t % 2],
                    {"dp": 2 * y + t // 2, "tensor": 2 * c + i},
                ),
                pltpu.make_async_copy(src, dst, local_sem.at[1]),
            )
        )
    arriving = [
        remote(
            tok_ref.at[n_ten], x_ref.at[pl.ds((group + i) * rows, rows), :],
            tok_send.at[group - 1], tok_recv.at[group - 1 + i], c_peer,
        )
        for i in range(n_seq)
    ]
    start_all(tokens)
    for here, away, near in shared:
        pl.when(here)(near.start)
        pl.when(jnp.logical_not(here))(away.start)
    peer_rows = [
        remote(rows_ref.at[i * half + n_ten], peer_rows_ref.at[2 * c + i], rows_send.at[i], rows_recv.at[i], c_peer)
        for i in range(n_seq)
    ]
    start_all(peer_rows)
    local = [
        pltpu.make_async_copy(
            tok_ref.at[sx * half + t], x_ref.at[pl.ds(pl.multiple_of(me * rows, rows), rows), :], local_sem.at[0]
        ),
    ]
    for i, (w_ref, out, s, by_rows) in enumerate(weights):
        local.append(pltpu.make_async_copy(w_ref, block(out, by_rows, 0, slices, t), local_sem.at[2 + i]))
    local.append(pltpu.make_async_copy(count_ref, counts_ref.at[dp], local_sem.at[6]))
    for i in range(n_seq):
        local.append(
            pltpu.make_async_copy(rows_ref.at[i * half + n_ten], peer_rows_ref.at[2 * c + i], local_sem.at[7 + i])
        )
    start_all(local)
    for k in range(1, 4):
        for earlier in stage[k - 1]:
            earlier.wait_recv()
        start_all(stage[k])
    for copy in stage[3]:
        copy.wait_recv()
    for copies in stage:
        for copy in copies:
            copy.wait_send()
    wait_all(local)
    wait_all(counts)
    wait_all(peer_rows)
    wait_all(tokens)
    for here, away, near in shared:
        pl.when(here)(near.wait)
        pl.when(jnp.logical_not(here))(away.wait_send)
    for i in range(n_seq):
        pl.when(jnp.logical_not((t // 2 == c) & (t % 2 == i)))(arriving[i].wait_recv)


def exchange_in(tok, w_query, w_key, w_value, w_out, count, out_grad, n_dp, n_seq, n_ten):
    windows, rows, width = tok.shape
    slices = n_dp * n_seq
    vmem = pl.BlockSpec(memory_space=pltpu.VMEM)
    square = jax.ShapeDtypeStruct((width, width), BF)
    group = n_seq * n_ten
    return pl.pallas_call(
        functools.partial(exchange_in_kernel, (n_seq, n_ten, windows // n_seq, rows, slices)),
        in_specs=[vmem] * 6 + [any_spec()],
        out_specs=[any_spec()] * 7,
        out_shape=[jax.ShapeDtypeStruct(((group + n_seq) * rows, width), BF)]
        + [square] * 4
        + [jax.ShapeDtypeStruct((n_dp,) + count.shape, count.dtype)]
        + [jax.ShapeDtypeStruct((2 * n_seq,) + out_grad.shape[1:], BF)],
        scratch_shapes=[
            pltpu.SemaphoreType.DMA((group + 1,)),
            pltpu.SemaphoreType.DMA((group + 1,)),
            pltpu.SemaphoreType.DMA((4, 4 * (n_ten - 1))),
            pltpu.SemaphoreType.DMA((4, 4 * (n_ten - 1))),
            pltpu.SemaphoreType.DMA((3,)),
            pltpu.SemaphoreType.DMA((3,)),
            pltpu.SemaphoreType.DMA((2,)),
            pltpu.SemaphoreType.DMA((2,)),
            pltpu.SemaphoreType.DMA((9,)),
        ],
        compiler_params=pltpu.CompilerParams(collective_id=0, has_side_effects=True),
        name="exchange_in",
    )(tok, w_query, w_key, w_value, w_out, count, out_grad)


def qkv_kernel(
    x_ref, gain_ref, bias_ref, wq_ref, wk_ref, wv_ref, cos_ref, sin_ref, part_cos_ref, part_sin_ref,
    first_ref, q_ref, k_ref, v_ref,
):
    shared = pl.program_id(0) == pl.num_programs(0) - 1
    normed, _ = layer_stats(x_ref[...].astype(F32))
    first_ref[...] = (normed * gain_ref[...] + bias_ref[...]).astype(BF)
    cos = jnp.where(shared, part_cos_ref[...], cos_ref[...])
    sin = jnp.where(shared, part_sin_ref[...], sin_ref[...])
    wide = 256
    for w_ref, out_ref, scale in ((wq_ref, q_ref, 1.0 / math.sqrt(HEAD_DIM)), (wk_ref, k_ref, 1.0), (wv_ref, v_ref, None)):
        for at in range(0, w_ref.shape[1], wide):
            acc = dot_n(first_ref[...], w_ref[:, at : at + wide])
            for c in range(0, wide, LANES):
                part = acc[:, c : c + LANES]
                if scale is not None:
                    part = (part * cos + swap_halves(part) * sin) * scale
                out_ref[:, at + c : at + c + LANES] = part.astype(BF)


def once(shape):
    return pl.BlockSpec(shape, lambda *_: (0,) * len(shape), pipeline_mode=pl.Buffered(1))


def norm_qkv(x, gain, bias, w_query, w_key, w_value, tables, part_tables):
    rows, width = x.shape
    tile = 256
    row = pl.BlockSpec((tile, width), lambda r: (r, 0))
    own = tables[0].shape[0] // tile
    table = pl.BlockSpec((tile, LANES), lambda r: (jnp.minimum(r, own - 1), 0))
    return pl.pallas_call(
        qkv_kernel,
        grid=(rows // tile,),
        in_specs=[row, once((1, width)), once((1, width))] + [once((width, width))] * 3 + [table, table] + [once((tile, LANES))] * 2,
        out_specs=[row] * 4,
        out_shape=[jax.ShapeDtypeStruct((rows, width), BF)] * 4,
        cost_estimate=pl.CostEstimate(flops=6 * rows * width * width, bytes_accessed=16 * rows * width, transcendentals=0),
        name="norm_qkv",
    )(x, gain.reshape(1, width), bias.reshape(1, width), w_query, w_key, w_value, *tables, *part_tables)


def attend_body(q_ref, k_ref, v_ref):
    q, k, v = q_ref[...], k_ref[...], v_ref[...]
    outs = []
    for h in range(LANES // HEAD_DIM):
        s = dot_t(q * head_mask(h), k)
        p = jnp.exp(s - jnp.max(s, axis=1, keepdims=True))
        norm = jnp.sum(p, axis=1, keepdims=True)
        outs.append(dot_n(p.astype(BF), v) / norm)
    lane = lax.broadcasted_iota(jnp.int32, outs[0].shape, 1)
    return jnp.where(lane < HEAD_DIM, outs[0], outs[1]).astype(BF)


def attend_specs(rows, tile):
    return [
        pl.BlockSpec((tile, LANES), lambda p, r: (r, p)),
        pl.BlockSpec((rows, LANES), lambda p, r: (0, p)),
        pl.BlockSpec((rows, LANES), lambda p, r: (0, p)),
    ]


def attend_cost(rows, pairs):
    return pl.CostEstimate(
        flops=16 * pairs * rows * rows * LANES, bytes_accessed=8 * rows * pairs * LANES, transcendentals=2 * pairs * rows * rows
    )


def attend_left_kernel(
    n_ten, q_ref, k_ref, v_ref, ag_in, au_in, ad_in, part_ref, ag_ref, au_ref, ad_ref, buf, send, recv, local_sem,
    route_send, route_recv,
):
    place, device = quad_place()
    r, p = pl.program_id(0), pl.program_id(1)
    last_pair = p == pl.num_programs(1) - 1
    hw = buf.shape[2]
    dst = part_ref.at[:, pl.ds(pl.multiple_of(place * hw, hw), hw)]
    route = WeightRoute((ag_ref, au_ref, ad_ref), None, n_ten, route_send, route_recv)
    hops = route.hop(1, 2) + route.hop(2, 0)

    @pl.when((p == 0) & (r == 0))
    def _():
        greet(quad_peers() + [route.y_peer] + [{"tensor": (route.t + j) % n_ten} for j in range(1, n_ten)])
        start_all(hops)
        pl.when(route.is_middle)(lambda: start_all(route.out_three()))

    buf[r, :, pl.ds(pl.multiple_of(p * LANES, LANES), LANES)] = attend_body(q_ref, k_ref, v_ref)

    def copy_to(j):
        to = (place + j) % QUAD
        return remote(buf.at[to], dst, send.at[j - 1], recv.at[j - 1], device(to))

    own = pltpu.make_async_copy(buf.at[place], dst, local_sem.at[0])
    for j in range(1, QUAD):
        pl.when(last_pair & (r == (place + j) % QUAD))(copy_to(j).start)
    pl.when(last_pair & (r == place))(own.start)

    @pl.when(last_pair & (r == QUAD - 1))
    def _():
        wait_all([copy_to(j) for j in range(1, QUAD)])
        own.wait()
        wait_all(hops)
        pl.when(route.is_middle)(lambda: sent_all(route.out_three()))
        pl.when(route.is_end)(lambda: route.arrived(3))


def attend_left(q, k, v, gathered, n_ten):
    rows, hw = q.shape
    tile, pairs = rows // QUAD, hw // LANES
    column = pl.BlockSpec((rows, LANES), lambda r, p: (0, p))
    return pl.pallas_call(
        functools.partial(attend_left_kernel, n_ten),
        grid=(QUAD, pairs),
        in_specs=[pl.BlockSpec((tile, LANES), lambda r, p: (r, p)), column, column] + [any_spec()] * 3,
        out_specs=[any_spec()] * 4,
        out_shape=[jax.ShapeDtypeStruct((tile, QUAD * hw), BF)] + [jax.ShapeDtypeStruct(w.shape, BF) for w in gathered],
        input_output_aliases={3: 1, 4: 2, 5: 3},
        scratch_shapes=[pltpu.VMEM((QUAD, tile, hw), BF)]
        + [pltpu.SemaphoreType.DMA((QUAD - 1,))] * 2
        + [pltpu.SemaphoreType.DMA((1,))]
        + route_sems(),
        compiler_params=pltpu.CompilerParams(collective_id=3, has_side_effects=True),
        cost_estimate=attend_cost(rows, pairs),
        name="attend_left",
    )(q, k, v, *gathered)


def swap_part(refs, outs, send, recv, local_sem, base):
    place, device = quad_place()
    share, hw = outs[0].shape[0] // QUAD, outs[0].shape[1]
    copies, local = [], []
    rows = pl.ds(base, share)
    mine = pl.ds(pl.multiple_of(place * share, share), share)
    for i, (ref, out) in enumerate(zip(refs, outs, strict=True)):
        for j in range(1, QUAD):
            to = (place + j) % QUAD
            src = ref.at[rows, pl.ds(pl.multiple_of(to * hw, hw), hw)]
            copies.append(remote(src, out.at[mine, :], send.at[i, j - 1], recv.at[i, j - 1], device(to)))
        src = ref.at[rows, pl.ds(pl.multiple_of(place * hw, hw), hw)]
        local.append(pltpu.make_async_copy(src, out.at[mine, :], local_sem.at[i]))
    return copies, local


def attend_swap_kernel(
    n_ten, length, q_ref, k_ref, v_ref, q_all, k_all, v_all, wg_ref, wu_ref, wd_ref, o_ref, lq_ref, lk_ref, lv_ref,
    ag_ref, au_ref, ad_ref, send, recv, local_sem, route_send, route_recv,
):
    step = pl.program_id(0) * pl.num_programs(1) + pl.program_id(1)
    steps = pl.num_programs(0) * pl.num_programs(1)
    copies, local = swap_part((q_all, k_all, v_all), (lq_ref, lk_ref, lv_ref), send, recv, local_sem, length)
    route = WeightRoute((ag_ref, au_ref, ad_ref), (wg_ref, wu_ref, wd_ref), n_ten, route_send, route_recv)

    @pl.when(step == 0)
    def _():
        greet(quad_peers() + [route.y_peer] + [{"tensor": (route.t + j) % n_ten} for j in range(1, n_ten)])
        start_all(route.to_in())
        pl.when(route.is_middle)(lambda: start_all(route.to_out()))
        start_all(copies + local)

    o_ref[...] = attend_body(q_ref, k_ref, v_ref)

    @pl.when(step == steps // 2)
    def _():
        route.arrived(1)
        start_all(route.hop(1, 0))

        @pl.when(route.is_middle)
        def _():
            route.arrived(2)
            start_all(route.in_far())
            start_all(route.out_two())

    @pl.when(step == steps * 3 // 4)
    def _():
        received(route.hop(1, 0))
        start_all(route.hop(1, 1))

    @pl.when(step == steps - 1)
    def _():
        wait_all(copies + local)
        received(route.hop(1, 1))
        sent_all(route.hop(1, 0) + route.hop(1, 1) + route.to_in())

        @pl.when(route.is_middle)
        def _():
            route.arrived(3)
            sent_all(route.to_out() + route.in_far() + route.out_two())

        @pl.when(route.is_end)
        def _():
            route.arrived(2)


def attend_swap(q, k, v, ffn, length, n_ten):
    width = q.shape[1]
    tile, pairs, hw = 512, width // LANES, width // QUAD
    left = jax.ShapeDtypeStruct((length, hw), BF)
    return pl.pallas_call(
        functools.partial(attend_swap_kernel, n_ten, length),
        grid=(pairs, length // tile),
        in_specs=attend_specs(length, tile) + [any_spec()] * 6,
        out_specs=[pl.BlockSpec((tile, LANES), lambda p, r: (r, p))] + [any_spec()] * 6,
        out_shape=[jax.ShapeDtypeStruct((length, width), BF), left, left, left]
        + [jax.ShapeDtypeStruct((width, n_ten * w.shape[1]), BF) for w in ffn[:2]]
        + [jax.ShapeDtypeStruct((n_ten * ffn[2].shape[0], width), BF)],
        scratch_shapes=[
            pltpu.SemaphoreType.DMA((3, QUAD - 1)),
            pltpu.SemaphoreType.DMA((3, QUAD - 1)),
            pltpu.SemaphoreType.DMA((3,)),
        ]
        + route_sems(),
        compiler_params=pltpu.CompilerParams(collective_id=1, has_side_effects=True),
        cost_estimate=attend_cost(length, pairs),
        name="attend_swap",
    )(q, k, v, q, k, v, *ffn)


def back_body(q_ref, g_ref, k_ref, v_ref, pick_ref, cos_ref, sin_ref, qcos_ref, qsin_ref):
    g, k, v, pick = g_ref[...], k_ref[...], v_ref[...], pick_ref[...]
    q = dot_n(pick, q_ref[...]).astype(BF)
    dq = []
    all_p, all_ds, all_q, all_g = [], [], [], []
    for h in range(LANES // HEAD_DIM):
        mask = head_mask(h)
        qh, gh = q * mask, g * mask
        s = dot_t(qh, k)
        p = jnp.exp(s - jnp.max(s, axis=1, keepdims=True))
        p = p / jnp.sum(p, axis=1, keepdims=True)
        dp = dot_t(gh, v)
        ds = (p * (dp - jnp.sum(p * dp, axis=1, keepdims=True))).astype(BF)
        dq.append(dot_n(ds, k))
        all_p.append(p.astype(BF))
        all_ds.append(ds)
        all_q.append(qh)
        all_g.append(gh)
    lane = lax.broadcasted_iota(jnp.int32, dq[0].shape, 1)
    dq = jnp.where(lane < HEAD_DIM, dq[0], dq[1]) * (1.0 / math.sqrt(HEAD_DIM))
    dq = (dq * qcos_ref[...] - swap_halves(dq) * qsin_ref[...]).astype(BF)
    dq = t_dot(pick, dq).astype(BF)
    dk = t_dot(jnp.concatenate(all_ds, axis=0), jnp.concatenate(all_q, axis=0))
    dk = (dk * cos_ref[...] - swap_halves(dk) * sin_ref[...]).astype(BF)
    dv = t_dot(jnp.concatenate(all_p, axis=0), jnp.concatenate(all_g, axis=0)).astype(BF)
    return dq, dk, dv


def back_kernel(q_ref, g_ref, k_ref, v_ref, pick_ref, cos_ref, sin_ref, qcos_ref, qsin_ref, dq_ref, dk_ref, dv_ref):
    dq_ref[...], dk_ref[...], dv_ref[...] = back_body(
        q_ref, g_ref, k_ref, v_ref, pick_ref, cos_ref, sin_ref, qcos_ref, qsin_ref
    )


def back_specs(length, masked):
    full = pl.BlockSpec((length, LANES), lambda p: (0, p))
    same = pl.BlockSpec((length, LANES), lambda p: (0, 0))
    row_same = pl.BlockSpec((masked, LANES), lambda p: (0, 0))
    return [
        full, pl.BlockSpec((masked, LANES), lambda p: (0, p)), full, full,
        pl.BlockSpec((masked, length), lambda p: (0, 0)), same, same, row_same, row_same,
    ]


def back_cost(length, masked, pairs):
    return pl.CostEstimate(
        flops=24 * pairs * length * masked * LANES, bytes_accessed=12 * length * pairs * LANES, transcendentals=2 * pairs * length * masked
    )


def back_left(q, grad_rows, k, v, pick, tables):
    masked, length = pick.shape
    width = q.shape[1]
    full = pl.BlockSpec((length, LANES), lambda p: (0, p))
    return pl.pallas_call(
        back_kernel,
        grid=(width // LANES,),
        in_specs=back_specs(length, masked),
        out_specs=[full] * 3,
        out_shape=[jax.ShapeDtypeStruct((length, width), BF)] * 3,
        cost_estimate=back_cost(length, masked, width // LANES),
        name="back_left",
    )(q, grad_rows, k, v, pick, *tables)


def back_swap_kernel(
    q_ref, g_ref, k_ref, v_ref, pick_ref, cos_ref, sin_ref, qcos_ref, qsin_ref, lq_ref, lk_ref, lv_ref,
    dq_ref, dk_ref, dv_ref, buf, out_sem, send, recv, local_sem,
):
    place, device = quad_place()
    step, steps = pl.program_id(0), pl.num_programs(0)
    length = q_ref.shape[0]
    share, hw = lq_ref.shape[0] // QUAD, lq_ref.shape[1]
    outs = (dq_ref, dk_ref, dv_ref)
    copies, local = [], []
    mine = pl.ds(pl.multiple_of(place * hw, hw), hw)
    for i, (ref, out) in enumerate(zip((lq_ref, lk_ref, lv_ref), outs, strict=True)):
        dst = out.at[pl.ds(length, share), mine]
        for j in range(1, QUAD):
            to = (place + j) % QUAD
            src = ref.at[pl.ds(pl.multiple_of(to * share, share), share), :]
            copies.append(remote(src, dst, send.at[i, j - 1], recv.at[i, j - 1], device(to)))
        src = ref.at[pl.ds(pl.multiple_of(place * share, share), share), :]
        local.append(pltpu.make_async_copy(src, dst, local_sem.at[i]))

    def out_copy(at, i):
        slot = at % 2
        columns = pl.ds(pl.multiple_of(at * LANES, LANES), LANES)
        return pltpu.make_async_copy(buf.at[slot, i], outs[i].at[pl.ds(0, length), columns], out_sem.at[slot, i])

    @pl.when(step == 0)
    def _():
        greet(quad_peers())
        start_all(copies + local)

    @pl.when(step >= 2)
    def _():
        for i in range(3):
            out_copy(step - 2, i).wait()

    results = back_body(q_ref, g_ref, k_ref, v_ref, pick_ref, cos_ref, sin_ref, qcos_ref, qsin_ref)
    for i in range(3):
        buf[step % 2, i] = results[i]
        out_copy(step, i).start()

    @pl.when(step == steps - 1)
    def _():
        for i in range(3):
            out_copy(step - 1, i).wait()
            out_copy(step, i).wait()
        wait_all(copies + local)


def back_swap(q, grad_rows, k, v, pick, tables, left):
    masked, length = pick.shape
    width = q.shape[1]
    share = left[0].shape[0] // QUAD
    return pl.pallas_call(
        back_swap_kernel,
        grid=(width // LANES,),
        in_specs=back_specs(length, masked) + [any_spec()] * 3,
        out_specs=[any_spec()] * 3,
        out_shape=[jax.ShapeDtypeStruct((length + share, width), BF)] * 3,
        scratch_shapes=[
            pltpu.VMEM((2, 3, length, LANES), BF),
            pltpu.SemaphoreType.DMA((2, 3)),
            pltpu.SemaphoreType.DMA((3, QUAD - 1)),
            pltpu.SemaphoreType.DMA((3, QUAD - 1)),
            pltpu.SemaphoreType.DMA((3,)),
        ],
        compiler_params=pltpu.CompilerParams(collective_id=2, has_side_effects=True),
        cost_estimate=back_cost(length, masked, width // LANES),
        name="back_swap",
    )(q, grad_rows, k, v, pick, *tables, *left)


def feed_kernel(
    n_ten, tok_ref, att_ref, left_ref, wo_ref, gain_ref, bias_ref, pick_ref, part_pick_ref, cot_ref, wg_ref, wu_ref, wd_ref,
    ag_in, au_in, ad_in, out_ref, out_left_ref, att_m_ref, gr2_ref, gatt_ref, left_gatt_ref, vec_ref, all_own_ref, all_left_ref,
    ag_ref, au_ref, ad_ref,
    x_ref, acc_ref, normed_ref, inv_ref, grad_ref, g_buf, u_buf, d_buf, rows_buf, rows_parts, own_m, left_m, gatt_buf, gatt_parts,
    buf_sem, small_send, small_recv, line_send, line_recv, local_sem, send, recv,
):
    step, steps = pl.program_id(0), pl.num_programs(0)
    rows, width = tok_ref.shape
    length = att_ref.shape[0]
    masked = cot_ref.shape[0]
    slots = masked // 2
    unit = g_buf.shape[2]
    units = wg_ref.shape[1]
    per = units // unit
    part, hw = rows_buf.shape[1], gatt_parts.shape[2]
    gain = gain_ref[...]
    own = (wg_ref, wu_ref, wd_ref)
    route = WeightRoute((ag_ref, au_ref, ad_ref), own, n_ten, send, recv)
    order = route.order
    place, device = quad_place()
    rows_copies, gatt_copies = [], []
    for j in range(1, QUAD):
        to = (place + j) % QUAD
        rows_copies.append(
            remote(rows_buf.at[to], rows_parts.at[j - 1], small_send.at[0, j - 1], small_recv.at[0, j - 1], device(to))
        )
        src = gatt_buf.at[:, pl.ds(pl.multiple_of(to * hw, hw), hw)]
        gatt_copies.append(
            remote(src, gatt_parts.at[j - 1], small_send.at[1, j - 1], small_recv.at[1, j - 1], device(to))
        )

    line_copies = [[], []]
    local = []
    for n, (src, out) in enumerate(((own_m, all_own_ref), (left_m, all_left_ref))):
        for j in range(1, n_ten):
            to = (route.t + j) % n_ten
            line_copies[n].append(
                remote(src, out.at[route.t], line_send.at[n, j - 1], line_recv.at[n, j - 1], {"tensor": to})
            )
        local.append(pltpu.make_async_copy(src, out.at[route.t], local_sem.at[n]))

    def fetch(at):
        slot, i, b = at % 2, at // per, at % per

        def make(refs, shard_at):
            base = pl.multiple_of(shard_at * units + b * unit, unit)
            return [
                pltpu.make_async_copy(refs[0].at[:, pl.ds(base, unit)], g_buf.at[slot], buf_sem.at[slot, 0]),
                pltpu.make_async_copy(refs[1].at[:, pl.ds(base, unit)], u_buf.at[slot], buf_sem.at[slot, 1]),
                pltpu.make_async_copy(refs[2].at[pl.ds(base, unit), :], d_buf.at[slot], buf_sem.at[slot, 2]),
            ]

        @pl.when(i == 0)
        def _():
            start_all(make(own, 0))

        @pl.when(i > 0)
        def _():
            which = order[1] * (i == 1) + order[2] * (i == 2) + order[3] * (i == 3)
            start_all(make((ag_ref, au_ref, ad_ref), which))

    def fetched(at):
        slot = at % 2
        wait_all(
            [
                pltpu.make_async_copy(wg_ref.at[:, pl.ds(0, unit)], g_buf.at[slot], buf_sem.at[slot, 0]),
                pltpu.make_async_copy(wu_ref.at[:, pl.ds(0, unit)], u_buf.at[slot], buf_sem.at[slot, 1]),
                pltpu.make_async_copy(wd_ref.at[pl.ds(0, unit), :], d_buf.at[slot], buf_sem.at[slot, 2]),
            ]
        )

    def norm(res):
        normed, inv_std = layer_stats(res)
        return normed, inv_std, (normed * gain + bias_ref[...]).astype(BF)

    @pl.when(step == 0)
    def _():
        greet(quad_peers() + [route.y_peer] + [{"tensor": (route.t + j) % n_ten} for j in range(1, n_ten)])
        start_all(route.hop(2, 1))
        start_all(route.hop(3, 0))
        fetch(0)
        tile = rows - length
        for i, (pick, att, tok) in enumerate(
            ((pick_ref[...], att_ref[...], tok_ref[:length, :]), (part_pick_ref[...], left_ref[...], tok_ref[length:, :]))
        ):
            here = slice(i * slots, (i + 1) * slots)
            att_m = dot_n(pick, att).astype(BF)
            att_m_ref[here, :] = att_m
            normed, inv_std, low = norm(dot_n(pick, tok) + dot_n(att_m, wo_ref[...]))
            normed_ref[here, :] = normed
            inv_ref[here, :] = jnp.broadcast_to(inv_std, (slots, LANES))
            here_too = jnp.sum(pick.astype(F32), axis=1, keepdims=True) > 0.0
            low = jnp.where(here_too, low.astype(F32), 0.0)
            x_ref[rows + i * slots : rows + (i + 1) * slots, :] = low.astype(BF)
            if i == 0:
                own_m[...] = low.astype(BF)
            else:
                for k in range(QUAD):
                    rows_buf[k] = low[k * part : (k + 1) * part, :].astype(BF)
        for at in range(0, rows, tile):
            att = att_ref[at : at + tile, :] if at < length else left_ref[...]
            res = tok_ref[at : at + tile, :].astype(F32) + dot_n(att, wo_ref[...])
            x_ref[at : at + tile, :] = norm(res)[2]
            acc_ref[at : at + tile, :] = res
        grad_ref[...] = jnp.zeros_like(grad_ref)

    fetched(step)

    @pl.when((step + 1 < steps) & ((step + 1) % per != 0))
    def _():
        fetch(step + 1)

    slot = step % 2
    x = x_ref[...]
    w_g, w_u, w_d = g_buf[slot], u_buf[slot], d_buf[slot]
    gate, up = dot_n(x, w_g), dot_n(x, w_u)
    sig = jax.nn.sigmoid(gate)
    act = gate * sig
    hidden = (act[:rows] * up[:rows]).astype(BF)
    for at in range(0, width, unit):
        acc_ref[:, at : at + unit] += dot_n(hidden, w_d[:, at : at + unit])
    back = dot_t(cot_ref[...].astype(BF), w_d)
    gate, up, sig, act = gate[rows:], up[rows:], sig[rows:], act[rows:]
    grad_gate = (back * up * sig * (1.0 + gate * (1.0 - sig))).astype(BF)
    grad_up = (back * act).astype(BF)
    grad_ref[...] += dot_t(grad_gate, w_g) + dot_t(grad_up, w_u)

    @pl.when(step == 1)
    def _():
        start_all(rows_copies)
        start_all(line_copies[0])
        local[0].start()

    @pl.when(step == 2 * per)
    def _():
        wait_all(rows_copies)
        whole = rows_buf[place].astype(F32)
        for j in range(QUAD - 1):
            whole = whole + rows_parts[j].astype(F32)
        left_m[...] = whole.astype(BF)

    @pl.when(step == 2 * per + 1)
    def _():
        start_all(line_copies[1])
        local[1].start()

    @pl.when(step == per + 1)
    def _():
        received(route.hop(2, 1))
        start_all(route.hop(2, 2))
        received(route.hop(3, 0))
        start_all(route.hop(3, 1))

    @pl.when(step == 2 * per - 1)
    def _():
        received(route.hop(2, 2))

    @pl.when(step == 2 * per + 2)
    def _():
        received(route.hop(3, 1))
        start_all(route.hop(3, 2))

    @pl.when(step == 3 * per - 1)
    def _():
        received(route.hop(3, 2))

    @pl.when((step + 1 < steps) & ((step + 1) % per == 0))
    def _():
        fetch(step + 1)

    @pl.when(step == steps - 1)
    def _():
        grad, normed = grad_ref[...], normed_ref[...]
        gr2 = (cot_ref[...] + norm_back(grad, normed, inv_ref[:, :1], gain)).astype(BF)
        gr2_ref[...] = gr2
        gatt = dot_t(gr2, wo_ref[...]).astype(BF)
        gatt_ref[...] = gatt[:slots]
        gatt_buf[...] = gatt[slots:]
        vec_ref[...] = jnp.concatenate(
            [jnp.sum(grad * normed, axis=0, keepdims=True), jnp.sum(grad, axis=0, keepdims=True)], axis=0
        )
        start_all(gatt_copies)
        out_ref[...] = acc_ref[:length, :].astype(BF)
        chunk = out_left_ref.shape[1]
        for i in range(2):
            out_left_ref[(i + route.t) % 2] = acc_ref[length + i * chunk : length + (i + 1) * chunk, :].astype(BF)
        sent_all(route.hop(2, 1) + route.hop(2, 2) + route.hop(3, 0) + route.hop(3, 1) + route.hop(3, 2))
        wait_all(gatt_copies)
        whole = gatt_buf[:, pl.ds(pl.multiple_of(place * hw, hw), hw)].astype(F32)
        for j in range(QUAD - 1):
            whole = whole + gatt_parts[j].astype(F32)
        left_gatt_ref[...] = whole.astype(BF)
        wait_all(line_copies[0] + line_copies[1])
        wait_all(local)


def feed_forward(tok, att, left_att, w_out, gain, bias, pick, part_pick, cot, ffn, gathered, n_ten):
    rows, width = tok.shape
    units = ffn[0].shape[1]
    masked = cot.shape[0]
    slots, hw = masked // 2, width // QUAD
    unit = 256
    whole = lambda *shape: pl.BlockSpec(shape, lambda i: (0,) * len(shape))
    low = jax.ShapeDtypeStruct((masked, width), BF)
    return pl.pallas_call(
        functools.partial(feed_kernel, n_ten),
        grid=(n_ten * units // unit,),
        in_specs=[once(x.shape) for x in (tok, att, left_att, w_out)]
        + [once((1, width)), once((1, width)), once(pick.shape), once(part_pick.shape), once(cot.shape)]
        + [any_spec()] * 6,
        out_specs=[whole(*att.shape), whole(2, left_att.shape[0] // 2, width)]
        + [whole(masked, width), whole(masked, width), whole(slots, width), whole(slots, hw)]
        + [whole(2, width)]
        + [any_spec()] * 5,
        out_shape=[
            jax.ShapeDtypeStruct(att.shape, BF), jax.ShapeDtypeStruct((2, left_att.shape[0] // 2, width), BF), low, low,
            jax.ShapeDtypeStruct((slots, width), BF), jax.ShapeDtypeStruct((slots, hw), BF),
            jax.ShapeDtypeStruct((2, width), F32),
            jax.ShapeDtypeStruct((n_ten, slots, width), BF), jax.ShapeDtypeStruct((n_ten, slots // QUAD, width), BF),
        ]
        + [jax.ShapeDtypeStruct(w.shape, BF) for w in gathered],
        input_output_aliases={12: 9, 13: 10, 14: 11},
        scratch_shapes=[
            pltpu.VMEM((rows + masked, width), BF),
            pltpu.VMEM((rows, width), F32),
            pltpu.VMEM((masked, width), F32),
            pltpu.VMEM((masked, LANES), F32),
            pltpu.VMEM((masked, width), F32),
            pltpu.VMEM((2, width, unit), BF),
            pltpu.VMEM((2, width, unit), BF),
            pltpu.VMEM((2, unit, width), BF),
            pltpu.VMEM((QUAD, slots // QUAD, width), BF),
            pltpu.VMEM((QUAD - 1, slots // QUAD, width), BF),
            pltpu.VMEM((slots, width), BF),
            pltpu.VMEM((slots // QUAD, width), BF),
            pltpu.VMEM((slots, width), BF),
            pltpu.VMEM((QUAD - 1, slots, hw), BF),
            pltpu.SemaphoreType.DMA((2, 3)),
            pltpu.SemaphoreType.DMA((2, QUAD - 1)),
            pltpu.SemaphoreType.DMA((2, QUAD - 1)),
            pltpu.SemaphoreType.DMA((2, n_ten - 1)),
            pltpu.SemaphoreType.DMA((2, n_ten - 1)),
            pltpu.SemaphoreType.DMA((2,)),
        ]
        + route_sems(),
        compiler_params=pltpu.CompilerParams(collective_id=5, has_side_effects=True),
        cost_estimate=pl.CostEstimate(
            flops=8 * rows * width * n_ten * units, bytes_accessed=6 * width * n_ten * units, transcendentals=rows * n_ten * units
        ),
        name="feed_forward",
    )(tok, att, left_att, w_out, gain.reshape(1, width), bias.reshape(1, width), pick, part_pick, cot, *ffn, *gathered)[:9]


def feed_grads_kernel(own_ref, left_ref, cot_ref, wg_ref, wu_ref, wd_ref, gg_ref, gu_ref, gd_ref, x_ref):
    @pl.when(pl.program_id(0) == 0)
    def _():
        x_ref[: own_ref.shape[0], :] = own_ref[...]
        x_ref[own_ref.shape[0] :, :] = left_ref[...]

    x, cot = x_ref[...], cot_ref[...]
    gate, up, back = dot_n(x, wg_ref[...]), dot_n(x, wu_ref[...]), dot_t(cot, wd_ref[...])
    sig = jax.nn.sigmoid(gate)
    act = gate * sig
    gg_ref[...] = t_dot((back * up * sig * (1.0 + gate * (1.0 - sig))).astype(BF), x).astype(BF)
    gu_ref[...] = t_dot((back * act).astype(BF), x).astype(BF)
    gd_ref[...] = t_dot((act * up).astype(BF), cot).astype(BF)


def feed_grads(own, left, cot, w_gate, w_up, w_down):
    rows, width = cot.shape
    units = w_gate.shape[1]
    unit = 512
    columns = pl.BlockSpec((width, unit), lambda i: (0, i))
    line = pl.BlockSpec((unit, width), lambda i: (i, 0))
    return pl.pallas_call(
        feed_grads_kernel,
        grid=(units // unit,),
        in_specs=[once(own.shape), once(left.shape), once(cot.shape), columns, columns, line],
        out_specs=[line] * 3,
        out_shape=[jax.ShapeDtypeStruct((units, width), BF)] * 3,
        scratch_shapes=[pltpu.VMEM((rows, width), BF)],
        cost_estimate=pl.CostEstimate(flops=12 * rows * width * units, bytes_accessed=12 * width * units, transcendentals=rows * units),
        name="feed_grads",
    )(own, left, cot, w_gate, w_up, w_down)


def token_back_kernel(
    tok_ref, dq_ref, dk_ref, dv_ref, wq_ref, wk_ref, wv_ref, gain_ref, pick_ref, rows_ref, out_ref, vec_ref
):
    acc = dot_t(dq_ref[...], wq_ref[...]) + dot_t(dk_ref[...], wk_ref[...]) + dot_t(dv_ref[...], wv_ref[...])
    normed, inv_std = layer_stats(tok_ref[...].astype(F32))
    direct = t_dot(pick_ref[...], rows_ref[0])
    out_ref[...] = (direct + norm_back(acc, normed, inv_std, gain_ref[...])).astype(BF)
    sums = jnp.concatenate([jnp.sum(acc * normed, axis=0, keepdims=True), jnp.sum(acc, axis=0, keepdims=True)], axis=0)

    @pl.when(pl.program_id(0) == 0)
    def _():
        vec_ref[...] = sums

    @pl.when(pl.program_id(0) > 0)
    def _():
        vec_ref[...] += sums


def token_back(tok, grads, weights, gain, pick, rows_m):
    rows, width = tok.shape
    slots = pick.shape[0]
    tile = 256
    row = pl.BlockSpec((tile, width), lambda r: (r, 0))
    own = rows // tile - 1
    return pl.pallas_call(
        token_back_kernel,
        grid=(rows // tile,),
        in_specs=[row] * 4
        + [once((width, width))] * 3
        + [
            once((1, width)),
            pl.BlockSpec((slots, tile), lambda r: (0, r)),
            pl.BlockSpec((1, slots, width), lambda r: (r // own, 0, 0)),
        ],
        out_specs=[row, pl.BlockSpec((2, width), lambda r: (0, 0))],
        out_shape=[jax.ShapeDtypeStruct((rows, width), BF), jax.ShapeDtypeStruct((2, width), F32)],
        cost_estimate=pl.CostEstimate(flops=6 * rows * width * width, bytes_accessed=16 * rows * width, transcendentals=0),
        name="token_back",
    )(tok, *grads, *weights, gain.reshape(1, width), pick, rows_m)


def exchange_out_kernel(
    sizes, go_ref, gq_ref, gk_ref, gv_ref, gg_ref, gu_ref, gd_ref, grad_ref, vec_ref, w_ref, ffn_ref, tok_ref, vec_out,
    mine, buf1, buf2, buf3, buf4, vec_buf, vec_sum, mine_sem,
    tok_send, tok_recv, send1, recv1, send2, recv2, send3, recv3, send4, recv4, vec_send, vec_recv, local_sem,
):
    n_seq, n_ten, half, rows = sizes
    dp, sx, t = lax.axis_index("dp"), lax.axis_index("seq"), lax.axis_index("tensor")
    y, c = dp // 2, dp % 2
    me = sx * n_ten + t
    group = n_seq * n_ten
    others = []
    for i in range(1, group):
        g = (me + i) % group
        others.append((g // n_ten, g % n_ten))
    y_peer, c_peer, x_peer = {"dp": (dp + 2) % 4}, {"dp": 2 * y + 1 - c}, {"seq": 1 - sx}
    z_peers = [{"tensor": (t + j) % n_ten} for j in range(1, n_ten)]
    beside = [{"dp": 2 * y + 1 - c, "tensor": (t + j) % n_ten} for j in range(1, n_ten)]
    greet([{"seq": a, "tensor": b} for a, b in others] + [y_peer, c_peer] + beside)
    grads = (go_ref, gq_ref, gk_ref, gv_ref, gg_ref, gu_ref, gd_ref)
    count, attn = len(grads), w_ref.shape[0]
    x_first = (False, False, False, False, False, True, True)
    height = gq_ref.shape[0]
    hw = height // n_ten

    def columns(b_y, b_c, b_x):
        return pl.ds(pl.multiple_of((b_y * 4 + b_c * 2 + b_x) * LANES, LANES), LANES)

    def add_rows(out, first, second):
        def body(i, carry):
            at = pl.ds(pl.multiple_of(i * hw, hw), hw)
            out[at, :] = (first[at, :].astype(F32) + second[at, :].astype(F32)).astype(BF)
            return carry

        lax.fori_loop(0, height // hw, body, 0)

    stage1 = []
    for a in range(count):
        stage1.append(
            [
                remote(
                    grads[a].at[:, columns(b_y, 1 - c, b_x)], buf1.at[a, b_y, b_x],
                    send1.at[a, 2 * b_y + b_x], recv1.at[a, 2 * b_y + b_x], c_peer,
                )
                for b_y in range(2)
                for b_x in range(2)
            ]
        )
    for copies in stage1:
        start_all(copies)
    kept = [
        [
            pltpu.make_async_copy(
                grads[a].at[:, columns(b_y, c, b_x)], mine.at[a, b_y, b_x], mine_sem.at[a, 2 * b_y + b_x]
            )
            for b_y in range(2)
            for b_x in range(2)
        ]
        for a in range(count)
    ]
    for copies in kept:
        start_all(copies)

    vec_hops = []
    hops = [c_peer, x_peer, y_peer]
    vec_sum[0] = vec_ref[...]
    for i, peer in enumerate(hops):
        vec_hops.append([remote(vec_sum.at[i], vec_buf.at[i], vec_send.at[i], vec_recv.at[i], peer)])
    vec_hops.append(
        [
            remote(vec_sum.at[3], vec_buf.at[3 + j], vec_send.at[3 + j], vec_recv.at[3 + j], peer)
            for j, peer in enumerate(z_peers)
        ]
    )
    start_all(vec_hops[0])

    tokens = []
    for i, (a, b) in enumerate(others):
        tokens.append(
            remote(
                grad_ref.at[pl.ds(pl.multiple_of((a * n_ten + b) * rows, rows), rows), :],
                tok_ref.at[sx * half + t],
                tok_send.at[i], tok_recv.at[i], {"seq": a, "tensor": b},
            )
        )
    shared = []
    for i in range(n_seq):
        src, dst = grad_ref.at[pl.ds((group + i) * rows, rows), :], tok_ref.at[t % 2 * half + n_ten]
        shared.append(
            (
                2 * c + i == t,
                remote(
                    src, dst, tok_send.at[group - 1 + i], tok_recv.at[group - 1 + t % 2],
                    {"dp": 2 * y + t // 2, "tensor": 2 * c + i},
                ),
                pltpu.make_async_copy(src, dst, local_sem.at[1]),
            )
        )
    arriving = [
        remote(
            grad_ref.at[pl.ds(0, rows), :], tok_ref.at[i * half + n_ten],
            tok_send.at[group - 1], tok_recv.at[group - 1 + i], c_peer,
        )
        for i in range(n_seq)
    ]
    start_all(tokens)
    for here, away, near in shared:
        pl.when(here)(near.start)
        pl.when(jnp.logical_not(here))(away.start)
    local = [
        pltpu.make_async_copy(
            grad_ref.at[pl.ds(pl.multiple_of(me * rows, rows), rows), :], tok_ref.at[sx * half + t], local_sem.at[0]
        ),
    ]
    start_all(local)

    stage2 = []
    for a in range(count):
        wait_all(kept[a])
        for copy in stage1[a]:
            copy.wait_recv()
        for b_y in range(2):
            for b_x in range(2):
                add_rows(buf1.at[a, b_y, b_x], mine.at[a, b_y, b_x], buf1.at[a, b_y, b_x])
        copies = []
        for b in range(2):
            src, peer = (buf1.at[a, b, 1 - sx], x_peer) if x_first[a] else (buf1.at[a, 1 - y, b], y_peer)
            copies.append(remote(src, buf2.at[a, b], send2.at[a, b], recv2.at[a, b], peer))
        start_all(copies)
        stage2.append(copies)
    vec_hops[0][0].wait_recv()
    vec_sum[1] = vec_sum[0] + vec_buf[0]
    start_all(vec_hops[1])
    stage3, stage4 = {}, {}

    def second(a):
        for copy in stage2[a]:
            copy.wait_recv()
        for b in range(2):
            own = buf1.at[a, b, sx] if x_first[a] else buf1.at[a, y, b]
            add_rows(buf2.at[a, b], own, buf2.at[a, b])
        src, peer = (buf2.at[a, 1 - y], y_peer) if x_first[a] else (buf2.at[a, 1 - sx], x_peer)
        stage3[a] = remote(src, buf3.at[a], send3.at[a], recv3.at[a], peer)
        stage3[a].start()

    def third(a):
        stage3[a].wait_recv()
        own = buf2.at[a, y] if x_first[a] else buf2.at[a, sx]
        if a >= attn:

            def final(i, carry):
                at = pl.ds(pl.multiple_of(i * hw, hw), hw)
                ffn_ref[a - attn, at, :] = own[at, :].astype(F32) + buf3[a, at, :].astype(F32)
                return carry

            lax.fori_loop(0, height // hw, final, 0)
            return
        add_rows(buf3.at[a], own, buf3.at[a])
        stage4[a] = []
        for j, peer in enumerate(z_peers):
            to = (t + 1 + j) % n_ten
            src = buf3.at[a, pl.ds(pl.multiple_of(to * hw, hw), hw), :]
            stage4[a].append(remote(src, buf4.at[a, j], send4.at[a, j], recv4.at[a, j], peer))
        start_all(stage4[a])

    vec_hops[1][0].wait_recv()
    vec_sum[2] = vec_sum[1] + vec_buf[1]
    start_all(vec_hops[2])
    for a in (0, 1, 2, 5, 3, 6):
        second(a)
    third(0)
    third(1)
    second(4)
    for a in (2, 3, 5, 6, 4):
        third(a)
    vec_hops[2][0].wait_recv()
    vec_sum[3] = vec_sum[2] + vec_buf[2]
    start_all(vec_hops[3])
    for n, copies in stage4.items():
        total = buf3[n, pl.ds(pl.multiple_of(t * hw, hw), hw), :].astype(F32)
        for j, copy in enumerate(copies):
            copy.wait_recv()
            total = total + buf4[n, j].astype(F32)
        w_ref[n] = total
    total = vec_sum[3]
    for j, copy in enumerate(vec_hops[3]):
        copy.wait_recv()
        total = total + vec_buf[3 + j]
    vec_out[...] = total
    for copies in stage1 + stage2 + list(stage4.values()) + [list(stage3.values())] + vec_hops:
        for copy in copies:
            copy.wait_send()
    wait_all(local)
    wait_all(tokens)
    for here, away, near in shared:
        pl.when(here)(near.wait)
        pl.when(jnp.logical_not(here))(away.wait_send)
    for i in range(n_seq):
        pl.when(jnp.logical_not(2 * c + i == t))(arriving[i].wait_recv)


def exchange_out(ffn_grads, attn_grads, grad_tok, vectors, n_seq, n_ten, half, rows):
    grads = (*attn_grads, *ffn_grads)
    ffn, attn = len(ffn_grads), len(attn_grads)
    height, width = grads[0].shape
    hw, count, group = height // n_ten, len(grads), n_seq * n_ten
    vmem = pl.BlockSpec(memory_space=pltpu.VMEM)
    dma = pltpu.SemaphoreType.DMA
    hops = 3 + n_ten - 1
    return pl.pallas_call(
        functools.partial(exchange_out_kernel, (n_seq, n_ten, half, rows)),
        in_specs=[any_spec()] * (count + 1) + [vmem],
        out_specs=[vmem, vmem, any_spec(), vmem],
        out_shape=[
            jax.ShapeDtypeStruct((attn, hw, LANES), F32),
            jax.ShapeDtypeStruct((ffn, height, LANES), F32),
            jax.ShapeDtypeStruct((n_seq * half, rows, width), BF),
            jax.ShapeDtypeStruct(vectors.shape, F32),
        ],
        scratch_shapes=[
            pltpu.VMEM((count, 2, 2, height, LANES), BF),
            pltpu.VMEM((count, 2, 2, height, LANES), BF),
            pltpu.VMEM((count, 2, height, LANES), BF),
            pltpu.VMEM((count, height, LANES), BF),
            pltpu.VMEM((attn, n_ten - 1, hw, LANES), BF),
            pltpu.VMEM((hops,) + vectors.shape, F32),
            pltpu.VMEM((4,) + vectors.shape, F32),
            dma((count, 4)),
            dma((group + 1,)), dma((group + 1,)),
            dma((count, 4)), dma((count, 4)),
            dma((count, 2)), dma((count, 2)),
            dma((count,)), dma((count,)),
            dma((attn, n_ten - 1)), dma((attn, n_ten - 1)),
            dma((hops,)), dma((hops,)),
            dma((2,)),
        ],
        compiler_params=pltpu.CompilerParams(collective_id=4, has_side_effects=True),
        name="exchange_out",
    )(*grads, grad_tok, vectors)


def rotary_lanes(cosine, sine):
    reps = LANES // HEAD_DIM
    return jnp.concatenate([cosine, cosine] * reps, axis=1), jnp.concatenate([-sine, sine] * reps, axis=1)


def position_tables(length):
    half_dim = HEAD_DIM // 2
    inv_freq = np.float32(10000.0) ** (-np.arange(half_dim, dtype=np.float32) * np.float32(2.0 / HEAD_DIM))
    angles = (np.arange(length, dtype=np.float32)[:, None] * inv_freq[None, :]).astype(np.float64)
    cosine, sine = np.cos(angles).astype(np.float32), np.sin(angles).astype(np.float32)
    reps = LANES // HEAD_DIM
    return np.concatenate([cosine, cosine] * reps, axis=1), np.concatenate([-sine, sine] * reps, axis=1)


def window_shards(
    tokens,
    norm1_gain,
    norm1_bias,
    w_query,
    w_key,
    w_value,
    w_out,
    norm2_gain,
    norm2_bias,
    w_gate,
    w_up,
    w_down,
    out_grad,
    masked_rows,
    window_counts,
):
    rows_local, windows, width = tokens.shape
    n_dp, n_seq, n_ten = lax.axis_size("dp"), lax.axis_size("seq"), lax.axis_size("tensor")
    dp_index, seq_index, ten_index = lax.axis_index("dp"), lax.axis_index("seq"), lax.axis_index("tensor")
    shard_index = dp_index * n_seq + seq_index
    core = dp_index % 2
    place = seq_index * 2 + core
    half = windows // n_seq
    length = rows_local * n_seq * n_ten
    share = length // QUAD
    hw = width // QUAD
    slots = masked_rows.shape[1]
    part = slots // QUAD

    live = jnp.arange(windows) < window_counts[0]
    valid = (masked_rows < length) & live[:, None]
    coded = jnp.where(valid, masked_rows, length)
    info = jnp.concatenate([coded, jnp.full((1, slots), jnp.sum(valid.astype(jnp.int32)))], axis=0)
    info = jnp.pad(info, ((0, -(windows + 1) % 8), (0, -slots % LANES)))
    both_tok, all_q, all_k, all_v, all_out, infos, left_grad = exchange_in(
        jnp.swapaxes(tokens, 0, 1), w_query, w_key, w_value, w_out, info, out_grad, n_dp, n_seq, n_ten
    )
    loss_weight = LOSS_SCALE / jnp.sum(infos[:, windows, 0]).astype(F32)
    pick_one = lambda x, at: lax.dynamic_index_in_dim(x, at, 0, keepdims=False)
    first_window = seq_index * half
    my_coded = lax.dynamic_slice_in_dim(coded, first_window, n_ten, 0)
    my_grad = lax.dynamic_slice_in_dim(out_grad, first_window, n_ten, 0)
    pair_infos = lax.dynamic_slice_in_dim(infos, dp_index - core, 2, 0)
    left_coded = jnp.stack([pair_infos[i // n_seq, i % n_seq * half + n_ten, :slots] for i in range(n_ten)])
    weigh = lambda grad, rows: jnp.where((rows < length)[..., None], grad.astype(F32) * loss_weight, 0.0)

    own_rows, left_rows = pick_one(my_coded, ten_index), pick_one(left_coded, ten_index)
    every = jnp.arange(length)
    my_left = place * share + jnp.arange(share)
    own_pick = (own_rows[:, None] == every[None, :]).astype(BF)
    left_pick = (left_rows[:, None] == every[None, :]).astype(BF)
    part_match = left_rows[:, None] == my_left[None, :]
    part_pick = part_match.astype(BF)
    left_here = jnp.where(jnp.any(part_match, axis=1), left_rows, length)
    my_cot = jnp.concatenate(
        [weigh(pick_one(my_grad, ten_index), own_rows), weigh(pick_one(left_grad, ten_index), left_here)], axis=0
    )

    tables = [jnp.asarray(x) for x in position_tables(length)]
    part_tables = [lax.dynamic_slice_in_dim(x, place * share, share, 0) for x in tables]
    own_tables = tables + list(rotary_lanes(*rotary_tables(own_rows)))
    left_tables = tables + list(rotary_lanes(*rotary_tables(left_rows)))

    ffn = (w_gate, w_up, w_down)
    first, q, k, v = norm_qkv(both_tok, norm1_gain, norm1_bias, all_q, all_k, all_v, tables, part_tables)
    own_att, left_q, left_k, left_v, *gathered = attend_swap(q, k, v, ffn, length, n_ten)
    left_att_part, *gathered = attend_left(left_q, left_k, left_v, gathered, n_ten)
    own_out, left_chunks, att_m, gr2, own_gatt, left_gatt, grad_norm2, all_own, all_left = feed_forward(
        both_tok, own_att, left_att_part, all_out, norm2_gain, norm2_bias, own_pick, part_pick, my_cot, ffn, gathered, n_ten
    )

    grad_w_out = t_dot(att_m, gr2).astype(BF)
    left_back = back_left(left_q, left_gatt, left_k, left_v, left_pick, left_tables)
    dq, dk, dv = back_swap(q, own_gatt, k, v, own_pick, own_tables, left_back)
    all_own, dq, dk, dv, own_out, left_chunks = lax.optimization_barrier((all_own, dq, dk, dv, own_out, left_chunks))

    part_of = lambda x: lax.dynamic_slice_in_dim(x, place * part, part, 1)
    down_in = jnp.concatenate(
        [
            weigh(my_grad, my_coded).reshape(n_ten * slots, width),
            weigh(part_of(left_grad), part_of(left_coded)).reshape(n_ten * part, width),
        ],
        axis=0,
    ).astype(BF)
    grad_w_ffn = feed_grads(all_own.reshape(-1, width), all_left.reshape(-1, width), down_in, *ffn)
    grad_w_attn = [grad_w_out] + [t_dot(d, first).astype(BF) for d in (dq, dk, dv)]
    grad_both, grad_norm1 = token_back(
        both_tok, (dq, dk, dv), (all_q, all_k, all_v), norm1_gain,
        jnp.concatenate([own_pick, part_pick], axis=1), gr2.reshape(2, slots, width),
    )

    own_out = lax.all_to_all(
        own_out.reshape(n_seq * n_ten, rows_local, width), ("seq", "tensor"), 0, 0, tiled=True
    ).reshape(n_seq, n_ten, rows_local, width)
    left_out = []
    for turn in range(2):
        perm = []
        for d in range(n_dp):
            for sx in range(n_seq):
                for p in range(n_ten):
                    to = d // 2 * 2 + p // 2, sx, d % 2 * 2 + (p % 2 ^ turn)
                    perm.append(((d * n_seq + sx) * n_ten + p, (to[0] * n_seq + to[1]) * n_ten + to[2]))
        left_out.append(lax.ppermute(left_chunks[turn], ("dp", "seq", "tensor"), perm))
    even = ten_index % 2 == 0
    left_out = jnp.stack([jnp.where(even, left_out[0], left_out[1]), jnp.where(even, left_out[1], left_out[0])])
    output = jnp.concatenate([own_out, left_out[:, None]], axis=1).reshape(windows, rows_local, width)
    output = jnp.swapaxes(output, 0, 1)
    vectors = jnp.concatenate(
        [grad_norm1, grad_norm2, jnp.zeros((4, width), F32)], axis=0
    )
    gw_attn, gw_ffn, grad_tokens, vectors = exchange_out(
        grad_w_ffn, grad_w_attn, grad_both, vectors, n_seq, n_ten, half, rows_local
    )
    grad_tokens = jnp.swapaxes(grad_tokens, 0, 1).astype(F32)
    small = width // (n_dp * n_seq * n_ten)
    vectors = lax.dynamic_slice_in_dim(vectors, (shard_index * n_ten + ten_index) * small, small, 1)

    return (
        output,
        grad_tokens,
        vectors[0],
        vectors[1],
        gw_attn[1].T,
        gw_attn[2].T,
        gw_attn[3].T,
        gw_attn[0],
        vectors[2],
        vectors[3],
        gw_ffn[0].T,
        gw_ffn[1].T,
        gw_ffn[2],
    )


def shards(tokens, *rest):
    n_dp, n_seq, n_ten = lax.axis_size("dp"), lax.axis_size("seq"), lax.axis_size("tensor")
    whole = n_dp == 4 and n_seq == 2 and n_ten == 4 and tokens.shape[1] == n_seq * (n_ten + 1)
    return (window_shards if whole else block_shards)(tokens, *rest)


def solution(mesh):
    return jax.shard_map(
        shards,
        mesh=mesh,
        in_specs=(
            P(("seq", "tensor"), "dp", None),
            P(),
            P(),
            P(None, "tensor"),
            P(None, "tensor"),
            P(None, "tensor"),
            P("tensor", None),
            P(),
            P(),
            P(None, "tensor"),
            P(None, "tensor"),
            P("tensor", None),
            P("dp", None, None),
            P("dp", None),
            P("dp"),
        ),
        out_specs=(
            P(("seq", "tensor"), "dp", None),
            P(("seq", "tensor"), "dp", None),
            P(("dp", "seq", "tensor")),
            P(("dp", "seq", "tensor")),
            P(("dp", "seq"), "tensor"),
            P(("dp", "seq"), "tensor"),
            P(("dp", "seq"), "tensor"),
            P("tensor", ("dp", "seq")),
            P(("dp", "seq", "tensor")),
            P(("dp", "seq", "tensor")),
            P(("dp", "seq"), "tensor"),
            P(("dp", "seq"), "tensor"),
            P("tensor", ("dp", "seq")),
        ),
        check_vma=False,
    )
```
